32 devices in a mesh: section: 2 (over core), shard: 2 (over x), replica: 8 (over z, y).
Axes of the slice: x: 2, y: 2, z: 4, core: 2. Of those that a mesh axis runs over, the one named last changes fastest.
Arguments:
- tokens: bfloat16 [8, 2, 512, 1024], P('replica', None, 'shard'), may hold values from -6 to 6
- cotangent: bfloat16 [8, 2, 512, 1024], P('replica', None, 'shard'), may hold values from -6 to 6
- attn_gain: bfloat16 [2, 1024], P('section', 'shard'), may hold values from 0.25 to 1.75
- attn_shift: bfloat16 [2, 1024], P('section', 'shard'), may hold values from -3 to 3
- qkv_weight: bfloat16 [2, 1024, 3072], P('section', 'shard'), may hold values from -0.1875 to 0.1875
- query_bias: bfloat16 [2, 1024], P('section', 'shard'), may hold values from -3 to 3
- value_bias: bfloat16 [2, 1024], P('section', 'shard'), may hold values from -0.59765625 to 0.59765625
- out_weight: bfloat16 [2, 1024, 1024], P('section', 'shard'), may hold values from -1 to 1
- out_bias: bfloat16 [2, 1024], P('section', 'shard'), may hold values from -1.796875 to 1.796875
- mlp_gain: bfloat16 [2, 1024], P('section', 'shard'), may hold values from 0.25 to 1.75
- mlp_shift: bfloat16 [2, 1024], P('section', 'shard'), may hold values from -3 to 3
- fc_weight: bfloat16 [2, 1024, 4096], P('section', 'shard'), may hold values from -0.1875 to 0.1875
- fc_bias: bfloat16 [2, 4096], P('section', 'shard'), may hold values from -3 to 3
- proj_weight: bfloat16 [2, 4096, 1024], P('section', 'shard'), may hold values from -0.09375 to 0.09375
- proj_bias: bfloat16 [2, 1024], P('section', 'shard'), may hold values from -1.796875 to 1.796875
Outputs:
- activations: bfloat16 [2, 8, 2, 512, 1024], P('section', 'replica', None, 'shard')
- input_grads: bfloat16 [2, 8, 2, 512, 1024], P('section', 'replica', None, 'shard')
- attn_gain_grad: float32 [2, 1024], P('section', 'shard')
- attn_shift_grad: float32 [2, 1024], P('section', 'shard')
- qkv_weight_grad: float32 [2, 1024, 3072], P('section', 'shard')
- query_bias_grad: float32 [2, 1024], P('section', 'shard')
- value_bias_grad: float32 [2, 1024], P('section', 'shard')
- out_weight_grad: float32 [2, 1024, 1024], P('section', 'shard')
- out_bias_grad: float32 [2, 1024], P('section', 'shard')
- mlp_gain_grad: float32 [2, 1024], P('section', 'shard')
- mlp_shift_grad: float32 [2, 1024], P('section', 'shard')
- fc_weight_grad: float32 [2, 1024, 4096], P('section', 'shard')
- fc_bias_grad: float32 [2, 4096], P('section', 'shard')
- proj_weight_grad: float32 [2, 4096, 1024], P('section', 'shard')
- proj_bias_grad: float32 [2, 1024], P('section', 'shard')
The draws below stay inside these ranges and needn't reach their ends.
All inputs are finite; a program needn't handle non-finite values.
Results may differ from the reference program's by a relative error of at most 0.023.
Values may be sent and summed in bfloat16 or wider, within the bound.
A program may use at most 320 MiB of HBM per device.

```python
import jax
import jax.numpy as jnp
from jax import lax

D = 1024
HEADS = 16
HEAD_DIM = 64
FF = 4096
MB = 2
LAYERS = 2
BLOCK = 512
SEQS = 8


def levels(rng, dims, pieces, low, top_value):
    def one(position, parts):
        draws = jax.random.uniform(jax.random.fold_in(jax.random.fold_in(rng, 6), position), (parts,), jnp.float32, low / len(pieces), top_value / len(pieces))
        return jnp.repeat(jnp.exp(draws), dims[position] // parts).reshape((-1,) + (1,) * (len(dims) - position - 1))

    loudness = one(*pieces[0])
    for cut in pieces[1:]:
        loudness = loudness * one(*cut)
    return loudness


def normal_values(stream_key, dims, spread, most, pieces=(), kind=jnp.bfloat16):
    entries = jax.random.normal(stream_key, dims, jnp.float32) * spread
    if len(pieces) > 0:
        entries = levels(stream_key, dims, pieces, -0.22, 0.18) * entries
    return jnp.clip(entries, min=-most, max=most).astype(kind)


def setup_inputs(seed: int = 0) -> dict:
    key_of = jax.random.split(jax.random.key(seed), 16)
    tokens = normal_values(key_of[0], (SEQS, MB, BLOCK, D), 1.0, 6.0, ((0, 8), (2, 2)))
    cotangent = normal_values(key_of[1], (SEQS, MB, BLOCK, D), 1.0, 6.0, ((0, 8), (2, 2)))
    attn_gain = jnp.clip(1.0 + 0.15 * jax.random.normal(key_of[2], (LAYERS, D), jnp.float32), 0.25, 1.75).astype(jnp.bfloat16)
    attn_shift = normal_values(key_of[3], (LAYERS, D), 0.5, 3.0, ((0, 2), (1, 2)))
    qkv_weight = normal_values(key_of[4], (LAYERS, D, 3 * D), D ** -0.5, 0.1875, ((0, 2), (1, 2)))
    query_bias = normal_values(key_of[5], (LAYERS, D), 0.5, 3.0, ((0, 2), (1, 2)))
    value_bias = normal_values(key_of[6], (LAYERS, D), 0.1, 0.59765625, ((0, 2), (1, 2)))
    out_weight = normal_values(key_of[7], (LAYERS, D, D), (D // 32) ** -0.5, 1.0, ((0, 2), (1, 2)))
    out_bias = normal_values(key_of[8], (LAYERS, D), 0.3, 1.796875, ((0, 2), (1, 2)))
    mlp_gain = jnp.clip(1.0 + 0.15 * jax.random.normal(key_of[9], (LAYERS, D), jnp.float32), 0.25, 1.75).astype(jnp.bfloat16)
    mlp_shift = normal_values(key_of[10], (LAYERS, D), 0.5, 3.0, ((0, 2), (1, 2)))
    fc_weight = normal_values(key_of[11], (LAYERS, D, FF), D ** -0.5, 0.1875, ((0, 2), (1, 2)))
    fc_bias = normal_values(key_of[12], (LAYERS, FF), 0.5, 3.0, ((0, 2), (1, 2)))
    proj_weight = normal_values(key_of[13], (LAYERS, FF, D), FF ** -0.5, 0.09375, ((0, 2), (1, 2)))
    proj_bias = normal_values(key_of[14], (LAYERS, D), 0.3, 1.796875, ((0, 2), (1, 2)))
    return {"tokens": tokens, "cotangent": cotangent, "attn_gain": attn_gain, "attn_shift": attn_shift, "qkv_weight": qkv_weight, "query_bias": query_bias, "value_bias": value_bias, "out_weight": out_weight, "out_bias": out_bias, "mlp_gain": mlp_gain, "mlp_shift": mlp_shift, "fc_weight": fc_weight, "fc_bias": fc_bias, "proj_weight": proj_weight, "proj_bias": proj_bias}


HIGH = lax.Precision.HIGHEST
EPSILON = 1e-05
GELU_SCALE = 0.7978845608028654
GELU_CUBIC = 0.044715

@jax.custom_vjp
def low(v):
    return lax.optimization_barrier(v.astype(jnp.bfloat16)).astype(jnp.float32)

@jax.custom_vjp
def low_back(v):
    return v

def low_keep(v):
    return (low(v), None)

def low_pass(kept, grad):
    return (grad,)

def back_keep(v):
    return (v, None)

def back_low(kept, grad):
    return (low(grad),)
low.defvjp(low_keep, low_pass)
low_back.defvjp(back_keep, back_low)

def norm(inputs, gain, shift):
    mean = lax.optimization_barrier(jnp.mean(inputs, axis=-1, keepdims=True))
    centered = inputs - mean
    variance = lax.optimization_barrier(jnp.mean(centered * centered, axis=-1, keepdims=True))
    return centered * lax.rsqrt(variance + EPSILON) * gain + shift

def gelu(pre):
    return 0.5 * pre * (1.0 + jnp.tanh(GELU_SCALE * (pre + GELU_CUBIC * pre * pre * pre)))

def layer(inputs, weights):
    attn_gain, attn_shift, qkv_weight, query_bias, value_bias, out_weight, out_bias, mlp_gain, mlp_shift, fc_weight, fc_bias, proj_weight, proj_bias = weights
    length = inputs.shape[0]
    scale = HEAD_DIM ** (-0.5)
    normed1 = low(norm(inputs, attn_gain, attn_shift))
    qkv = jnp.dot(normed1, qkv_weight, precision=HIGH)
    query = low_back(low(qkv[:, :D] + query_bias)).reshape(length, HEADS, HEAD_DIM)
    keys = low_back(low(qkv[:, D:2 * D])).reshape(length, HEADS, HEAD_DIM)
    values = low_back(low(qkv[:, 2 * D:] + value_bias)).reshape(length, HEADS, HEAD_DIM)
    scores = low_back(jnp.einsum('qhe,khe->hqk', query, keys, precision=HIGH) * scale)
    positions = jnp.arange(length, dtype=jnp.int32)
    allowed = positions[None, :] <= positions[:, None]
    scores = jnp.where(allowed[None], scores, -jnp.inf)
    top = lax.optimization_barrier(jnp.max(scores, axis=-1, keepdims=True))
    expo = jnp.exp(scores - top)
    probs = low_back(low(expo / lax.optimization_barrier(jnp.sum(expo, axis=-1, keepdims=True))))
    mixed = jnp.einsum('hqk,khe->qhe', probs, values, precision=HIGH).reshape(length, D)
    mixed = low_back(low(mixed))
    attn = low_back(jnp.dot(mixed, out_weight, precision=HIGH) + out_bias)
    hidden = inputs + attn
    normed2 = low(norm(hidden, mlp_gain, mlp_shift))
    pre = low_back(jnp.dot(normed2, fc_weight, precision=HIGH) + fc_bias)
    act = low(gelu(pre))
    branch = low_back(jnp.dot(act, proj_weight, precision=HIGH) + proj_bias)
    return hidden + branch

def reference(tokens, cotangent, attn_gain, attn_shift, qkv_weight, query_bias, value_bias, out_weight, out_bias, mlp_gain, mlp_shift, fc_weight, fc_bias, proj_weight, proj_bias):
    params = tuple((item.astype(jnp.float32) for item in (attn_gain, attn_shift, qkv_weight, query_bias, value_bias, out_weight, out_bias, mlp_gain, mlp_shift, fc_weight, fc_bias, proj_weight, proj_bias)))
    first_layer = tuple((item[0] for item in params))
    second_layer = tuple((item[1] for item in params))

    def model(inputs, early, late, offset_term):
        middle = low_back(low(layer(inputs, early)))
        return (middle, layer(middle + offset_term, late))

    def visit(totals, item):
        shape = item[0].shape
        inputs = item[0].astype(jnp.float32).reshape(-1, shape[-1])
        grad_top = item[1].astype(jnp.float32).reshape(-1, shape[-1])
        blank = jnp.zeros_like(inputs)
        (middle, final), pull = jax.vjp(model, inputs, first_layer, second_layer, blank)
        d_inputs, d_early, d_late, d_middle = pull((jnp.zeros_like(middle), grad_top))
        early_total = tuple((a + b for a, b in zip(totals[0], d_early)))
        late_total = tuple((a + b for a, b in zip(totals[1], d_late)))
        results = (middle.reshape(shape).astype(jnp.bfloat16), final.reshape(shape).astype(jnp.bfloat16), d_inputs.reshape(shape).astype(jnp.bfloat16), d_middle.reshape(shape).astype(jnp.bfloat16))
        return ((early_total, late_total), results)
    start = (tuple((jnp.zeros_like(item) for item in first_layer)), tuple((jnp.zeros_like(item) for item in second_layer)))
    (early_sum, late_sum), (middles, finals, d_tokens, d_middles) = lax.scan(visit, start, (tokens, cotangent))
    activations = jnp.stack([middles, finals])
    input_grads = jnp.stack([d_tokens, d_middles])
    grads = [jnp.stack([a, b]) for a, b in zip(early_sum, late_sum)]
    return (activations, input_grads, grads[0], grads[1], grads[2], grads[3], grads[4], grads[5], grads[6], grads[7], grads[8], grads[9], grads[10], grads[11], grads[12])
```

```python
import functools

import jax
import jax.numpy as jnp
from jax import lax
from jax.experimental import pallas as pl
from jax.experimental.pallas import tpu as pltpu
from jax.sharding import PartitionSpec as P

HEAD_DIM = 64
EPSILON = 1e-05
GELU_SCALE = 0.7978845608028654
GELU_CUBIC = 0.044715
ROWS_CONTRACT = (((0,), (0,)), ((), ()))
COLS_CONTRACT = (((1,), (1,)), ((), ()))
BF = jnp.bfloat16
F32 = jnp.float32
MESH = pl.DeviceIdType.MESH
QTILE = 256
VMEM_LIMIT = 56 * 1024 * 1024

CROSS_SAME = [(1, 0), (2, 3)]
CROSS_SWAP = [(1, 2), (2, 1)]
CORE_OUT = [(0, 2), (3, 1)]
CORE_IN = [(1, 3), (2, 0)]
CROSS_BACK = [(0, 1), (3, 2)]
PAIR = ("section", "shard")


def rows_product(left, right):
    return lax.dot_general(left, right, ROWS_CONTRACT, preferred_element_type=F32)


def cols_product(left, right):
    return lax.dot_general(left, right, COLS_CONTRACT, preferred_element_type=F32)


def core_swap(value):
    return lax.ppermute(value, "section", [(0, 1), (1, 0)])


def replica_swap(value):
    size = lax.axis_size("replica")
    return lax.ppermute(value, "replica", [(i, i ^ 1) for i in range(size)])


def ordered(flag, first, second, axis):
    return jnp.concatenate(
        [jnp.where(flag, first, second), jnp.where(flag, second, first)], axis=axis
    )


def norm_parts(inputs):
    mean = jnp.mean(inputs, axis=-1, keepdims=True)
    centered = inputs - mean
    inverse = lax.rsqrt(jnp.mean(centered * centered, axis=-1, keepdims=True) + EPSILON)
    return centered * inverse, inverse


def norm_backward(d_normed, scaled, inverse, gain):
    d_scaled = d_normed * gain
    return inverse * (
        d_scaled
        - jnp.mean(d_scaled, axis=-1, keepdims=True)
        - scaled * jnp.mean(d_scaled * scaled, axis=-1, keepdims=True)
    )


def gelu_pair(pre):
    tangent = jnp.tanh(GELU_SCALE * (pre + GELU_CUBIC * pre * pre * pre))
    value = 0.5 * pre * (1.0 + tangent)
    slope = 0.5 * (1.0 + tangent) + 0.5 * pre * (1.0 - tangent * tangent) * GELU_SCALE * (
        1.0 + 3.0 * GELU_CUBIC * pre * pre
    )
    return value, slope


def head_parts(pair):
    low = lax.broadcasted_iota(jnp.int32, pair.shape, 1) < HEAD_DIM
    zero = jnp.zeros_like(pair)
    return jnp.where(low, pair, zero), jnp.where(low, zero, pair)


def masked_scores(keys, query, length):
    scores = cols_product(keys, query)
    tail = scores[length - QTILE :]
    key_pos = lax.broadcasted_iota(jnp.int32, tail.shape, 0)
    query_pos = lax.broadcasted_iota(jnp.int32, tail.shape, 1)
    tail = jnp.where(key_pos <= query_pos, tail, -1e30)
    if length == QTILE:
        return tail
    return jnp.concatenate([scores[: length - QTILE], tail], axis=0)


def attend_kernel(block_ref, q_ref, k_ref, v_ref, out_ref, lse_ref):
    block = block_ref[0]
    rows = q_ref.shape[0]
    for index in range(k_ref.shape[0] // rows):

        @pl.when(block == index)
        def _(index=index):
            for tile in range(rows // QTILE):
                span = pl.ds(tile * QTILE, QTILE)
                length = index * rows + (tile + 1) * QTILE
                keys = k_ref[:length, :]
                values = v_ref[:length, :]
                mixed = []
                for head, part in enumerate(head_parts(q_ref[span, :])):
                    scores = masked_scores(keys, part * BF(HEAD_DIM**-0.5), length)
                    top = jnp.max(scores, axis=0, keepdims=True)
                    probs = jnp.exp(scores - top)
                    total = jnp.sum(probs, axis=0, keepdims=True)
                    lse_ref[0, pl.ds(head, 1), span] = top + jnp.log(total)
                    piece = rows_product(values, probs.astype(BF))
                    piece = piece[head * HEAD_DIM : (head + 1) * HEAD_DIM]
                    mixed.append(piece * (1.0 / total))
                mixed = jnp.concatenate(mixed, axis=0)
                out_ref[span, :] = jnp.transpose(mixed).astype(BF)


def attend(block, query, keys, values):
    rows, width = query.shape
    pairs = width // 128
    total = keys.shape[0]
    return pl.pallas_call(
        attend_kernel,
        grid_spec=pltpu.PrefetchScalarGridSpec(
            num_scalar_prefetch=1,
            grid=(pairs,),
            in_specs=[
                pl.BlockSpec((rows, 128), lambda i, b: (0, i)),
                pl.BlockSpec((total, 128), lambda i, b: (0, i)),
                pl.BlockSpec((total, 128), lambda i, b: (0, i)),
            ],
            out_specs=[
                pl.BlockSpec((rows, 128), lambda i, b: (0, i)),
                pl.BlockSpec((1, 8, rows), lambda i, b: (i, 0, 0)),
            ],
        ),
        out_shape=[
            jax.ShapeDtypeStruct((rows, width), BF),
            jax.ShapeDtypeStruct((pairs, 8, rows), F32),
        ],
        compiler_params=pltpu.CompilerParams(vmem_limit_bytes=VMEM_LIMIT),
        cost_estimate=pl.CostEstimate(
            flops=4 * rows * total * width, bytes_accessed=4 * total * width, transcendentals=0
        ),
        name="attend",
    )(block, query, keys, values)


def attend_back_kernel(
    block_ref,
    q_ref,
    k_ref,
    v_ref,
    o_ref,
    do_ref,
    lse_ref,
    pend_k_ref,
    pend_v_ref,
    dq_ref,
    dk_ref,
    dv_ref,
    new_k_ref,
    new_v_ref,
    sum_k,
    sum_v,
):
    block = block_ref[0]
    rows = q_ref.shape[0]
    scale = HEAD_DIM**-0.5
    for index in range(k_ref.shape[0] // rows):

        @pl.when(block == index)
        def _(index=index):
            end = (index + 1) * rows
            if index == 0:
                sum_k[:rows, :] = pend_k_ref[...]
                sum_v[:rows, :] = pend_v_ref[...]
            else:
                sum_k[:end, :] = jnp.zeros((end, 128), F32)
                sum_v[:end, :] = jnp.zeros((end, 128), F32)
            for tile in range(rows // QTILE):
                span = pl.ds(tile * QTILE, QTILE)
                length = index * rows + (tile + 1) * QTILE
                keys = k_ref[:length, :]
                values = v_ref[:length, :]
                grads = do_ref[span, :]
                products = jnp.transpose(grads.astype(F32) * o_ref[span, :].astype(F32))
                queries = head_parts(q_ref[span, :])
                grads = head_parts(grads)
                d_query = []
                d_keys = d_values = None
                for head in range(2):
                    take = slice(head * HEAD_DIM, (head + 1) * HEAD_DIM)
                    query = queries[head] * BF(scale)
                    scores = masked_scores(keys, query, length)
                    weights = jnp.exp(scores - lse_ref[0, pl.ds(head, 1), span])
                    d_probs = cols_product(values, grads[head])
                    delta = jnp.sum(products[take], axis=0, keepdims=True)
                    d_scores = (weights * (d_probs - delta)).astype(BF)
                    d_value = jnp.dot(weights.astype(BF), grads[head], preferred_element_type=F32)
                    d_key = jnp.dot(d_scores, query, preferred_element_type=F32)
                    d_values = d_value if head == 0 else d_values + d_value
                    d_keys = d_key if head == 0 else d_keys + d_key
                    d_query.append(rows_product(keys, d_scores)[take])
                sum_k[:length, :] += d_keys
                sum_v[:length, :] += d_values
                d_query = jnp.concatenate(d_query, axis=0) * scale
                dq_ref[span, :] = jnp.transpose(d_query).astype(BF)
            dk_ref[...] = sum_k[index * rows : end, :].astype(BF)
            dv_ref[...] = sum_v[index * rows : end, :].astype(BF)
            if index == 0:
                new_k_ref[...] = pend_k_ref[...]
                new_v_ref[...] = pend_v_ref[...]
            else:
                new_k_ref[...] = sum_k[:rows, :]
                new_v_ref[...] = sum_v[:rows, :]


def attend_back(block, query, keys, values, mixed, d_mixed, lse, pending):
    rows, width = query.shape
    pairs = width // 128
    total = keys.shape[0]
    assert total == 2 * rows
    small = pl.BlockSpec((rows, 128), lambda i, b: (0, i))
    large = pl.BlockSpec((total, 128), lambda i, b: (0, i))
    low = jax.ShapeDtypeStruct((rows, width), BF)
    wide = jax.ShapeDtypeStruct((rows, width), F32)
    return pl.pallas_call(
        attend_back_kernel,
        grid_spec=pltpu.PrefetchScalarGridSpec(
            num_scalar_prefetch=1,
            grid=(pairs,),
            in_specs=[
                small,
                large,
                large,
                small,
                small,
                pl.BlockSpec((1, 8, rows), lambda i, b: (i, 0, 0)),
                small,
                small,
            ],
            out_specs=[small] * 5,
            scratch_shapes=[pltpu.VMEM((total, 128), F32), pltpu.VMEM((total, 128), F32)],
        ),
        out_shape=[low, low, low, wide, wide],
        compiler_params=pltpu.CompilerParams(vmem_limit_bytes=VMEM_LIMIT),
        cost_estimate=pl.CostEstimate(
            flops=10 * rows * total * width, bytes_accessed=8 * total * width, transcendentals=0
        ),
        name="attend_back",
    )(block, query, keys, values, mixed, d_mixed, lse, *pending)


def ring_place(size):
    index = lax.axis_index("replica")
    odd = index % 2
    half = index // 2
    place = (1 - odd) * half + odd * (size - 1 - half)

    def device(spot):
        upper = spot // (size // 2)
        return (1 - upper) * (2 * spot) + upper * (2 * (size - 1 - spot) + 1)

    return place, device((place + 1) % size), device((place + size - 1) % size)


def ring_barrier(following, previous):
    barrier = pltpu.get_barrier_semaphore()
    for neighbour in (following, previous):
        pl.semaphore_signal(barrier, inc=1, device_id={"replica": neighbour}, device_id_type=MESH)
    pl.semaphore_wait(barrier, 2)


def scatter_kernel(size, count, *refs):
    own, out, landed = refs[:count], refs[count : 2 * count], refs[2 * count : 3 * count]
    send_sem, recv_sem = refs[3 * count :]
    place, following, previous = ring_place(size)
    targets = (following, previous)
    ring_barrier(following, previous)

    def send(way, item, source, slot):
        return pltpu.make_async_remote_copy(
            src_ref=source,
            dst_ref=landed[item].at[way, slot],
            send_sem=send_sem.at[way, item, slot],
            recv_sem=recv_sem.at[way, item, slot],
            device_id={"replica": targets[way]},
            device_id_type=MESH,
        )

    def chunk_of(way, slot):
        if way == 0:
            return (place + 2 * size - 2 - slot) % size
        return (place + 2 + slot) % size

    for item in range(count):
        send(0, item, own[item].at[0, (place + size - 1) % size], 0).start()
        send(1, item, own[item].at[1, (place + 1) % size], 0).start()

    def step(slot, carry):
        for item in range(count):
            for way in range(2):
                here = landed[item].at[way, slot]
                send(way, item, here, slot).wait_recv()
                here[...] += own[item][way, chunk_of(way, slot)]
                send(way, item, here, slot + 1).start()
        return carry

    lax.fori_loop(0, size - 2, step, 0)
    last = size - 2
    for item in range(count):
        for way in range(2):
            here = landed[item].at[way, last]
            send(way, item, here, last).wait_recv()
            out[item][way] = here[...] + own[item][way, place]

    def finish(slot, carry):
        for item in range(count):
            for way in range(2):
                send(way, item, landed[item].at[way, slot], slot).wait_send()
        return carry

    lax.fori_loop(0, size - 1, finish, 0)


def ring_scatter(pieces):
    size = pieces[0].shape[1]
    count = len(pieces)
    whole = pl.BlockSpec(memory_space=pltpu.VMEM)
    return pl.pallas_call(
        functools.partial(scatter_kernel, size, count),
        out_shape=[jax.ShapeDtypeStruct((2,) + item.shape[2:], BF) for item in pieces],
        in_specs=[whole] * count,
        out_specs=[whole] * count,
        scratch_shapes=[pltpu.VMEM((2, size - 1) + item.shape[2:], BF) for item in pieces]
        + [pltpu.SemaphoreType.DMA((2, count, size - 1))] * 2,
        compiler_params=pltpu.CompilerParams(
            collective_id=0, has_side_effects=True, vmem_limit_bytes=VMEM_LIMIT
        ),
        name="ring_scatter",
    )(*pieces)


def gather_kernel(size, count, *refs):
    own, out = refs[:count], refs[count : 2 * count]
    send_sem, recv_sem, local_sem = refs[2 * count :]
    place, following, previous = ring_place(size)
    targets = (following, previous)
    ring_barrier(following, previous)

    def send(way, item, source, chunk, slot):
        return pltpu.make_async_remote_copy(
            src_ref=source,
            dst_ref=out[item].at[way, chunk],
            send_sem=send_sem.at[way, item, slot],
            recv_sem=recv_sem.at[way, item, slot],
            device_id={"replica": targets[way]},
            device_id_type=MESH,
        )

    def chunk_of(way, slot):
        if way == 0:
            return (place + size - 1 - slot) % size
        return (place + 1 + slot) % size

    keep = []
    for item in range(count):
        for way in range(2):
            send(way, item, own[item].at[way], place, 0).start()
            copy = pltpu.make_async_copy(
                own[item].at[way], out[item].at[way, place], local_sem.at[way, item]
            )
            copy.start()
            keep.append(copy)

    def step(slot, carry):
        for item in range(count):
            for way in range(2):
                chunk = chunk_of(way, slot)
                here = out[item].at[way, chunk]
                send(way, item, here, chunk, slot).wait_recv()
                send(way, item, here, chunk, slot + 1).start()
        return carry

    lax.fori_loop(0, size - 2, step, 0)
    last = size - 2
    for item in range(count):
        for way in range(2):
            chunk = chunk_of(way, last)
            send(way, item, out[item].at[way, chunk], chunk, last).wait_recv()
    for copy in keep:
        copy.wait()

    def finish(slot, carry):
        for item in range(count):
            for way in range(2):
                send(way, item, own[item].at[way], place, slot).wait_send()
        return carry

    lax.fori_loop(0, size - 1, finish, 0)


def ring_gather(pieces, size):
    count = len(pieces)
    spot = pl.BlockSpec(memory_space=pl.ANY)
    return pl.pallas_call(
        functools.partial(gather_kernel, size, count),
        out_shape=[
            jax.ShapeDtypeStruct((2, size) + item.shape[1:], BF) for item in pieces
        ],
        in_specs=[spot] * count,
        out_specs=[spot] * count,
        scratch_shapes=[pltpu.SemaphoreType.DMA((2, count, size - 1))] * 2
        + [pltpu.SemaphoreType.DMA((2, count))],
        compiler_params=pltpu.CompilerParams(collective_id=1, has_side_effects=True),
        name="ring_gather",
    )(*pieces)


def shards(
    tokens,
    cotangent,
    attn_gain,
    attn_shift,
    qkv_weight,
    query_bias,
    value_bias,
    out_weight,
    out_bias,
    mlp_gain,
    mlp_shift,
    fc_weight,
    fc_bias,
    proj_weight,
    proj_bias,
):
    core = lax.axis_index("section")
    layer = lax.axis_index("shard")
    size = lax.axis_size("replica")
    parity = lax.axis_index("replica") % 2
    own = core == layer
    first = layer == 0
    left = core == 0
    micro, part, width = tokens.shape[1:]
    assert micro == 2
    rows = 2 * part
    half = width // 2
    hidden_half = fc_weight.shape[2] // 2

    def pair_permute(value, pairs):
        return lax.ppermute(value, PAIR, pairs)

    small = jnp.concatenate(
        [
            item[0]
            for item in (
                attn_gain,
                attn_shift,
                out_bias,
                mlp_gain,
                mlp_shift,
                proj_bias,
                query_bias,
                value_bias,
                fc_bias,
            )
        ]
    ).reshape(-1, 128)
    small = jnp.where(own, small, pair_permute(small, CROSS_SWAP))
    small_other = core_swap(small[: 6 * half // 128])
    full_small = jnp.concatenate(
        [
            jnp.where(left, small[: 6 * half // 128], small_other).reshape(6, half),
            jnp.where(left, small_other, small[: 6 * half // 128]).reshape(6, half),
        ],
        axis=1,
    ).astype(F32)
    gain1, shift1, bias_o, gain2, shift2, bias_p = (full_small[i] for i in range(6))
    flat = small.reshape(-1).astype(F32)
    bias_q = flat[6 * half : 7 * half]
    bias_v = flat[7 * half : 8 * half]
    bias_f = flat[8 * half :]

    def fetch(index):
        mine = jnp.where(first, tokens[0, index], cotangent[0, index])
        give = jnp.where(first, cotangent[0, index], tokens[0, index])
        give = lax.dynamic_slice_in_dim(give, core * (part // 2), part // 2, 0)
        got = lax.ppermute(give, "shard", [(0, 1), (1, 0)])
        other = ordered(left, got, core_swap(got), 0)
        return ordered(first, mine, other, 0)

    outer = [fetch(0)]

    def crossed(value, axis, pairs):
        length = value.shape[axis] // 2
        piece = lax.dynamic_slice_in_dim(value, parity * length, length, axis)
        pieces = [pair_permute(piece, each) for each in pairs]
        got = pieces[0] if len(pieces) == 1 else jnp.where(own, pieces[0], pieces[1])
        return ordered(parity == 0, got, replica_swap(got), axis)

    def column_halves(weight, groups):
        depth = weight.shape[0]
        parts = weight.reshape(depth, groups, 2, -1)
        mine = jnp.where(left, parts[:, :, 0], parts[:, :, 1]).reshape(depth, -1)
        other = jnp.where(left, parts[:, :, 1], parts[:, :, 0]).reshape(depth, -1)
        return mine, other

    def fetch_columns(weight, groups):
        mine, other = column_halves(weight, groups)
        sibling = pair_permute(other, CORE_OUT)
        length = mine.shape[0] // 2
        piece_mine = lax.dynamic_slice_in_dim(mine, parity * length, length, 0)
        piece_other = lax.dynamic_slice_in_dim(other, parity * length, length, 0)
        got = jnp.where(
            own, pair_permute(piece_mine, CROSS_SAME), pair_permute(piece_other, CROSS_SWAP)
        )
        far = ordered(parity == 0, got, replica_swap(got), 0)
        near = jnp.where(own, mine, sibling)
        return ordered(first, near, far, 0)

    def fetch_rows(weight):
        length = weight.shape[0] // 2
        piece = lax.dynamic_slice_in_dim(weight, parity * length, length, 0)
        got = pair_permute(piece, CROSS_SWAP)
        far = ordered(parity == 0, got, replica_swap(got), 0)
        return jnp.where(own, weight, far)

    w_qkv = fetch_columns(qkv_weight[0], 3)
    w_out = fetch_rows(out_weight[0])
    w_fc = fetch_columns(fc_weight[0], 1)
    w_proj = fetch_rows(proj_weight[0])
    outer.append(fetch(1))

    def exchanged(partial):
        return partial + core_swap(partial.astype(BF)).astype(F32)

    def passed(value, pairs):
        give = lax.dynamic_slice_in_dim(value, core * part, part, 0)
        got = lax.ppermute(give, "shard", pairs)
        return ordered(left, got, core_swap(got), 0)

    keys_all = jnp.zeros((micro * rows, half), BF)
    values_all = jnp.zeros((micro * rows, half), BF)
    received = [jnp.zeros((rows, width), BF)]
    kept_list, outputs = [], []
    for step in range(micro + 1):
        index = jnp.where(first, min(step, micro - 1), max(step - 1, 0)).astype(jnp.int32)
        inputs = jnp.where(first, outer[min(step, micro - 1)], received[step])
        scaled1, inverse1 = norm_parts(inputs.astype(F32))
        normed1 = (scaled1 * gain1 + shift1).astype(BF)
        qkv = jnp.dot(normed1, w_qkv, preferred_element_type=F32)
        query = (qkv[:, :half] + bias_q).astype(BF)
        keys = qkv[:, half : 2 * half].astype(BF)
        values = (qkv[:, 2 * half :] + bias_v).astype(BF)
        keys_all = lax.dynamic_update_slice_in_dim(keys_all, keys, index * rows, 0)
        values_all = lax.dynamic_update_slice_in_dim(values_all, values, index * rows, 0)
        mixed, lse = attend(index[None], query, keys_all, values_all)
        partial = jnp.dot(mixed, w_out, preferred_element_type=F32)
        hidden = inputs.astype(F32) + exchanged(partial) + bias_o
        scaled2, inverse2 = norm_parts(hidden)
        normed2 = (scaled2 * gain2 + shift2).astype(BF)
        pre = jnp.dot(normed2, w_fc, preferred_element_type=F32) + bias_f
        activated, slope = gelu_pair(pre)
        act = activated.astype(BF)
        partial = jnp.dot(act, w_proj, preferred_element_type=F32)
        output = (hidden + exchanged(partial) + bias_p).astype(BF)
        outputs.append(output)
        kept_list.append(
            (inputs, normed1, query, lse, mixed, scaled2.astype(BF), inverse2, normed2,
             slope.astype(BF), act)
        )
        if step < micro:
            received.append(passed(output, [(0, 1)]))

    pending = (jnp.zeros((rows, half), F32), jnp.zeros((rows, half), F32))
    grad_received = [jnp.zeros((rows, width), BF)]
    terms_list, results, sums = [], [], None
    for step in range(micro + 1):
        index = jnp.where(first, min(micro - step, micro - 1), max(micro - 1 - step, 0)).astype(
            jnp.int32
        )
        active = jnp.where(first, 1.0 if step >= 1 else 0.0, 1.0 if step < micro else 0.0)
        grad = jnp.where(first, grad_received[step], outer[max(micro - 1 - step, 0)])
        inputs, normed1, query, lse, mixed, scaled2, inverse2, normed2, slope, act = kept_list[
            micro - step
        ]
        d_pre = (cols_product(grad, w_proj) * slope.astype(F32)).astype(BF)
        d_normed2 = exchanged(cols_product(d_pre, w_fc))
        scaled2 = scaled2.astype(F32)
        d_hidden = grad.astype(F32) + norm_backward(d_normed2, scaled2, inverse2, gain2)
        d_branch = d_hidden.astype(BF)
        d_mixed = cols_product(d_branch, w_out).astype(BF)
        d_query, d_keys, d_values, *pending = attend_back(
            index[None], query, keys_all, values_all, mixed, d_mixed, lse, pending
        )
        d_qkv = jnp.concatenate([d_query, d_keys, d_values], axis=1)
        d_normed1 = exchanged(cols_product(d_qkv, w_qkv))
        scaled1, inverse1 = norm_parts(inputs.astype(F32))
        d_inputs = d_hidden + norm_backward(d_normed1, scaled1, inverse1, gain1)
        result = d_inputs.astype(BF)
        results.append(result)
        if step < micro:
            grad_received.append(passed(result, [(1, 0)]))
        full = jnp.stack(
            [
                jnp.sum(d_normed1 * scaled1, axis=0),
                jnp.sum(d_normed1, axis=0),
                jnp.sum(d_branch.astype(F32), axis=0),
                jnp.sum(d_normed2 * scaled2, axis=0),
                jnp.sum(d_normed2, axis=0),
                jnp.sum(grad.astype(F32), axis=0),
            ]
        )
        full = lax.dynamic_slice_in_dim(full, core * half, half, 1)
        vector = jnp.concatenate(
            [
                full.reshape(-1),
                jnp.sum(d_query.astype(F32), axis=0),
                jnp.sum(d_values.astype(F32), axis=0),
                jnp.sum(d_pre.astype(F32), axis=0),
            ]
        )
        sums = active * vector if sums is None else sums + active * vector
        terms_list.append((normed1, d_qkv, mixed, d_branch, normed2, d_pre, act, grad))

    late = [jnp.where(first, a, b) for a, b in zip(terms_list[2], terms_list[0])]
    both = [jnp.concatenate([a, b], axis=0) for a, b in zip(terms_list[1], late)]
    chunk = half // size
    wide = hidden_half // size
    pieces = [
        rows_product(both[0], both[1]).astype(BF).reshape(2, size, chunk, 3 * half),
        rows_product(both[4], both[5]).astype(BF).reshape(2, size, chunk, hidden_half),
        rows_product(both[2], both[3]).astype(BF).reshape(size, 2, chunk // 2, width),
        rows_product(both[6], both[7]).astype(BF).reshape(size, 2, wide // 2, width),
    ]
    pieces[2] = jnp.swapaxes(pieces[2], 0, 1)
    pieces[3] = jnp.swapaxes(pieces[3], 0, 1)
    g_qkv, g_fc, g_out, g_proj = ring_scatter(pieces)

    def return_columns(piece, groups):
        near = jnp.where(first, piece[0], piece[1])
        far = jnp.where(first, piece[1], piece[0])
        near_core = pair_permute(near, CORE_IN)
        far_same = pair_permute(far, CROSS_BACK)
        far_swap = pair_permute(far, CROSS_SWAP)
        mine = jnp.where(own, near, far_same).reshape(chunk, groups, 1, -1)
        other = jnp.where(own, near_core, far_swap).reshape(chunk, groups, 1, -1)
        return ordered(left, mine, other, 2).reshape(2, chunk // 2, -1)

    def return_rows(piece):
        return jnp.where(own, piece, pair_permute(piece, CROSS_SWAP))

    owned = [
        return_columns(g_qkv, 3),
        return_columns(g_fc, 1),
        return_rows(g_out),
        return_rows(g_proj),
    ]
    gathered = ring_gather(owned, size)

    def finished(item):
        full = jnp.swapaxes(item, 0, 1).astype(F32)
        return full.reshape(1, -1, item.shape[-1])

    qkv_grad, fc_grad, out_grad, proj_grad = (finished(item) for item in gathered)

    sums = lax.all_gather(sums.astype(BF).reshape(-1, 128), "replica", axis=0)
    sums = jnp.sum(sums.astype(F32), axis=0)
    sums = jnp.where(own, sums, pair_permute(sums, CROSS_SWAP)).reshape(-1)
    vectors = [sums[i * half : (i + 1) * half][None] for i in range(8)] + [sums[8 * half :][None]]

    def placed(mine, arrived, pairs, far):
        near = lax.dynamic_slice_in_dim(mine, layer * part, part, 0)
        give = lax.dynamic_slice_in_dim(mine, (1 - layer) * part, part, 0)
        sent = pair_permute(give, pairs)
        piped = lax.dynamic_slice_in_dim(arrived, layer * part, part, 0)
        return jnp.where(own, near, jnp.where(far, piped, sent))

    activations = jnp.stack(
        [
            placed(
                jnp.where(first, outputs[i], outputs[i + 1]),
                received[i + 1],
                [(3, 2)],
                layer == 1,
            )
            for i in range(micro)
        ]
    )[None, None]
    input_grads = jnp.stack(
        [
            placed(
                jnp.where(first, results[micro - i], results[micro - 1 - i]),
                grad_received[micro - i],
                [(0, 1)],
                layer == 0,
            )
            for i in range(micro)
        ]
    )[None, None]
    return (
        activations,
        input_grads,
        vectors[0],
        vectors[1],
        qkv_grad,
        vectors[6],
        vectors[7],
        out_grad,
        vectors[2],
        vectors[3],
        vectors[4],
        fc_grad,
        vectors[8],
        proj_grad,
        vectors[5],
    )


def solution(mesh):
    block = P("replica", None, "shard", None)
    layers = P("section", "replica", None, "shard", None)
    vector = P("section", "shard")
    matrix = P("section", "shard", None)
    kinds = (
        vector,
        vector,
        matrix,
        vector,
        vector,
        matrix,
        vector,
        vector,
        vector,
        matrix,
        vector,
        matrix,
        vector,
    )
    return jax.shard_map(
        shards,
        mesh=mesh,
        in_specs=(block, block) + kinds,
        out_specs=(layers, layers) + kinds,
        check_vma=False,
    )
```

```python
import functools

import jax
import jax.numpy as jnp
from jax import lax
from jax.experimental import pallas as pl
from jax.experimental.pallas import tpu as pltpu
from jax.sharding import PartitionSpec as P

HEAD_DIM = 64
EPSILON = 1e-05
GELU_SCALE = 0.7978845608028654
GELU_CUBIC = 0.044715
ROWS_CONTRACT = (((0,), (0,)), ((), ()))
COLS_CONTRACT = (((1,), (1,)), ((), ()))
BF = jnp.bfloat16
F32 = jnp.float32
MESH = pl.DeviceIdType.MESH
QTILE = 256
VMEM_LIMIT = 56 * 1024 * 1024

CROSS_SWAP = [(1, 2), (2, 1)]
PAIR = ("section", "shard")


def rows_product(left, right):
    return lax.dot_general(left, right, ROWS_CONTRACT, preferred_element_type=F32)


def cols_product(left, right):
    return lax.dot_general(left, right, COLS_CONTRACT, preferred_element_type=F32)


def core_swap(value):
    return lax.ppermute(value, "section", [(0, 1), (1, 0)])


def ordered(flag, first, second, axis):
    return jnp.concatenate(
        [jnp.where(flag, first, second), jnp.where(flag, second, first)], axis=axis
    )


def norm_parts(inputs):
    mean = jnp.mean(inputs, axis=-1, keepdims=True)
    centered = inputs - mean
    inverse = lax.rsqrt(jnp.mean(centered * centered, axis=-1, keepdims=True) + EPSILON)
    return centered * inverse, inverse


def norm_backward(d_normed, scaled, inverse, gain):
    d_scaled = d_normed * gain
    return inverse * (
        d_scaled
        - jnp.mean(d_scaled, axis=-1, keepdims=True)
        - scaled * jnp.mean(d_scaled * scaled, axis=-1, keepdims=True)
    )


def gelu_pair(pre):
    tangent = jnp.tanh(GELU_SCALE * (pre + GELU_CUBIC * pre * pre * pre))
    value = 0.5 * pre * (1.0 + tangent)
    slope = 0.5 * (1.0 + tangent) + 0.5 * pre * (1.0 - tangent * tangent) * GELU_SCALE * (
        1.0 + 3.0 * GELU_CUBIC * pre * pre
    )
    return value, slope


def head_parts(pair):
    low = lax.broadcasted_iota(jnp.int32, pair.shape, 1) < HEAD_DIM
    zero = jnp.zeros_like(pair)
    return jnp.where(low, pair, zero), jnp.where(low, zero, pair)


def masked_scores(keys, query, length):
    scores = cols_product(keys, query)
    tail = scores[length - QTILE :]
    key_pos = lax.broadcasted_iota(jnp.int32, tail.shape, 0)
    query_pos = lax.broadcasted_iota(jnp.int32, tail.shape, 1)
    tail = jnp.where(key_pos <= query_pos, tail, -1e30)
    if length == QTILE:
        return tail
    return jnp.concatenate([scores[: length - QTILE], tail], axis=0)


def attend_kernel(block_ref, q_ref, k_ref, v_ref, out_ref, lse_ref):
    block = block_ref[0]
    rows = q_ref.shape[0]
    for index in range(k_ref.shape[0] // rows):

        @pl.when(block == index)
        def _(index=index):
            for tile in range(rows // QTILE):
                span = pl.ds(tile * QTILE, QTILE)
                length = index * rows + (tile + 1) * QTILE
                keys = k_ref[:length, :]
                values = v_ref[:length, :]
                mixed = []
                for head, part in enumerate(head_parts(q_ref[span, :])):
                    scores = masked_scores(keys, part * BF(HEAD_DIM**-0.5), length)
                    top = jnp.max(scores, axis=0, keepdims=True)
                    probs = jnp.exp(scores - top)
                    total = jnp.sum(probs, axis=0, keepdims=True)
                    lse_ref[0, pl.ds(head, 1), span] = top + jnp.log(total)
                    piece = rows_product(values, probs.astype(BF))
                    piece = piece[head * HEAD_DIM : (head + 1) * HEAD_DIM]
                    mixed.append(piece * (1.0 / total))
                mixed = jnp.concatenate(mixed, axis=0)
                out_ref[span, :] = jnp.transpose(mixed).astype(BF)


def attend(block, query, keys, values):
    rows, width = query.shape
    pairs = width // 128
    total = keys.shape[0]
    return pl.pallas_call(
        attend_kernel,
        grid_spec=pltpu.PrefetchScalarGridSpec(
            num_scalar_prefetch=1,
            grid=(pairs,),
            in_specs=[
                pl.BlockSpec((rows, 128), lambda i, b: (0, i)),
                pl.BlockSpec((total, 128), lambda i, b: (0, i)),
                pl.BlockSpec((total, 128), lambda i, b: (0, i)),
            ],
            out_specs=[
                pl.BlockSpec((rows, 128), lambda i, b: (0, i)),
                pl.BlockSpec((1, 8, rows), lambda i, b: (i, 0, 0)),
            ],
        ),
        out_shape=[
            jax.ShapeDtypeStruct((rows, width), BF),
            jax.ShapeDtypeStruct((pairs, 8, rows), F32),
        ],
        compiler_params=pltpu.CompilerParams(vmem_limit_bytes=VMEM_LIMIT),
        cost_estimate=pl.CostEstimate(
            flops=4 * rows * total * width, bytes_accessed=4 * total * width, transcendentals=0
        ),
        name="attend",
    )(block, query, keys, values)


def attend_back_kernel(
    block_ref,
    q_ref,
    k_ref,
    v_ref,
    o_ref,
    do_ref,
    lse_ref,
    pend_k_ref,
    pend_v_ref,
    dq_ref,
    dk_ref,
    dv_ref,
    new_k_ref,
    new_v_ref,
    sum_k,
    sum_v,
):
    block = block_ref[0]
    rows = q_ref.shape[0]
    scale = HEAD_DIM**-0.5
    for index in range(k_ref.shape[0] // rows):

        @pl.when(block == index)
        def _(index=index):
            end = (index + 1) * rows
            if index == 0:
                sum_k[:rows, :] = pend_k_ref[...]
                sum_v[:rows, :] = pend_v_ref[...]
            else:
                sum_k[:end, :] = jnp.zeros((end, 128), F32)
                sum_v[:end, :] = jnp.zeros((end, 128), F32)
            for tile in range(rows // QTILE):
                span = pl.ds(tile * QTILE, QTILE)
                length = index * rows + (tile + 1) * QTILE
                keys = k_ref[:length, :]
                values = v_ref[:length, :]
                grads = do_ref[span, :]
                products = jnp.transpose(grads.astype(F32) * o_ref[span, :].astype(F32))
                queries = head_parts(q_ref[span, :])
                grads = head_parts(grads)
                d_query = []
                d_keys = d_values = None
                for head in range(2):
                    take = slice(head * HEAD_DIM, (head + 1) * HEAD_DIM)
                    query = queries[head] * BF(scale)
                    scores = masked_scores(keys, query, length)
                    weights = jnp.exp(scores - lse_ref[0, pl.ds(head, 1), span])
                    d_probs = cols_product(values, grads[head])
                    delta = jnp.sum(products[take], axis=0, keepdims=True)
                    d_scores = (weights * (d_probs - delta)).astype(BF)
                    d_value = jnp.dot(weights.astype(BF), grads[head], preferred_element_type=F32)
                    d_key = jnp.dot(d_scores, query, preferred_element_type=F32)
                    d_values = d_value if head == 0 else d_values + d_value
                    d_keys = d_key if head == 0 else d_keys + d_key
                    d_query.append(rows_product(keys, d_scores)[take])
                sum_k[:length, :] += d_keys
                sum_v[:length, :] += d_values
                d_query = jnp.concatenate(d_query, axis=0) * scale
                dq_ref[span, :] = jnp.transpose(d_query).astype(BF)
            dk_ref[...] = sum_k[index * rows : end, :].astype(BF)
            dv_ref[...] = sum_v[index * rows : end, :].astype(BF)
            if index == 0:
                new_k_ref[...] = pend_k_ref[...]
                new_v_ref[...] = pend_v_ref[...]
            else:
                new_k_ref[...] = sum_k[:rows, :]
                new_v_ref[...] = sum_v[:rows, :]


def attend_back(block, query, keys, values, mixed, d_mixed, lse, pending):
    rows, width = query.shape
    pairs = width // 128
    total = keys.shape[0]
    assert total == 2 * rows
    small = pl.BlockSpec((rows, 128), lambda i, b: (0, i))
    large = pl.BlockSpec((total, 128), lambda i, b: (0, i))
    low = jax.ShapeDtypeStruct((rows, width), BF)
    wide = jax.ShapeDtypeStruct((rows, width), F32)
    return pl.pallas_call(
        attend_back_kernel,
        grid_spec=pltpu.PrefetchScalarGridSpec(
            num_scalar_prefetch=1,
            grid=(pairs,),
            in_specs=[
                small,
                large,
                large,
                small,
                small,
                pl.BlockSpec((1, 8, rows), lambda i, b: (i, 0, 0)),
                small,
                small,
            ],
            out_specs=[small] * 5,
            scratch_shapes=[pltpu.VMEM((total, 128), F32), pltpu.VMEM((total, 128), F32)],
        ),
        out_shape=[low, low, low, wide, wide],
        compiler_params=pltpu.CompilerParams(vmem_limit_bytes=VMEM_LIMIT),
        cost_estimate=pl.CostEstimate(
            flops=10 * rows * total * width, bytes_accessed=8 * total * width, transcendentals=0
        ),
        name="attend_back",
    )(block, query, keys, values, mixed, d_mixed, lse, *pending)


def ring_place(size):
    index = lax.axis_index("replica")
    odd = index % 2
    half = index // 2
    place = (1 - odd) * half + odd * (size - 1 - half)

    def device(spot):
        upper = spot // (size // 2)
        return (1 - upper) * (2 * spot) + upper * (2 * (size - 1 - spot) + 1)

    return place, device((place + 1) % size), device((place + size - 1) % size)


def neighbours():
    core, layer = lax.axis_index("section"), lax.axis_index("shard")
    sibling = {"section": 1 - core}
    across = {"shard": 1 - layer}
    diagonal = {"section": 1 - core, "shard": 1 - layer}
    return core, layer, sibling, across, diagonal


def greet(devices):
    barrier = pltpu.get_barrier_semaphore()
    for device in devices:
        pl.semaphore_signal(barrier, inc=1, device_id=device, device_id_type=MESH)
    pl.semaphore_wait(barrier, len(devices))


def scatter_kernel(size, count, *refs):
    own, refs = refs[: count + 1], refs[count + 1 :]
    out, refs = refs[: count + 1], refs[count + 1 :]
    landed, refs = refs[:count], refs[count:]
    send_sem, recv_sem, small_send, small_recv = refs
    small, small_out = own[count], out[count]
    place, following, previous = ring_place(size)
    targets = ({"replica": following}, {"replica": previous})
    greet(targets)

    def send(way, item, source, slot):
        return pltpu.make_async_remote_copy(
            src_ref=source,
            dst_ref=landed[item].at[way, slot],
            send_sem=send_sem.at[way, item, slot],
            recv_sem=recv_sem.at[way, item, slot],
            device_id=targets[way],
            device_id_type=MESH,
        )

    def send_small(chunk, slot):
        return pltpu.make_async_remote_copy(
            src_ref=small_out.at[chunk],
            dst_ref=small_out.at[chunk],
            send_sem=small_send.at[slot],
            recv_sem=small_recv.at[slot],
            device_id=targets[0],
            device_id_type=MESH,
        )

    def chunk_of(way, slot):
        if way == 0:
            return (place + 2 * size - 2 - slot) % size
        return (place + 2 + slot) % size

    for item in range(count):
        send(0, item, own[item].at[0, (place + size - 1) % size], 0).start()
        send(1, item, own[item].at[1, (place + 1) % size], 0).start()
    small_out[place] = small[...]
    send_small(place, 0).start()

    def step(slot, carry):
        for item in range(count):
            for way in range(2):
                here = landed[item].at[way, slot]
                send(way, item, here, slot).wait_recv()
                here[...] += own[item][way, chunk_of(way, slot)]
                send(way, item, here, slot + 1).start()
        chunk = (place + size - 1 - slot) % size
        send_small(chunk, slot).wait_recv()
        send_small(chunk, slot + 1).start()
        return carry

    lax.fori_loop(0, size - 2, step, 0)
    last = size - 2
    for item in range(count):
        for way in range(2):
            here = landed[item].at[way, last]
            send(way, item, here, last).wait_recv()
            out[item][way] = here[...] + own[item][way, place]
    send_small((place + 1) % size, last).wait_recv()

    def finish(slot, carry):
        for item in range(count):
            for way in range(2):
                send(way, item, landed[item].at[way, slot], slot).wait_send()
        send_small(place, slot).wait_send()
        return carry

    lax.fori_loop(0, size - 1, finish, 0)


def ring_scatter(pieces, small):
    size = pieces[0].shape[1]
    count = len(pieces)
    whole = pl.BlockSpec(memory_space=pltpu.VMEM)
    return pl.pallas_call(
        functools.partial(scatter_kernel, size, count),
        out_shape=[jax.ShapeDtypeStruct((2,) + item.shape[2:], BF) for item in pieces]
        + [jax.ShapeDtypeStruct((size,) + small.shape, small.dtype)],
        in_specs=[whole] * (count + 1),
        out_specs=[whole] * (count + 1),
        scratch_shapes=[pltpu.VMEM((2, size - 1) + item.shape[2:], BF) for item in pieces]
        + [pltpu.SemaphoreType.DMA((2, count, size - 1))] * 2
        + [pltpu.SemaphoreType.DMA((size - 1,))] * 2,
        compiler_params=pltpu.CompilerParams(
            collective_id=0, has_side_effects=True, vmem_limit_bytes=VMEM_LIMIT
        ),
        name="ring_scatter",
    )(*pieces, small)


def gather_kernel(size, groups, *refs):
    count = 4
    own, out = refs[:count], refs[count : 2 * count]
    swap_send, swap_recv, send_sem, recv_sem = refs[2 * count :]
    place, following, previous = ring_place(size)
    targets = ({"replica": following}, {"replica": previous})
    core, layer, sibling, across, diagonal = neighbours()
    same = core == layer
    greet(targets + (sibling, across, diagonal))

    def parts(item, source_half, sender):
        if item < len(groups):
            width = own[item].shape[2] // groups[item]
            for group in range(groups[item]):
                start = pl.multiple_of((2 * group + sender) * width, width)
                yield (
                    own[item].at[source_half, :, pl.ds(group * width, width)],
                    out[item].at[place, :, pl.ds(start, width)],
                )
        else:
            deep = own[item].shape[1]
            for half in range(2):
                yield own[item].at[half], out[item].at[place, pl.ds(half * deep, deep)]

    def copies(item, source_half, lane, kind, device=None):
        for number, (source, target) in enumerate(parts(item, source_half, core)):
            send, recv = swap_send.at[item, lane, number], swap_recv.at[item, kind, number]
            if device is None:
                yield pltpu.make_async_copy(source, target, recv)
            else:
                yield pltpu.make_async_remote_copy(
                    src_ref=source,
                    dst_ref=target,
                    send_sem=send,
                    recv_sem=recv,
                    device_id=device,
                    device_id_type=MESH,
                )

    @pl.when(same)
    def _():
        for item in range(count):
            for copy in copies(item, layer, 0, 0):
                copy.start()
            if item < len(groups):
                for copy in copies(item, 1 - layer, 0, 2, across):
                    copy.start()

    @pl.when(core != layer)
    def _():
        for item in range(count):
            for copy in copies(item, 1 - layer, 0, 3, diagonal):
                copy.start()
            if item < len(groups):
                for copy in copies(item, layer, 1, 1, sibling):
                    copy.start()

    def send(way, item, chunk, slot):
        deep = out[item].shape[1] // 2
        here = out[item].at[chunk, pl.ds(way * deep, deep)]
        return pltpu.make_async_remote_copy(
            src_ref=here,
            dst_ref=here,
            send_sem=send_sem.at[way, item, slot],
            recv_sem=recv_sem.at[way, item, slot],
            device_id=targets[way],
            device_id_type=MESH,
        )

    def chunk_of(way, slot):
        if way == 0:
            return (place + size - 1 - slot) % size
        return (place + 1 + slot) % size

    for item in range(count):

        @pl.when(same)
        def _(item=item):
            for copy in copies(item, layer, 0, 0):
                copy.wait()
            if item < len(groups):
                for copy in copies(item, layer, 1, 1, sibling):
                    copy.wait_recv()

        @pl.when(core != layer)
        def _(item=item):
            for copy in copies(item, layer, 0, 3, diagonal):
                copy.wait_recv()
            if item < len(groups):
                for copy in copies(item, layer, 0, 2, across):
                    copy.wait_recv()

        for way in range(2):
            send(way, item, place, 0).start()

    def step(slot, carry):
        for item in range(count):
            for way in range(2):
                chunk = chunk_of(way, slot)
                send(way, item, chunk, slot).wait_recv()
                send(way, item, chunk, slot + 1).start()
        return carry

    lax.fori_loop(0, size - 2, step, 0)
    last = size - 2
    for item in range(count):
        for way in range(2):
            send(way, item, chunk_of(way, last), last).wait_recv()

    @pl.when(same)
    def _():
        for item in range(len(groups)):
            for copy in copies(item, 1 - layer, 0, 2, across):
                copy.wait_send()

    @pl.when(core != layer)
    def _():
        for item in range(count):
            for copy in copies(item, 1 - layer, 0, 3, diagonal):
                copy.wait_send()
            if item < len(groups):
                for copy in copies(item, layer, 1, 1, sibling):
                    copy.wait_send()

    def finish(slot, carry):
        for item in range(count):
            for way in range(2):
                send(way, item, place, slot).wait_send()
        return carry

    lax.fori_loop(0, size - 1, finish, 0)


def ring_gather(pieces, groups, size):
    spot = pl.BlockSpec(memory_space=pl.ANY)
    shapes = [(size, item.shape[1], 2 * item.shape[2]) for item in pieces[: len(groups)]]
    shapes += [(size, 2 * item.shape[1], item.shape[2]) for item in pieces[len(groups) :]]
    count = len(pieces)
    return pl.pallas_call(
        functools.partial(gather_kernel, size, groups),
        out_shape=[jax.ShapeDtypeStruct(shape, BF) for shape in shapes],
        in_specs=[pl.BlockSpec(memory_space=pltpu.VMEM)] * count,
        out_specs=[spot] * count,
        scratch_shapes=[
            pltpu.SemaphoreType.DMA((count, 2, 3)),
            pltpu.SemaphoreType.DMA((count, 4, 3)),
        ]
        + [pltpu.SemaphoreType.DMA((2, count, size - 1))] * 2,
        compiler_params=pltpu.CompilerParams(collective_id=1, has_side_effects=True),
        name="ring_gather",
    )(*pieces)


def fetch_kernel(*refs):
    tokens, cotangent, small, qkv, fc, out, proj = refs[:7]
    outer, small_out, w_qkv, w_fc, w_out, w_proj = refs[7:13]
    send_sem, recv_sem, extra_send, extra_recv, local_sem = refs[13:18]
    buffers = refs[18:]
    core, layer, sibling, across, diagonal = neighbours()
    index = lax.axis_index("replica")
    quarter = index % 4
    low, high = index % 2, (index // 2) % 2
    beside = {"replica": index + 1 - 2 * low}
    above = {"replica": index + 2 - 4 * high}
    beside_quarter = quarter + 1 - 2 * low
    above_quarter = quarter + 2 - 4 * high
    same = core == layer
    far_quarter = 3 - quarter
    greet((sibling, across, diagonal, beside, above))

    depth = qkv.shape[0]
    span = qkv.shape[1] // 6
    wide = fc.shape[1] // 2
    turn = proj.shape[0] // 2
    cols = [
        (qkv, w_qkv, lambda s, g=g: pl.multiple_of((2 * g + s) * span, span), g * span, span)
        for g in range(3)
    ]
    cols.append((fc, w_fc, lambda s: pl.multiple_of(s * wide, wide), 0, wide))
    rows = [(out, w_out, 0, out.shape[0]), (proj, w_proj, 0, turn), (proj, w_proj, turn, turn)]
    order = [0, 1, 2, 4, 3, 5, 6]

    def rows_of(item):
        return depth if item < 4 else rows[item - 4][3]

    def target(item, base, which, part=None):
        deep = rows_of(item) // 4
        start = base + which * deep
        if part is not None:
            deep = deep // 2
            start = start + part * deep
        place = pl.ds(pl.multiple_of(start, deep), deep)
        if item < 4:
            return cols[item][1].at[place, pl.ds(cols[item][3], cols[item][4])]
        return rows[item - 4][1].at[place]

    def base_of(item, shard):
        return shard * depth if item < 4 else rows[item - 4][2]

    def remote(stage, item, source, dest, device, lane=0):
        return pltpu.make_async_remote_copy(
            src_ref=source,
            dst_ref=dest,
            send_sem=send_sem.at[stage + lane, item],
            recv_sem=recv_sem.at[stage, item],
            device_id=device,
            device_id_type=MESH,
        )

    def cross(item, receiver):
        deep = rows_of(item) // 4
        place = pl.multiple_of(base_of(item, 0) + quarter * deep, deep)
        dest = target(item, base_of(item, layer), quarter)
        if item < 4:
            columns = cols[item][2](receiver)
            source = cols[item][0].at[pl.ds(place, deep), pl.ds(columns, cols[item][4])]
        else:
            source = rows[item - 4][0].at[pl.ds(place, deep)]
        return source, dest

    def cross_same(item):
        return remote(0, item, *cross(item, core), across, 5)

    def cross_swap(item):
        return remote(0, item, *cross(item, 1 - core), diagonal)

    def pass_on(stage, item, which, device, part=None):
        here = target(item, base_of(item, 1 - layer), which, part)
        return remote(stage, item, here, here, device)

    def to_sibling(item):
        columns = cols[item][2](1 - core)
        source = cols[item][0].at[:, pl.ds(columns, cols[item][4])]
        start = pl.multiple_of(layer * depth, depth)
        dest = cols[item][1].at[pl.ds(start, depth), pl.ds(cols[item][3], cols[item][4])]
        return remote(6, item, source, dest, sibling)

    def through(source, dest, number):
        return (
            pltpu.make_async_copy(source, buffers[number], local_sem.at[number]),
            pltpu.make_async_copy(buffers[number], dest, local_sem.at[number]),
        )

    def keep_local(item):
        if item < 4:
            columns = cols[item][2](core)
            source = cols[item][0].at[:, pl.ds(columns, cols[item][4])]
            start = pl.multiple_of(layer * depth, depth)
            dest = cols[item][1].at[pl.ds(start, depth), pl.ds(cols[item][3], cols[item][4])]
        else:
            source, dest, start, deep = rows[item - 4]
            source, dest = source.at[pl.ds(start, deep)], dest.at[pl.ds(start, deep)]
        return through(source, dest, item)

    part = tokens.shape[1]
    half = part // 2

    def outer_rows(shard, which):
        return pl.ds(pl.multiple_of(shard * part + which * half, half), half)

    def outer_cross(block):
        place = pl.ds(pl.multiple_of(core * half, half), half)

        def copy(source):
            return pltpu.make_async_remote_copy(
                src_ref=source.at[block, place],
                dst_ref=outer.at[block, outer_rows(layer, core)],
                send_sem=extra_send.at[block],
                recv_sem=extra_recv.at[block],
                device_id=across,
                device_id_type=MESH,
            )

        return copy

    def outer_pass(block):
        here = outer.at[block, outer_rows(1 - layer, core)]
        return pltpu.make_async_remote_copy(
            src_ref=here,
            dst_ref=here,
            send_sem=extra_send.at[2 + block],
            recv_sem=extra_recv.at[2 + block],
            device_id=sibling,
            device_id_type=MESH,
        )

    def outer_local(source):
        place = pl.ds(pl.multiple_of(layer * part, part), part)
        return through(source, outer.at[:, place], 7)

    def small_swap():
        return pltpu.make_async_remote_copy(
            src_ref=small,
            dst_ref=small_out.at[1 - core],
            send_sem=extra_send.at[4],
            recv_sem=extra_recv.at[4],
            device_id=diagonal,
            device_id_type=MESH,
        )

    def small_pass():
        return pltpu.make_async_remote_copy(
            src_ref=small_out.at[core],
            dst_ref=small_out.at[core],
            send_sem=extra_send.at[5],
            recv_sem=extra_recv.at[5],
            device_id=sibling,
            device_id_type=MESH,
        )

    def small_local():
        return through(small, small_out.at[core], 8)

    def start_outer(block):
        @pl.when(layer == 0)
        def _():
            outer_cross(block)(cotangent).start()

        @pl.when(layer == 1)
        def _():
            outer_cross(block)(tokens).start()

    def crossings(item):
        if item < 4:
            cross_same(item).start()
        cross_swap(item).start()

    @pl.when(same)
    def _():
        small_local()[0].start()

    @pl.when(core != layer)
    def _():
        small_swap().start()

    start_outer(0)

    @pl.when(core != layer)
    def _():
        crossings(order[0])
        crossings(order[1])

    @pl.when(layer == 0)
    def _():
        outer_local(tokens)[0].start()

    @pl.when(layer == 1)
    def _():
        outer_local(cotangent)[0].start()

    @pl.when(same)
    def _():
        for item in range(4):
            to_sibling(item).start()
        load, store = small_local()
        load.wait()
        store.start()
        store.wait()

    @pl.when(core != layer)
    def _():
        small_swap().wait_recv()

    small_pass().start()
    outer_local(tokens)[0].wait()
    outer_local(tokens)[1].start()

    @pl.when(same)
    def _():
        for item in range(7):
            keep_local(item)[0].start()

    def relay(sequence, ahead):
        def onward(item):
            pass_on(1, item, beside_quarter, beside).wait_recv()
            pass_on(4, item, beside_quarter, above, 0).start()
            pass_on(2, item, above_quarter, above).wait_recv()
            pass_on(3, item, above_quarter, beside, 1).start()

        for number, item in enumerate(sequence):
            pass_on(0, item, quarter, beside).wait_recv()
            if ahead and number + 2 < len(sequence):
                crossings(sequence[number + 2])
            pass_on(1, item, quarter, beside).start()
            pass_on(2, item, quarter, above).start()
            if number >= 1:
                onward(sequence[number - 1])
            if number == 0:
                outer_cross(0)(tokens).wait_recv()
                outer_pass(0).start()
                start_outer(1)
        onward(sequence[-1])
        for item in sequence:
            pass_on(3, item, far_quarter, beside, 1).wait_recv()
            pass_on(4, item, far_quarter, above, 0).wait_recv()
            for stage in (1, 2):
                pass_on(stage, item, quarter, beside).wait_send()
            for stage, which in ((3, 1), (4, 0)):
                pass_on(stage, item, quarter, beside, which).wait_send()

    @pl.when(same)
    def _():
        for item in range(7):
            load, store = keep_local(item)
            load.wait()
            store.start()
        relay([0, 1, 2, 3], False)
        for item in range(4):
            to_sibling(item).wait_send()
        for item in range(7):
            keep_local(item)[1].wait()

    @pl.when(core != layer)
    def _():
        relay(order, True)
        for item in range(4):
            to_sibling(item).wait_recv()
            cross_same(item).wait_send()
        for item in range(7):
            cross_swap(item).wait_send()
        small_swap().wait_send()

    outer_cross(1)(tokens).wait_recv()
    outer_pass(1).start()
    outer_local(tokens)[1].wait()
    small_pass().wait()
    for block in range(2):
        outer_cross(block)(tokens).wait_send()
        outer_pass(block).wait()


def fetch_inputs(tokens, cotangent, small, qkv, fc, out, proj):
    spot = pl.BlockSpec(memory_space=pl.ANY)
    micro, part, width = tokens.shape
    shapes = [
        (micro, 2 * part, width),
        (2,) + small.shape,
        (2 * qkv.shape[0], qkv.shape[1] // 2),
        (2 * fc.shape[0], fc.shape[1] // 2),
        out.shape,
        proj.shape,
    ]
    return pl.pallas_call(
        fetch_kernel,
        out_shape=[jax.ShapeDtypeStruct(shape, BF) for shape in shapes],
        in_specs=[spot] * 7,
        out_specs=[spot] * 6,
        scratch_shapes=[
            pltpu.SemaphoreType.DMA((7, 7)),
            pltpu.SemaphoreType.DMA((7, 7)),
            pltpu.SemaphoreType.DMA((6,)),
            pltpu.SemaphoreType.DMA((6,)),
            pltpu.SemaphoreType.DMA((9,)),
        ]
        + [pltpu.VMEM((qkv.shape[0], qkv.shape[1] // 6), BF)] * 3
        + [
            pltpu.VMEM((fc.shape[0], fc.shape[1] // 2), BF),
            pltpu.VMEM(out.shape, BF),
            pltpu.VMEM((proj.shape[0] // 2, width), BF),
            pltpu.VMEM((proj.shape[0] // 2, width), BF),
            pltpu.VMEM(tokens.shape, BF),
            pltpu.VMEM(small.shape, BF),
        ],
        compiler_params=pltpu.CompilerParams(
            collective_id=2, has_side_effects=True, vmem_limit_bytes=VMEM_LIMIT
        ),
        name="fetch_inputs",
    )(tokens, cotangent, small, qkv, fc, out, proj)


def shards(
    tokens,
    cotangent,
    attn_gain,
    attn_shift,
    qkv_weight,
    query_bias,
    value_bias,
    out_weight,
    out_bias,
    mlp_gain,
    mlp_shift,
    fc_weight,
    fc_bias,
    proj_weight,
    proj_bias,
):
    core = lax.axis_index("section")
    layer = lax.axis_index("shard")
    size = lax.axis_size("replica")
    own = core == layer
    first = layer == 0
    left = core == 0
    micro, part, width = tokens.shape[1:]
    assert micro == 2
    rows = 2 * part
    half = width // 2
    hidden_half = fc_weight.shape[2] // 2

    def pair_permute(value, pairs):
        return lax.ppermute(value, PAIR, pairs)

    small = jnp.concatenate(
        [
            item[0]
            for item in (
                attn_gain,
                attn_shift,
                out_bias,
                mlp_gain,
                mlp_shift,
                proj_bias,
                query_bias,
                value_bias,
                fc_bias,
            )
        ]
    ).reshape(-1, 128)
    outer, small_both, w_qkv, w_fc, w_out, w_proj = fetch_inputs(
        tokens[0], cotangent[0], small, qkv_weight[0], fc_weight[0], out_weight[0], proj_weight[0]
    )
    flat = small_both.reshape(2, -1).astype(F32)
    full_small = jnp.concatenate(
        [flat[0, : 6 * half].reshape(6, half), flat[1, : 6 * half].reshape(6, half)], axis=1
    )
    gain1, shift1, bias_o, gain2, shift2, bias_p = (full_small[i] for i in range(6))
    flat = jnp.where(left, flat[0], flat[1])
    bias_q = flat[6 * half : 7 * half]
    bias_v = flat[7 * half : 8 * half]
    bias_f = flat[8 * half :]

    def exchanged(partial):
        return partial + core_swap(partial.astype(BF)).astype(F32)

    def passed(value, pairs):
        give = lax.dynamic_slice_in_dim(value, core * part, part, 0)
        got = lax.ppermute(give, "shard", pairs)
        return ordered(left, got, core_swap(got), 0)

    keys_all = jnp.zeros((micro * rows, half), BF)
    values_all = jnp.zeros((micro * rows, half), BF)
    received = [jnp.zeros((rows, width), BF)]
    kept_list, outputs = [], []
    for step in range(micro + 1):
        index = jnp.where(first, min(step, micro - 1), max(step - 1, 0)).astype(jnp.int32)
        inputs = jnp.where(first, outer[min(step, micro - 1)], received[step])
        scaled1, inverse1 = norm_parts(inputs.astype(F32))
        normed1 = (scaled1 * gain1 + shift1).astype(BF)
        qkv = jnp.dot(normed1, w_qkv, preferred_element_type=F32)
        query = (qkv[:, :half] + bias_q).astype(BF)
        keys = qkv[:, half : 2 * half].astype(BF)
        values = (qkv[:, 2 * half :] + bias_v).astype(BF)
        keys_all = lax.dynamic_update_slice_in_dim(keys_all, keys, index * rows, 0)
        values_all = lax.dynamic_update_slice_in_dim(values_all, values, index * rows, 0)
        mixed, lse = attend(index[None], query, keys_all, values_all)
        partial = jnp.dot(mixed, w_out, preferred_element_type=F32)
        hidden = inputs.astype(F32) + exchanged(partial) + bias_o
        scaled2, inverse2 = norm_parts(hidden)
        normed2 = (scaled2 * gain2 + shift2).astype(BF)
        pre = jnp.dot(normed2, w_fc, preferred_element_type=F32) + bias_f
        activated, slope = gelu_pair(pre)
        act = activated.astype(BF)
        partial = jnp.dot(act, w_proj, preferred_element_type=F32)
        output = (hidden + exchanged(partial) + bias_p).astype(BF)
        outputs.append(output)
        kept_list.append(
            (inputs, normed1, query, lse, mixed, scaled2.astype(BF), inverse2, normed2,
             slope.astype(BF), act)
        )
        if step < micro:
            received.append(passed(output, [(0, 1)]))

    pending = (jnp.zeros((rows, half), F32), jnp.zeros((rows, half), F32))
    grad_received = [jnp.zeros((rows, width), BF)]
    terms_list, results, sums = [], [], None
    for step in range(micro + 1):
        index = jnp.where(first, min(micro - step, micro - 1), max(micro - 1 - step, 0)).astype(
            jnp.int32
        )
        active = jnp.where(first, 1.0 if step >= 1 else 0.0, 1.0 if step < micro else 0.0)
        grad = jnp.where(first, grad_received[step], outer[max(micro - 1 - step, 0)])
        inputs, normed1, query, lse, mixed, scaled2, inverse2, normed2, slope, act = kept_list[
            micro - step
        ]
        d_pre = (cols_product(grad, w_proj) * slope.astype(F32)).astype(BF)
        d_normed2 = exchanged(cols_product(d_pre, w_fc))
        scaled2 = scaled2.astype(F32)
        d_hidden = grad.astype(F32) + norm_backward(d_normed2, scaled2, inverse2, gain2)
        d_branch = d_hidden.astype(BF)
        d_mixed = cols_product(d_branch, w_out).astype(BF)
        d_query, d_keys, d_values, *pending = attend_back(
            index[None], query, keys_all, values_all, mixed, d_mixed, lse, pending
        )
        d_qkv = jnp.concatenate([d_query, d_keys, d_values], axis=1)
        d_normed1 = exchanged(cols_product(d_qkv, w_qkv))
        scaled1, inverse1 = norm_parts(inputs.astype(F32))
        d_inputs = d_hidden + norm_backward(d_normed1, scaled1, inverse1, gain1)
        result = d_inputs.astype(BF)
        results.append(result)
        if step < micro:
            grad_received.append(passed(result, [(1, 0)]))
        full = jnp.stack(
            [
                jnp.sum(d_normed1 * scaled1, axis=0),
                jnp.sum(d_normed1, axis=0),
                jnp.sum(d_branch.astype(F32), axis=0),
                jnp.sum(d_normed2 * scaled2, axis=0),
                jnp.sum(d_normed2, axis=0),
                jnp.sum(grad.astype(F32), axis=0),
            ]
        )
        full = lax.dynamic_slice_in_dim(full, core * half, half, 1)
        vector = jnp.concatenate(
            [
                full.reshape(-1),
                jnp.sum(d_query.astype(F32), axis=0),
                jnp.sum(d_values.astype(F32), axis=0),
                jnp.sum(d_pre.astype(F32), axis=0),
            ]
        )
        sums = active * vector if sums is None else sums + active * vector
        terms_list.append((normed1, d_qkv, mixed, d_branch, normed2, d_pre, act, grad))

    late = [jnp.where(first, a, b) for a, b in zip(terms_list[2], terms_list[0])]
    both = [jnp.concatenate([a, b], axis=0) for a, b in zip(terms_list[1], late)]
    chunk = half // size
    wide = hidden_half // size
    pieces = [
        rows_product(both[0], both[1]).astype(BF).reshape(2, size, chunk, 3 * half),
        rows_product(both[4], both[5]).astype(BF).reshape(2, size, chunk, hidden_half),
        rows_product(both[2], both[3]).astype(BF).reshape(size, 2, chunk // 2, width),
        rows_product(both[6], both[7]).astype(BF).reshape(size, 2, wide // 2, width),
    ]
    pieces[2] = jnp.swapaxes(pieces[2], 0, 1)
    pieces[3] = jnp.swapaxes(pieces[3], 0, 1)
    sums = sums.reshape(-1, 128)
    sums = jnp.where(own, sums, pair_permute(sums, CROSS_SWAP))
    *reduced, sums = ring_scatter(pieces, sums)
    sums = jnp.sum(sums, axis=0).reshape(-1)
    vectors = [sums[i * half : (i + 1) * half][None] for i in range(8)] + [sums[8 * half :][None]]
    qkv_grad, fc_grad, out_grad, proj_grad = (
        item.astype(F32).reshape(1, -1, item.shape[-1])
        for item in ring_gather(reduced, (3, 1), size)
    )

    def placed(mine, arrived, pairs, far):
        near = lax.dynamic_slice_in_dim(mine, layer * part, part, 0)
        give = lax.dynamic_slice_in_dim(mine, (1 - layer) * part, part, 0)
        sent = pair_permute(give, pairs)
        piped = lax.dynamic_slice_in_dim(arrived, layer * part, part, 0)
        return jnp.where(own, near, jnp.where(far, piped, sent))

    activations = jnp.stack(
        [
            placed(
                jnp.where(first, outputs[i], outputs[i + 1]),
                received[i + 1],
                [(3, 2)],
                layer == 1,
            )
            for i in range(micro)
        ]
    )[None, None]
    input_grads = jnp.stack(
        [
            placed(
                jnp.where(first, results[micro - i], results[micro - 1 - i]),
                grad_received[micro - i],
                [(0, 1)],
                layer == 0,
            )
            for i in range(micro)
        ]
    )[None, None]
    return (
        activations,
        input_grads,
        vectors[0],
        vectors[1],
        qkv_grad,
        vectors[6],
        vectors[7],
        out_grad,
        vectors[2],
        vectors[3],
        vectors[4],
        fc_grad,
        vectors[8],
        proj_grad,
        vectors[5],
    )


def solution(mesh):
    block = P("replica", None, "shard", None)
    layers = P("section", "replica", None, "shard", None)
    vector = P("section", "shard")
    matrix = P("section", "shard", None)
    kinds = (
        vector,
        vector,
        matrix,
        vector,
        vector,
        matrix,
        vector,
        vector,
        vector,
        matrix,
        vector,
        matrix,
        vector,
    )
    return jax.shard_map(
        shards,
        mesh=mesh,
        in_specs=(block, block) + kinds,
        out_specs=(layers, layers) + kinds,
        check_vma=False,
    )
```

```python
import functools

import jax
import jax.numpy as jnp
from jax import lax
from jax.experimental import pallas as pl
from jax.experimental.pallas import tpu as pltpu
from jax.sharding import PartitionSpec as P

HEAD_DIM = 64
EPSILON = 1e-05
GELU_SCALE = 0.7978845608028654
GELU_CUBIC = 0.044715
ROWS_CONTRACT = (((0,), (0,)), ((), ()))
COLS_CONTRACT = (((1,), (1,)), ((), ()))
BF = jnp.bfloat16
F32 = jnp.float32
MESH = pl.DeviceIdType.MESH
QTILE = 256
VMEM_LIMIT = 56 * 1024 * 1024

CROSS_SWAP = [(1, 2), (2, 1)]
PAIR = ("section", "shard")


def rows_product(left, right):
    return lax.dot_general(left, right, ROWS_CONTRACT, preferred_element_type=F32)


def cols_product(left, right):
    return lax.dot_general(left, right, COLS_CONTRACT, preferred_element_type=F32)


def norm_parts(inputs):
    mean = jnp.mean(inputs, axis=-1, keepdims=True)
    centered = inputs - mean
    inverse = lax.rsqrt(jnp.mean(centered * centered, axis=-1, keepdims=True) + EPSILON)
    return centered * inverse, inverse


def norm_backward(d_normed, scaled, inverse, gain):
    d_scaled = d_normed * gain
    return inverse * (
        d_scaled
        - jnp.mean(d_scaled, axis=-1, keepdims=True)
        - scaled * jnp.mean(d_scaled * scaled, axis=-1, keepdims=True)
    )


def gelu_pair(pre):
    tangent = jnp.tanh(GELU_SCALE * (pre + GELU_CUBIC * pre * pre * pre))
    value = 0.5 * pre * (1.0 + tangent)
    slope = 0.5 * (1.0 + tangent) + 0.5 * pre * (1.0 - tangent * tangent) * GELU_SCALE * (
        1.0 + 3.0 * GELU_CUBIC * pre * pre
    )
    return value, slope


def head_parts(pair):
    low = lax.broadcasted_iota(jnp.int32, pair.shape, 1) < HEAD_DIM
    zero = jnp.zeros_like(pair)
    return jnp.where(low, pair, zero), jnp.where(low, zero, pair)


def masked_scores(keys, query, length):
    scores = cols_product(keys, query)
    tail = scores[length - QTILE :]
    key_pos = lax.broadcasted_iota(jnp.int32, tail.shape, 0)
    query_pos = lax.broadcasted_iota(jnp.int32, tail.shape, 1)
    tail = jnp.where(key_pos <= query_pos, tail, -1e30)
    if length == QTILE:
        return tail
    return jnp.concatenate([scores[: length - QTILE], tail], axis=0)


def ring_place(size):
    index = lax.axis_index("replica")
    odd = index % 2
    half = index // 2
    place = (1 - odd) * half + odd * (size - 1 - half)

    def device(spot):
        upper = spot // (size // 2)
        return (1 - upper) * (2 * spot) + upper * (2 * (size - 1 - spot) + 1)

    return place, device((place + 1) % size), device((place + size - 1) % size)


def neighbours():
    core, layer = lax.axis_index("section"), lax.axis_index("shard")
    sibling = {"section": 1 - core}
    across = {"shard": 1 - layer}
    diagonal = {"section": 1 - core, "shard": 1 - layer}
    return core, layer, sibling, across, diagonal


def greet(devices):
    barrier = pltpu.get_barrier_semaphore()
    for device in devices:
        pl.semaphore_signal(barrier, inc=1, device_id=device, device_id_type=MESH)
    pl.semaphore_wait(barrier, len(devices))


def scatter_kernel(size, count, *refs):
    own, refs = refs[: count + 1], refs[count + 1 :]
    out, refs = refs[: count + 1], refs[count + 1 :]
    landed, refs = refs[:count], refs[count:]
    send_sem, recv_sem, small_send, small_recv = refs
    small, small_out = own[count], out[count]
    place, following, previous = ring_place(size)
    targets = ({"replica": following}, {"replica": previous})
    greet(targets)

    def send(way, item, source, slot):
        return pltpu.make_async_remote_copy(
            src_ref=source,
            dst_ref=landed[item].at[way, slot],
            send_sem=send_sem.at[way, item, slot],
            recv_sem=recv_sem.at[way, item, slot],
            device_id=targets[way],
            device_id_type=MESH,
        )

    def send_small(chunk, slot):
        return pltpu.make_async_remote_copy(
            src_ref=small_out.at[chunk],
            dst_ref=small_out.at[chunk],
            send_sem=small_send.at[slot],
            recv_sem=small_recv.at[slot],
            device_id=targets[0],
            device_id_type=MESH,
        )

    def chunk_of(way, slot):
        if way == 0:
            return (place + 2 * size - 2 - slot) % size
        return (place + 2 + slot) % size

    for item in range(count):
        send(0, item, own[item].at[0, (place + size - 1) % size], 0).start()
        send(1, item, own[item].at[1, (place + 1) % size], 0).start()
    small_out[place] = small[...]
    send_small(place, 0).start()

    def step(slot, carry):
        for item in range(count):
            for way in range(2):
                here = landed[item].at[way, slot]
                send(way, item, here, slot).wait_recv()
                here[...] += own[item][way, chunk_of(way, slot)]
                send(way, item, here, slot + 1).start()
        chunk = (place + size - 1 - slot) % size
        send_small(chunk, slot).wait_recv()
        send_small(chunk, slot + 1).start()
        return carry

    lax.fori_loop(0, size - 2, step, 0)
    last = size - 2
    for item in range(count):
        for way in range(2):
            here = landed[item].at[way, last]
            send(way, item, here, last).wait_recv()
            out[item][way] = here[...] + own[item][way, place]
    send_small((place + 1) % size, last).wait_recv()

    def finish(slot, carry):
        for item in range(count):
            for way in range(2):
                send(way, item, landed[item].at[way, slot], slot).wait_send()
        send_small(place, slot).wait_send()
        return carry

    lax.fori_loop(0, size - 1, finish, 0)


def ring_scatter(pieces, small):
    size = pieces[0].shape[1]
    count = len(pieces)
    whole = pl.BlockSpec(memory_space=pltpu.VMEM)
    return pl.pallas_call(
        functools.partial(scatter_kernel, size, count),
        out_shape=[jax.ShapeDtypeStruct((2,) + item.shape[2:], BF) for item in pieces]
        + [jax.ShapeDtypeStruct((size,) + small.shape, small.dtype)],
        in_specs=[whole] * (count + 1),
        out_specs=[whole] * (count + 1),
        scratch_shapes=[pltpu.VMEM((2, size - 1) + item.shape[2:], BF) for item in pieces]
        + [pltpu.SemaphoreType.DMA((2, count, size - 1))] * 2
        + [pltpu.SemaphoreType.DMA((size - 1,))] * 2,
        compiler_params=pltpu.CompilerParams(
            collective_id=0, has_side_effects=True, vmem_limit_bytes=VMEM_LIMIT
        ),
        name="ring_scatter",
    )(*pieces, small)


def gather_kernel(size, groups, *refs):
    count = 4
    own, out = refs[:count], refs[count : 2 * count]
    swap_send, swap_recv, send_sem, recv_sem = refs[2 * count :]
    place, following, previous = ring_place(size)
    targets = ({"replica": following}, {"replica": previous})
    core, layer, sibling, across, diagonal = neighbours()
    same = core == layer
    greet(targets + (sibling, across, diagonal))

    def parts(item, source_half, sender):
        if item < len(groups):
            width = own[item].shape[2] // groups[item]
            for group in range(groups[item]):
                start = pl.multiple_of((2 * group + sender) * width, width)
                yield (
                    own[item].at[source_half, :, pl.ds(group * width, width)],
                    out[item].at[place, :, pl.ds(start, width)],
                )
        else:
            deep = own[item].shape[1]
            for half in range(2):
                yield own[item].at[half], out[item].at[place, pl.ds(half * deep, deep)]

    def copies(item, source_half, lane, kind, device=None):
        for number, (source, target) in enumerate(parts(item, source_half, core)):
            send, recv = swap_send.at[item, lane, number], swap_recv.at[item, kind, number]
            if device is None:
                yield pltpu.make_async_copy(source, target, recv)
            else:
                yield pltpu.make_async_remote_copy(
                    src_ref=source,
                    dst_ref=target,
                    send_sem=send,
                    recv_sem=recv,
                    device_id=device,
                    device_id_type=MESH,
                )

    @pl.when(same)
    def _():
        for item in range(count):
            for copy in copies(item, layer, 0, 0):
                copy.start()
            if item < len(groups):
                for copy in copies(item, 1 - layer, 0, 2, across):
                    copy.start()

    @pl.when(core != layer)
    def _():
        for item in range(count):
            for copy in copies(item, 1 - layer, 0, 3, diagonal):
                copy.start()
            if item < len(groups):
                for copy in copies(item, layer, 1, 1, sibling):
                    copy.start()

    def send(way, item, chunk, slot):
        deep = out[item].shape[1] // 2
        here = out[item].at[chunk, pl.ds(way * deep, deep)]
        return pltpu.make_async_remote_copy(
            src_ref=here,
            dst_ref=here,
            send_sem=send_sem.at[way, item, slot],
            recv_sem=recv_sem.at[way, item, slot],
            device_id=targets[way],
            device_id_type=MESH,
        )

    def chunk_of(way, slot):
        if way == 0:
            return (place + size - 1 - slot) % size
        return (place + 1 + slot) % size

    for item in range(count):

        @pl.when(same)
        def _(item=item):
            for copy in copies(item, layer, 0, 0):
                copy.wait()
            if item < len(groups):
                for copy in copies(item, layer, 1, 1, sibling):
                    copy.wait_recv()

        @pl.when(core != layer)
        def _(item=item):
            for copy in copies(item, layer, 0, 3, diagonal):
                copy.wait_recv()
            if item < len(groups):
                for copy in copies(item, layer, 0, 2, across):
                    copy.wait_recv()

        for way in range(2):
            send(way, item, place, 0).start()

    def step(slot, carry):
        for item in range(count):
            for way in range(2):
                chunk = chunk_of(way, slot)
                send(way, item, chunk, slot).wait_recv()
                send(way, item, chunk, slot + 1).start()
        return carry

    lax.fori_loop(0, size - 2, step, 0)
    last = size - 2
    for item in range(count):
        for way in range(2):
            send(way, item, chunk_of(way, last), last).wait_recv()

    @pl.when(same)
    def _():
        for item in range(len(groups)):
            for copy in copies(item, 1 - layer, 0, 2, across):
                copy.wait_send()

    @pl.when(core != layer)
    def _():
        for item in range(count):
            for copy in copies(item, 1 - layer, 0, 3, diagonal):
                copy.wait_send()
            if item < len(groups):
                for copy in copies(item, layer, 1, 1, sibling):
                    copy.wait_send()

    def finish(slot, carry):
        for item in range(count):
            for way in range(2):
                send(way, item, place, slot).wait_send()
        return carry

    lax.fori_loop(0, size - 1, finish, 0)


def ring_gather(pieces, groups, size):
    spot = pl.BlockSpec(memory_space=pl.ANY)
    shapes = [(size, item.shape[1], 2 * item.shape[2]) for item in pieces[: len(groups)]]
    shapes += [(size, 2 * item.shape[1], item.shape[2]) for item in pieces[len(groups) :]]
    count = len(pieces)
    return pl.pallas_call(
        functools.partial(gather_kernel, size, groups),
        out_shape=[jax.ShapeDtypeStruct(shape, BF) for shape in shapes],
        in_specs=[pl.BlockSpec(memory_space=pltpu.VMEM)] * count,
        out_specs=[spot] * count,
        scratch_shapes=[
            pltpu.SemaphoreType.DMA((count, 2, 3)),
            pltpu.SemaphoreType.DMA((count, 4, 3)),
        ]
        + [pltpu.SemaphoreType.DMA((2, count, size - 1))] * 2,
        compiler_params=pltpu.CompilerParams(collective_id=1, has_side_effects=True),
        name="ring_gather",
    )(*pieces)


def fetch_kernel(*refs):
    tokens, cotangent, small, qkv, fc, out, proj = refs[:7]
    outer, small_out, w_qkv, w_fc, w_out, w_proj = refs[7:13]
    send_sem, recv_sem, extra_send, extra_recv, local_sem = refs[13:18]
    buffers = refs[18:]
    core, layer, sibling, across, diagonal = neighbours()
    index = lax.axis_index("replica")
    quarter = index % 4
    low, high = index % 2, (index // 2) % 2
    beside = {"replica": index + 1 - 2 * low}
    above = {"replica": index + 2 - 4 * high}
    beside_quarter = quarter + 1 - 2 * low
    above_quarter = quarter + 2 - 4 * high
    same = core == layer
    far_quarter = 3 - quarter
    greet((sibling, across, diagonal, beside, above))

    depth = qkv.shape[0]
    span = qkv.shape[1] // 6
    wide = fc.shape[1] // 2
    turn = proj.shape[0] // 2
    cols = [
        (qkv, w_qkv, lambda s, g=g: pl.multiple_of((2 * g + s) * span, span), g * span, span)
        for g in range(3)
    ]
    cols.append((fc, w_fc, lambda s: pl.multiple_of(s * wide, wide), 0, wide))
    rows = [(out, w_out, 0, out.shape[0]), (proj, w_proj, 0, turn), (proj, w_proj, turn, turn)]
    order = [0, 1, 2, 4, 3, 5, 6]

    def rows_of(item):
        return depth if item < 4 else rows[item - 4][3]

    def target(item, base, which, part=None):
        deep = rows_of(item) // 4
        start = base + which * deep
        if part is not None:
            deep = deep // 2
            start = start + part * deep
        place = pl.ds(pl.multiple_of(start, deep), deep)
        if item < 4:
            return cols[item][1].at[place, pl.ds(cols[item][3], cols[item][4])]
        return rows[item - 4][1].at[place]

    def base_of(item, shard):
        return shard * depth if item < 4 else rows[item - 4][2]

    def remote(stage, item, source, dest, device, lane=0):
        return pltpu.make_async_remote_copy(
            src_ref=source,
            dst_ref=dest,
            send_sem=send_sem.at[stage + lane, item],
            recv_sem=recv_sem.at[stage, item],
            device_id=device,
            device_id_type=MESH,
        )

    def cross(item, receiver):
        deep = rows_of(item) // 4
        place = pl.multiple_of(base_of(item, 0) + quarter * deep, deep)
        dest = target(item, base_of(item, layer), quarter)
        if item < 4:
            columns = cols[item][2](receiver)
            source = cols[item][0].at[pl.ds(place, deep), pl.ds(columns, cols[item][4])]
        else:
            source = rows[item - 4][0].at[pl.ds(place, deep)]
        return source, dest

    def cross_same(item):
        return remote(0, item, *cross(item, core), across, 5)

    def cross_swap(item):
        return remote(0, item, *cross(item, 1 - core), diagonal)

    def pass_on(stage, item, which, device, part=None):
        here = target(item, base_of(item, 1 - layer), which, part)
        return remote(stage, item, here, here, device)

    def to_sibling(item):
        columns = cols[item][2](1 - core)
        source = cols[item][0].at[:, pl.ds(columns, cols[item][4])]
        start = pl.multiple_of(layer * depth, depth)
        dest = cols[item][1].at[pl.ds(start, depth), pl.ds(cols[item][3], cols[item][4])]
        return remote(6, item, source, dest, sibling)

    def through(source, dest, number):
        return (
            pltpu.make_async_copy(source, buffers[number], local_sem.at[number]),
            pltpu.make_async_copy(buffers[number], dest, local_sem.at[number]),
        )

    def keep_local(item):
        if item < 4:
            columns = cols[item][2](core)
            source = cols[item][0].at[:, pl.ds(columns, cols[item][4])]
            start = pl.multiple_of(layer * depth, depth)
            dest = cols[item][1].at[pl.ds(start, depth), pl.ds(cols[item][3], cols[item][4])]
        else:
            source, dest, start, deep = rows[item - 4]
            source, dest = source.at[pl.ds(start, deep)], dest.at[pl.ds(start, deep)]
        return through(source, dest, item)

    part = tokens.shape[1]
    half = part // 2

    def outer_rows(shard, which):
        return pl.ds(pl.multiple_of(shard * part + which * half, half), half)

    def outer_cross(block):
        place = pl.ds(pl.multiple_of(core * half, half), half)

        def copy(source):
            return pltpu.make_async_remote_copy(
                src_ref=source.at[block, place],
                dst_ref=outer.at[block, outer_rows(layer, core)],
                send_sem=extra_send.at[block],
                recv_sem=extra_recv.at[block],
                device_id=across,
                device_id_type=MESH,
            )

        return copy

    def outer_pass(block):
        here = outer.at[block, outer_rows(1 - layer, core)]
        return pltpu.make_async_remote_copy(
            src_ref=here,
            dst_ref=here,
            send_sem=extra_send.at[2 + block],
            recv_sem=extra_recv.at[2 + block],
            device_id=sibling,
            device_id_type=MESH,
        )

    def outer_local(source):
        place = pl.ds(pl.multiple_of(layer * part, part), part)
        return through(source, outer.at[:, place], 7)

    def small_swap():
        return pltpu.make_async_remote_copy(
            src_ref=small,
            dst_ref=small_out.at[1 - core],
            send_sem=extra_send.at[4],
            recv_sem=extra_recv.at[4],
            device_id=diagonal,
            device_id_type=MESH,
        )

    def small_pass():
        return pltpu.make_async_remote_copy(
            src_ref=small_out.at[core],
            dst_ref=small_out.at[core],
            send_sem=extra_send.at[5],
            recv_sem=extra_recv.at[5],
            device_id=sibling,
            device_id_type=MESH,
        )

    def small_local():
        return through(small, small_out.at[core], 8)

    def start_outer(block):
        @pl.when(layer == 0)
        def _():
            outer_cross(block)(cotangent).start()

        @pl.when(layer == 1)
        def _():
            outer_cross(block)(tokens).start()

    def crossings(item):
        if item < 4:
            cross_same(item).start()
        cross_swap(item).start()

    @pl.when(same)
    def _():
        small_local()[0].start()

    @pl.when(core != layer)
    def _():
        small_swap().start()

    start_outer(0)

    @pl.when(core != layer)
    def _():
        crossings(order[0])
        crossings(order[1])

    @pl.when(layer == 0)
    def _():
        outer_local(tokens)[0].start()

    @pl.when(layer == 1)
    def _():
        outer_local(cotangent)[0].start()

    @pl.when(same)
    def _():
        for item in range(4):
            to_sibling(item).start()
        load, store = small_local()
        load.wait()
        store.start()
        store.wait()

    @pl.when(core != layer)
    def _():
        small_swap().wait_recv()

    small_pass().start()
    outer_local(tokens)[0].wait()
    outer_local(tokens)[1].start()

    @pl.when(same)
    def _():
        for item in range(7):
            keep_local(item)[0].start()

    def relay(sequence, ahead):
        def onward(item):
            pass_on(1, item, beside_quarter, beside).wait_recv()
            pass_on(4, item, beside_quarter, above, 0).start()
            pass_on(2, item, above_quarter, above).wait_recv()
            pass_on(3, item, above_quarter, beside, 1).start()

        for number, item in enumerate(sequence):
            pass_on(0, item, quarter, beside).wait_recv()
            if ahead and number + 2 < len(sequence):
                crossings(sequence[number + 2])
            pass_on(1, item, quarter, beside).start()
            pass_on(2, item, quarter, above).start()
            if number >= 1:
                onward(sequence[number - 1])
            if number == 0:
                outer_cross(0)(tokens).wait_recv()
                outer_pass(0).start()
                start_outer(1)
        onward(sequence[-1])
        for item in sequence:
            pass_on(3, item, far_quarter, beside, 1).wait_recv()
            pass_on(4, item, far_quarter, above, 0).wait_recv()
            for stage in (1, 2):
                pass_on(stage, item, quarter, beside).wait_send()
            for stage, which in ((3, 1), (4, 0)):
                pass_on(stage, item, quarter, beside, which).wait_send()

    @pl.when(same)
    def _():
        for item in range(7):
            load, store = keep_local(item)
            load.wait()
            store.start()
        relay([0, 1, 2, 3], False)
        for item in range(4):
            to_sibling(item).wait_send()
        for item in range(7):
            keep_local(item)[1].wait()

    @pl.when(core != layer)
    def _():
        relay(order, True)
        for item in range(4):
            to_sibling(item).wait_recv()
            cross_same(item).wait_send()
        for item in range(7):
            cross_swap(item).wait_send()
        small_swap().wait_send()

    outer_cross(1)(tokens).wait_recv()
    outer_pass(1).start()
    outer_local(tokens)[1].wait()
    small_pass().wait()
    for block in range(2):
        outer_cross(block)(tokens).wait_send()
        outer_pass(block).wait()


def fetch_inputs(tokens, cotangent, small, qkv, fc, out, proj):
    spot = pl.BlockSpec(memory_space=pl.ANY)
    micro, part, width = tokens.shape
    shapes = [
        (micro, 2 * part, width),
        (2,) + small.shape,
        (2 * qkv.shape[0], qkv.shape[1] // 2),
        (2 * fc.shape[0], fc.shape[1] // 2),
        out.shape,
        proj.shape,
    ]
    return pl.pallas_call(
        fetch_kernel,
        out_shape=[jax.ShapeDtypeStruct(shape, BF) for shape in shapes],
        in_specs=[spot] * 7,
        out_specs=[spot] * 6,
        scratch_shapes=[
            pltpu.SemaphoreType.DMA((7, 7)),
            pltpu.SemaphoreType.DMA((7, 7)),
            pltpu.SemaphoreType.DMA((6,)),
            pltpu.SemaphoreType.DMA((6,)),
            pltpu.SemaphoreType.DMA((9,)),
        ]
        + [pltpu.VMEM((qkv.shape[0], qkv.shape[1] // 6), BF)] * 3
        + [
            pltpu.VMEM((fc.shape[0], fc.shape[1] // 2), BF),
            pltpu.VMEM(out.shape, BF),
            pltpu.VMEM((proj.shape[0] // 2, width), BF),
            pltpu.VMEM((proj.shape[0] // 2, width), BF),
            pltpu.VMEM(tokens.shape, BF),
            pltpu.VMEM(small.shape, BF),
        ],
        compiler_params=pltpu.CompilerParams(
            collective_id=2, has_side_effects=True, vmem_limit_bytes=VMEM_LIMIT
        ),
        name="fetch_inputs",
    )(tokens, cotangent, small, qkv, fc, out, proj)


TILES = 2


class Loads:
    def __init__(self, sem):
        self.sem, self.count, self.made = sem, 0, {}

    def start(self, name, source, buffer):
        copy = pltpu.make_async_copy(source, buffer, self.sem.at[self.count])
        self.count += 1
        copy.start()
        self.made[name] = copy

    def wait(self, *names):
        for name in names:
            self.made.pop(name).wait()


def chosen_load(first_ref, other_ref, buffer, sem):
    layer = lax.axis_index("shard")

    @pl.when(layer == 0)
    def _():
        pltpu.make_async_copy(first_ref, buffer, sem).start()

    @pl.when(layer != 0)
    def _():
        pltpu.make_async_copy(other_ref, buffer, sem).start()

    return pltpu.make_async_copy(first_ref, buffer, sem)


def greet_step(sender, passing):
    core, layer, sibling, across, _ = neighbours()
    barrier = pltpu.get_barrier_semaphore()
    pl.semaphore_signal(barrier, inc=1, device_id=sibling, device_id_type=MESH)
    if not passing:
        pl.semaphore_wait(barrier, 1)
        return

    @pl.when(layer != sender)
    def _():
        pl.semaphore_signal(barrier, inc=1, device_id=across, device_id_type=MESH)
        pl.semaphore_wait(barrier, 1)

    @pl.when(layer == sender)
    def _():
        pl.semaphore_wait(barrier, 2)


class Exchange:
    def __init__(self, send_buf, recv_buf, send_sem, recv_sem):
        self.refs = (send_buf, recv_buf, send_sem, recv_sem)

    def copy(self, slot):
        send_buf, recv_buf, send_sem, recv_sem = self.refs
        return pltpu.make_async_remote_copy(
            src_ref=send_buf.at[slot],
            dst_ref=recv_buf.at[slot],
            send_sem=send_sem.at[slot],
            recv_sem=recv_sem.at[slot],
            device_id={"section": 1 - lax.axis_index("section")},
            device_id_type=MESH,
        )

    def give(self, slot, partial):
        self.refs[0][slot] = partial.astype(BF)
        self.copy(slot).start()

    def take(self, slot):
        self.copy(slot).wait_recv()
        return self.refs[1][slot].astype(F32)

    def finish(self, count):
        for slot in range(count):
            self.copy(slot).wait_send()


class Across:
    def __init__(self, sender, source, dest, sems):
        self.sender, self.source, self.dest, self.sems = sender, source, dest, sems
        self.core, self.layer, self.sibling, self.across, _ = neighbours()

    def copy(self, tile, stage):
        rows = self.dest.shape[0] // (2 * TILES)
        place = pl.ds(pl.multiple_of((2 * tile + self.core) * rows, rows), rows)
        source = self.source if stage == 0 else self.dest
        return pltpu.make_async_remote_copy(
            src_ref=source.at[place],
            dst_ref=self.dest.at[place],
            send_sem=self.sems.at[stage, tile],
            recv_sem=self.sems.at[2 + stage, tile],
            device_id=self.across if stage == 0 else self.sibling,
            device_id_type=MESH,
        )

    def send(self, tile):
        @pl.when(self.layer == self.sender)
        def _():
            self.copy(tile, 0).start()

    def finish(self):
        @pl.when(self.layer == self.sender)
        def _():
            for tile in range(TILES):
                self.copy(tile, 0).wait_send()

        @pl.when(self.layer != self.sender)
        def _():
            for tile in range(TILES):
                self.copy(tile, 0).wait_recv()
                self.copy(tile, 1).start()
            for tile in range(TILES):
                self.copy(tile, 1).wait()


def by_past(mode, body):
    if mode is not None:
        body(mode)
        return
    layer = lax.axis_index("shard")

    @pl.when(layer == 0)
    def _():
        body(True)

    @pl.when(layer != 0)
    def _():
        body(False)


FORWARD_LOADS = 7


def forward_kernel(mode, passing, *refs):
    x_first, x_other, params, w_qkv, w_out, w_fc, w_proj, k_past, v_past = refs[:9]
    refs = refs[9:]
    (normed1, query, keys, values, mixed, lse, scaled2, inverse2, normed2, slope, act, out, passed) = refs[:13]
    refs = refs[13:]
    (x_v, wq_v, wo_v, wf_v, wp_v, k_v, v_v, hid_v, part_v, send_v, recv_v) = refs[:11]
    refs = refs[11:]
    (n1_v, q_v, m_v, lse_v, s2_v, i2_v, n2_v, sl_v, a_v, o_v) = refs[:10]
    load_sem, store_sem, send_sem, recv_sem, across_sem = refs[10:]
    rows, width = x_v.shape
    half = q_v.shape[1]
    tile_rows = rows // TILES
    wide = a_v.shape[1]

    loads = Loads(load_sem)
    load_x = chosen_load(x_first, x_other, x_v, load_sem.at[FORWARD_LOADS])
    loads.start("qkv", w_qkv, wq_v)
    if mode is not False:
        loads.start("k", k_past, k_v.at[pl.ds(0, rows)])
        loads.start("v", v_past, v_v.at[pl.ds(0, rows)])
    loads.start("out", w_out, wo_v)
    loads.start("fc", w_fc, wf_v)
    loads.start("proj", w_proj, wp_v)
    greet_step(0, passing)
    exchange = Exchange(send_v, recv_v, send_sem, recv_sem)
    across = Across(0, o_v, passed, across_sem)
    stores = []

    def store(buffer, dest):
        copy = pltpu.make_async_copy(buffer, dest, store_sem.at[len(stores)])
        copy.start()
        stores.append(copy)

    def vector(row, start=0, size=None):
        return params[row : row + 1, start : start + (size or width)]

    load_x.wait()
    for tile in range(TILES):
        span = pl.ds(tile * tile_rows, tile_rows)
        scaled, _ = norm_parts(x_v[span, :].astype(F32))
        n1_v[span, :] = (scaled * vector(0) + vector(1)).astype(BF)
    store(n1_v, normed1)
    loads.wait("qkv")
    own_rows = pl.ds(rows, rows)
    for tile in range(TILES):
        span = pl.ds(tile * tile_rows, tile_rows)
        later = pl.ds(rows + tile * tile_rows, tile_rows)
        normed = n1_v[span, :]
        piece = jnp.dot(normed, wq_v[:, :half], preferred_element_type=F32)
        q_v[span, :] = (piece + vector(6, 0, half)).astype(BF)
        piece = jnp.dot(normed, wq_v[:, half : 2 * half], preferred_element_type=F32)
        k_v[later, :] = piece.astype(BF)
        piece = jnp.dot(normed, wq_v[:, 2 * half :], preferred_element_type=F32)
        v_v[later, :] = (piece + vector(6, half, half)).astype(BF)
    store(q_v, query)
    store(k_v.at[own_rows], keys)
    store(v_v.at[own_rows], values)
    if mode is not False:
        loads.wait("k", "v")
    loads.wait("out")

    def attention(past):
        first_key = 0 if past else rows
        for tile in range(TILES):
            span = pl.ds(tile * tile_rows, tile_rows)
            length = (rows if past else 0) + (tile + 1) * tile_rows
            reach = pl.ds(first_key, length)

            def pair(number, carry):
                lanes = pl.ds(pl.multiple_of(number * 128, 128), 128)
                key, value = k_v[reach, lanes], v_v[reach, lanes]
                pieces = []
                for head, part in enumerate(head_parts(q_v[span, lanes])):
                    scores = masked_scores(key, part * BF(HEAD_DIM**-0.5), length)
                    top = jnp.max(scores, axis=0, keepdims=True)
                    probs = jnp.exp(scores - top)
                    total = jnp.sum(probs, axis=0, keepdims=True)
                    lse_v[number, pl.ds(head, 1), span] = top + jnp.log(total)
                    piece = rows_product(value, probs.astype(BF))
                    piece = piece[head * HEAD_DIM : (head + 1) * HEAD_DIM]
                    pieces.append(piece * (1.0 / total))
                m_v[span, lanes] = jnp.transpose(jnp.concatenate(pieces, axis=0)).astype(BF)
                return carry

            lax.fori_loop(0, half // 128, pair, 0)
            partial = jnp.dot(m_v[span, :], wo_v[...], preferred_element_type=F32)
            part_v[tile] = partial
            exchange.give(tile, partial)

    by_past(mode, attention)
    store(m_v, mixed)
    store(lse_v, lse)
    loads.wait("fc", "proj")
    for tile in range(TILES):
        span = pl.ds(tile * tile_rows, tile_rows)
        hidden = x_v[span, :].astype(F32) + (part_v[tile] + exchange.take(tile)) + vector(2)
        hid_v[span, :] = hidden
        scaled, inverse = norm_parts(hidden)
        s2_v[span, :] = scaled.astype(BF)
        i2_v[span, :] = jnp.broadcast_to(inverse, (tile_rows, 128))
        normed = (scaled * vector(3) + vector(4)).astype(BF)
        n2_v[span, :] = normed
        chunk = width // 2
        for part in range(wide // chunk):
            columns = pl.ds(part * chunk, chunk)
            pre = jnp.dot(normed, wf_v[:, columns], preferred_element_type=F32)
            bias = vector(7 + part * chunk // width, part * chunk % width, chunk)
            activated, inclined = gelu_pair(pre + bias)
            a_v[span, columns] = activated.astype(BF)
            sl_v[span, columns] = inclined.astype(BF)
        partial = jnp.dot(a_v[span, :], wp_v[...], preferred_element_type=F32)
        part_v[TILES + tile] = partial
        exchange.give(TILES + tile, partial)
    store(s2_v, scaled2)
    store(i2_v, inverse2)
    store(n2_v, normed2)
    store(sl_v, slope)
    store(a_v, act)
    for tile in range(TILES):
        span = pl.ds(tile * tile_rows, tile_rows)
        total = part_v[TILES + tile] + exchange.take(TILES + tile)
        o_v[span, :] = (hid_v[span, :] + total + vector(5)).astype(BF)
        if passing:
            across.send(tile)
    store(o_v, out)
    for copy in stores:
        copy.wait()
    exchange.finish(2 * TILES)
    if passing:
        across.finish()


def step_sems(loads, stores):
    return [
        pltpu.SemaphoreType.DMA((loads,)),
        pltpu.SemaphoreType.DMA((stores,)),
        pltpu.SemaphoreType.DMA((2 * TILES,)),
        pltpu.SemaphoreType.DMA((2 * TILES,)),
        pltpu.SemaphoreType.DMA((4, TILES)),
    ]


def forward_step(mode, passing, x_first, x_other, params, weights, past):
    rows, width = x_first.shape
    half = width // 2
    wide = weights[2].shape[1]
    pairs = half // 128
    tile_rows = rows // TILES
    spot = pl.BlockSpec(memory_space=pl.ANY)
    low = lambda columns: ((rows, columns), BF)
    outs = [
        low(width),
        low(half),
        low(half),
        low(half),
        low(half),
        ((pairs, 8, rows), F32),
        low(width),
        ((rows, 128), F32),
        low(width),
        low(wide),
        low(wide),
        low(width),
        low(width),
    ]
    scratch = [
        low(width),
        *((item.shape, BF) for item in weights),
        ((2 * rows, half), BF),
        ((2 * rows, half), BF),
        ((rows, width), F32),
        ((2 * TILES, tile_rows, width), F32),
        ((2 * TILES, tile_rows, width), BF),
        ((2 * TILES, tile_rows, width), BF),
        low(width),
        low(half),
        low(half),
        ((pairs, 8, rows), F32),
        low(width),
        ((rows, 128), F32),
        low(width),
        low(wide),
        low(wide),
        low(width),
    ]
    number = {(False, True): 3, (None, True): 4, (True, False): 5}[(mode, passing)]
    return pl.pallas_call(
        functools.partial(forward_kernel, mode, passing),
        out_shape=[jax.ShapeDtypeStruct(*item) for item in outs],
        in_specs=[spot] * 2 + [pl.BlockSpec(memory_space=pltpu.VMEM)] + [spot] * 6,
        out_specs=[spot] * len(outs),
        scratch_shapes=[pltpu.VMEM(*item) for item in scratch]
        + step_sems(FORWARD_LOADS + 1, len(outs)),
        compiler_params=pltpu.CompilerParams(
            collective_id=number, has_side_effects=True, vmem_limit_bytes=VMEM_LIMIT
        ),
        name="forward_step",
    )(x_first, x_other, params, *weights, *past)


BACKWARD_LOADS = 16


def backward_kernel(mode, passing, *refs):
    (g_first, g_other, x_first, x_other, params, w_qkv, w_out, w_fc, w_proj) = refs[:9]
    (query, keys, values, k_past, v_past, mixed, lse, scaled2, inverse2, slope, pend_k, pend_v) = refs[9:21]
    refs = refs[21:]
    (d_qkv, d_branch, d_pre, out, next_k, next_v, sums, passed) = refs[:8]
    refs = refs[8:]
    (g_v, x_v, wq_v, wo_v, wf_v, wp_v, q_v, k_v, v_v, m_v, lse_v, s2_v, i2_v, sl_v) = refs[:14]
    refs = refs[14:]
    (dk_v, dv_v, hid_v, part_v, send_v, recv_v, dqkv_v, db_v, dp_v, dm_v, o_v, sum_v) = refs[:12]
    load_sem, store_sem, send_sem, recv_sem, across_sem = refs[12:]
    rows, width = x_v.shape
    half = q_v.shape[1]
    wide = dp_v.shape[1]
    tile_rows = rows // TILES
    own_rows, past_rows = pl.ds(rows, rows), pl.ds(0, rows)
    scale = HEAD_DIM**-0.5

    loads = Loads(load_sem)
    load_g = chosen_load(g_first, g_other, g_v, load_sem.at[BACKWARD_LOADS])
    loads.start("proj", w_proj, wp_v)
    loads.start("slope", slope, sl_v)
    loads.start("fc", w_fc, wf_v)
    loads.start("scaled2", scaled2, s2_v)
    loads.start("inverse2", inverse2, i2_v)
    loads.start("out", w_out, wo_v)
    loads.start("q", query, q_v)
    loads.start("k", keys, k_v.at[own_rows])
    loads.start("v", values, v_v.at[own_rows])
    if mode is not False:
        loads.start("k_past", k_past, k_v.at[past_rows])
        loads.start("v_past", v_past, v_v.at[past_rows])
    loads.start("mixed", mixed, m_v)
    loads.start("lse", lse, lse_v)
    if mode is not True:
        loads.start("pend_k", pend_k, dk_v.at[own_rows])
        loads.start("pend_v", pend_v, dv_v.at[own_rows])
    loads.start("qkv", w_qkv, wq_v)
    load_x = chosen_load(x_first, x_other, x_v, load_sem.at[BACKWARD_LOADS + 1])
    greet_step(1, passing)
    exchange = Exchange(send_v, recv_v, send_sem, recv_sem)
    across = Across(1, o_v, passed, across_sem)
    stores = []

    def store(buffer, dest):
        copy = pltpu.make_async_copy(buffer, dest, store_sem.at[len(stores)])
        copy.start()
        stores.append(copy)

    def vector(row, start=0, size=None):
        return params[row : row + 1, start : start + (size or width)]

    sum_v[...] = jnp.zeros_like(sum_v)

    def tally(row, piece, start=0):
        place = (slice(row, row + 1), slice(start, start + piece.shape[1]))
        sum_v[place] += jnp.sum(piece, axis=0, keepdims=True)

    load_g.wait()
    loads.wait("proj", "slope", "fc")
    chunk = width // 2
    for tile in range(TILES):
        span = pl.ds(tile * tile_rows, tile_rows)
        grad = g_v[span, :]
        for part in range(wide // chunk):
            columns = pl.ds(part * chunk, chunk)
            d_act = cols_product(grad, wp_v[columns, :])
            piece = (d_act * sl_v[span, columns].astype(F32)).astype(BF)
            dp_v[span, columns] = piece
            tally(7 + part * chunk // width, piece.astype(F32), part * chunk % width)
        partial = cols_product(dp_v[span, :], wf_v[...])
        part_v[tile] = partial
        exchange.give(tile, partial)
        tally(5, grad.astype(F32))
    store(dp_v, d_pre)
    loads.wait("scaled2", "inverse2", "out")
    for tile in range(TILES):
        span = pl.ds(tile * tile_rows, tile_rows)
        d_normed = part_v[tile] + exchange.take(tile)
        scaled = s2_v[span, :].astype(F32)
        tally(3, d_normed * scaled)
        tally(4, d_normed)
        d_hidden = g_v[span, :].astype(F32) + norm_backward(
            d_normed, scaled, i2_v[span, 0:1], vector(3)
        )
        hid_v[span, :] = d_hidden
        branch = d_hidden.astype(BF)
        db_v[span, :] = branch
        tally(2, branch.astype(F32))
        dm_v[span, :] = cols_product(branch, wo_v[...]).astype(BF)
    store(db_v, d_branch)
    loads.wait("q", "k", "v", "mixed", "lse")
    if mode is not False:
        loads.wait("k_past", "v_past")
    if mode is not True:
        loads.wait("pend_k", "pend_v")

    def attention(past):
        first_key = 0 if past else rows
        if past:
            dk_v[...] = jnp.zeros_like(dk_v)
            dv_v[...] = jnp.zeros_like(dv_v)
        for tile in range(TILES):
            span = pl.ds(tile * tile_rows, tile_rows)
            length = (rows if past else 0) + (tile + 1) * tile_rows
            reach = pl.ds(first_key, length)

            def pair(number, carry):
                lanes = pl.ds(pl.multiple_of(number * 128, 128), 128)
                key, value = k_v[reach, lanes], v_v[reach, lanes]
                grads = dm_v[span, lanes]
                products = jnp.transpose(grads.astype(F32) * m_v[span, lanes].astype(F32))
                queries, grads = head_parts(q_v[span, lanes]), head_parts(grads)
                d_query = []
                d_key = d_value = None
                for head in range(2):
                    take = slice(head * HEAD_DIM, (head + 1) * HEAD_DIM)
                    scaled_query = queries[head] * BF(scale)
                    scores = masked_scores(key, scaled_query, length)
                    weights = jnp.exp(scores - lse_v[number, pl.ds(head, 1), span])
                    d_probs = cols_product(value, grads[head])
                    delta = jnp.sum(products[take], axis=0, keepdims=True)
                    d_scores = (weights * (d_probs - delta)).astype(BF)
                    one = jnp.dot(weights.astype(BF), grads[head], preferred_element_type=F32)
                    two = jnp.dot(d_scores, scaled_query, preferred_element_type=F32)
                    d_value = one if head == 0 else d_value + one
                    d_key = two if head == 0 else d_key + two
                    d_query.append(rows_product(key, d_scores)[take])
                dk_v[reach, lanes] += d_key
                dv_v[reach, lanes] += d_value
                d_query = jnp.transpose(jnp.concatenate(d_query, axis=0) * scale)
                dqkv_v[span, lanes] = d_query.astype(BF)
                return carry

            lax.fori_loop(0, half // 128, pair, 0)

    by_past(mode, attention)
    if mode is not False:
        store(dk_v.at[past_rows], next_k)
        store(dv_v.at[past_rows], next_v)
    loads.wait("qkv")
    load_x.wait()
    for tile in range(TILES):
        span = pl.ds(tile * tile_rows, tile_rows)
        later = pl.ds(rows + tile * tile_rows, tile_rows)
        dqkv_v[span, half : 2 * half] = dk_v[later, :].astype(BF)
        dqkv_v[span, 2 * half :] = dv_v[later, :].astype(BF)
        piece = dqkv_v[span, :]
        partial = cols_product(piece, wq_v[...])
        part_v[TILES + tile] = partial
        exchange.give(TILES + tile, partial)
        tally(6, piece[:, :half].astype(F32))
        tally(6, piece[:, 2 * half :].astype(F32), half)
    store(dqkv_v, d_qkv)
    for tile in range(TILES):
        span = pl.ds(tile * tile_rows, tile_rows)
        scaled, inverse = norm_parts(x_v[span, :].astype(F32))
        d_normed = part_v[TILES + tile] + exchange.take(TILES + tile)
        tally(0, d_normed * scaled)
        tally(1, d_normed)
        d_inputs = hid_v[span, :] + norm_backward(d_normed, scaled, inverse, vector(0))
        o_v[span, :] = d_inputs.astype(BF)
        if passing:
            across.send(tile)
    store(o_v, out)
    store(sum_v, sums)
    for copy in stores:
        copy.wait()
    exchange.finish(2 * TILES)
    if passing:
        across.finish()


def backward_step(mode, passing, grads, inputs, params, weights, kept, pending):
    rows, width = inputs[0].shape
    half = width // 2
    wide = weights[2].shape[1]
    pairs = half // 128
    tile_rows = rows // TILES
    spot = pl.BlockSpec(memory_space=pl.ANY)
    low = lambda columns: ((rows, columns), BF)
    outs = [
        low(3 * half),
        low(width),
        low(wide),
        low(width),
        ((rows, half), F32),
        ((rows, half), F32),
        ((16, width), F32),
        low(width),
    ]
    scratch = [
        low(width),
        low(width),
        *((item.shape, BF) for item in weights),
        low(half),
        ((2 * rows, half), BF),
        ((2 * rows, half), BF),
        low(half),
        ((pairs, 8, rows), F32),
        low(width),
        ((rows, 128), F32),
        low(wide),
        ((2 * rows, half), F32),
        ((2 * rows, half), F32),
        ((rows, width), F32),
        ((2 * TILES, tile_rows, width), F32),
        ((2 * TILES, tile_rows, width), BF),
        ((2 * TILES, tile_rows, width), BF),
        low(3 * half),
        low(width),
        low(wide),
        low(half),
        low(width),
        ((16, width), F32),
    ]
    number = {(True, True): 6, (None, True): 7, (False, False): 8}[(mode, passing)]
    return pl.pallas_call(
        functools.partial(backward_kernel, mode, passing),
        out_shape=[jax.ShapeDtypeStruct(*item) for item in outs],
        in_specs=[spot] * 4 + [pl.BlockSpec(memory_space=pltpu.VMEM)] + [spot] * 16,
        out_specs=[spot] * len(outs),
        scratch_shapes=[pltpu.VMEM(*item) for item in scratch]
        + step_sems(BACKWARD_LOADS + 2, len(outs)),
        compiler_params=pltpu.CompilerParams(
            collective_id=number, has_side_effects=True, vmem_limit_bytes=VMEM_LIMIT
        ),
        name="backward_step",
    )(*grads, *inputs, params, *weights, *kept, *pending)


def shards(
    tokens,
    cotangent,
    attn_gain,
    attn_shift,
    qkv_weight,
    query_bias,
    value_bias,
    out_weight,
    out_bias,
    mlp_gain,
    mlp_shift,
    fc_weight,
    fc_bias,
    proj_weight,
    proj_bias,
):
    core = lax.axis_index("section")
    layer = lax.axis_index("shard")
    size = lax.axis_size("replica")
    own = core == layer
    first = layer == 0
    left = core == 0
    micro, part, width = tokens.shape[1:]
    assert micro == 2
    rows = 2 * part
    half = width // 2
    hidden_half = fc_weight.shape[2] // 2

    def pair_permute(value, pairs):
        return lax.ppermute(value, PAIR, pairs)

    small = jnp.concatenate(
        [
            item[0]
            for item in (
                attn_gain,
                attn_shift,
                out_bias,
                mlp_gain,
                mlp_shift,
                proj_bias,
                query_bias,
                value_bias,
                fc_bias,
            )
        ]
    ).reshape(-1, 128)
    outer, small_both, w_qkv, w_fc, w_out, w_proj = fetch_inputs(
        tokens[0], cotangent[0], small, qkv_weight[0], fc_weight[0], out_weight[0], proj_weight[0]
    )
    flat = small_both.reshape(2, -1).astype(F32)
    mine = jnp.where(left, flat[0], flat[1])
    params = jnp.concatenate(
        [
            flat[0, : 6 * half].reshape(6, half),
            flat[1, : 6 * half].reshape(6, half),
        ],
        axis=1,
    )
    params = jnp.concatenate(
        [params, mine[6 * half :].reshape(-1, width), jnp.zeros((7, width), F32)], axis=0
    )
    weights = (w_qkv, w_out, w_fc, w_proj)

    empty = jnp.zeros((rows, half), BF)
    received, kept_list, outputs, past = [outer[0]], [], [], (empty, empty)
    for step in range(micro + 1):
        mode = (False, None, True)[step]
        normed1, query, keys, values, mixed, lse, scaled2, inverse2, normed2, slope, act, output, got = (
            forward_step(
                mode,
                step < micro,
                outer[min(step, micro - 1)],
                received[step],
                params,
                weights,
                past,
            )
        )
        outputs.append(output)
        kept = (query, keys, values, *past, mixed, lse, scaled2, inverse2, slope)
        kept_list.append((kept, normed1, normed2, act))
        past = (keys, values)
        received.append(got)

    pending = (jnp.zeros((rows, half), F32), jnp.zeros((rows, half), F32))
    grad_received = [outer[0]]
    terms_list, results, sums = [], [], None
    for step in range(micro + 1):
        mode = (True, None, False)[step]
        active = jnp.where(first, step >= 1, step < micro)
        last = micro - step
        kept, normed1, normed2, act = kept_list[last]
        grads = (grad_received[step], outer[max(micro - 1 - step, 0)])
        d_qkv, d_branch, d_pre, result, *pending, vector, got = backward_step(
            mode,
            step < micro,
            grads,
            (outer[min(last, micro - 1)], received[last]),
            params,
            weights,
            kept,
            pending,
        )
        results.append(result)
        grad_received.append(got)
        vector = jnp.where(active, vector, 0.0)
        sums = vector if sums is None else sums + vector
        grad = jnp.where(first, *grads)
        terms_list.append((normed1, d_qkv, kept[5], d_branch, normed2, d_pre, act, grad))
    full = lax.dynamic_slice_in_dim(sums[:6], core * half, half, 1)
    sums = jnp.concatenate([full.reshape(-1), sums[6:9].reshape(-1)])

    late = [jnp.where(first, a, b) for a, b in zip(terms_list[2], terms_list[0])]
    both = [jnp.concatenate([a, b], axis=0) for a, b in zip(terms_list[1], late)]
    chunk = half // size
    wide = hidden_half // size
    pieces = [
        rows_product(both[0], both[1]).astype(BF).reshape(2, size, chunk, 3 * half),
        rows_product(both[4], both[5]).astype(BF).reshape(2, size, chunk, hidden_half),
        rows_product(both[2], both[3]).astype(BF).reshape(size, 2, chunk // 2, width),
        rows_product(both[6], both[7]).astype(BF).reshape(size, 2, wide // 2, width),
    ]
    pieces[2] = jnp.swapaxes(pieces[2], 0, 1)
    pieces[3] = jnp.swapaxes(pieces[3], 0, 1)
    sums = sums.reshape(-1, 128)
    sums = jnp.where(own, sums, pair_permute(sums, CROSS_SWAP))
    *reduced, sums = ring_scatter(pieces, sums)
    sums = jnp.sum(sums, axis=0).reshape(-1)
    vectors = [sums[i * half : (i + 1) * half][None] for i in range(8)] + [sums[8 * half :][None]]
    qkv_grad, fc_grad, out_grad, proj_grad = (
        item.astype(F32).reshape(1, -1, item.shape[-1])
        for item in ring_gather(reduced, (3, 1), size)
    )

    def placed(mine, arrived, pairs, far):
        near = lax.dynamic_slice_in_dim(mine, layer * part, part, 0)
        give = lax.dynamic_slice_in_dim(mine, (1 - layer) * part, part, 0)
        sent = pair_permute(give, pairs)
        piped = lax.dynamic_slice_in_dim(arrived, layer * part, part, 0)
        return jnp.where(own, near, jnp.where(far, piped, sent))

    activations = jnp.stack(
        [
            placed(
                jnp.where(first, outputs[i], outputs[i + 1]),
                received[i + 1],
                [(3, 2)],
                layer == 1,
            )
            for i in range(micro)
        ]
    )[None, None]
    input_grads = jnp.stack(
        [
            placed(
                jnp.where(first, results[micro - i], results[micro - 1 - i]),
                grad_received[micro - i],
                [(0, 1)],
                layer == 0,
            )
            for i in range(micro)
        ]
    )[None, None]
    return (
        activations,
        input_grads,
        vectors[0],
        vectors[1],
        qkv_grad,
        vectors[6],
        vectors[7],
        out_grad,
        vectors[2],
        vectors[3],
        vectors[4],
        fc_grad,
        vectors[8],
        proj_grad,
        vectors[5],
    )


def solution(mesh):
    block = P("replica", None, "shard", None)
    layers = P("section", "replica", None, "shard", None)
    vector = P("section", "shard")
    matrix = P("section", "shard", None)
    kinds = (
        vector,
        vector,
        matrix,
        vector,
        vector,
        matrix,
        vector,
        vector,
        vector,
        matrix,
        vector,
        matrix,
        vector,
    )
    return jax.shard_map(
        shards,
        mesh=mesh,
        in_specs=(block, block) + kinds,
        out_specs=(layers, layers) + kinds,
        check_vma=False,
    )
```

```python
import functools

import jax
import jax.numpy as jnp
from jax import lax
from jax.experimental import pallas as pl
from jax.experimental.pallas import tpu as pltpu
from jax.sharding import PartitionSpec as P

HEAD_DIM = 64
EPSILON = 1e-05
GELU_SCALE = 0.7978845608028654
GELU_CUBIC = 0.044715
ROWS_CONTRACT = (((0,), (0,)), ((), ()))
COLS_CONTRACT = (((1,), (1,)), ((), ()))
BF = jnp.bfloat16
F32 = jnp.float32
MESH = pl.DeviceIdType.MESH
QTILE = 256
VMEM_LIMIT = 56 * 1024 * 1024

CROSS_SWAP = [(1, 2), (2, 1)]
PAIR = ("section", "shard")


def rows_product(left, right):
    return lax.dot_general(left, right, ROWS_CONTRACT, preferred_element_type=F32)


def cols_product(left, right):
    return lax.dot_general(left, right, COLS_CONTRACT, preferred_element_type=F32)


def norm_parts(inputs):
    mean = jnp.mean(inputs, axis=-1, keepdims=True)
    centered = inputs - mean
    inverse = lax.rsqrt(jnp.mean(centered * centered, axis=-1, keepdims=True) + EPSILON)
    return centered * inverse, inverse


def norm_backward(d_normed, scaled, inverse, gain):
    d_scaled = d_normed * gain
    return inverse * (
        d_scaled
        - jnp.mean(d_scaled, axis=-1, keepdims=True)
        - scaled * jnp.mean(d_scaled * scaled, axis=-1, keepdims=True)
    )


def gelu_pair(pre):
    tangent = jnp.tanh(GELU_SCALE * (pre + GELU_CUBIC * pre * pre * pre))
    value = 0.5 * pre * (1.0 + tangent)
    slope = 0.5 * (1.0 + tangent) + 0.5 * pre * (1.0 - tangent * tangent) * GELU_SCALE * (
        1.0 + 3.0 * GELU_CUBIC * pre * pre
    )
    return value, slope


def head_parts(pair):
    low = lax.broadcasted_iota(jnp.int32, pair.shape, 1) < HEAD_DIM
    zero = jnp.zeros_like(pair)
    return jnp.where(low, pair, zero), jnp.where(low, zero, pair)


def masked_scores(keys, query, length):
    scores = cols_product(keys, query)
    tail = scores[length - QTILE :]
    key_pos = lax.broadcasted_iota(jnp.int32, tail.shape, 0)
    query_pos = lax.broadcasted_iota(jnp.int32, tail.shape, 1)
    tail = jnp.where(key_pos <= query_pos, tail, -1e30)
    if length == QTILE:
        return tail
    return jnp.concatenate([scores[: length - QTILE], tail], axis=0)


def ring_place(size):
    index = lax.axis_index("replica")
    odd = index % 2
    half = index // 2
    place = (1 - odd) * half + odd * (size - 1 - half)

    def device(spot):
        upper = spot // (size // 2)
        return (1 - upper) * (2 * spot) + upper * (2 * (size - 1 - spot) + 1)

    return place, device((place + 1) % size), device((place + size - 1) % size)


def neighbours():
    core, layer = lax.axis_index("section"), lax.axis_index("shard")
    sibling = {"section": 1 - core}
    across = {"shard": 1 - layer}
    diagonal = {"section": 1 - core, "shard": 1 - layer}
    return core, layer, sibling, across, diagonal


def greet(devices):
    barrier = pltpu.get_barrier_semaphore()
    for device in devices:
        pl.semaphore_signal(barrier, inc=1, device_id=device, device_id_type=MESH)
    pl.semaphore_wait(barrier, len(devices))


def scatter_kernel(size, count, *refs):
    sources, refs = refs[: 6 * count], refs[6 * count :]
    small, refs = refs[0], refs[1:]
    out, refs = refs[: count + 1], refs[count + 1 :]
    held, refs = refs[: 2 * count], refs[2 * count :]
    own, refs = refs[:count], refs[count:]
    landed, refs = refs[:count], refs[count:]
    load_sem, send_sem, recv_sem, small_send, small_recv = refs
    small_out = out[count]
    place, following, previous = ring_place(size)
    targets = ({"replica": following}, {"replica": previous})
    layer = lax.axis_index("shard")

    def load(number, which):
        rows = held[number].shape[0] // 2
        source = sources[3 * number + which]
        part = pl.ds(0 if which == 1 else rows, rows)
        return pltpu.make_async_copy(
            source, held[number].at[part], load_sem.at[number, 0 if which == 1 else 1]
        )

    for number in range(2 * count):
        load(number, 1).start()

        @pl.when(layer == 0)
        def _(number=number):
            load(number, 0).start()

        @pl.when(layer != 0)
        def _(number=number):
            load(number, 2).start()

    greet(targets)

    def send(way, item, source, slot):
        return pltpu.make_async_remote_copy(
            src_ref=source,
            dst_ref=landed[item].at[way, slot],
            send_sem=send_sem.at[way, item, slot],
            recv_sem=recv_sem.at[way, item, slot],
            device_id=targets[way],
            device_id_type=MESH,
        )

    def send_small(chunk, slot):
        return pltpu.make_async_remote_copy(
            src_ref=small_out.at[chunk],
            dst_ref=small_out.at[chunk],
            send_sem=small_send.at[slot],
            recv_sem=small_recv.at[slot],
            device_id=targets[0],
            device_id_type=MESH,
        )

    def chunk_of(way, slot):
        if way == 0:
            return (place + 2 * size - 2 - slot) % size
        return (place + 2 + slot) % size

    first = ((place + size - 1) % size, (place + 1) % size)
    group = size // 2

    def product(item, way, part):
        deep = own[item].shape[2]
        columns = pl.multiple_of((way * size + part * group) * deep, 128)
        left = held[2 * item][:, pl.ds(columns, group * deep)]
        result = rows_product(left, held[2 * item + 1][...])
        for index in range(group):
            own[item][way, part * group + index] = result[index * deep : (index + 1) * deep].astype(BF)

    small_out[place] = small[...]
    send_small(place, 0).start()
    for item in range(count):
        for number in (2 * item, 2 * item + 1):
            load(number, 1).wait()
            load(number, 0).wait()
        for way in range(2):
            product(item, way, first[way] // group)
            send(way, item, own[item].at[way, first[way]], 0).start()
    for item in range(count):
        for way in range(2):
            product(item, way, 1 - first[way] // group)

    def step(slot, carry):
        for item in range(count):
            for way in range(2):
                here = landed[item].at[way, slot]
                send(way, item, here, slot).wait_recv()
                here[...] += own[item][way, chunk_of(way, slot)]
                send(way, item, here, slot + 1).start()
        chunk = (place + size - 1 - slot) % size
        send_small(chunk, slot).wait_recv()
        send_small(chunk, slot + 1).start()
        return carry

    lax.fori_loop(0, size - 2, step, 0)
    last = size - 2
    for item in range(count):
        for way in range(2):
            here = landed[item].at[way, last]
            send(way, item, here, last).wait_recv()
            out[item][way] = here[...] + own[item][way, place]
    send_small((place + 1) % size, last).wait_recv()

    def finish(slot, carry):
        for item in range(count):
            for way in range(2):
                send(way, item, landed[item].at[way, slot], slot).wait_send()
        send_small(place, slot).wait_send()
        return carry

    lax.fori_loop(0, size - 1, finish, 0)


def ring_scatter(factors, small, size):
    count = len(factors)
    flat = [item for pair in factors for item in pair]
    shapes = [(2 * item[0].shape[0], item[0].shape[1]) for item in flat]
    chunks = [
        (shapes[2 * i][1] // (2 * size), shapes[2 * i + 1][1]) for i in range(count)
    ]
    whole = pl.BlockSpec(memory_space=pltpu.VMEM)
    spot = pl.BlockSpec(memory_space=pl.ANY)
    return pl.pallas_call(
        functools.partial(scatter_kernel, size, count),
        out_shape=[jax.ShapeDtypeStruct((2,) + chunk, BF) for chunk in chunks]
        + [jax.ShapeDtypeStruct((size,) + small.shape, small.dtype)],
        in_specs=[spot] * (6 * count) + [whole],
        out_specs=[whole] * (count + 1),
        scratch_shapes=[pltpu.VMEM(shape, BF) for shape in shapes]
        + [pltpu.VMEM((2, size) + chunk, BF) for chunk in chunks]
        + [pltpu.VMEM((2, size - 1) + chunk, BF) for chunk in chunks]
        + [pltpu.SemaphoreType.DMA((2 * count, 2))]
        + [pltpu.SemaphoreType.DMA((2, count, size - 1))] * 2
        + [pltpu.SemaphoreType.DMA((size - 1,))] * 2,
        compiler_params=pltpu.CompilerParams(
            collective_id=0, has_side_effects=True, vmem_limit_bytes=VMEM_LIMIT
        ),
        name="ring_scatter",
    )(*[block for item in flat for block in item], small)


def gather_kernel(size, groups, *refs):
    count = 4
    own, out = refs[:count], refs[count : 2 * count]
    swap_send, swap_recv, send_sem, recv_sem = refs[2 * count :]
    place, following, previous = ring_place(size)
    targets = ({"replica": following}, {"replica": previous})
    core, layer, sibling, across, diagonal = neighbours()
    same = core == layer
    greet(targets + (sibling, across, diagonal))

    def parts(item, source_half, sender):
        if item < len(groups):
            width = own[item].shape[2] // groups[item]
            for group in range(groups[item]):
                start = pl.multiple_of((2 * group + sender) * width, width)
                yield (
                    own[item].at[source_half, :, pl.ds(group * width, width)],
                    out[item].at[place, :, pl.ds(start, width)],
                )
        else:
            for half in range(2):
                yield own[item].at[half], out[item].at[half, place]

    def copies(item, source_half, lane, kind, device=None):
        for number, (source, target) in enumerate(parts(item, source_half, core)):
            send, recv = swap_send.at[item, lane, number], swap_recv.at[item, kind, number]
            if device is None:
                yield pltpu.make_async_copy(source, target, recv)
            else:
                yield pltpu.make_async_remote_copy(
                    src_ref=source,
                    dst_ref=target,
                    send_sem=send,
                    recv_sem=recv,
                    device_id=device,
                    device_id_type=MESH,
                )

    @pl.when(same)
    def _():
        for item in range(count):
            for copy in copies(item, layer, 0, 0):
                copy.start()
            if item < len(groups):
                for copy in copies(item, 1 - layer, 0, 2, across):
                    copy.start()

    @pl.when(core != layer)
    def _():
        for item in range(count):
            for copy in copies(item, 1 - layer, 0, 3, diagonal):
                copy.start()
            if item < len(groups):
                for copy in copies(item, layer, 1, 1, sibling):
                    copy.start()

    def send(way, item, chunk, slot):
        if item < len(groups):
            deep = out[item].shape[1] // 2
            here = out[item].at[chunk, pl.ds(way * deep, deep)]
        else:
            here = out[item].at[way, chunk]
        return pltpu.make_async_remote_copy(
            src_ref=here,
            dst_ref=here,
            send_sem=send_sem.at[way, item, slot],
            recv_sem=recv_sem.at[way, item, slot],
            device_id=targets[way],
            device_id_type=MESH,
        )

    def chunk_of(way, slot):
        if way == 0:
            return (place + size - 1 - slot) % size
        return (place + 1 + slot) % size

    for item in range(count):

        @pl.when(same)
        def _(item=item):
            for copy in copies(item, layer, 0, 0):
                copy.wait()
            if item < len(groups):
                for copy in copies(item, layer, 1, 1, sibling):
                    copy.wait_recv()

        @pl.when(core != layer)
        def _(item=item):
            for copy in copies(item, layer, 0, 3, diagonal):
                copy.wait_recv()
            if item < len(groups):
                for copy in copies(item, layer, 0, 2, across):
                    copy.wait_recv()

        for way in range(2):
            send(way, item, place, 0).start()

    def step(slot, carry):
        for item in range(count):
            for way in range(2):
                chunk = chunk_of(way, slot)
                send(way, item, chunk, slot).wait_recv()
                send(way, item, chunk, slot + 1).start()
        return carry

    lax.fori_loop(0, size - 2, step, 0)
    last = size - 2
    for item in range(count):
        for way in range(2):
            send(way, item, chunk_of(way, last), last).wait_recv()

    @pl.when(same)
    def _():
        for item in range(len(groups)):
            for copy in copies(item, 1 - layer, 0, 2, across):
                copy.wait_send()

    @pl.when(core != layer)
    def _():
        for item in range(count):
            for copy in copies(item, 1 - layer, 0, 3, diagonal):
                copy.wait_send()
            if item < len(groups):
                for copy in copies(item, layer, 1, 1, sibling):
                    copy.wait_send()

    def finish(slot, carry):
        for item in range(count):
            for way in range(2):
                send(way, item, place, slot).wait_send()
        return carry

    lax.fori_loop(0, size - 1, finish, 0)


def ring_gather(pieces, groups, size):
    spot = pl.BlockSpec(memory_space=pl.ANY)
    shapes = [(size, item.shape[1], 2 * item.shape[2]) for item in pieces[: len(groups)]]
    shapes += [(2, size) + item.shape[1:] for item in pieces[len(groups) :]]
    count = len(pieces)
    return pl.pallas_call(
        functools.partial(gather_kernel, size, groups),
        out_shape=[jax.ShapeDtypeStruct(shape, BF) for shape in shapes],
        in_specs=[pl.BlockSpec(memory_space=pltpu.VMEM)] * count,
        out_specs=[spot] * count,
        scratch_shapes=[
            pltpu.SemaphoreType.DMA((count, 2, 3)),
            pltpu.SemaphoreType.DMA((count, 4, 3)),
        ]
        + [pltpu.SemaphoreType.DMA((2, count, size - 1))] * 2,
        compiler_params=pltpu.CompilerParams(collective_id=1, has_side_effects=True),
        name="ring_gather",
    )(*pieces)


def fetch_kernel(*refs):
    tokens, cotangent, small, qkv, fc, out, proj = refs[:7]
    *outer, small_out, w_qkv, w_fc, w_out, w_proj = refs[7:14]
    send_sem, recv_sem, extra_send, extra_recv, local_sem = refs[14:19]
    buffers = refs[19:]
    core, layer, sibling, across, diagonal = neighbours()
    index = lax.axis_index("replica")
    quarter = index % 4
    low, high = index % 2, (index // 2) % 2
    beside = {"replica": index + 1 - 2 * low}
    above = {"replica": index + 2 - 4 * high}
    beside_quarter = quarter + 1 - 2 * low
    above_quarter = quarter + 2 - 4 * high
    same = core == layer
    far_quarter = 3 - quarter
    greet((sibling, across, diagonal, beside, above))

    depth = qkv.shape[0]
    span = qkv.shape[1] // 6
    wide = fc.shape[1] // 2
    turn = proj.shape[0] // 2
    cols = [
        (qkv, w_qkv, lambda s, g=g: pl.multiple_of((2 * g + s) * span, span), g * span, span)
        for g in range(3)
    ]
    cols.append((fc, w_fc, lambda s: pl.multiple_of(s * wide, wide), 0, wide))
    rows = [(out, w_out, 0, out.shape[0]), (proj, w_proj, 0, turn), (proj, w_proj, turn, turn)]
    order = [0, 1, 2, 4, 3, 5, 6]

    def rows_of(item):
        return depth if item < 4 else rows[item - 4][3]

    def target(item, base, which, part=None):
        deep = rows_of(item) // 4
        start = base + which * deep
        if part is not None:
            deep = deep // 2
            start = start + part * deep
        place = pl.ds(pl.multiple_of(start, deep), deep)
        if item < 4:
            return cols[item][1].at[place, pl.ds(cols[item][3], cols[item][4])]
        return rows[item - 4][1].at[place]

    def base_of(item, shard):
        return shard * depth if item < 4 else rows[item - 4][2]

    def remote(stage, item, source, dest, device, lane=0):
        return pltpu.make_async_remote_copy(
            src_ref=source,
            dst_ref=dest,
            send_sem=send_sem.at[stage + lane, item],
            recv_sem=recv_sem.at[stage, item],
            device_id=device,
            device_id_type=MESH,
        )

    def cross(item, receiver):
        deep = rows_of(item) // 4
        place = pl.multiple_of(base_of(item, 0) + quarter * deep, deep)
        dest = target(item, base_of(item, layer), quarter)
        if item < 4:
            columns = cols[item][2](receiver)
            source = cols[item][0].at[pl.ds(place, deep), pl.ds(columns, cols[item][4])]
        else:
            source = rows[item - 4][0].at[pl.ds(place, deep)]
        return source, dest

    def cross_same(item):
        return remote(0, item, *cross(item, core), across, 5)

    def cross_swap(item):
        return remote(0, item, *cross(item, 1 - core), diagonal)

    def pass_on(stage, item, which, device, part=None):
        here = target(item, base_of(item, 1 - layer), which, part)
        return remote(stage, item, here, here, device)

    def to_sibling(item):
        columns = cols[item][2](1 - core)
        source = cols[item][0].at[:, pl.ds(columns, cols[item][4])]
        start = pl.multiple_of(layer * depth, depth)
        dest = cols[item][1].at[pl.ds(start, depth), pl.ds(cols[item][3], cols[item][4])]
        return remote(6, item, source, dest, sibling)

    def through(source, dest, number):
        return (
            lambda: pltpu.make_async_copy(source, buffers[number], local_sem.at[number]),
            lambda: pltpu.make_async_copy(buffers[number], dest, local_sem.at[number]),
        )

    def keep_local(item):
        if item < 4:
            columns = cols[item][2](core)
            source = cols[item][0].at[:, pl.ds(columns, cols[item][4])]
            start = pl.multiple_of(layer * depth, depth)
            dest = cols[item][1].at[pl.ds(start, depth), pl.ds(cols[item][3], cols[item][4])]
        else:
            source, dest, start, deep = rows[item - 4]
            source, dest = source.at[pl.ds(start, deep)], dest.at[pl.ds(start, deep)]
        return through(source, dest, item)

    part = tokens.shape[1]
    half = part // 2

    def outer_rows(shard, which):
        return pl.ds(pl.multiple_of(shard * part + which * half, half), half)

    def outer_cross(block):
        place = pl.ds(pl.multiple_of(core * half, half), half)

        def copy(source):
            return pltpu.make_async_remote_copy(
                src_ref=source.at[block, place],
                dst_ref=outer[block].at[outer_rows(layer, core)],
                send_sem=extra_send.at[block],
                recv_sem=extra_recv.at[block],
                device_id=across,
                device_id_type=MESH,
            )

        return copy

    def outer_pass(block):
        here = outer[block].at[outer_rows(1 - layer, core)]
        return pltpu.make_async_remote_copy(
            src_ref=here,
            dst_ref=here,
            send_sem=extra_send.at[2 + block],
            recv_sem=extra_recv.at[2 + block],
            device_id=sibling,
            device_id_type=MESH,
        )

    def outer_local(source, block):
        place = pl.ds(pl.multiple_of(layer * part, part), part)
        return through(source.at[block], outer[block].at[place], 7 + block)

    def small_swap():
        return pltpu.make_async_remote_copy(
            src_ref=small,
            dst_ref=small_out.at[1 - core],
            send_sem=extra_send.at[4],
            recv_sem=extra_recv.at[4],
            device_id=diagonal,
            device_id_type=MESH,
        )

    def small_pass():
        return pltpu.make_async_remote_copy(
            src_ref=small_out.at[core],
            dst_ref=small_out.at[core],
            send_sem=extra_send.at[5],
            recv_sem=extra_recv.at[5],
            device_id=sibling,
            device_id_type=MESH,
        )

    def small_local():
        return through(small, small_out.at[core], 9)

    def start_outer(block):
        @pl.when(layer == 0)
        def _():
            outer_cross(block)(cotangent).start()

        @pl.when(layer == 1)
        def _():
            outer_cross(block)(tokens).start()

    def crossings(item):
        if item < 4:
            cross_same(item).start()
        cross_swap(item).start()

    @pl.when(same)
    def _():
        small_local()[0]().start()

    @pl.when(core != layer)
    def _():
        small_swap().start()

    start_outer(0)

    @pl.when(core != layer)
    def _():
        crossings(order[0])
        crossings(order[1])

    @pl.when(layer == 0)
    def _():
        for block in range(2):
            outer_local(tokens, block)[0]().start()

    @pl.when(layer == 1)
    def _():
        for block in range(2):
            outer_local(cotangent, block)[0]().start()

    @pl.when(same)
    def _():
        for item in range(4):
            to_sibling(item).start()
        load, store = small_local()
        load().wait()
        store().start()
        store().wait()

    @pl.when(core != layer)
    def _():
        small_swap().wait_recv()

    small_pass().start()
    for block in range(2):
        load, store = outer_local(tokens, block)
        load().wait()
        store().start()

    @pl.when(same)
    def _():
        for item in range(7):
            keep_local(item)[0]().start()

    def relay(sequence, ahead):
        def onward(item):
            pass_on(1, item, beside_quarter, beside).wait_recv()
            pass_on(4, item, beside_quarter, above, 0).start()
            pass_on(2, item, above_quarter, above).wait_recv()
            pass_on(3, item, above_quarter, beside, 1).start()

        for number, item in enumerate(sequence):
            pass_on(0, item, quarter, beside).wait_recv()
            if ahead and number + 2 < len(sequence):
                crossings(sequence[number + 2])
            pass_on(1, item, quarter, beside).start()
            pass_on(2, item, quarter, above).start()
            if number >= 1:
                onward(sequence[number - 1])
            if number == 0:
                outer_cross(0)(tokens).wait_recv()
                outer_pass(0).start()
                start_outer(1)
        onward(sequence[-1])
        for item in sequence:
            pass_on(3, item, far_quarter, beside, 1).wait_recv()
            pass_on(4, item, far_quarter, above, 0).wait_recv()
            for stage in (1, 2):
                pass_on(stage, item, quarter, beside).wait_send()
            for stage, which in ((3, 1), (4, 0)):
                pass_on(stage, item, quarter, beside, which).wait_send()

    @pl.when(same)
    def _():
        for item in range(7):
            load, store = keep_local(item)
            load().wait()
            store().start()
        relay([0, 1, 2, 3], False)
        for item in range(4):
            to_sibling(item).wait_send()
        for item in range(7):
            keep_local(item)[1]().wait()

    @pl.when(core != layer)
    def _():
        relay(order, True)
        for item in range(4):
            to_sibling(item).wait_recv()
            cross_same(item).wait_send()
        for item in range(7):
            cross_swap(item).wait_send()
        small_swap().wait_send()

    outer_cross(1)(tokens).wait_recv()
    outer_pass(1).start()
    for block in range(2):
        outer_local(tokens, block)[1]().wait()
    small_pass().wait()
    for block in range(2):
        outer_cross(block)(tokens).wait_send()
        outer_pass(block).wait()


def fetch_inputs(tokens, cotangent, small, qkv, fc, out, proj):
    spot = pl.BlockSpec(memory_space=pl.ANY)
    _, part, width = tokens.shape
    shapes = [
        (2 * part, width),
        (2 * part, width),
        (2,) + small.shape,
        (2 * qkv.shape[0], qkv.shape[1] // 2),
        (2 * fc.shape[0], fc.shape[1] // 2),
        out.shape,
        proj.shape,
    ]
    return pl.pallas_call(
        fetch_kernel,
        out_shape=[jax.ShapeDtypeStruct(shape, BF) for shape in shapes],
        in_specs=[spot] * 7,
        out_specs=[spot] * 7,
        scratch_shapes=[
            pltpu.SemaphoreType.DMA((7, 7)),
            pltpu.SemaphoreType.DMA((7, 7)),
            pltpu.SemaphoreType.DMA((6,)),
            pltpu.SemaphoreType.DMA((6,)),
            pltpu.SemaphoreType.DMA((10,)),
        ]
        + [pltpu.VMEM((qkv.shape[0], qkv.shape[1] // 6), BF)] * 3
        + [
            pltpu.VMEM((fc.shape[0], fc.shape[1] // 2), BF),
            pltpu.VMEM(out.shape, BF),
            pltpu.VMEM((proj.shape[0] // 2, width), BF),
            pltpu.VMEM((proj.shape[0] // 2, width), BF),
            pltpu.VMEM(tokens.shape[1:], BF),
            pltpu.VMEM(tokens.shape[1:], BF),
            pltpu.VMEM(small.shape, BF),
        ],
        compiler_params=pltpu.CompilerParams(
            collective_id=2, has_side_effects=True, vmem_limit_bytes=VMEM_LIMIT
        ),
        name="fetch_inputs",
    )(tokens, cotangent, small, qkv, fc, out, proj)


TILES = 2


class Loads:
    def __init__(self, sem):
        self.sem, self.count, self.made = sem, 0, {}

    def start(self, name, source, buffer):
        copy = pltpu.make_async_copy(source, buffer, self.sem.at[self.count])
        self.count += 1
        copy.start()
        self.made[name] = copy

    def wait(self, *names):
        for name in names:
            self.made.pop(name).wait()


def greet_step(sender, passing):
    core, layer, sibling, across, _ = neighbours()
    barrier = pltpu.get_barrier_semaphore()
    pl.semaphore_signal(barrier, inc=1, device_id=sibling, device_id_type=MESH)
    if not passing:
        pl.semaphore_wait(barrier, 1)
        return

    @pl.when(layer != sender)
    def _():
        pl.semaphore_signal(barrier, inc=1, device_id=across, device_id_type=MESH)
        pl.semaphore_wait(barrier, 1)

    @pl.when(layer == sender)
    def _():
        pl.semaphore_wait(barrier, 2)


class Exchange:
    def __init__(self, send_buf, recv_buf, send_sem, recv_sem):
        self.refs = (send_buf, recv_buf, send_sem, recv_sem)

    def copy(self, slot):
        send_buf, recv_buf, send_sem, recv_sem = self.refs
        return pltpu.make_async_remote_copy(
            src_ref=send_buf.at[slot],
            dst_ref=recv_buf.at[slot],
            send_sem=send_sem.at[slot],
            recv_sem=recv_sem.at[slot],
            device_id={"section": 1 - lax.axis_index("section")},
            device_id_type=MESH,
        )

    def give(self, slot, partial):
        self.refs[0][slot] = partial.astype(BF)
        self.copy(slot).start()

    def take(self, slot):
        self.copy(slot).wait_recv()
        return self.refs[1][slot].astype(F32)

    def finish(self, count):
        for slot in range(count):
            self.copy(slot).wait_send()


class Across:
    def __init__(self, sender, source, dest, sems):
        self.sender, self.source, self.dest, self.sems = sender, source, dest, sems
        self.core, self.layer, self.sibling, self.across, _ = neighbours()

    def copy(self, tile, stage):
        rows = self.dest.shape[0] // (2 * TILES)
        place = pl.ds(pl.multiple_of((2 * tile + self.core) * rows, rows), rows)
        source = self.source if stage == 0 else self.dest
        return pltpu.make_async_remote_copy(
            src_ref=source.at[place],
            dst_ref=self.dest.at[place],
            send_sem=self.sems.at[stage, tile],
            recv_sem=self.sems.at[2 + stage, tile],
            device_id=self.across if stage == 0 else self.sibling,
            device_id_type=MESH,
        )

    def send(self, tile):
        @pl.when(self.layer == self.sender)
        def _():
            self.copy(tile, 0).start()

    def receive(self, tile):
        @pl.when(self.layer != self.sender)
        def _():
            self.copy(tile, 0).wait_recv()
            self.copy(tile, 1).start()
            self.copy(tile, 1).wait_recv()

    def finish(self):
        @pl.when(self.layer == self.sender)
        def _():
            for tile in range(TILES):
                self.copy(tile, 0).wait_send()

        @pl.when(self.layer != self.sender)
        def _():
            for tile in range(TILES):
                self.copy(tile, 1).wait_send()


class Opening:
    def __init__(self, passing, sender, first_ref, other_ref, earlier, buffer, sem, sems):
        self.passing, self.sender, self.layer = passing, sender, lax.axis_index("shard")
        self.load = lambda ref: pltpu.make_async_copy(ref, buffer, sem)
        self.refs = (first_ref, other_ref)
        self.across = Across(sender, earlier, buffer, sems)

    def start(self):
        for layer, ref in enumerate(self.refs):
            if self.passing and layer != self.sender:
                continue

            @pl.when(self.layer == layer)
            def _(ref=ref):
                self.load(ref).start()

    def send(self):
        if self.passing:
            for tile in range(TILES):
                self.across.send(tile)

    def take(self, tile):
        if self.passing:
            if tile == 0:

                @pl.when(self.layer == self.sender)
                def _():
                    self.load(self.refs[0]).wait()

            self.across.receive(tile)
        elif tile == 0:
            self.load(self.refs[0]).wait()

    def finish(self):
        if self.passing:
            self.across.finish()


def by_past(mode, body):
    if mode is not None:
        body(mode)
        return
    layer = lax.axis_index("shard")

    @pl.when(layer == 0)
    def _():
        body(True)

    @pl.when(layer != 0)
    def _():
        body(False)


FORWARD_LOADS = 7


def forward_kernel(mode, passing, *refs):
    x_first, x_other, earlier, params, w_qkv, w_out, w_fc, w_proj, k_past, v_past = refs[:10]
    refs = refs[10:]
    (x_used, normed1, query, keys, values, mixed, lse, scaled2, inverse2, normed2, slope, act, out, passed) = refs[:14]
    refs = refs[14:]
    (x_v, wq_v, wo_v, wf_v, wp_v, k_v, v_v, hid_v, part_v, send_v, recv_v) = refs[:11]
    refs = refs[11:]
    (n1_v, q_v, m_v, lse_v, s2_v, i2_v, n2_v, sl_v, a_v, o_v) = refs[:10]
    load_sem, store_sem, send_sem, recv_sem, open_sem, across_sem = refs[10:]
    rows, width = x_v.shape
    half = q_v.shape[1]
    tile_rows = rows // TILES
    wide = a_v.shape[1]

    loads = Loads(load_sem)
    opening = Opening(passing, 0, x_first, x_other, earlier, x_v, load_sem.at[FORWARD_LOADS], open_sem)
    opening.start()
    loads.start("qkv", w_qkv, wq_v)
    if mode is not False:
        loads.start("k", k_past, k_v.at[pl.ds(0, rows)])
        loads.start("v", v_past, v_v.at[pl.ds(0, rows)])
    loads.start("out", w_out, wo_v)
    loads.start("fc", w_fc, wf_v)
    loads.start("proj", w_proj, wp_v)
    greet_step(0, passing)
    opening.send()
    exchange = Exchange(send_v, recv_v, send_sem, recv_sem)
    across = Across(0, o_v, passed, across_sem)
    stores = []

    def store(buffer, dest):
        copy = pltpu.make_async_copy(buffer, dest, store_sem.at[len(stores)])
        copy.start()
        stores.append(copy)

    def vector(row, start=0, size=None):
        return params[row : row + 1, start : start + (size or width)]

    own_rows = pl.ds(rows, rows)
    for tile in range(TILES):
        span = pl.ds(tile * tile_rows, tile_rows)
        later = pl.ds(rows + tile * tile_rows, tile_rows)
        opening.take(tile)
        scaled, _ = norm_parts(x_v[span, :].astype(F32))
        normed = (scaled * vector(0) + vector(1)).astype(BF)
        n1_v[span, :] = normed
        if tile == 0:
            loads.wait("qkv")
        piece = jnp.dot(normed, wq_v[:, :half], preferred_element_type=F32)
        q_v[span, :] = (piece + vector(6, 0, half)).astype(BF)
        piece = jnp.dot(normed, wq_v[:, half : 2 * half], preferred_element_type=F32)
        k_v[later, :] = piece.astype(BF)
        piece = jnp.dot(normed, wq_v[:, 2 * half :], preferred_element_type=F32)
        v_v[later, :] = (piece + vector(6, half, half)).astype(BF)
    store(x_v, x_used)
    store(n1_v, normed1)
    store(q_v, query)
    store(k_v.at[own_rows], keys)
    store(v_v.at[own_rows], values)
    if mode is not False:
        loads.wait("k", "v")
    loads.wait("out")

    def attention(past):
        first_key = 0 if past else rows
        for tile in range(TILES):
            span = pl.ds(tile * tile_rows, tile_rows)
            length = (rows if past else 0) + (tile + 1) * tile_rows
            reach = pl.ds(first_key, length)

            def pair(number, carry):
                lanes = pl.ds(pl.multiple_of(number * 128, 128), 128)
                key, value = k_v[reach, lanes], v_v[reach, lanes]
                pieces = []
                for head, part in enumerate(head_parts(q_v[span, lanes])):
                    scores = masked_scores(key, part * BF(HEAD_DIM**-0.5), length)
                    top = jnp.max(scores, axis=0, keepdims=True)
                    probs = jnp.exp(scores - top)
                    total = jnp.sum(probs, axis=0, keepdims=True)
                    lse_v[number, pl.ds(head, 1), span] = top + jnp.log(total)
                    piece = rows_product(value, probs.astype(BF))
                    piece = piece[head * HEAD_DIM : (head + 1) * HEAD_DIM]
                    pieces.append(piece * (1.0 / total))
                m_v[span, lanes] = jnp.transpose(jnp.concatenate(pieces, axis=0)).astype(BF)
                return carry

            lax.fori_loop(0, half // 128, pair, 0)
            partial = jnp.dot(m_v[span, :], wo_v[...], preferred_element_type=F32)
            part_v[tile] = partial
            exchange.give(tile, partial)

    by_past(mode, attention)
    store(m_v, mixed)
    store(lse_v, lse)
    loads.wait("fc", "proj")

    def conclude(tile):
        span = pl.ds(tile * tile_rows, tile_rows)
        total = part_v[TILES + tile] + exchange.take(TILES + tile)
        o_v[span, :] = (hid_v[span, :] + total + vector(5)).astype(BF)
        if passing:
            across.send(tile)

    for tile in range(TILES):
        span = pl.ds(tile * tile_rows, tile_rows)
        hidden = x_v[span, :].astype(F32) + (part_v[tile] + exchange.take(tile)) + vector(2)
        hid_v[span, :] = hidden
        scaled, inverse = norm_parts(hidden)
        s2_v[span, :] = scaled.astype(BF)
        i2_v[span, :] = jnp.broadcast_to(inverse, (tile_rows, 128))
        normed = (scaled * vector(3) + vector(4)).astype(BF)
        n2_v[span, :] = normed
        chunk = width // 2
        for part in range(wide // chunk):
            columns = pl.ds(part * chunk, chunk)
            pre = jnp.dot(normed, wf_v[:, columns], preferred_element_type=F32)
            bias = vector(7 + part * chunk // width, part * chunk % width, chunk)
            activated, inclined = gelu_pair(pre + bias)
            a_v[span, columns] = activated.astype(BF)
            sl_v[span, columns] = inclined.astype(BF)
        if tile > 0:
            conclude(tile - 1)
        partial = jnp.dot(a_v[span, :], wp_v[...], preferred_element_type=F32)
        part_v[TILES + tile] = partial
        exchange.give(TILES + tile, partial)
    store(s2_v, scaled2)
    store(i2_v, inverse2)
    store(n2_v, normed2)
    store(sl_v, slope)
    store(a_v, act)
    conclude(TILES - 1)
    store(o_v, out)
    for copy in stores:
        copy.wait()
    exchange.finish(2 * TILES)
    opening.finish()
    if passing:
        for tile in range(TILES):
            across.receive(tile)
        across.finish()


def step_sems(loads, stores):
    return [
        pltpu.SemaphoreType.DMA((loads,)),
        pltpu.SemaphoreType.DMA((stores,)),
        pltpu.SemaphoreType.DMA((2 * TILES,)),
        pltpu.SemaphoreType.DMA((2 * TILES,)),
        pltpu.SemaphoreType.DMA((4, TILES)),
        pltpu.SemaphoreType.DMA((4, TILES)),
    ]


def forward_step(mode, passing, inputs, params, weights, past):
    rows, width = inputs[0].shape
    half = width // 2
    wide = weights[2].shape[1]
    pairs = half // 128
    tile_rows = rows // TILES
    spot = pl.BlockSpec(memory_space=pl.ANY)
    low = lambda columns: ((rows, columns), BF)
    outs = [
        low(width),
        low(width),
        low(half),
        low(half),
        low(half),
        low(half),
        ((pairs, 8, rows), F32),
        low(width),
        ((rows, 128), F32),
        low(width),
        low(wide),
        low(wide),
        low(width),
        low(width),
    ]
    scratch = [
        low(width),
        *((item.shape, BF) for item in weights),
        ((2 * rows, half), BF),
        ((2 * rows, half), BF),
        ((rows, width), F32),
        ((2 * TILES, tile_rows, width), F32),
        ((2 * TILES, tile_rows, width), BF),
        ((2 * TILES, tile_rows, width), BF),
        low(width),
        low(half),
        low(half),
        ((pairs, 8, rows), F32),
        low(width),
        ((rows, 128), F32),
        low(width),
        low(wide),
        low(wide),
        low(width),
    ]
    number = {False: 3, None: 4, True: 5}[mode]
    return pl.pallas_call(
        functools.partial(forward_kernel, mode, passing),
        out_shape=[jax.ShapeDtypeStruct(*item) for item in outs],
        in_specs=[spot] * 3 + [pl.BlockSpec(memory_space=pltpu.VMEM)] + [spot] * 6,
        out_specs=[spot] * len(outs),
        scratch_shapes=[pltpu.VMEM(*item) for item in scratch]
        + step_sems(FORWARD_LOADS + 1, len(outs)),
        compiler_params=pltpu.CompilerParams(
            collective_id=number, has_side_effects=True, vmem_limit_bytes=VMEM_LIMIT
        ),
        name="forward_step",
    )(*inputs, params, *weights, *past)


BACKWARD_LOADS = 17


def backward_kernel(mode, passing, *refs):
    (g_first, g_other, earlier, x_used, params, w_qkv, w_out, w_fc, w_proj) = refs[:9]
    (query, keys, values, k_past, v_past, mixed, lse, scaled2, inverse2, slope, pend_k, pend_v) = refs[9:21]
    refs = refs[21:]
    (g_used, d_qkv, d_branch, d_pre, out, next_k, next_v, sums, passed) = refs[:9]
    refs = refs[9:]
    (g_v, x_v, wq_v, wo_v, wf_v, wp_v, q_v, k_v, v_v, m_v, lse_v, s2_v, i2_v, sl_v) = refs[:14]
    refs = refs[14:]
    (dk_v, dv_v, hid_v, part_v, send_v, recv_v, dqkv_v, db_v, dp_v, dm_v, o_v, sum_v) = refs[:12]
    load_sem, store_sem, send_sem, recv_sem, open_sem, across_sem = refs[12:]
    rows, width = x_v.shape
    half = q_v.shape[1]
    wide = dp_v.shape[1]
    tile_rows = rows // TILES
    own_rows, past_rows = pl.ds(rows, rows), pl.ds(0, rows)
    scale = HEAD_DIM**-0.5

    loads = Loads(load_sem)
    opening = Opening(passing, 1, g_first, g_other, earlier, g_v, load_sem.at[BACKWARD_LOADS], open_sem)
    opening.start()
    loads.start("proj", w_proj, wp_v)
    loads.start("slope", slope, sl_v)
    loads.start("fc", w_fc, wf_v)
    loads.start("scaled2", scaled2, s2_v)
    loads.start("inverse2", inverse2, i2_v)
    loads.start("out", w_out, wo_v)
    loads.start("q", query, q_v)
    loads.start("k", keys, k_v.at[own_rows])
    loads.start("v", values, v_v.at[own_rows])
    if mode is not False:
        loads.start("k_past", k_past, k_v.at[past_rows])
        loads.start("v_past", v_past, v_v.at[past_rows])
    loads.start("mixed", mixed, m_v)
    loads.start("lse", lse, lse_v)
    if mode is not True:
        loads.start("pend_k", pend_k, dk_v.at[own_rows])
        loads.start("pend_v", pend_v, dv_v.at[own_rows])
    loads.start("qkv", w_qkv, wq_v)
    loads.start("x", x_used, x_v)
    greet_step(1, passing)
    opening.send()
    exchange = Exchange(send_v, recv_v, send_sem, recv_sem)
    across = Across(1, o_v, passed, across_sem)
    stores = []

    def store(buffer, dest):
        copy = pltpu.make_async_copy(buffer, dest, store_sem.at[len(stores)])
        copy.start()
        stores.append(copy)

    def vector(row, start=0, size=None):
        return params[row : row + 1, start : start + (size or width)]

    sum_v[...] = jnp.zeros_like(sum_v)

    def tally(row, piece, start=0):
        place = (slice(row, row + 1), slice(start, start + piece.shape[1]))
        sum_v[place] += jnp.sum(piece, axis=0, keepdims=True)

    loads.wait("proj", "slope", "fc")
    chunk = width // 2
    for tile in range(TILES):
        span = pl.ds(tile * tile_rows, tile_rows)
        opening.take(tile)
        grad = g_v[span, :]
        for part in range(wide // chunk):
            columns = pl.ds(part * chunk, chunk)
            d_act = cols_product(grad, wp_v[columns, :])
            piece = (d_act * sl_v[span, columns].astype(F32)).astype(BF)
            dp_v[span, columns] = piece
            tally(7 + part * chunk // width, piece.astype(F32), part * chunk % width)
        partial = cols_product(dp_v[span, :], wf_v[...])
        part_v[tile] = partial
        exchange.give(tile, partial)
        tally(5, grad.astype(F32))
    store(g_v, g_used)
    store(dp_v, d_pre)
    loads.wait("scaled2", "inverse2", "out")
    for tile in range(TILES):
        span = pl.ds(tile * tile_rows, tile_rows)
        d_normed = part_v[tile] + exchange.take(tile)
        scaled = s2_v[span, :].astype(F32)
        tally(3, d_normed * scaled)
        tally(4, d_normed)
        d_hidden = g_v[span, :].astype(F32) + norm_backward(
            d_normed, scaled, i2_v[span, 0:1], vector(3)
        )
        hid_v[span, :] = d_hidden
        branch = d_hidden.astype(BF)
        db_v[span, :] = branch
        tally(2, branch.astype(F32))
        dm_v[span, :] = cols_product(branch, wo_v[...]).astype(BF)
    store(db_v, d_branch)
    loads.wait("q", "k", "v", "mixed", "lse")
    if mode is not False:
        loads.wait("k_past", "v_past")
    if mode is not True:
        loads.wait("pend_k", "pend_v")

    def attention(past):
        first_key = 0 if past else rows
        if past:
            dk_v[...] = jnp.zeros_like(dk_v)
            dv_v[...] = jnp.zeros_like(dv_v)
        for tile in range(TILES):
            span = pl.ds(tile * tile_rows, tile_rows)
            length = (rows if past else 0) + (tile + 1) * tile_rows
            reach = pl.ds(first_key, length)

            def pair(number, carry):
                lanes = pl.ds(pl.multiple_of(number * 128, 128), 128)
                key, value = k_v[reach, lanes], v_v[reach, lanes]
                grads = dm_v[span, lanes]
                products = jnp.transpose(grads.astype(F32) * m_v[span, lanes].astype(F32))
                queries, grads = head_parts(q_v[span, lanes]), head_parts(grads)
                d_query = []
                d_key = d_value = None
                for head in range(2):
                    take = slice(head * HEAD_DIM, (head + 1) * HEAD_DIM)
                    scaled_query = queries[head] * BF(scale)
                    scores = masked_scores(key, scaled_query, length)
                    weights = jnp.exp(scores - lse_v[number, pl.ds(head, 1), span])
                    d_probs = cols_product(value, grads[head])
                    delta = jnp.sum(products[take], axis=0, keepdims=True)
                    d_scores = (weights * (d_probs - delta)).astype(BF)
                    one = jnp.dot(weights.astype(BF), grads[head], preferred_element_type=F32)
                    two = jnp.dot(d_scores, scaled_query, preferred_element_type=F32)
                    d_value = one if head == 0 else d_value + one
                    d_key = two if head == 0 else d_key + two
                    d_query.append(rows_product(key, d_scores)[take])
                dk_v[reach, lanes] += d_key
                dv_v[reach, lanes] += d_value
                d_query = jnp.transpose(jnp.concatenate(d_query, axis=0) * scale)
                dqkv_v[span, lanes] = d_query.astype(BF)
                return carry

            lax.fori_loop(0, half // 128, pair, 0)

    by_past(mode, attention)
    if mode is not False:
        store(dk_v.at[past_rows], next_k)
        store(dv_v.at[past_rows], next_v)
    loads.wait("qkv", "x")
    for tile in range(TILES):
        span = pl.ds(tile * tile_rows, tile_rows)
        later = pl.ds(rows + tile * tile_rows, tile_rows)
        dqkv_v[span, half : 2 * half] = dk_v[later, :].astype(BF)
        dqkv_v[span, 2 * half :] = dv_v[later, :].astype(BF)
        piece = dqkv_v[span, :]
        partial = cols_product(piece, wq_v[...])
        part_v[TILES + tile] = partial
        exchange.give(TILES + tile, partial)
        tally(6, piece[:, :half].astype(F32))
        tally(6, piece[:, 2 * half :].astype(F32), half)
    store(dqkv_v, d_qkv)
    for tile in range(TILES):
        span = pl.ds(tile * tile_rows, tile_rows)
        scaled, inverse = norm_parts(x_v[span, :].astype(F32))
        d_normed = part_v[TILES + tile] + exchange.take(TILES + tile)
        tally(0, d_normed * scaled)
        tally(1, d_normed)
        d_inputs = hid_v[span, :] + norm_backward(d_normed, scaled, inverse, vector(0))
        o_v[span, :] = d_inputs.astype(BF)
        if passing:
            across.send(tile)
    store(o_v, out)
    store(sum_v, sums)
    for copy in stores:
        copy.wait()
    exchange.finish(2 * TILES)
    opening.finish()
    if passing:
        for tile in range(TILES):
            across.receive(tile)
        across.finish()


def backward_step(mode, passing, grads, inputs, params, weights, kept, pending):
    rows, width = inputs.shape
    half = width // 2
    wide = weights[2].shape[1]
    pairs = half // 128
    tile_rows = rows // TILES
    spot = pl.BlockSpec(memory_space=pl.ANY)
    low = lambda columns: ((rows, columns), BF)
    outs = [
        low(width),
        low(3 * half),
        low(width),
        low(wide),
        low(width),
        ((rows, half), F32),
        ((rows, half), F32),
        ((16, width), F32),
        low(width),
    ]
    scratch = [
        low(width),
        low(width),
        *((item.shape, BF) for item in weights),
        low(half),
        ((2 * rows, half), BF),
        ((2 * rows, half), BF),
        low(half),
        ((pairs, 8, rows), F32),
        low(width),
        ((rows, 128), F32),
        low(wide),
        ((2 * rows, half), F32),
        ((2 * rows, half), F32),
        ((rows, width), F32),
        ((2 * TILES, tile_rows, width), F32),
        ((2 * TILES, tile_rows, width), BF),
        ((2 * TILES, tile_rows, width), BF),
        low(3 * half),
        low(width),
        low(wide),
        low(half),
        low(width),
        ((16, width), F32),
    ]
    number = {True: 6, None: 7, False: 8}[mode]
    return pl.pallas_call(
        functools.partial(backward_kernel, mode, passing),
        out_shape=[jax.ShapeDtypeStruct(*item) for item in outs],
        in_specs=[spot] * 4 + [pl.BlockSpec(memory_space=pltpu.VMEM)] + [spot] * 16,
        out_specs=[spot] * len(outs),
        scratch_shapes=[pltpu.VMEM(*item) for item in scratch]
        + step_sems(BACKWARD_LOADS + 1, len(outs)),
        compiler_params=pltpu.CompilerParams(
            collective_id=number, has_side_effects=True, vmem_limit_bytes=VMEM_LIMIT
        ),
        name="backward_step",
    )(*grads, inputs, params, *weights, *kept, *pending)


def shards(
    tokens,
    cotangent,
    attn_gain,
    attn_shift,
    qkv_weight,
    query_bias,
    value_bias,
    out_weight,
    out_bias,
    mlp_gain,
    mlp_shift,
    fc_weight,
    fc_bias,
    proj_weight,
    proj_bias,
):
    core = lax.axis_index("section")
    layer = lax.axis_index("shard")
    size = lax.axis_size("replica")
    own = core == layer
    first = layer == 0
    left = core == 0
    micro, part, width = tokens.shape[1:]
    assert micro == 2
    rows = 2 * part
    half = width // 2

    def pair_permute(value, pairs):
        return lax.ppermute(value, PAIR, pairs)

    small = jnp.concatenate(
        [
            item[0]
            for item in (
                attn_gain,
                attn_shift,
                out_bias,
                mlp_gain,
                mlp_shift,
                proj_bias,
                query_bias,
                value_bias,
                fc_bias,
            )
        ]
    ).reshape(-1, 128)
    *outer, small_both, w_qkv, w_fc, w_out, w_proj = fetch_inputs(
        tokens[0], cotangent[0], small, qkv_weight[0], fc_weight[0], out_weight[0], proj_weight[0]
    )
    flat = small_both.reshape(2, -1).astype(F32)
    mine = jnp.where(left, flat[0], flat[1])
    params = jnp.concatenate(
        [
            flat[0, : 6 * half].reshape(6, half),
            flat[1, : 6 * half].reshape(6, half),
        ],
        axis=1,
    )
    params = jnp.concatenate(
        [params, mine[6 * half :].reshape(-1, width), jnp.zeros((7, width), F32)], axis=0
    )
    weights = (w_qkv, w_out, w_fc, w_proj)

    empty = jnp.zeros((rows, half), BF)
    received, kept_list, outputs, past, got = [], [], [], (empty, empty), outer[0]
    for step in range(micro + 1):
        output = outputs[-1] if outputs else outer[0]
        used, normed1, *state, normed2, slope, act, output, got = forward_step(
            (False, None, True)[step],
            step == 1,
            (outer[min(step, micro - 1)], got, output),
            params,
            weights,
            past,
        )
        query, keys, values, mixed, lse, scaled2, inverse2 = state
        outputs.append(output)
        received.append(used)
        kept = (query, keys, values, *past, mixed, lse, scaled2, inverse2, slope)
        kept_list.append((kept, normed1, normed2, act))
        past = (keys, values)

    pending = (jnp.zeros((rows, half), F32), jnp.zeros((rows, half), F32))
    grad_received, terms_list, results, sums, got = [], [], [], None, outer[1]
    for step in range(micro + 1):
        active = jnp.where(first, step >= 1, step < micro)
        last = micro - step
        kept, normed1, normed2, act = kept_list[last]
        result = results[-1] if results else outer[1]
        grad, d_qkv, d_branch, d_pre, result, *pending, vector, got = backward_step(
            (True, None, False)[step],
            step == 1,
            (got, outer[max(micro - 1 - step, 0)], result),
            received[last],
            params,
            weights,
            kept,
            pending,
        )
        results.append(result)
        grad_received.append(grad)
        vector = jnp.where(active, vector, 0.0)
        sums = vector if sums is None else sums + vector
        terms_list.append((normed1, d_qkv, kept[5], d_branch, normed2, d_pre, act, grad))
    full = lax.dynamic_slice_in_dim(sums[:6], core * half, half, 1)
    sums = jnp.concatenate([full.reshape(-1), sums[6:9].reshape(-1)])

    def factor(number):
        return tuple(terms_list[step][number] for step in (2, 1, 0))

    factors = [(factor(i), factor(i + 1)) for i in (0, 4, 2, 6)]
    sums = sums.reshape(-1, 128)
    sums = jnp.where(own, sums, pair_permute(sums, CROSS_SWAP))
    *reduced, sums = ring_scatter(factors, sums, size)
    sums = jnp.sum(sums, axis=0).reshape(-1)
    vectors = [sums[i * half : (i + 1) * half][None] for i in range(8)] + [sums[8 * half :][None]]
    qkv_grad, fc_grad, out_grad, proj_grad = (
        item.astype(F32).reshape(1, -1, item.shape[-1])
        for item in ring_gather(reduced, (3, 1), size)
    )

    def placed(mine, arrived, pairs, far):
        near = lax.dynamic_slice_in_dim(mine, layer * part, part, 0)
        give = lax.dynamic_slice_in_dim(mine, (1 - layer) * part, part, 0)
        sent = pair_permute(give, pairs)
        piped = lax.dynamic_slice_in_dim(arrived, layer * part, part, 0)
        return jnp.where(own, near, jnp.where(far, piped, sent))

    activations = jnp.stack(
        [
            placed(
                jnp.where(first, outputs[i], outputs[i + 1]),
                received[i + 1],
                [(3, 2)],
                layer == 1,
            )
            for i in range(micro)
        ]
    )[None, None]
    input_grads = jnp.stack(
        [
            placed(
                jnp.where(first, results[micro - i], results[micro - 1 - i]),
                grad_received[micro - i],
                [(0, 1)],
                layer == 0,
            )
            for i in range(micro)
        ]
    )[None, None]
    return (
        activations,
        input_grads,
        vectors[0],
        vectors[1],
        qkv_grad,
        vectors[6],
        vectors[7],
        out_grad,
        vectors[2],
        vectors[3],
        vectors[4],
        fc_grad,
        vectors[8],
        proj_grad,
        vectors[5],
    )


def solution(mesh):
    block = P("replica", None, "shard", None)
    layers = P("section", "replica", None, "shard", None)
    vector = P("section", "shard")
    matrix = P("section", "shard", None)
    kinds = (
        vector,
        vector,
        matrix,
        vector,
        vector,
        matrix,
        vector,
        vector,
        vector,
        matrix,
        vector,
        matrix,
        vector,
    )
    return jax.shard_map(
        shards,
        mesh=mesh,
        in_specs=(block, block) + kinds,
        out_specs=(layers, layers) + kinds,
        check_vma=False,
    )
```

```python
import functools

import jax
import jax.numpy as jnp
from jax import lax
from jax.experimental import pallas as pl
from jax.experimental.pallas import tpu as pltpu
from jax.sharding import PartitionSpec as P

HEAD_DIM = 64
EPSILON = 1e-05
GELU_SCALE = 0.7978845608028654
GELU_CUBIC = 0.044715
ROWS_CONTRACT = (((0,), (0,)), ((), ()))
COLS_CONTRACT = (((1,), (1,)), ((), ()))
BF = jnp.bfloat16
F32 = jnp.float32
MESH = pl.DeviceIdType.MESH
QTILE = 256
VMEM_LIMIT = 56 * 1024 * 1024


def rows_product(left, right):
    return lax.dot_general(left, right, ROWS_CONTRACT, preferred_element_type=F32)


def cols_product(left, right):
    return lax.dot_general(left, right, COLS_CONTRACT, preferred_element_type=F32)


def norm_parts(inputs):
    mean = jnp.mean(inputs, axis=-1, keepdims=True)
    centered = inputs - mean
    inverse = lax.rsqrt(jnp.mean(centered * centered, axis=-1, keepdims=True) + EPSILON)
    return centered * inverse, inverse


def norm_backward(d_normed, scaled, inverse, gain):
    d_scaled = d_normed * gain
    return inverse * (
        d_scaled
        - jnp.mean(d_scaled, axis=-1, keepdims=True)
        - scaled * jnp.mean(d_scaled * scaled, axis=-1, keepdims=True)
    )


def gelu_pair(pre):
    tangent = jnp.tanh(GELU_SCALE * (pre + GELU_CUBIC * pre * pre * pre))
    value = 0.5 * pre * (1.0 + tangent)
    slope = 0.5 * (1.0 + tangent) + 0.5 * pre * (1.0 - tangent * tangent) * GELU_SCALE * (
        1.0 + 3.0 * GELU_CUBIC * pre * pre
    )
    return value, slope


def head_parts(pair):
    low = lax.broadcasted_iota(jnp.int32, pair.shape, 1) < HEAD_DIM
    zero = jnp.zeros_like(pair)
    return jnp.where(low, pair, zero), jnp.where(low, zero, pair)


def masked_scores(keys, query, length):
    scores = cols_product(keys, query)
    tail = scores[length - QTILE :]
    key_pos = lax.broadcasted_iota(jnp.int32, tail.shape, 0)
    query_pos = lax.broadcasted_iota(jnp.int32, tail.shape, 1)
    tail = jnp.where(key_pos <= query_pos, tail, -1e30)
    if length == QTILE:
        return tail
    return jnp.concatenate([scores[: length - QTILE], tail], axis=0)


def ring_place(size):
    index = lax.axis_index("replica")
    odd = index % 2
    half = index // 2
    place = (1 - odd) * half + odd * (size - 1 - half)

    def device(spot):
        upper = spot // (size // 2)
        return (1 - upper) * (2 * spot) + upper * (2 * (size - 1 - spot) + 1)

    return place, device((place + 1) % size), device((place + size - 1) % size)


def neighbours():
    core, layer = lax.axis_index("section"), lax.axis_index("shard")
    sibling = {"section": 1 - core}
    across = {"shard": 1 - layer}
    diagonal = {"section": 1 - core, "shard": 1 - layer}
    return core, layer, sibling, across, diagonal


def greet(devices):
    barrier = pltpu.get_barrier_semaphore()
    for device in devices:
        pl.semaphore_signal(barrier, inc=1, device_id=device, device_id_type=MESH)
    pl.semaphore_wait(barrier, len(devices))


def scatter_kernel(size, count, *refs):
    sources, refs = refs[: 6 * count], refs[6 * count :]
    tallies, refs = refs[:3], refs[3:]
    out, refs = refs[:count], refs[count:]
    packed, refs = refs[0], refs[1:]
    held, refs = refs[: 2 * count], refs[2 * count :]
    own, refs = refs[:count], refs[count:]
    landed, refs = refs[:count], refs[count:]
    load_sem, send_sem, recv_sem, small_send, small_recv, swap_sem, total, small, small_out = refs
    place, following, previous = ring_place(size)
    targets = ({"replica": following}, {"replica": previous})
    core, layer, _, _, diagonal = neighbours()

    def load(number, which):
        rows = held[number].shape[0] // 2
        source = sources[3 * number + which]
        part = pl.ds(0 if which == 1 else rows, rows)
        return pltpu.make_async_copy(
            source, held[number].at[part], load_sem.at[number, 0 if which == 1 else 1]
        )

    for number in range(2 * count):
        load(number, 1).start()

        @pl.when(layer == 0)
        def _(number=number):
            load(number, 0).start()

        @pl.when(layer != 0)
        def _(number=number):
            load(number, 2).start()

    greet(targets + (diagonal,))

    def send(way, item, source, slot):
        return pltpu.make_async_remote_copy(
            src_ref=source,
            dst_ref=landed[item].at[way, slot],
            send_sem=send_sem.at[way, item, slot],
            recv_sem=recv_sem.at[way, item, slot],
            device_id=targets[way],
            device_id_type=MESH,
        )

    def send_small(chunk, slot):
        return pltpu.make_async_remote_copy(
            src_ref=small_out.at[chunk],
            dst_ref=small_out.at[chunk],
            send_sem=small_send.at[slot],
            recv_sem=small_recv.at[slot],
            device_id=targets[0],
            device_id_type=MESH,
        )

    def chunk_of(way, slot):
        if way == 0:
            return (place + 2 * size - 2 - slot) % size
        return (place + 2 + slot) % size

    first = ((place + size - 1) % size, (place + 1) % size)
    group = size // 2

    def product(item, way, part):
        deep = own[item].shape[2]
        columns = pl.multiple_of((way * size + part * group) * deep, 128)
        left = held[2 * item][:, pl.ds(columns, group * deep)]
        result = rows_product(left, held[2 * item + 1][...])
        for index in range(group):
            own[item][way, part * group + index] = result[index * deep : (index + 1) * deep].astype(BF)

    half = small.shape[1]

    @pl.when(layer == 0)
    def _():
        total[...] = tallies[1][...] + tallies[2][...]

    @pl.when(layer != 0)
    def _():
        total[...] = tallies[0][...] + tallies[1][...]

    small[...] = jnp.zeros_like(small)
    small[0:6, :] = total[0:6, pl.ds(pl.multiple_of(core * half, half), half)]
    for row in range(3):
        for side in range(2):
            line = 6 + 2 * row + side
            small[line : line + 1, :] = total[6 + row : 7 + row, side * half : (side + 1) * half]

    def swap():
        return pltpu.make_async_remote_copy(
            src_ref=small,
            dst_ref=small_out.at[place],
            send_sem=swap_sem.at[0],
            recv_sem=swap_sem.at[1],
            device_id=diagonal,
            device_id_type=MESH,
        )

    @pl.when(core == layer)
    def _():
        small_out[place] = small[...]

    @pl.when(core != layer)
    def _():
        swap().start()

    for item in range(count):
        for number in (2 * item, 2 * item + 1):
            load(number, 1).wait()
            load(number, 0).wait()
        for way in range(2):
            product(item, way, first[way] // group)
            send(way, item, own[item].at[way, first[way]], 0).start()

    @pl.when(core != layer)
    def _():
        swap().wait()

    send_small(place, 0).start()
    for item in range(count):
        for way in range(2):
            product(item, way, 1 - first[way] // group)

    def step(slot, carry):
        for item in range(count):
            for way in range(2):
                here = landed[item].at[way, slot]
                send(way, item, here, slot).wait_recv()
                here[...] += own[item][way, chunk_of(way, slot)]
                send(way, item, here, slot + 1).start()
        chunk = (place + size - 1 - slot) % size
        send_small(chunk, slot).wait_recv()
        send_small(chunk, slot + 1).start()
        return carry

    lax.fori_loop(0, size - 2, step, 0)
    last = size - 2
    for item in range(count):
        for way in range(2):
            here = landed[item].at[way, last]
            send(way, item, here, last).wait_recv()
            out[item][way] = here[...] + own[item][way, place]
    send_small((place + 1) % size, last).wait_recv()
    gathered = small_out[0]
    for index in range(1, size):
        gathered = gathered + small_out[index]
    packed[...] = gathered

    def finish(slot, carry):
        for item in range(count):
            for way in range(2):
                send(way, item, landed[item].at[way, slot], slot).wait_send()
        send_small(place, slot).wait_send()
        return carry

    lax.fori_loop(0, size - 1, finish, 0)


def ring_scatter(factors, tallies, size):
    count = len(factors)
    flat = [item for pair in factors for item in pair]
    half = tallies[0].shape[1] // 2
    shapes = [(2 * item[0].shape[0], item[0].shape[1]) for item in flat]
    chunks = [
        (shapes[2 * i][1] // (2 * size), shapes[2 * i + 1][1]) for i in range(count)
    ]
    whole = pl.BlockSpec(memory_space=pltpu.VMEM)
    spot = pl.BlockSpec(memory_space=pl.ANY)
    return pl.pallas_call(
        functools.partial(scatter_kernel, size, count),
        out_shape=[jax.ShapeDtypeStruct((2,) + chunk, BF) for chunk in chunks]
        + [jax.ShapeDtypeStruct((16, half), F32)],
        in_specs=[spot] * (6 * count) + [whole] * 3,
        out_specs=[whole] * (count + 1),
        scratch_shapes=[pltpu.VMEM(shape, BF) for shape in shapes]
        + [pltpu.VMEM((2, size) + chunk, BF) for chunk in chunks]
        + [pltpu.VMEM((2, size - 1) + chunk, BF) for chunk in chunks]
        + [pltpu.SemaphoreType.DMA((2 * count, 2))]
        + [pltpu.SemaphoreType.DMA((2, count, size - 1))] * 2
        + [pltpu.SemaphoreType.DMA((size - 1,))] * 2
        + [pltpu.SemaphoreType.DMA((2,))]
        + [
            pltpu.VMEM((16, 2 * half), F32),
            pltpu.VMEM((16, half), F32),
            pltpu.VMEM((size, 16, half), F32),
        ],
        compiler_params=pltpu.CompilerParams(
            collective_id=0, has_side_effects=True, vmem_limit_bytes=VMEM_LIMIT
        ),
        name="ring_scatter",
    )(*[block for item in flat for block in item], *tallies)


def gather_kernel(size, groups, *refs):
    count = 4
    own, refs = refs[:count], refs[count:]
    near, refs = refs[:12], refs[12:]
    out, refs = refs[:count], refs[count:]
    placed, refs = refs[:2], refs[2:]
    swap_send, swap_recv, send_sem, recv_sem, place_send, place_recv, load_sem, bounce = refs
    place, following, previous = ring_place(size)
    targets = ({"replica": following}, {"replica": previous})
    core, layer, sibling, across, diagonal = neighbours()
    same = core == layer
    greet(targets + (sibling, across, diagonal))

    def parts(item, source_half, sender):
        if item < len(groups):
            width = own[item].shape[2] // groups[item]
            for group in range(groups[item]):
                start = pl.multiple_of((2 * group + sender) * width, width)
                yield (
                    own[item].at[source_half, :, pl.ds(group * width, width)],
                    out[item].at[place, :, pl.ds(start, width)],
                )
        else:
            for half in range(2):
                yield own[item].at[half], out[item].at[half, place]

    def copies(item, source_half, lane, kind, device=None):
        for number, (source, target) in enumerate(parts(item, source_half, core)):
            send, recv = swap_send.at[item, lane, number], swap_recv.at[item, kind, number]
            if device is None:
                yield pltpu.make_async_copy(source, target, recv)
            else:
                yield pltpu.make_async_remote_copy(
                    src_ref=source,
                    dst_ref=target,
                    send_sem=send,
                    recv_sem=recv,
                    device_id=device,
                    device_id_type=MESH,
                )

    @pl.when(same)
    def _():
        for item in range(count):
            for copy in copies(item, layer, 0, 0):
                copy.start()
            if item < len(groups):
                for copy in copies(item, 1 - layer, 0, 2, across):
                    copy.start()

    @pl.when(core != layer)
    def _():
        for item in range(count):
            for copy in copies(item, 1 - layer, 0, 3, diagonal):
                copy.start()
            if item < len(groups):
                for copy in copies(item, layer, 1, 1, sibling):
                    copy.start()

    part = placed[0].shape[1]

    def near_rows(number, block, shard):
        return near[6 * block + number].at[pl.ds(shard * part, part)]

    def place_remote(kind, block):
        number, shard = ((1, 0), (3, 1))[kind]
        return pltpu.make_async_remote_copy(
            src_ref=near_rows(number, block, shard),
            dst_ref=placed[kind].at[block],
            send_sem=place_send.at[block],
            recv_sem=place_recv.at[block],
            device_id=across,
            device_id_type=MESH,
        )

    def place_load(number, block, shard):
        lane = 2 * (number // 3) + block
        return pltpu.make_async_copy(near_rows(number, block, shard), bounce.at[lane], load_sem.at[lane])

    def place_store(number, block):
        kind = number // 3
        lane = 2 * kind + block
        return pltpu.make_async_copy(bounce.at[lane], placed[kind].at[block], load_sem.at[lane])

    local = {(0, 0): (0, 3), (0, 1): (2,), (1, 0): (5,), (1, 1): (1, 4)}

    def on_device(action):
        for (at_core, at_layer), numbers in local.items():

            @pl.when((core == at_core) & (layer == at_layer))
            def _(numbers=numbers, at_layer=at_layer):
                for number in numbers:
                    for block in range(2):
                        action(number, block, at_layer)

    @pl.when(same & (layer == 1))
    def _():
        for block in range(2):
            place_remote(0, block).start()

    @pl.when(same & (layer == 0))
    def _():
        for block in range(2):
            place_remote(1, block).start()

    on_device(lambda number, block, shard: place_load(number, block, shard).start())

    def send(way, item, chunk, slot):
        if item < len(groups):
            deep = out[item].shape[1] // 2
            here = out[item].at[chunk, pl.ds(way * deep, deep)]
        else:
            here = out[item].at[way, chunk]
        return pltpu.make_async_remote_copy(
            src_ref=here,
            dst_ref=here,
            send_sem=send_sem.at[way, item, slot],
            recv_sem=recv_sem.at[way, item, slot],
            device_id=targets[way],
            device_id_type=MESH,
        )

    def chunk_of(way, slot):
        if way == 0:
            return (place + size - 1 - slot) % size
        return (place + 1 + slot) % size

    for item in range(count):

        @pl.when(same)
        def _(item=item):
            for copy in copies(item, layer, 0, 0):
                copy.wait()
            if item < len(groups):
                for copy in copies(item, layer, 1, 1, sibling):
                    copy.wait_recv()

        @pl.when(core != layer)
        def _(item=item):
            for copy in copies(item, layer, 0, 3, diagonal):
                copy.wait_recv()
            if item < len(groups):
                for copy in copies(item, layer, 0, 2, across):
                    copy.wait_recv()

        for way in range(2):
            send(way, item, place, 0).start()

    def step(slot, carry):
        for item in range(count):
            for way in range(2):
                chunk = chunk_of(way, slot)
                send(way, item, chunk, slot).wait_recv()
                send(way, item, chunk, slot + 1).start()
        return carry

    def moved(number, block, shard):
        place_load(number, block, shard).wait()
        place_store(number, block).start()

    on_device(moved)
    lax.fori_loop(0, size - 2, step, 0)
    last = size - 2
    for item in range(count):
        for way in range(2):
            send(way, item, chunk_of(way, last), last).wait_recv()
    on_device(lambda number, block, shard: place_store(number, block).wait())

    @pl.when(same)
    def _():
        for block in range(2):
            place_remote(0, block).wait_send()

    @pl.when((core != layer) & (layer == 0))
    def _():
        for block in range(2):
            place_remote(0, block).wait_recv()

    @pl.when((core != layer) & (layer == 1))
    def _():
        for block in range(2):
            place_remote(1, block).wait_recv()

    @pl.when(same)
    def _():
        for item in range(len(groups)):
            for copy in copies(item, 1 - layer, 0, 2, across):
                copy.wait_send()

    @pl.when(core != layer)
    def _():
        for item in range(count):
            for copy in copies(item, 1 - layer, 0, 3, diagonal):
                copy.wait_send()
            if item < len(groups):
                for copy in copies(item, layer, 1, 1, sibling):
                    copy.wait_send()

    def finish(slot, carry):
        for item in range(count):
            for way in range(2):
                send(way, item, place, slot).wait_send()
        return carry

    lax.fori_loop(0, size - 1, finish, 0)


def ring_gather(pieces, groups, near, size):
    spot = pl.BlockSpec(memory_space=pl.ANY)
    shapes = [(size, item.shape[1], 2 * item.shape[2]) for item in pieces[: len(groups)]]
    shapes += [(2, size) + item.shape[1:] for item in pieces[len(groups) :]]
    count = len(pieces)
    rows = (near[0].shape[0] // 2, near[0].shape[1])
    whole = pl.BlockSpec(memory_space=pltpu.VMEM)
    return pl.pallas_call(
        functools.partial(gather_kernel, size, groups),
        out_shape=[jax.ShapeDtypeStruct(shape, BF) for shape in shapes]
        + [jax.ShapeDtypeStruct((2,) + rows, BF)] * 2,
        in_specs=[whole] * count + [spot] * 12,
        out_specs=[whole] * count + [spot] * 2,
        scratch_shapes=[
            pltpu.SemaphoreType.DMA((count, 2, 3)),
            pltpu.SemaphoreType.DMA((count, 4, 3)),
        ]
        + [pltpu.SemaphoreType.DMA((2, count, size - 1))] * 2
        + [pltpu.SemaphoreType.DMA((2,))] * 2
        + [pltpu.SemaphoreType.DMA((4,)), pltpu.VMEM((4,) + rows, BF)],
        compiler_params=pltpu.CompilerParams(
            collective_id=1, has_side_effects=True, vmem_limit_bytes=VMEM_LIMIT
        ),
        name="ring_gather",
    )(*pieces, *near)


def finish_kernel(*refs):
    gathered, packed, placed = refs[:4], refs[4], refs[5:7]
    wide, vectors, moved = refs[7:11], refs[11:20], refs[20:22]
    buffers, bounce = refs[22:26], refs[26]
    store_sem, load_sem = refs[27:]
    loads = [pltpu.make_async_copy(placed[i], bounce.at[i], load_sem.at[i]) for i in range(2)]
    for copy in loads:
        copy.start()
    half = packed.shape[1]
    for number in range(9):
        for index in range(vectors[number].shape[1] // half):
            row = number + index
            vectors[number][:, index * half : (index + 1) * half] = packed[row : row + 1, :]
    stores = [pltpu.make_async_copy(bounce.at[i], moved[i], load_sem.at[i]) for i in range(2)]
    for i in range(2):
        loads[i].wait()
        stores[i].start()

    def store(item, chunk):
        deep = gathered[item].shape[1]
        place = pl.ds(pl.multiple_of(chunk * deep, deep), deep)
        return pltpu.make_async_copy(
            buffers[item].at[chunk], wide[item].at[place], store_sem.at[item, chunk]
        )

    for item in range(4):

        def step(chunk, carry, item=item):
            buffers[item][chunk] = gathered[item][chunk].astype(F32)
            store(item, chunk).start()
            return carry

        lax.fori_loop(0, gathered[item].shape[0], step, 0)
    for item in range(4):

        def drain(chunk, carry, item=item):
            store(item, chunk).wait()
            return carry

        lax.fori_loop(0, gathered[item].shape[0], drain, 0)
    for copy in stores:
        copy.wait()


def finish(gathered, packed, placed):
    spot = pl.BlockSpec(memory_space=pl.ANY)
    whole = pl.BlockSpec(memory_space=pltpu.VMEM)
    gathered = [item.reshape((-1,) + item.shape[-2:]) for item in gathered]
    half = packed.shape[1]
    return pl.pallas_call(
        finish_kernel,
        out_shape=[
            jax.ShapeDtypeStruct((item.shape[0] * item.shape[1], item.shape[2]), F32)
            for item in gathered
        ]
        + [jax.ShapeDtypeStruct((1, half), F32)] * 8
        + [jax.ShapeDtypeStruct((1, 4 * half), F32)]
        + [jax.ShapeDtypeStruct(item.shape, BF) for item in placed],
        in_specs=[whole] * 5 + [spot] * 2,
        out_specs=[spot] * 4 + [whole] * 9 + [spot] * 2,
        scratch_shapes=[pltpu.VMEM(item.shape, F32) for item in gathered]
        + [pltpu.VMEM((2,) + placed[0].shape, BF)]
        + [
            pltpu.SemaphoreType.DMA((4, max(item.shape[0] for item in gathered))),
            pltpu.SemaphoreType.DMA((2,)),
        ],
        compiler_params=pltpu.CompilerParams(vmem_limit_bytes=VMEM_LIMIT),
        name="finish",
    )(*gathered, packed, *placed)


def fetch_kernel(*refs):
    tokens, cotangent, qkv, fc, out, proj = refs[:6]
    vectors, refs = refs[6:15], refs[15:]
    *outer, params, w_qkv, w_fc, w_out, w_proj = refs[:7]
    send_sem, recv_sem, extra_send, extra_recv, local_sem, vector_sem = refs[7:13]
    raw, small, small_out = refs[13:22], refs[22], refs[23]
    buffers = refs[24:]
    core, layer, sibling, across, diagonal = neighbours()
    index = lax.axis_index("replica")
    quarter = index % 4
    low, high = index % 2, (index // 2) % 2
    beside = {"replica": index + 1 - 2 * low}
    above = {"replica": index + 2 - 4 * high}
    beside_quarter = quarter + 1 - 2 * low
    above_quarter = quarter + 2 - 4 * high
    same = core == layer
    far_quarter = 3 - quarter
    for number in range(9):
        pltpu.make_async_copy(vectors[number], raw[number], vector_sem.at[number]).start()
    greet((sibling, across, diagonal, beside, above))

    depth = qkv.shape[0]
    span = qkv.shape[1] // 6
    wide = fc.shape[1] // 2
    turn = proj.shape[0] // 2
    cols = [
        (qkv, w_qkv, lambda s, g=g: pl.multiple_of((2 * g + s) * span, span), g * span, span)
        for g in range(3)
    ]
    cols.append((fc, w_fc, lambda s: pl.multiple_of(s * wide, wide), 0, wide))
    rows = [(out, w_out, 0, out.shape[0]), (proj, w_proj, 0, turn), (proj, w_proj, turn, turn)]
    order = [0, 1, 2, 4, 3, 5, 6]

    def rows_of(item):
        return depth if item < 4 else rows[item - 4][3]

    def target(item, base, which, part=None):
        deep = rows_of(item) // 4
        start = base + which * deep
        if part is not None:
            deep = deep // 2
            start = start + part * deep
        place = pl.ds(pl.multiple_of(start, deep), deep)
        if item < 4:
            return cols[item][1].at[place, pl.ds(cols[item][3], cols[item][4])]
        return rows[item - 4][1].at[place]

    def base_of(item, shard):
        return shard * depth if item < 4 else rows[item - 4][2]

    def remote(stage, item, source, dest, device, lane=0):
        return pltpu.make_async_remote_copy(
            src_ref=source,
            dst_ref=dest,
            send_sem=send_sem.at[stage + lane, item],
            recv_sem=recv_sem.at[stage, item],
            device_id=device,
            device_id_type=MESH,
        )

    def cross(item, receiver):
        deep = rows_of(item) // 4
        place = pl.multiple_of(base_of(item, 0) + quarter * deep, deep)
        dest = target(item, base_of(item, layer), quarter)
        if item < 4:
            columns = cols[item][2](receiver)
            source = cols[item][0].at[pl.ds(place, deep), pl.ds(columns, cols[item][4])]
        else:
            source = rows[item - 4][0].at[pl.ds(place, deep)]
        return source, dest

    def cross_same(item):
        return remote(0, item, *cross(item, core), across, 5)

    def cross_swap(item):
        return remote(0, item, *cross(item, 1 - core), diagonal)

    def pass_on(stage, item, which, device, part=None):
        here = target(item, base_of(item, 1 - layer), which, part)
        return remote(stage, item, here, here, device)

    def to_sibling(item):
        columns = cols[item][2](1 - core)
        source = cols[item][0].at[:, pl.ds(columns, cols[item][4])]
        start = pl.multiple_of(layer * depth, depth)
        dest = cols[item][1].at[pl.ds(start, depth), pl.ds(cols[item][3], cols[item][4])]
        return remote(6, item, source, dest, sibling)

    def through(source, dest, number):
        return (
            lambda: pltpu.make_async_copy(source, buffers[number], local_sem.at[number]),
            lambda: pltpu.make_async_copy(buffers[number], dest, local_sem.at[number]),
        )

    def keep_local(item):
        if item < 4:
            columns = cols[item][2](core)
            source = cols[item][0].at[:, pl.ds(columns, cols[item][4])]
            start = pl.multiple_of(layer * depth, depth)
            dest = cols[item][1].at[pl.ds(start, depth), pl.ds(cols[item][3], cols[item][4])]
        else:
            source, dest, start, deep = rows[item - 4]
            source, dest = source.at[pl.ds(start, deep)], dest.at[pl.ds(start, deep)]
        return through(source, dest, item)

    part = tokens.shape[1]
    half = part // 2

    def outer_rows(shard, which):
        return pl.ds(pl.multiple_of(shard * part + which * half, half), half)

    def outer_cross(block):
        place = pl.ds(pl.multiple_of(core * half, half), half)

        def copy(source):
            return pltpu.make_async_remote_copy(
                src_ref=source.at[block, place],
                dst_ref=outer[block].at[outer_rows(layer, core)],
                send_sem=extra_send.at[block],
                recv_sem=extra_recv.at[block],
                device_id=across,
                device_id_type=MESH,
            )

        return copy

    def outer_pass(block):
        here = outer[block].at[outer_rows(1 - layer, core)]
        return pltpu.make_async_remote_copy(
            src_ref=here,
            dst_ref=here,
            send_sem=extra_send.at[2 + block],
            recv_sem=extra_recv.at[2 + block],
            device_id=sibling,
            device_id_type=MESH,
        )

    def outer_local(source, block):
        place = pl.ds(pl.multiple_of(layer * part, part), part)
        return through(source.at[block], outer[block].at[place], 7 + block)

    def small_swap():
        return pltpu.make_async_remote_copy(
            src_ref=small,
            dst_ref=small_out.at[1 - core],
            send_sem=extra_send.at[4],
            recv_sem=extra_recv.at[4],
            device_id=diagonal,
            device_id_type=MESH,
        )

    def small_pass():
        return pltpu.make_async_remote_copy(
            src_ref=small_out.at[core],
            dst_ref=small_out.at[core],
            send_sem=extra_send.at[5],
            recv_sem=extra_recv.at[5],
            device_id=sibling,
            device_id_type=MESH,
        )

    def start_outer(block):
        @pl.when(layer == 0)
        def _():
            outer_cross(block)(cotangent).start()

        @pl.when(layer == 1)
        def _():
            outer_cross(block)(tokens).start()

    def crossings(item):
        if item < 4:
            cross_same(item).start()
        cross_swap(item).start()

    start_outer(0)

    @pl.when(core != layer)
    def _():
        crossings(order[0])
        crossings(order[1])

    @pl.when(layer == 0)
    def _():
        for block in range(2):
            outer_local(tokens, block)[0]().start()

    @pl.when(layer == 1)
    def _():
        for block in range(2):
            outer_local(cotangent, block)[0]().start()

    @pl.when(same)
    def _():
        for item in range(4):
            to_sibling(item).start()

    span_small = small.shape[1]
    for number in range(9):
        pltpu.make_async_copy(vectors[number], raw[number], vector_sem.at[number]).wait()
        values = raw[number][...].astype(F32)
        for index in range(values.shape[1] // span_small):
            row = number + index
            small[row : row + 1, :] = values[:, index * span_small : (index + 1) * span_small]

    @pl.when(same)
    def _():
        small_out[core] = small[...]

    @pl.when(core != layer)
    def _():
        small_swap().start()
        small_swap().wait_recv()

    small_pass().start()
    for block in range(2):
        load, store = outer_local(tokens, block)
        load().wait()
        store().start()

    @pl.when(same)
    def _():
        for item in range(7):
            keep_local(item)[0]().start()

    def relay(sequence, ahead):
        def onward(item):
            pass_on(1, item, beside_quarter, beside).wait_recv()
            pass_on(4, item, beside_quarter, above, 0).start()
            pass_on(2, item, above_quarter, above).wait_recv()
            pass_on(3, item, above_quarter, beside, 1).start()

        for number, item in enumerate(sequence):
            pass_on(0, item, quarter, beside).wait_recv()
            if ahead and number + 2 < len(sequence):
                crossings(sequence[number + 2])
            pass_on(1, item, quarter, beside).start()
            pass_on(2, item, quarter, above).start()
            if number >= 1:
                onward(sequence[number - 1])
            if number == 0:
                outer_cross(0)(tokens).wait_recv()
                outer_pass(0).start()
                start_outer(1)
        onward(sequence[-1])
        for item in sequence:
            pass_on(3, item, far_quarter, beside, 1).wait_recv()
            pass_on(4, item, far_quarter, above, 0).wait_recv()
            for stage in (1, 2):
                pass_on(stage, item, quarter, beside).wait_send()
            for stage, which in ((3, 1), (4, 0)):
                pass_on(stage, item, quarter, beside, which).wait_send()

    @pl.when(same)
    def _():
        for item in range(7):
            load, store = keep_local(item)
            load().wait()
            store().start()
        relay([0, 1, 2, 3], False)
        for item in range(4):
            to_sibling(item).wait_send()
        for item in range(7):
            keep_local(item)[1]().wait()

    @pl.when(core != layer)
    def _():
        relay(order, True)
        for item in range(4):
            to_sibling(item).wait_recv()
            cross_same(item).wait_send()
        for item in range(7):
            cross_swap(item).wait_send()
        small_swap().wait_send()

    outer_cross(1)(tokens).wait_recv()
    outer_pass(1).start()
    for block in range(2):
        outer_local(tokens, block)[1]().wait()
    small_pass().wait()
    params[...] = jnp.zeros_like(params)
    for side in range(2):
        lanes = slice(side * span_small, (side + 1) * span_small)
        params[0:6, lanes] = small_out[side, 0:6]
        for row in range(3):
            line = 6 + 2 * row + side
            params[6 + row : 7 + row, lanes] = small_out[core, line : line + 1]
    for block in range(2):
        outer_cross(block)(tokens).wait_send()
        outer_pass(block).wait()


def fetch_inputs(tokens, cotangent, qkv, fc, out, proj, vectors):
    spot = pl.BlockSpec(memory_space=pl.ANY)
    _, part, width = tokens.shape
    shapes = [
        (2 * part, width),
        (2 * part, width),
        (2 * qkv.shape[0], qkv.shape[1] // 2),
        (2 * fc.shape[0], fc.shape[1] // 2),
        out.shape,
        proj.shape,
    ]
    return pl.pallas_call(
        fetch_kernel,
        out_shape=[jax.ShapeDtypeStruct(shape, BF) for shape in shapes[:2]]
        + [jax.ShapeDtypeStruct((16, width), F32)]
        + [jax.ShapeDtypeStruct(shape, BF) for shape in shapes[2:]],
        in_specs=[spot] * 15,
        out_specs=[spot] * 2 + [pl.BlockSpec(memory_space=pltpu.VMEM)] + [spot] * 4,
        scratch_shapes=[
            pltpu.SemaphoreType.DMA((7, 7)),
            pltpu.SemaphoreType.DMA((7, 7)),
            pltpu.SemaphoreType.DMA((6,)),
            pltpu.SemaphoreType.DMA((6,)),
            pltpu.SemaphoreType.DMA((9,)),
            pltpu.SemaphoreType.DMA((9,)),
        ]
        + [pltpu.VMEM(item.shape, BF) for item in vectors]
        + [pltpu.VMEM((16, width // 2), F32), pltpu.VMEM((2, 16, width // 2), F32)]
        + [pltpu.VMEM((qkv.shape[0], qkv.shape[1] // 6), BF)] * 3
        + [
            pltpu.VMEM((fc.shape[0], fc.shape[1] // 2), BF),
            pltpu.VMEM(out.shape, BF),
            pltpu.VMEM((proj.shape[0] // 2, width), BF),
            pltpu.VMEM((proj.shape[0] // 2, width), BF),
            pltpu.VMEM(tokens.shape[1:], BF),
            pltpu.VMEM(tokens.shape[1:], BF),
        ],
        compiler_params=pltpu.CompilerParams(
            collective_id=2, has_side_effects=True, vmem_limit_bytes=VMEM_LIMIT
        ),
        name="fetch_inputs",
    )(tokens, cotangent, qkv, fc, out, proj, *vectors)


TILES = 2


class Loads:
    def __init__(self, sem):
        self.sem, self.count, self.made = sem, 0, {}

    def start(self, name, source, buffer):
        copy = pltpu.make_async_copy(source, buffer, self.sem.at[self.count])
        self.count += 1
        copy.start()
        self.made[name] = copy

    def wait(self, *names):
        for name in names:
            self.made.pop(name).wait()


def greet_step(sender, passing):
    core, layer, sibling, across, _ = neighbours()
    barrier = pltpu.get_barrier_semaphore()
    pl.semaphore_signal(barrier, inc=1, device_id=sibling, device_id_type=MESH)
    if not passing:
        pl.semaphore_wait(barrier, 1)
        return

    @pl.when(layer != sender)
    def _():
        pl.semaphore_signal(barrier, inc=1, device_id=across, device_id_type=MESH)
        pl.semaphore_wait(barrier, 1)

    @pl.when(layer == sender)
    def _():
        pl.semaphore_wait(barrier, 2)


class Exchange:
    def __init__(self, send_buf, recv_buf, send_sem, recv_sem):
        self.refs = (send_buf, recv_buf, send_sem, recv_sem)

    def copy(self, slot):
        send_buf, recv_buf, send_sem, recv_sem = self.refs
        return pltpu.make_async_remote_copy(
            src_ref=send_buf.at[slot],
            dst_ref=recv_buf.at[slot],
            send_sem=send_sem.at[slot],
            recv_sem=recv_sem.at[slot],
            device_id={"section": 1 - lax.axis_index("section")},
            device_id_type=MESH,
        )

    def give(self, slot, partial):
        self.refs[0][slot] = partial.astype(BF)
        self.copy(slot).start()

    def take(self, slot):
        self.copy(slot).wait_recv()
        return self.refs[1][slot].astype(F32)

    def finish(self, count):
        for slot in range(count):
            self.copy(slot).wait_send()


class Across:
    def __init__(self, sender, source, dest, sems):
        self.sender, self.source, self.dest, self.sems = sender, source, dest, sems
        self.core, self.layer, self.sibling, self.across, _ = neighbours()

    def copy(self, tile, stage):
        rows = self.dest.shape[0] // (2 * TILES)
        place = pl.ds(pl.multiple_of((2 * tile + self.core) * rows, rows), rows)
        source = self.source if stage == 0 else self.dest
        return pltpu.make_async_remote_copy(
            src_ref=source.at[place],
            dst_ref=self.dest.at[place],
            send_sem=self.sems.at[stage, tile],
            recv_sem=self.sems.at[2 + stage, tile],
            device_id=self.across if stage == 0 else self.sibling,
            device_id_type=MESH,
        )

    def send(self, tile):
        @pl.when(self.layer == self.sender)
        def _():
            self.copy(tile, 0).start()

    def receive(self, tile):
        @pl.when(self.layer != self.sender)
        def _():
            self.copy(tile, 0).wait_recv()
            self.copy(tile, 1).start()
            self.copy(tile, 1).wait_recv()

    def finish(self):
        @pl.when(self.layer == self.sender)
        def _():
            for tile in range(TILES):
                self.copy(tile, 0).wait_send()

        @pl.when(self.layer != self.sender)
        def _():
            for tile in range(TILES):
                self.copy(tile, 1).wait_send()


class Opening:
    def __init__(self, passing, sender, first_ref, other_ref, earlier, buffer, sem, sems):
        self.passing, self.sender, self.layer = passing, sender, lax.axis_index("shard")
        self.load = lambda ref: pltpu.make_async_copy(ref, buffer, sem)
        self.refs = (first_ref, other_ref)
        self.across = Across(sender, earlier, buffer, sems)

    def start(self):
        for layer, ref in enumerate(self.refs):
            if self.passing and layer != self.sender:
                continue

            @pl.when(self.layer == layer)
            def _(ref=ref):
                self.load(ref).start()

    def send(self):
        if self.passing:
            for tile in range(TILES):
                self.across.send(tile)

    def take(self, tile):
        if self.passing:
            if tile == 0:

                @pl.when(self.layer == self.sender)
                def _():
                    self.load(self.refs[0]).wait()

            self.across.receive(tile)
        elif tile == 0:
            self.load(self.refs[0]).wait()

    def finish(self):
        if self.passing:
            self.across.finish()


def by_past(mode, body):
    if mode is not None:
        body(mode)
        return
    layer = lax.axis_index("shard")

    @pl.when(layer == 0)
    def _():
        body(True)

    @pl.when(layer != 0)
    def _():
        body(False)


FORWARD_LOADS = 7


def forward_kernel(mode, passing, *refs):
    x_first, x_other, earlier, params, w_qkv, w_out, w_fc, w_proj, k_past, v_past = refs[:10]
    refs = refs[10:]
    (x_used, normed1, query, keys, values, mixed, lse, scaled2, inverse2, normed2, slope, act, out, passed) = refs[:14]
    refs = refs[14:]
    (x_v, wq_v, wo_v, wf_v, wp_v, k_v, v_v, hid_v, part_v, send_v, recv_v) = refs[:11]
    refs = refs[11:]
    (n1_v, q_v, m_v, lse_v, s2_v, i2_v, n2_v, sl_v, a_v, o_v) = refs[:10]
    load_sem, store_sem, send_sem, recv_sem, open_sem, across_sem = refs[10:]
    rows, width = x_v.shape
    half = q_v.shape[1]
    tile_rows = rows // TILES
    wide = a_v.shape[1]

    loads = Loads(load_sem)
    opening = Opening(passing, 0, x_first, x_other, earlier, x_v, load_sem.at[FORWARD_LOADS], open_sem)
    opening.start()
    loads.start("qkv", w_qkv, wq_v)
    if mode is not False:
        loads.start("k", k_past, k_v.at[pl.ds(0, rows)])
        loads.start("v", v_past, v_v.at[pl.ds(0, rows)])
    loads.start("out", w_out, wo_v)
    loads.start("fc", w_fc, wf_v)
    loads.start("proj", w_proj, wp_v)
    greet_step(0, passing)
    opening.send()
    exchange = Exchange(send_v, recv_v, send_sem, recv_sem)
    across = Across(0, o_v, passed, across_sem)
    stores = []

    def store(buffer, dest):
        copy = pltpu.make_async_copy(buffer, dest, store_sem.at[len(stores)])
        copy.start()
        stores.append(copy)

    def vector(row, start=0, size=None):
        return params[row : row + 1, start : start + (size or width)]

    own_rows = pl.ds(rows, rows)
    for tile in range(TILES):
        span = pl.ds(tile * tile_rows, tile_rows)
        later = pl.ds(rows + tile * tile_rows, tile_rows)
        opening.take(tile)
        scaled, _ = norm_parts(x_v[span, :].astype(F32))
        normed = (scaled * vector(0) + vector(1)).astype(BF)
        n1_v[span, :] = normed
        if tile == 0:
            loads.wait("qkv")
        piece = jnp.dot(normed, wq_v[:, :half], preferred_element_type=F32)
        q_v[span, :] = (piece + vector(6, 0, half)).astype(BF)
        piece = jnp.dot(normed, wq_v[:, half : 2 * half], preferred_element_type=F32)
        k_v[later, :] = piece.astype(BF)
        piece = jnp.dot(normed, wq_v[:, 2 * half :], preferred_element_type=F32)
        v_v[later, :] = (piece + vector(6, half, half)).astype(BF)
    store(x_v, x_used)
    store(n1_v, normed1)
    store(q_v, query)
    store(k_v.at[own_rows], keys)
    store(v_v.at[own_rows], values)
    if mode is not False:
        loads.wait("k", "v")
    loads.wait("out")

    def attention(past):
        first_key = 0 if past else rows
        for tile in range(TILES):
            span = pl.ds(tile * tile_rows, tile_rows)
            length = (rows if past else 0) + (tile + 1) * tile_rows
            reach = pl.ds(first_key, length)

            def pair(number, carry):
                lanes = pl.ds(pl.multiple_of(number * 128, 128), 128)
                key, value = k_v[reach, lanes], v_v[reach, lanes]
                pieces = []
                for head, part in enumerate(head_parts(q_v[span, lanes])):
                    scores = masked_scores(key, part * BF(HEAD_DIM**-0.5), length)
                    top = jnp.max(scores, axis=0, keepdims=True)
                    probs = jnp.exp(scores - top)
                    total = jnp.sum(probs, axis=0, keepdims=True)
                    lse_v[number, pl.ds(head, 1), span] = top + jnp.log(total)
                    piece = rows_product(value, probs.astype(BF))
                    piece = piece[head * HEAD_DIM : (head + 1) * HEAD_DIM]
                    pieces.append(piece * (1.0 / total))
                m_v[span, lanes] = jnp.transpose(jnp.concatenate(pieces, axis=0)).astype(BF)
                return carry

            lax.fori_loop(0, half // 128, pair, 0)
            partial = jnp.dot(m_v[span, :], wo_v[...], preferred_element_type=F32)
            part_v[tile] = partial
            exchange.give(tile, partial)

    by_past(mode, attention)
    store(m_v, mixed)
    store(lse_v, lse)
    loads.wait("fc", "proj")

    def conclude(tile):
        span = pl.ds(tile * tile_rows, tile_rows)
        total = part_v[TILES + tile] + exchange.take(TILES + tile)
        o_v[span, :] = (hid_v[span, :] + total + vector(5)).astype(BF)
        if passing:
            across.send(tile)

    for tile in range(TILES):
        span = pl.ds(tile * tile_rows, tile_rows)
        hidden = x_v[span, :].astype(F32) + (part_v[tile] + exchange.take(tile)) + vector(2)
        hid_v[span, :] = hidden
        scaled, inverse = norm_parts(hidden)
        s2_v[span, :] = scaled.astype(BF)
        i2_v[span, :] = jnp.broadcast_to(inverse, (tile_rows, 128))
        normed = (scaled * vector(3) + vector(4)).astype(BF)
        n2_v[span, :] = normed
        chunk = width // 2
        for part in range(wide // chunk):
            columns = pl.ds(part * chunk, chunk)
            pre = jnp.dot(normed, wf_v[:, columns], preferred_element_type=F32)
            bias = vector(7 + part * chunk // width, part * chunk % width, chunk)
            activated, inclined = gelu_pair(pre + bias)
            a_v[span, columns] = activated.astype(BF)
            sl_v[span, columns] = inclined.astype(BF)
        if tile > 0:
            conclude(tile - 1)
        partial = jnp.dot(a_v[span, :], wp_v[...], preferred_element_type=F32)
        part_v[TILES + tile] = partial
        exchange.give(TILES + tile, partial)
    store(s2_v, scaled2)
    store(i2_v, inverse2)
    store(n2_v, normed2)
    store(sl_v, slope)
    store(a_v, act)
    conclude(TILES - 1)
    store(o_v, out)
    for copy in stores:
        copy.wait()
    exchange.finish(2 * TILES)
    opening.finish()
    if passing:
        for tile in range(TILES):
            across.receive(tile)
        across.finish()


def step_sems(loads, stores):
    return [
        pltpu.SemaphoreType.DMA((loads,)),
        pltpu.SemaphoreType.DMA((stores,)),
        pltpu.SemaphoreType.DMA((2 * TILES,)),
        pltpu.SemaphoreType.DMA((2 * TILES,)),
        pltpu.SemaphoreType.DMA((4, TILES)),
        pltpu.SemaphoreType.DMA((4, TILES)),
    ]


def forward_step(mode, passing, inputs, params, weights, past):
    rows, width = inputs[0].shape
    half = width // 2
    wide = weights[2].shape[1]
    pairs = half // 128
    tile_rows = rows // TILES
    spot = pl.BlockSpec(memory_space=pl.ANY)
    low = lambda columns: ((rows, columns), BF)
    outs = [
        low(width),
        low(width),
        low(half),
        low(half),
        low(half),
        low(half),
        ((pairs, 8, rows), F32),
        low(width),
        ((rows, 128), F32),
        low(width),
        low(wide),
        low(wide),
        low(width),
        low(width),
    ]
    scratch = [
        low(width),
        *((item.shape, BF) for item in weights),
        ((2 * rows, half), BF),
        ((2 * rows, half), BF),
        ((rows, width), F32),
        ((2 * TILES, tile_rows, width), F32),
        ((2 * TILES, tile_rows, width), BF),
        ((2 * TILES, tile_rows, width), BF),
        low(width),
        low(half),
        low(half),
        ((pairs, 8, rows), F32),
        low(width),
        ((rows, 128), F32),
        low(width),
        low(wide),
        low(wide),
        low(width),
    ]
    number = {False: 3, None: 4, True: 5}[mode]
    return pl.pallas_call(
        functools.partial(forward_kernel, mode, passing),
        out_shape=[jax.ShapeDtypeStruct(*item) for item in outs],
        in_specs=[spot] * 3 + [pl.BlockSpec(memory_space=pltpu.VMEM)] + [spot] * 6,
        out_specs=[spot] * len(outs),
        scratch_shapes=[pltpu.VMEM(*item) for item in scratch]
        + step_sems(FORWARD_LOADS + 1, len(outs)),
        compiler_params=pltpu.CompilerParams(
            collective_id=number, has_side_effects=True, vmem_limit_bytes=VMEM_LIMIT
        ),
        name="forward_step",
    )(*inputs, params, *weights, *past)


BACKWARD_LOADS = 17


def backward_kernel(mode, passing, *refs):
    (g_first, g_other, earlier, x_used, params, w_qkv, w_out, w_fc, w_proj) = refs[:9]
    (query, keys, values, k_past, v_past, mixed, lse, scaled2, inverse2, slope, pend_k, pend_v) = refs[9:21]
    refs = refs[21:]
    (g_used, d_qkv, d_branch, d_pre, out, next_k, next_v, sums, passed) = refs[:9]
    refs = refs[9:]
    (g_v, x_v, wq_v, wo_v, wf_v, wp_v, q_v, k_v, v_v, m_v, lse_v, s2_v, i2_v, sl_v) = refs[:14]
    refs = refs[14:]
    (dk_v, dv_v, hid_v, part_v, send_v, recv_v, dqkv_v, db_v, dp_v, dm_v, o_v, sum_v) = refs[:12]
    load_sem, store_sem, send_sem, recv_sem, open_sem, across_sem = refs[12:]
    rows, width = x_v.shape
    half = q_v.shape[1]
    wide = dp_v.shape[1]
    tile_rows = rows // TILES
    own_rows, past_rows = pl.ds(rows, rows), pl.ds(0, rows)
    scale = HEAD_DIM**-0.5

    loads = Loads(load_sem)
    opening = Opening(passing, 1, g_first, g_other, earlier, g_v, load_sem.at[BACKWARD_LOADS], open_sem)
    opening.start()
    loads.start("proj", w_proj, wp_v)
    loads.start("slope", slope, sl_v)
    loads.start("fc", w_fc, wf_v)
    loads.start("scaled2", scaled2, s2_v)
    loads.start("inverse2", inverse2, i2_v)
    loads.start("out", w_out, wo_v)
    loads.start("q", query, q_v)
    loads.start("k", keys, k_v.at[own_rows])
    loads.start("v", values, v_v.at[own_rows])
    if mode is not False:
        loads.start("k_past", k_past, k_v.at[past_rows])
        loads.start("v_past", v_past, v_v.at[past_rows])
    loads.start("mixed", mixed, m_v)
    loads.start("lse", lse, lse_v)
    if mode is not True:
        loads.start("pend_k", pend_k, dk_v.at[own_rows])
        loads.start("pend_v", pend_v, dv_v.at[own_rows])
    loads.start("qkv", w_qkv, wq_v)
    loads.start("x", x_used, x_v)
    greet_step(1, passing)
    opening.send()
    exchange = Exchange(send_v, recv_v, send_sem, recv_sem)
    across = Across(1, o_v, passed, across_sem)
    stores = []

    def store(buffer, dest):
        copy = pltpu.make_async_copy(buffer, dest, store_sem.at[len(stores)])
        copy.start()
        stores.append(copy)

    def vector(row, start=0, size=None):
        return params[row : row + 1, start : start + (size or width)]

    sum_v[...] = jnp.zeros_like(sum_v)

    def tally(row, piece, start=0):
        place = (slice(row, row + 1), slice(start, start + piece.shape[1]))
        sum_v[place] += jnp.sum(piece, axis=0, keepdims=True)

    loads.wait("proj", "slope", "fc")
    chunk = width // 2
    for tile in range(TILES):
        span = pl.ds(tile * tile_rows, tile_rows)
        opening.take(tile)
        grad = g_v[span, :]
        for part in range(wide // chunk):
            columns = pl.ds(part * chunk, chunk)
            d_act = cols_product(grad, wp_v[columns, :])
            piece = (d_act * sl_v[span, columns].astype(F32)).astype(BF)
            dp_v[span, columns] = piece
            tally(7 + part * chunk // width, piece.astype(F32), part * chunk % width)
        partial = cols_product(dp_v[span, :], wf_v[...])
        part_v[tile] = partial
        exchange.give(tile, partial)
        tally(5, grad.astype(F32))
    store(g_v, g_used)
    store(dp_v, d_pre)
    loads.wait("scaled2", "inverse2", "out")
    for tile in range(TILES):
        span = pl.ds(tile * tile_rows, tile_rows)
        d_normed = part_v[tile] + exchange.take(tile)
        scaled = s2_v[span, :].astype(F32)
        tally(3, d_normed * scaled)
        tally(4, d_normed)
        d_hidden = g_v[span, :].astype(F32) + norm_backward(
            d_normed, scaled, i2_v[span, 0:1], vector(3)
        )
        hid_v[span, :] = d_hidden
        branch = d_hidden.astype(BF)
        db_v[span, :] = branch
        tally(2, branch.astype(F32))
        dm_v[span, :] = cols_product(branch, wo_v[...]).astype(BF)
    store(db_v, d_branch)
    loads.wait("q", "k", "v", "mixed", "lse")
    if mode is not False:
        loads.wait("k_past", "v_past")
    if mode is not True:
        loads.wait("pend_k", "pend_v")

    def attention(past):
        first_key = 0 if past else rows
        if past:
            dk_v[...] = jnp.zeros_like(dk_v)
            dv_v[...] = jnp.zeros_like(dv_v)
        for tile in range(TILES):
            span = pl.ds(tile * tile_rows, tile_rows)
            length = (rows if past else 0) + (tile + 1) * tile_rows
            reach = pl.ds(first_key, length)

            def pair(number, carry):
                lanes = pl.ds(pl.multiple_of(number * 128, 128), 128)
                key, value = k_v[reach, lanes], v_v[reach, lanes]
                grads = dm_v[span, lanes]
                products = jnp.transpose(grads.astype(F32) * m_v[span, lanes].astype(F32))
                queries, grads = head_parts(q_v[span, lanes]), head_parts(grads)
                d_query = []
                d_key = d_value = None
                for head in range(2):
                    take = slice(head * HEAD_DIM, (head + 1) * HEAD_DIM)
                    scaled_query = queries[head] * BF(scale)
                    scores = masked_scores(key, scaled_query, length)
                    weights = jnp.exp(scores - lse_v[number, pl.ds(head, 1), span])
                    d_probs = cols_product(value, grads[head])
                    delta = jnp.sum(products[take], axis=0, keepdims=True)
                    d_scores = (weights * (d_probs - delta)).astype(BF)
                    one = jnp.dot(weights.astype(BF), grads[head], preferred_element_type=F32)
                    two = jnp.dot(d_scores, scaled_query, preferred_element_type=F32)
                    d_value = one if head == 0 else d_value + one
                    d_key = two if head == 0 else d_key + two
                    d_query.append(rows_product(key, d_scores)[take])
                dk_v[reach, lanes] += d_key
                dv_v[reach, lanes] += d_value
                d_query = jnp.transpose(jnp.concatenate(d_query, axis=0) * scale)
                dqkv_v[span, lanes] = d_query.astype(BF)
                return carry

            lax.fori_loop(0, half // 128, pair, 0)

    by_past(mode, attention)
    if mode is not False:
        store(dk_v.at[past_rows], next_k)
        store(dv_v.at[past_rows], next_v)
    loads.wait("qkv", "x")
    for tile in range(TILES):
        span = pl.ds(tile * tile_rows, tile_rows)
        later = pl.ds(rows + tile * tile_rows, tile_rows)
        dqkv_v[span, half : 2 * half] = dk_v[later, :].astype(BF)
        dqkv_v[span, 2 * half :] = dv_v[later, :].astype(BF)
        piece = dqkv_v[span, :]
        partial = cols_product(piece, wq_v[...])
        part_v[TILES + tile] = partial
        exchange.give(TILES + tile, partial)
        tally(6, piece[:, :half].astype(F32))
        tally(6, piece[:, 2 * half :].astype(F32), half)
    store(dqkv_v, d_qkv)
    for tile in range(TILES):
        span = pl.ds(tile * tile_rows, tile_rows)
        scaled, inverse = norm_parts(x_v[span, :].astype(F32))
        d_normed = part_v[TILES + tile] + exchange.take(TILES + tile)
        tally(0, d_normed * scaled)
        tally(1, d_normed)
        d_inputs = hid_v[span, :] + norm_backward(d_normed, scaled, inverse, vector(0))
        o_v[span, :] = d_inputs.astype(BF)
        if passing:
            across.send(tile)
    store(o_v, out)
    store(sum_v, sums)
    for copy in stores:
        copy.wait()
    exchange.finish(2 * TILES)
    opening.finish()
    if passing:
        for tile in range(TILES):
            across.receive(tile)
        across.finish()


def backward_step(mode, passing, grads, inputs, params, weights, kept, pending):
    rows, width = inputs.shape
    half = width // 2
    wide = weights[2].shape[1]
    pairs = half // 128
    tile_rows = rows // TILES
    spot = pl.BlockSpec(memory_space=pl.ANY)
    low = lambda columns: ((rows, columns), BF)
    outs = [
        low(width),
        low(3 * half),
        low(width),
        low(wide),
        low(width),
        ((rows, half), F32),
        ((rows, half), F32),
        ((16, width), F32),
        low(width),
    ]
    scratch = [
        low(width),
        low(width),
        *((item.shape, BF) for item in weights),
        low(half),
        ((2 * rows, half), BF),
        ((2 * rows, half), BF),
        low(half),
        ((pairs, 8, rows), F32),
        low(width),
        ((rows, 128), F32),
        low(wide),
        ((2 * rows, half), F32),
        ((2 * rows, half), F32),
        ((rows, width), F32),
        ((2 * TILES, tile_rows, width), F32),
        ((2 * TILES, tile_rows, width), BF),
        ((2 * TILES, tile_rows, width), BF),
        low(3 * half),
        low(width),
        low(wide),
        low(half),
        low(width),
        ((16, width), F32),
    ]
    number = {True: 6, None: 7, False: 8}[mode]
    return pl.pallas_call(
        functools.partial(backward_kernel, mode, passing),
        out_shape=[jax.ShapeDtypeStruct(*item) for item in outs],
        in_specs=[spot] * 4 + [pl.BlockSpec(memory_space=pltpu.VMEM)] + [spot] * 16,
        out_specs=[spot] * len(outs),
        scratch_shapes=[pltpu.VMEM(*item) for item in scratch]
        + step_sems(BACKWARD_LOADS + 1, len(outs)),
        compiler_params=pltpu.CompilerParams(
            collective_id=number, has_side_effects=True, vmem_limit_bytes=VMEM_LIMIT
        ),
        name="backward_step",
    )(*grads, inputs, params, *weights, *kept, *pending)


def shards(
    tokens,
    cotangent,
    attn_gain,
    attn_shift,
    qkv_weight,
    query_bias,
    value_bias,
    out_weight,
    out_bias,
    mlp_gain,
    mlp_shift,
    fc_weight,
    fc_bias,
    proj_weight,
    proj_bias,
):
    size = lax.axis_size("replica")
    micro = tokens.shape[1]
    assert micro == 2
    *outer, params, w_qkv, w_fc, w_out, w_proj = fetch_inputs(
        tokens[0],
        cotangent[0],
        qkv_weight[0],
        fc_weight[0],
        out_weight[0],
        proj_weight[0],
        (
            attn_gain,
            attn_shift,
            out_bias,
            mlp_gain,
            mlp_shift,
            proj_bias,
            query_bias,
            value_bias,
            fc_bias,
        ),
    )
    weights = (w_qkv, w_out, w_fc, w_proj)

    received, kept_list, outputs, past, got = [], [], [], (w_out, w_out), outer[0]
    for step in range(micro + 1):
        output = outputs[-1] if outputs else outer[0]
        used, normed1, *state, normed2, slope, act, output, got = forward_step(
            (False, None, True)[step],
            step == 1,
            (outer[min(step, micro - 1)], got, output),
            params,
            weights,
            past,
        )
        query, keys, values, mixed, lse, scaled2, inverse2 = state
        outputs.append(output)
        received.append(used)
        kept = (query, keys, values, *past, mixed, lse, scaled2, inverse2, slope)
        kept_list.append((kept, normed1, normed2, act))
        past = (keys, values)

    pending = (params, params)
    grad_received, terms_list, results, tallies, got = [], [], [], [], outer[1]
    for step in range(micro + 1):
        last = micro - step
        kept, normed1, normed2, act = kept_list[last]
        result = results[-1] if results else outer[1]
        grad, d_qkv, d_branch, d_pre, result, *pending, vector, got = backward_step(
            (True, None, False)[step],
            step == 1,
            (got, outer[max(micro - 1 - step, 0)], result),
            received[last],
            params,
            weights,
            kept,
            pending,
        )
        results.append(result)
        grad_received.append(grad)
        tallies.append(vector)
        terms_list.append((normed1, d_qkv, kept[5], d_branch, normed2, d_pre, act, grad))
    def factor(number):
        return tuple(terms_list[step][number] for step in (2, 1, 0))

    factors = [(factor(i), factor(i + 1)) for i in (0, 4, 2, 6)]
    reduced = ring_scatter(factors, tallies, size)
    reduced, packed = reduced[:4], reduced[4]
    near = []
    for i in range(micro):
        near += [outputs[i], outputs[i + 1], received[i + 1]]
        near += [results[micro - i], results[micro - 1 - i], grad_received[micro - i]]
    *gathered, activations, input_grads = ring_gather(reduced, (3, 1), near, size)
    finished = finish(gathered, packed, (activations, input_grads))
    qkv_grad, fc_grad, out_grad, proj_grad = (item[None] for item in finished[:4])
    vectors = finished[4:13]
    activations, input_grads = finished[13:]
    return (
        activations[None, None],
        input_grads[None, None],
        vectors[0],
        vectors[1],
        qkv_grad,
        vectors[6],
        vectors[7],
        out_grad,
        vectors[2],
        vectors[3],
        vectors[4],
        fc_grad,
        vectors[8],
        proj_grad,
        vectors[5],
    )


def solution(mesh):
    block = P("replica", None, "shard", None)
    layers = P("section", "replica", None, "shard", None)
    vector = P("section", "shard")
    matrix = P("section", "shard", None)
    kinds = (
        vector,
        vector,
        matrix,
        vector,
        vector,
        matrix,
        vector,
        vector,
        vector,
        matrix,
        vector,
        matrix,
        vector,
    )
    return jax.shard_map(
        shards,
        mesh=mesh,
        in_specs=(block, block) + kinds,
        out_specs=(layers, layers) + kinds,
        check_vma=False,
    )
```

```python
import functools

import jax
import jax.numpy as jnp
from jax import lax
from jax.experimental import pallas as pl
from jax.experimental.pallas import tpu as pltpu
from jax.sharding import PartitionSpec as P

HEAD_DIM = 64
EPSILON = 1e-05
GELU_SCALE = 0.7978845608028654
GELU_CUBIC = 0.044715
ROWS_CONTRACT = (((0,), (0,)), ((), ()))
COLS_CONTRACT = (((1,), (1,)), ((), ()))
BF = jnp.bfloat16
F32 = jnp.float32
MESH = pl.DeviceIdType.MESH
QTILE = 256
VMEM_LIMIT = 56 * 1024 * 1024


def rows_product(left, right):
    return lax.dot_general(left, right, ROWS_CONTRACT, preferred_element_type=F32)


def cols_product(left, right):
    return lax.dot_general(left, right, COLS_CONTRACT, preferred_element_type=F32)


def norm_parts(inputs):
    mean = jnp.mean(inputs, axis=-1, keepdims=True)
    centered = inputs - mean
    inverse = lax.rsqrt(jnp.mean(centered * centered, axis=-1, keepdims=True) + EPSILON)
    return centered * inverse, inverse


def norm_backward(d_normed, scaled, inverse, gain):
    d_scaled = d_normed * gain
    return inverse * (
        d_scaled
        - jnp.mean(d_scaled, axis=-1, keepdims=True)
        - scaled * jnp.mean(d_scaled * scaled, axis=-1, keepdims=True)
    )


def gelu_pair(pre):
    tangent = jnp.tanh(GELU_SCALE * (pre + GELU_CUBIC * pre * pre * pre))
    value = 0.5 * pre * (1.0 + tangent)
    slope = 0.5 * (1.0 + tangent) + 0.5 * pre * (1.0 - tangent * tangent) * GELU_SCALE * (
        1.0 + 3.0 * GELU_CUBIC * pre * pre
    )
    return value, slope


def head_parts(pair):
    low = lax.broadcasted_iota(jnp.int32, pair.shape, 1) < HEAD_DIM
    zero = jnp.zeros_like(pair)
    return jnp.where(low, pair, zero), jnp.where(low, zero, pair)


def masked_scores(keys, query, length):
    scores = cols_product(keys, query)
    tail = scores[length - QTILE :]
    key_pos = lax.broadcasted_iota(jnp.int32, tail.shape, 0)
    query_pos = lax.broadcasted_iota(jnp.int32, tail.shape, 1)
    tail = jnp.where(key_pos <= query_pos, tail, -1e30)
    if length == QTILE:
        return tail
    return jnp.concatenate([scores[: length - QTILE], tail], axis=0)


def ring_place(size):
    index = lax.axis_index("replica")
    odd = index % 2
    half = index // 2
    place = (1 - odd) * half + odd * (size - 1 - half)

    def device(spot):
        upper = spot // (size // 2)
        return (1 - upper) * (2 * spot) + upper * (2 * (size - 1 - spot) + 1)

    return place, device((place + 1) % size), device((place + size - 1) % size)


def neighbours():
    core, layer = lax.axis_index("section"), lax.axis_index("shard")
    sibling = {"section": 1 - core}
    across = {"shard": 1 - layer}
    diagonal = {"section": 1 - core, "shard": 1 - layer}
    return core, layer, sibling, across, diagonal


def greet(devices):
    barrier = pltpu.get_barrier_semaphore()
    for device in devices:
        pl.semaphore_signal(barrier, inc=1, device_id=device, device_id_type=MESH)
    pl.semaphore_wait(barrier, len(devices))


def scatter_kernel(size, count, *refs):
    sources, refs = refs[: 6 * count], refs[6 * count :]
    tallies, refs = refs[:3], refs[3:]
    out, refs = refs[:count], refs[count:]
    packed, refs = refs[0], refs[1:]
    held, refs = refs[: 2 * count], refs[2 * count :]
    own, refs = refs[:count], refs[count:]
    landed, refs = refs[:count], refs[count:]
    load_sem, send_sem, recv_sem, small_send, small_recv, swap_sem, total, small, small_out = refs
    place, following, previous = ring_place(size)
    targets = ({"replica": following}, {"replica": previous})
    core, layer, _, _, diagonal = neighbours()

    def load(number, which):
        rows = held[number].shape[0] // 2
        source = sources[3 * number + which]
        part = pl.ds(0 if which == 1 else rows, rows)
        return pltpu.make_async_copy(
            source, held[number].at[part], load_sem.at[number, 0 if which == 1 else 1]
        )

    for number in range(2 * count):
        load(number, 1).start()

        @pl.when(layer == 0)
        def _(number=number):
            load(number, 0).start()

        @pl.when(layer != 0)
        def _(number=number):
            load(number, 2).start()

    greet(targets + (diagonal,))

    def send(way, item, source, slot):
        return pltpu.make_async_remote_copy(
            src_ref=source,
            dst_ref=landed[item].at[way, slot],
            send_sem=send_sem.at[way, item, slot],
            recv_sem=recv_sem.at[way, item, slot],
            device_id=targets[way],
            device_id_type=MESH,
        )

    def send_small(chunk, slot):
        return pltpu.make_async_remote_copy(
            src_ref=small_out.at[chunk],
            dst_ref=small_out.at[chunk],
            send_sem=small_send.at[slot],
            recv_sem=small_recv.at[slot],
            device_id=targets[0],
            device_id_type=MESH,
        )

    def chunk_of(way, slot):
        if way == 0:
            return (place + 2 * size - 2 - slot) % size
        return (place + 2 + slot) % size

    first = ((place + size - 1) % size, (place + 1) % size)
    group = size // 2

    def product(item, way, part):
        deep = own[item].shape[2]
        columns = pl.multiple_of((way * size + part * group) * deep, 128)
        left = held[2 * item][:, pl.ds(columns, group * deep)]
        result = rows_product(left, held[2 * item + 1][...])
        for index in range(group):
            own[item][way, part * group + index] = result[index * deep : (index + 1) * deep].astype(BF)

    half = small.shape[1]

    @pl.when(layer == 0)
    def _():
        total[...] = tallies[1][...] + tallies[2][...]

    @pl.when(layer != 0)
    def _():
        total[...] = tallies[0][...] + tallies[1][...]

    small[...] = jnp.zeros_like(small)
    small[0:6, :] = total[0:6, pl.ds(pl.multiple_of(core * half, half), half)]
    for row in range(3):
        for side in range(2):
            line = 6 + 2 * row + side
            small[line : line + 1, :] = total[6 + row : 7 + row, side * half : (side + 1) * half]

    def swap():
        return pltpu.make_async_remote_copy(
            src_ref=small,
            dst_ref=small_out.at[place],
            send_sem=swap_sem.at[0],
            recv_sem=swap_sem.at[1],
            device_id=diagonal,
            device_id_type=MESH,
        )

    @pl.when(core == layer)
    def _():
        small_out[place] = small[...]

    @pl.when(core != layer)
    def _():
        swap().start()

    for item in range(count):
        for number in (2 * item, 2 * item + 1):
            load(number, 1).wait()
            load(number, 0).wait()
        for way in range(2):
            product(item, way, first[way] // group)
            send(way, item, own[item].at[way, first[way]], 0).start()

    @pl.when(core != layer)
    def _():
        swap().wait()

    send_small(place, 0).start()
    for item in range(count):
        for way in range(2):
            product(item, way, 1 - first[way] // group)

    def step(slot, carry):
        for item in range(count):
            for way in range(2):
                here = landed[item].at[way, slot]
                send(way, item, here, slot).wait_recv()
                here[...] += own[item][way, chunk_of(way, slot)]
                send(way, item, here, slot + 1).start()
        chunk = (place + size - 1 - slot) % size
        send_small(chunk, slot).wait_recv()
        send_small(chunk, slot + 1).start()
        return carry

    lax.fori_loop(0, size - 2, step, 0)
    last = size - 2
    for item in range(count):
        for way in range(2):
            here = landed[item].at[way, last]
            send(way, item, here, last).wait_recv()
            out[item][way] = here[...] + own[item][way, place]
    send_small((place + 1) % size, last).wait_recv()
    gathered = small_out[0]
    for index in range(1, size):
        gathered = gathered + small_out[index]
    packed[...] = gathered

    def finish(slot, carry):
        for item in range(count):
            for way in range(2):
                send(way, item, landed[item].at[way, slot], slot).wait_send()
        send_small(place, slot).wait_send()
        return carry

    lax.fori_loop(0, size - 1, finish, 0)


def ring_scatter(factors, tallies, size):
    count = len(factors)
    flat = [item for pair in factors for item in pair]
    half = tallies[0].shape[1] // 2
    shapes = [(2 * item[0].shape[0], item[0].shape[1]) for item in flat]
    chunks = [
        (shapes[2 * i][1] // (2 * size), shapes[2 * i + 1][1]) for i in range(count)
    ]
    whole = pl.BlockSpec(memory_space=pltpu.VMEM)
    spot = pl.BlockSpec(memory_space=pl.ANY)
    return pl.pallas_call(
        functools.partial(scatter_kernel, size, count),
        out_shape=[jax.ShapeDtypeStruct((2,) + chunk, BF) for chunk in chunks]
        + [jax.ShapeDtypeStruct((16, half), F32)],
        in_specs=[spot] * (6 * count) + [whole] * 3,
        out_specs=[whole] * (count + 1),
        scratch_shapes=[pltpu.VMEM(shape, BF) for shape in shapes]
        + [pltpu.VMEM((2, size) + chunk, BF) for chunk in chunks]
        + [pltpu.VMEM((2, size - 1) + chunk, BF) for chunk in chunks]
        + [pltpu.SemaphoreType.DMA((2 * count, 2))]
        + [pltpu.SemaphoreType.DMA((2, count, size - 1))] * 2
        + [pltpu.SemaphoreType.DMA((size - 1,))] * 2
        + [pltpu.SemaphoreType.DMA((2,))]
        + [
            pltpu.VMEM((16, 2 * half), F32),
            pltpu.VMEM((16, half), F32),
            pltpu.VMEM((size, 16, half), F32),
        ],
        compiler_params=pltpu.CompilerParams(
            collective_id=0, has_side_effects=True, vmem_limit_bytes=VMEM_LIMIT
        ),
        name="ring_scatter",
    )(*[block for item in flat for block in item], *tallies)


def gather_kernel(size, groups, *refs):
    count = 4
    own, refs = refs[:count], refs[count:]
    near, refs = refs[:12], refs[12:]
    out, refs = refs[:count], refs[count:]
    placed, refs = refs[:2], refs[2:]
    swap_send, swap_recv, send_sem, recv_sem, place_send, place_recv, load_sem, bounce = refs
    place, following, previous = ring_place(size)
    targets = ({"replica": following}, {"replica": previous})
    core, layer, sibling, across, diagonal = neighbours()
    same = core == layer
    greet(targets + (sibling, across, diagonal))

    def parts(item, source_half, sender):
        if item < len(groups):
            width = own[item].shape[2] // groups[item]
            for group in range(groups[item]):
                start = pl.multiple_of((2 * group + sender) * width, width)
                yield (
                    own[item].at[source_half, :, pl.ds(group * width, width)],
                    out[item].at[place, :, pl.ds(start, width)],
                )
        else:
            for half in range(2):
                yield own[item].at[half], out[item].at[half, place]

    def copies(item, source_half, lane, kind, device=None):
        for number, (source, target) in enumerate(parts(item, source_half, core)):
            send, recv = swap_send.at[item, lane, number], swap_recv.at[item, kind, number]
            if device is None:
                yield pltpu.make_async_copy(source, target, recv)
            else:
                yield pltpu.make_async_remote_copy(
                    src_ref=source,
                    dst_ref=target,
                    send_sem=send,
                    recv_sem=recv,
                    device_id=device,
                    device_id_type=MESH,
                )

    @pl.when(same)
    def _():
        for item in range(count):
            for copy in copies(item, layer, 0, 0):
                copy.start()
            if item < len(groups):
                for copy in copies(item, 1 - layer, 0, 2, across):
                    copy.start()

    @pl.when(core != layer)
    def _():
        for item in range(count):
            for copy in copies(item, 1 - layer, 0, 3, diagonal):
                copy.start()
            if item < len(groups):
                for copy in copies(item, layer, 1, 1, sibling):
                    copy.start()

    part = placed[0].shape[1]

    def near_rows(number, block, shard):
        return near[6 * block + number].at[pl.ds(shard * part, part)]

    def place_remote(kind, block):
        number, shard = ((1, 0), (3, 1))[kind]
        return pltpu.make_async_remote_copy(
            src_ref=near_rows(number, block, shard),
            dst_ref=placed[kind].at[block],
            send_sem=place_send.at[block],
            recv_sem=place_recv.at[block],
            device_id=across,
            device_id_type=MESH,
        )

    def place_load(number, block, shard):
        lane = 2 * (number // 3) + block
        return pltpu.make_async_copy(near_rows(number, block, shard), bounce.at[lane], load_sem.at[lane])

    def place_store(number, block):
        kind = number // 3
        lane = 2 * kind + block
        return pltpu.make_async_copy(bounce.at[lane], placed[kind].at[block], load_sem.at[lane])

    local = {(0, 0): (0, 3), (0, 1): (2,), (1, 0): (5,), (1, 1): (1, 4)}

    def on_device(action):
        for (at_core, at_layer), numbers in local.items():

            @pl.when((core == at_core) & (layer == at_layer))
            def _(numbers=numbers, at_layer=at_layer):
                for number in numbers:
                    for block in range(2):
                        action(number, block, at_layer)

    @pl.when(same & (layer == 1))
    def _():
        for block in range(2):
            place_remote(0, block).start()

    @pl.when(same & (layer == 0))
    def _():
        for block in range(2):
            place_remote(1, block).start()

    on_device(lambda number, block, shard: place_load(number, block, shard).start())

    def send(way, item, chunk, slot):
        if item < len(groups):
            deep = out[item].shape[1] // 2
            here = out[item].at[chunk, pl.ds(way * deep, deep)]
        else:
            here = out[item].at[way, chunk]
        return pltpu.make_async_remote_copy(
            src_ref=here,
            dst_ref=here,
            send_sem=send_sem.at[way, item, slot],
            recv_sem=recv_sem.at[way, item, slot],
            device_id=targets[way],
            device_id_type=MESH,
        )

    def chunk_of(way, slot):
        if way == 0:
            return (place + size - 1 - slot) % size
        return (place + 1 + slot) % size

    for item in range(count):

        @pl.when(same)
        def _(item=item):
            for copy in copies(item, layer, 0, 0):
                copy.wait()
            if item < len(groups):
                for copy in copies(item, layer, 1, 1, sibling):
                    copy.wait_recv()

        @pl.when(core != layer)
        def _(item=item):
            for copy in copies(item, layer, 0, 3, diagonal):
                copy.wait_recv()
            if item < len(groups):
                for copy in copies(item, layer, 0, 2, across):
                    copy.wait_recv()

        for way in range(2):
            send(way, item, place, 0).start()

    def step(slot, carry):
        for item in range(count):
            for way in range(2):
                chunk = chunk_of(way, slot)
                send(way, item, chunk, slot).wait_recv()
                send(way, item, chunk, slot + 1).start()
        return carry

    def moved(number, block, shard):
        place_load(number, block, shard).wait()
        place_store(number, block).start()

    on_device(moved)
    lax.fori_loop(0, size - 2, step, 0)
    last = size - 2
    for item in range(count):
        for way in range(2):
            send(way, item, chunk_of(way, last), last).wait_recv()
    on_device(lambda number, block, shard: place_store(number, block).wait())

    @pl.when(same)
    def _():
        for block in range(2):
            place_remote(0, block).wait_send()

    @pl.when((core != layer) & (layer == 0))
    def _():
        for block in range(2):
            place_remote(0, block).wait_recv()

    @pl.when((core != layer) & (layer == 1))
    def _():
        for block in range(2):
            place_remote(1, block).wait_recv()

    @pl.when(same)
    def _():
        for item in range(len(groups)):
            for copy in copies(item, 1 - layer, 0, 2, across):
                copy.wait_send()

    @pl.when(core != layer)
    def _():
        for item in range(count):
            for copy in copies(item, 1 - layer, 0, 3, diagonal):
                copy.wait_send()
            if item < len(groups):
                for copy in copies(item, layer, 1, 1, sibling):
                    copy.wait_send()

    def finish(slot, carry):
        for item in range(count):
            for way in range(2):
                send(way, item, place, slot).wait_send()
        return carry

    lax.fori_loop(0, size - 1, finish, 0)


def ring_gather(pieces, groups, near, size):
    spot = pl.BlockSpec(memory_space=pl.ANY)
    shapes = [(size, item.shape[1], 2 * item.shape[2]) for item in pieces[: len(groups)]]
    shapes += [(2, size) + item.shape[1:] for item in pieces[len(groups) :]]
    count = len(pieces)
    rows = (near[0].shape[0] // 2, near[0].shape[1])
    whole = pl.BlockSpec(memory_space=pltpu.VMEM)
    return pl.pallas_call(
        functools.partial(gather_kernel, size, groups),
        out_shape=[jax.ShapeDtypeStruct(shape, BF) for shape in shapes]
        + [jax.ShapeDtypeStruct((2,) + rows, BF)] * 2,
        in_specs=[whole] * count + [spot] * 12,
        out_specs=[spot] * (count + 2),
        scratch_shapes=[
            pltpu.SemaphoreType.DMA((count, 2, 3)),
            pltpu.SemaphoreType.DMA((count, 4, 3)),
        ]
        + [pltpu.SemaphoreType.DMA((2, count, size - 1))] * 2
        + [pltpu.SemaphoreType.DMA((2,))] * 2
        + [pltpu.SemaphoreType.DMA((4,)), pltpu.VMEM((4,) + rows, BF)],
        compiler_params=pltpu.CompilerParams(
            collective_id=1, has_side_effects=True, vmem_limit_bytes=VMEM_LIMIT
        ),
        name="ring_gather",
    )(*pieces, *near)


def finish_kernel(*refs):
    gathered, packed, placed = refs[:4], refs[4], refs[5:7]
    wide, vectors, moved = refs[7:11], refs[11:20], refs[20:22]
    low, high, bounce = refs[22:26], refs[26:30], refs[30]
    fetch_sem, store_sem, load_sem = refs[31:]

    def fetch(item, chunk):
        return pltpu.make_async_copy(
            gathered[item].at[chunk], low[item].at[chunk], fetch_sem.at[item, chunk]
        )

    def store(item, chunk):
        deep = low[item].shape[1]
        place = pl.ds(pl.multiple_of(chunk * deep, deep), deep)
        return pltpu.make_async_copy(
            high[item].at[chunk], wide[item].at[place], store_sem.at[item, chunk]
        )

    def every(action):
        for item in range(4):

            def step(chunk, carry, item=item):
                action(item, chunk)
                return carry

            lax.fori_loop(0, low[item].shape[0], step, 0)

    def widen(item, chunk):
        fetch(item, chunk).wait()
        high[item][chunk] = low[item][chunk].astype(F32)
        store(item, chunk).start()

    every(lambda item, chunk: fetch(item, chunk).start())
    loads = [pltpu.make_async_copy(placed[i], bounce.at[i], load_sem.at[i]) for i in range(2)]
    for copy in loads:
        copy.start()
    half = packed.shape[1]
    for number in range(9):
        for index in range(vectors[number].shape[1] // half):
            row = number + index
            vectors[number][:, index * half : (index + 1) * half] = packed[row : row + 1, :]
    every(widen)
    stores = []
    for i in range(2):
        loads[i].wait()
        copy = pltpu.make_async_copy(bounce.at[i], moved[i], load_sem.at[i])
        copy.start()
        stores.append(copy)
    every(lambda item, chunk: store(item, chunk).wait())
    for copy in stores:
        copy.wait()


def finish(gathered, packed, placed):
    spot = pl.BlockSpec(memory_space=pl.ANY)
    whole = pl.BlockSpec(memory_space=pltpu.VMEM)
    gathered = [item.reshape((-1,) + item.shape[-2:]) for item in gathered]
    half = packed.shape[1]
    most = max(item.shape[0] for item in gathered)
    return pl.pallas_call(
        finish_kernel,
        out_shape=[
            jax.ShapeDtypeStruct((item.shape[0] * item.shape[1], item.shape[2]), F32)
            for item in gathered
        ]
        + [jax.ShapeDtypeStruct((1, half), F32)] * 8
        + [jax.ShapeDtypeStruct((1, 4 * half), F32)]
        + [jax.ShapeDtypeStruct(item.shape, BF) for item in placed],
        in_specs=[spot] * 4 + [whole] + [spot] * 2,
        out_specs=[spot] * 4 + [whole] * 9 + [spot] * 2,
        scratch_shapes=[pltpu.VMEM(item.shape, BF) for item in gathered]
        + [pltpu.VMEM(item.shape, F32) for item in gathered]
        + [
            pltpu.VMEM((2,) + placed[0].shape, BF),
            pltpu.SemaphoreType.DMA((4, most)),
            pltpu.SemaphoreType.DMA((4, most)),
            pltpu.SemaphoreType.DMA((2,)),
        ],
        compiler_params=pltpu.CompilerParams(vmem_limit_bytes=VMEM_LIMIT),
        name="finish",
    )(*gathered, packed, *placed)


def fetch_kernel(*refs):
    tokens, cotangent, qkv, fc, out, proj = refs[:6]
    vectors, refs = refs[6:15], refs[15:]
    *outer, params, w_qkv, w_fc, w_out, w_proj = refs[:7]
    send_sem, recv_sem, extra_send, extra_recv, local_sem, vector_sem = refs[7:13]
    raw, small, small_out = refs[13:22], refs[22], refs[23]
    buffers = refs[24:]
    core, layer, sibling, across, diagonal = neighbours()
    index = lax.axis_index("replica")
    quarter = index % 4
    low, high = index % 2, (index // 2) % 2
    beside = {"replica": index + 1 - 2 * low}
    above = {"replica": index + 2 - 4 * high}
    beside_quarter = quarter + 1 - 2 * low
    above_quarter = quarter + 2 - 4 * high
    same = core == layer
    far_quarter = 3 - quarter
    for number in range(9):
        pltpu.make_async_copy(vectors[number], raw[number], vector_sem.at[number]).start()
    greet((sibling, across, diagonal, beside, above))

    depth = qkv.shape[0]
    span = qkv.shape[1] // 6
    wide = fc.shape[1] // 2
    turn = proj.shape[0] // 2
    cols = [
        (qkv, w_qkv, lambda s, g=g: pl.multiple_of((2 * g + s) * span, span), g * span, span)
        for g in range(3)
    ]
    cols.append((fc, w_fc, lambda s: pl.multiple_of(s * wide, wide), 0, wide))
    rows = [(out, w_out, 0, out.shape[0]), (proj, w_proj, 0, turn), (proj, w_proj, turn, turn)]
    order = [0, 1, 2, 4, 3, 5, 6]

    def rows_of(item):
        return depth if item < 4 else rows[item - 4][3]

    def target(item, base, which, part=None):
        deep = rows_of(item) // 4
        start = base + which * deep
        if part is not None:
            deep = deep // 2
            start = start + part * deep
        place = pl.ds(pl.multiple_of(start, deep), deep)
        if item < 4:
            return cols[item][1].at[place, pl.ds(cols[item][3], cols[item][4])]
        return rows[item - 4][1].at[place]

    def base_of(item, shard):
        return shard * depth if item < 4 else rows[item - 4][2]

    def remote(stage, item, source, dest, device, lane=0):
        return pltpu.make_async_remote_copy(
            src_ref=source,
            dst_ref=dest,
            send_sem=send_sem.at[stage + lane, item],
            recv_sem=recv_sem.at[stage, item],
            device_id=device,
            device_id_type=MESH,
        )

    def cross(item, receiver):
        deep = rows_of(item) // 4
        place = pl.multiple_of(base_of(item, 0) + quarter * deep, deep)
        dest = target(item, base_of(item, layer), quarter)
        if item < 4:
            columns = cols[item][2](receiver)
            source = cols[item][0].at[pl.ds(place, deep), pl.ds(columns, cols[item][4])]
        else:
            source = rows[item - 4][0].at[pl.ds(place, deep)]
        return source, dest

    def cross_same(item):
        return remote(0, item, *cross(item, core), across, 5)

    def cross_swap(item):
        return remote(0, item, *cross(item, 1 - core), diagonal)

    def pass_on(stage, item, which, device, part=None):
        here = target(item, base_of(item, 1 - layer), which, part)
        return remote(stage, item, here, here, device)

    def to_sibling(item):
        columns = cols[item][2](1 - core)
        source = cols[item][0].at[:, pl.ds(columns, cols[item][4])]
        start = pl.multiple_of(layer * depth, depth)
        dest = cols[item][1].at[pl.ds(start, depth), pl.ds(cols[item][3], cols[item][4])]
        return remote(6, item, source, dest, sibling)

    def through(source, dest, number):
        return (
            lambda: pltpu.make_async_copy(source, buffers[number], local_sem.at[number]),
            lambda: pltpu.make_async_copy(buffers[number], dest, local_sem.at[number]),
        )

    def keep_local(item):
        if item < 4:
            columns = cols[item][2](core)
            source = cols[item][0].at[:, pl.ds(columns, cols[item][4])]
            start = pl.multiple_of(layer * depth, depth)
            dest = cols[item][1].at[pl.ds(start, depth), pl.ds(cols[item][3], cols[item][4])]
        else:
            source, dest, start, deep = rows[item - 4]
            source, dest = source.at[pl.ds(start, deep)], dest.at[pl.ds(start, deep)]
        return through(source, dest, item)

    part = tokens.shape[1]
    half = part // 2

    def outer_rows(shard, which):
        return pl.ds(pl.multiple_of(shard * part + which * half, half), half)

    def outer_cross(block):
        place = pl.ds(pl.multiple_of(core * half, half), half)

        def copy(source):
            return pltpu.make_async_remote_copy(
                src_ref=source.at[block, place],
                dst_ref=outer[block].at[outer_rows(layer, core)],
                send_sem=extra_send.at[block],
                recv_sem=extra_recv.at[block],
                device_id=across,
                device_id_type=MESH,
            )

        return copy

    def outer_pass(block):
        here = outer[block].at[outer_rows(1 - layer, core)]
        return pltpu.make_async_remote_copy(
            src_ref=here,
            dst_ref=here,
            send_sem=extra_send.at[2 + block],
            recv_sem=extra_recv.at[2 + block],
            device_id=sibling,
            device_id_type=MESH,
        )

    def outer_local(source, block):
        place = pl.ds(pl.multiple_of(layer * part, part), part)
        return through(source.at[block], outer[block].at[place], 7 + block)

    def small_swap():
        return pltpu.make_async_remote_copy(
            src_ref=small,
            dst_ref=small_out.at[1 - core],
            send_sem=extra_send.at[4],
            recv_sem=extra_recv.at[4],
            device_id=diagonal,
            device_id_type=MESH,
        )

    def small_pass():
        return pltpu.make_async_remote_copy(
            src_ref=small_out.at[core],
            dst_ref=small_out.at[core],
            send_sem=extra_send.at[5],
            recv_sem=extra_recv.at[5],
            device_id=sibling,
            device_id_type=MESH,
        )

    def start_outer(block):
        @pl.when(layer == 0)
        def _():
            outer_cross(block)(cotangent).start()

        @pl.when(layer == 1)
        def _():
            outer_cross(block)(tokens).start()

    def crossings(item):
        if item < 4:
            cross_same(item).start()
        cross_swap(item).start()

    start_outer(0)

    @pl.when(core != layer)
    def _():
        crossings(order[0])
        crossings(order[1])
        crossings(order[2])

    @pl.when(layer == 0)
    def _():
        for block in range(2):
            outer_local(tokens, block)[0]().start()

    @pl.when(layer == 1)
    def _():
        for block in range(2):
            outer_local(cotangent, block)[0]().start()

    @pl.when(same)
    def _():
        for item in range(4):
            to_sibling(item).start()

    span_small = small.shape[1]
    for number in range(9):
        pltpu.make_async_copy(vectors[number], raw[number], vector_sem.at[number]).wait()
        values = raw[number][...].astype(F32)
        for index in range(values.shape[1] // span_small):
            row = number + index
            small[row : row + 1, :] = values[:, index * span_small : (index + 1) * span_small]

    @pl.when(same)
    def _():
        small_out[core] = small[...]

    @pl.when(core != layer)
    def _():
        small_swap().start()
        small_swap().wait_recv()

    small_pass().start()
    for block in range(2):
        load, store = outer_local(tokens, block)
        load().wait()
        store().start()

    @pl.when(same)
    def _():
        for item in range(7):
            keep_local(item)[0]().start()

    def relay(sequence, ahead):
        def onward(item):
            pass_on(1, item, beside_quarter, beside).wait_recv()
            pass_on(4, item, beside_quarter, above, 0).start()
            pass_on(2, item, above_quarter, above).wait_recv()
            pass_on(3, item, above_quarter, beside, 1).start()

        for number, item in enumerate(sequence):
            pass_on(0, item, quarter, beside).wait_recv()
            if ahead and number + 3 < len(sequence):
                crossings(sequence[number + 3])
            pass_on(1, item, quarter, beside).start()
            pass_on(2, item, quarter, above).start()
            if number >= 1:
                onward(sequence[number - 1])
            if number == 0:
                outer_cross(0)(tokens).wait_recv()
                outer_pass(0).start()
            if number == len(sequence) - 2:
                start_outer(1)
        onward(sequence[-1])
        for item in sequence:
            pass_on(3, item, far_quarter, beside, 1).wait_recv()
            pass_on(4, item, far_quarter, above, 0).wait_recv()
            for stage in (1, 2):
                pass_on(stage, item, quarter, beside).wait_send()
            for stage, which in ((3, 1), (4, 0)):
                pass_on(stage, item, quarter, beside, which).wait_send()

    @pl.when(same)
    def _():
        for item in range(7):
            load, store = keep_local(item)
            load().wait()
            store().start()
        relay([0, 1, 2, 3], False)
        for item in range(4):
            to_sibling(item).wait_send()
        for item in range(7):
            keep_local(item)[1]().wait()

    @pl.when(core != layer)
    def _():
        relay(order, True)
        for item in range(4):
            to_sibling(item).wait_recv()
            cross_same(item).wait_send()
        for item in range(7):
            cross_swap(item).wait_send()
        small_swap().wait_send()

    outer_cross(1)(tokens).wait_recv()
    outer_pass(1).start()
    for block in range(2):
        outer_local(tokens, block)[1]().wait()
    small_pass().wait()
    params[...] = jnp.zeros_like(params)
    for side in range(2):
        lanes = slice(side * span_small, (side + 1) * span_small)
        params[0:6, lanes] = small_out[side, 0:6]
        for row in range(3):
            line = 6 + 2 * row + side
            params[6 + row : 7 + row, lanes] = small_out[core, line : line + 1]
    for block in range(2):
        outer_cross(block)(tokens).wait_send()
        outer_pass(block).wait()


def fetch_inputs(tokens, cotangent, qkv, fc, out, proj, vectors):
    spot = pl.BlockSpec(memory_space=pl.ANY)
    _, part, width = tokens.shape
    shapes = [
        (2 * part, width),
        (2 * part, width),
        (2 * qkv.shape[0], qkv.shape[1] // 2),
        (2 * fc.shape[0], fc.shape[1] // 2),
        out.shape,
        proj.shape,
    ]
    return pl.pallas_call(
        fetch_kernel,
        out_shape=[jax.ShapeDtypeStruct(shape, BF) for shape in shapes[:2]]
        + [jax.ShapeDtypeStruct((16, width), F32)]
        + [jax.ShapeDtypeStruct(shape, BF) for shape in shapes[2:]],
        in_specs=[spot] * 15,
        out_specs=[spot] * 2 + [pl.BlockSpec(memory_space=pltpu.VMEM)] + [spot] * 4,
        scratch_shapes=[
            pltpu.SemaphoreType.DMA((7, 7)),
            pltpu.SemaphoreType.DMA((7, 7)),
            pltpu.SemaphoreType.DMA((6,)),
            pltpu.SemaphoreType.DMA((6,)),
            pltpu.SemaphoreType.DMA((9,)),
            pltpu.SemaphoreType.DMA((9,)),
        ]
        + [pltpu.VMEM(item.shape, BF) for item in vectors]
        + [pltpu.VMEM((16, width // 2), F32), pltpu.VMEM((2, 16, width // 2), F32)]
        + [pltpu.VMEM((qkv.shape[0], qkv.shape[1] // 6), BF)] * 3
        + [
            pltpu.VMEM((fc.shape[0], fc.shape[1] // 2), BF),
            pltpu.VMEM(out.shape, BF),
            pltpu.VMEM((proj.shape[0] // 2, width), BF),
            pltpu.VMEM((proj.shape[0] // 2, width), BF),
            pltpu.VMEM(tokens.shape[1:], BF),
            pltpu.VMEM(tokens.shape[1:], BF),
        ],
        compiler_params=pltpu.CompilerParams(
            collective_id=2, has_side_effects=True, vmem_limit_bytes=VMEM_LIMIT
        ),
        name="fetch_inputs",
    )(tokens, cotangent, qkv, fc, out, proj, *vectors)


TILES = 2


class Loads:
    def __init__(self, sem):
        self.sem, self.count, self.made = sem, 0, {}

    def start(self, name, source, buffer):
        copy = pltpu.make_async_copy(source, buffer, self.sem.at[self.count])
        self.count += 1
        copy.start()
        self.made[name] = copy

    def wait(self, *names):
        for name in names:
            self.made.pop(name).wait()


def greet_step(sender, passing):
    core, layer, sibling, across, _ = neighbours()
    barrier = pltpu.get_barrier_semaphore()
    pl.semaphore_signal(barrier, inc=1, device_id=sibling, device_id_type=MESH)
    if not passing:
        pl.semaphore_wait(barrier, 1)
        return

    @pl.when(layer != sender)
    def _():
        pl.semaphore_signal(barrier, inc=1, device_id=across, device_id_type=MESH)
        pl.semaphore_wait(barrier, 1)

    @pl.when(layer == sender)
    def _():
        pl.semaphore_wait(barrier, 2)


class Exchange:
    def __init__(self, send_buf, recv_buf, send_sem, recv_sem):
        self.refs = (send_buf, recv_buf, send_sem, recv_sem)

    def copy(self, slot):
        send_buf, recv_buf, send_sem, recv_sem = self.refs
        return pltpu.make_async_remote_copy(
            src_ref=send_buf.at[slot],
            dst_ref=recv_buf.at[slot],
            send_sem=send_sem.at[slot],
            recv_sem=recv_sem.at[slot],
            device_id={"section": 1 - lax.axis_index("section")},
            device_id_type=MESH,
        )

    def give(self, slot, partial):
        self.refs[0][slot] = partial.astype(BF)
        self.copy(slot).start()

    def take(self, slot):
        self.copy(slot).wait_recv()
        return self.refs[1][slot].astype(F32)

    def finish(self, count):
        for slot in range(count):
            self.copy(slot).wait_send()


class Across:
    def __init__(self, sender, source, dest, sems):
        self.sender, self.source, self.dest, self.sems = sender, source, dest, sems
        self.core, self.layer, self.sibling, self.across, _ = neighbours()

    def copy(self, tile, stage):
        rows = self.dest.shape[0] // (2 * TILES)
        place = pl.ds(pl.multiple_of((2 * tile + self.core) * rows, rows), rows)
        source = self.source if stage == 0 else self.dest
        return pltpu.make_async_remote_copy(
            src_ref=source.at[place],
            dst_ref=self.dest.at[place],
            send_sem=self.sems.at[stage, tile],
            recv_sem=self.sems.at[2 + stage, tile],
            device_id=self.across if stage == 0 else self.sibling,
            device_id_type=MESH,
        )

    def send(self, tile):
        @pl.when(self.layer == self.sender)
        def _():
            self.copy(tile, 0).start()

    def receive(self, tile):
        @pl.when(self.layer != self.sender)
        def _():
            self.copy(tile, 0).wait_recv()
            self.copy(tile, 1).start()
            self.copy(tile, 1).wait_recv()

    def finish(self):
        @pl.when(self.layer == self.sender)
        def _():
            for tile in range(TILES):
                self.copy(tile, 0).wait_send()

        @pl.when(self.layer != self.sender)
        def _():
            for tile in range(TILES):
                self.copy(tile, 1).wait_send()


class Opening:
    def __init__(self, passing, sender, first_ref, other_ref, earlier, buffer, sem, sems):
        self.passing, self.sender, self.layer = passing, sender, lax.axis_index("shard")
        self.load = lambda ref: pltpu.make_async_copy(ref, buffer, sem)
        self.refs = (first_ref, other_ref)
        self.across = Across(sender, earlier, buffer, sems)

    def start(self):
        for layer, ref in enumerate(self.refs):
            if self.passing and layer != self.sender:
                continue

            @pl.when(self.layer == layer)
            def _(ref=ref):
                self.load(ref).start()

    def send(self):
        if self.passing:
            for tile in range(TILES):
                self.across.send(tile)

    def take(self, tile):
        if self.passing:
            if tile == 0:

                @pl.when(self.layer == self.sender)
                def _():
                    self.load(self.refs[0]).wait()

            self.across.receive(tile)
        elif tile == 0:
            self.load(self.refs[0]).wait()

    def finish(self):
        if self.passing:
            self.across.finish()


def by_past(mode, body):
    if mode is not None:
        body(mode)
        return
    layer = lax.axis_index("shard")

    @pl.when(layer == 0)
    def _():
        body(True)

    @pl.when(layer != 0)
    def _():
        body(False)


FORWARD_LOADS = 7


def forward_kernel(mode, passing, *refs):
    x_first, x_other, earlier, params, w_qkv, w_out, w_fc, w_proj, k_past, v_past = refs[:10]
    refs = refs[10:]
    (x_used, normed1, query, keys, values, mixed, lse, scaled2, inverse2, normed2, slope, act, out, passed) = refs[:14]
    refs = refs[14:]
    (x_v, wq_v, wo_v, wf_v, wp_v, k_v, v_v, hid_v, part_v, send_v, recv_v) = refs[:11]
    refs = refs[11:]
    (n1_v, q_v, m_v, lse_v, s2_v, i2_v, n2_v, sl_v, a_v, o_v) = refs[:10]
    load_sem, store_sem, send_sem, recv_sem, open_sem, across_sem = refs[10:]
    rows, width = x_v.shape
    half = q_v.shape[1]
    tile_rows = rows // TILES
    wide = a_v.shape[1]

    loads = Loads(load_sem)
    opening = Opening(passing, 0, x_first, x_other, earlier, x_v, load_sem.at[FORWARD_LOADS], open_sem)
    opening.start()
    loads.start("qkv", w_qkv, wq_v)
    if mode is not False:
        loads.start("k", k_past, k_v.at[pl.ds(0, rows)])
        loads.start("v", v_past, v_v.at[pl.ds(0, rows)])
    loads.start("out", w_out, wo_v)
    loads.start("fc", w_fc, wf_v)
    loads.start("proj", w_proj, wp_v)
    greet_step(0, passing)
    opening.send()
    exchange = Exchange(send_v, recv_v, send_sem, recv_sem)
    across = Across(0, o_v, passed, across_sem)
    stores = []

    def store(buffer, dest):
        copy = pltpu.make_async_copy(buffer, dest, store_sem.at[len(stores)])
        copy.start()
        stores.append(copy)

    def store_rows(tile, *pairs):
        place = pl.ds(tile * tile_rows, tile_rows)
        for buffer, dest in pairs:
            store(buffer.at[place], dest.at[place])

    def vector(row, start=0, size=None):
        return params[row : row + 1, start : start + (size or width)]

    own_rows = pl.ds(rows, rows)
    for tile in range(TILES):
        span = pl.ds(tile * tile_rows, tile_rows)
        later = pl.ds(rows + tile * tile_rows, tile_rows)
        opening.take(tile)
        scaled, _ = norm_parts(x_v[span, :].astype(F32))
        normed = (scaled * vector(0) + vector(1)).astype(BF)
        n1_v[span, :] = normed
        if tile == 0:
            loads.wait("qkv")
        piece = jnp.dot(normed, wq_v[:, :half], preferred_element_type=F32)
        q_v[span, :] = (piece + vector(6, 0, half)).astype(BF)
        piece = jnp.dot(normed, wq_v[:, half : 2 * half], preferred_element_type=F32)
        k_v[later, :] = piece.astype(BF)
        piece = jnp.dot(normed, wq_v[:, 2 * half :], preferred_element_type=F32)
        v_v[later, :] = (piece + vector(6, half, half)).astype(BF)
        store_rows(tile, (x_v, x_used), (n1_v, normed1), (q_v, query))
    store(k_v.at[own_rows], keys)
    store(v_v.at[own_rows], values)
    if mode is not False:
        loads.wait("k", "v")
    loads.wait("out")

    def attention(past):
        first_key = 0 if past else rows
        for tile in range(TILES):
            span = pl.ds(tile * tile_rows, tile_rows)
            length = (rows if past else 0) + (tile + 1) * tile_rows
            reach = pl.ds(first_key, length)

            def pair(number, carry):
                lanes = pl.ds(pl.multiple_of(number * 128, 128), 128)
                key, value = k_v[reach, lanes], v_v[reach, lanes]
                pieces = []
                for head, part in enumerate(head_parts(q_v[span, lanes])):
                    scores = masked_scores(key, part * BF(HEAD_DIM**-0.5), length)
                    top = jnp.max(scores, axis=0, keepdims=True)
                    probs = jnp.exp(scores - top)
                    total = jnp.sum(probs, axis=0, keepdims=True)
                    lse_v[number, pl.ds(head, 1), span] = top + jnp.log(total)
                    piece = rows_product(value, probs.astype(BF))
                    piece = piece[head * HEAD_DIM : (head + 1) * HEAD_DIM]
                    pieces.append(piece * (1.0 / total))
                m_v[span, lanes] = jnp.transpose(jnp.concatenate(pieces, axis=0)).astype(BF)
                return carry

            lax.fori_loop(0, half // 128, pair, 0, unroll=mode is not None)
            partial = jnp.dot(m_v[span, :], wo_v[...], preferred_element_type=F32)
            part_v[tile] = partial
            exchange.give(tile, partial)

    by_past(mode, attention)
    store(m_v, mixed)
    store(lse_v, lse)
    loads.wait("fc", "proj")

    def conclude(tile):
        span = pl.ds(tile * tile_rows, tile_rows)
        total = part_v[TILES + tile] + exchange.take(TILES + tile)
        o_v[span, :] = (hid_v[span, :] + total + vector(5)).astype(BF)
        store_rows(tile, (o_v, out))
        if passing:
            across.send(tile)

    for tile in range(TILES):
        span = pl.ds(tile * tile_rows, tile_rows)
        hidden = x_v[span, :].astype(F32) + (part_v[tile] + exchange.take(tile)) + vector(2)
        hid_v[span, :] = hidden
        scaled, inverse = norm_parts(hidden)
        s2_v[span, :] = scaled.astype(BF)
        i2_v[span, :] = jnp.broadcast_to(inverse, (tile_rows, 128))
        normed = (scaled * vector(3) + vector(4)).astype(BF)
        n2_v[span, :] = normed
        store_rows(tile, (s2_v, scaled2), (i2_v, inverse2), (n2_v, normed2))
        chunk = width // 2
        for part in range(wide // chunk):
            columns = pl.ds(part * chunk, chunk)
            pre = jnp.dot(normed, wf_v[:, columns], preferred_element_type=F32)
            bias = vector(7 + part * chunk // width, part * chunk % width, chunk)
            activated, inclined = gelu_pair(pre + bias)
            a_v[span, columns] = activated.astype(BF)
            sl_v[span, columns] = inclined.astype(BF)
        store_rows(tile, (sl_v, slope), (a_v, act))
        if tile > 0:
            conclude(tile - 1)
        partial = jnp.dot(a_v[span, :], wp_v[...], preferred_element_type=F32)
        part_v[TILES + tile] = partial
        exchange.give(TILES + tile, partial)
    conclude(TILES - 1)
    for copy in stores:
        copy.wait()
    exchange.finish(2 * TILES)
    opening.finish()
    if passing:
        for tile in range(TILES):
            across.receive(tile)
        across.finish()


def step_sems(loads, stores):
    return [
        pltpu.SemaphoreType.DMA((loads,)),
        pltpu.SemaphoreType.DMA((stores,)),
        pltpu.SemaphoreType.DMA((2 * TILES,)),
        pltpu.SemaphoreType.DMA((2 * TILES,)),
        pltpu.SemaphoreType.DMA((4, TILES)),
        pltpu.SemaphoreType.DMA((4, TILES)),
    ]


def forward_step(mode, passing, inputs, params, weights, past):
    rows, width = inputs[0].shape
    half = width // 2
    wide = weights[2].shape[1]
    pairs = half // 128
    tile_rows = rows // TILES
    spot = pl.BlockSpec(memory_space=pl.ANY)
    low = lambda columns: ((rows, columns), BF)
    outs = [
        low(width),
        low(width),
        low(half),
        low(half),
        low(half),
        low(half),
        ((pairs, 8, rows), F32),
        low(width),
        ((rows, 128), F32),
        low(width),
        low(wide),
        low(wide),
        low(width),
        low(width),
    ]
    scratch = [
        low(width),
        *((item.shape, BF) for item in weights),
        ((2 * rows, half), BF),
        ((2 * rows, half), BF),
        ((rows, width), F32),
        ((2 * TILES, tile_rows, width), F32),
        ((2 * TILES, tile_rows, width), BF),
        ((2 * TILES, tile_rows, width), BF),
        low(width),
        low(half),
        low(half),
        ((pairs, 8, rows), F32),
        low(width),
        ((rows, 128), F32),
        low(width),
        low(wide),
        low(wide),
        low(width),
    ]
    number = {False: 3, None: 4, True: 5}[mode]
    return pl.pallas_call(
        functools.partial(forward_kernel, mode, passing),
        out_shape=[jax.ShapeDtypeStruct(*item) for item in outs],
        in_specs=[spot] * 3 + [pl.BlockSpec(memory_space=pltpu.VMEM)] + [spot] * 6,
        out_specs=[spot] * len(outs),
        scratch_shapes=[pltpu.VMEM(*item) for item in scratch]
        + step_sems(FORWARD_LOADS + 1, 2 * len(outs)),
        compiler_params=pltpu.CompilerParams(
            collective_id=number, has_side_effects=True, vmem_limit_bytes=VMEM_LIMIT
        ),
        name="forward_step",
    )(*inputs, params, *weights, *past)


BACKWARD_LOADS = 17


def backward_kernel(mode, passing, *refs):
    (g_first, g_other, earlier, x_used, params, w_qkv, w_out, w_fc, w_proj) = refs[:9]
    (query, keys, values, k_past, v_past, mixed, lse, scaled2, inverse2, slope, pend_k, pend_v) = refs[9:21]
    refs = refs[21:]
    (g_used, d_qkv, d_branch, d_pre, out, next_k, next_v, sums, passed) = refs[:9]
    refs = refs[9:]
    (g_v, x_v, wq_v, wo_v, wf_v, wp_v, q_v, k_v, v_v, m_v, lse_v, s2_v, i2_v, sl_v) = refs[:14]
    refs = refs[14:]
    (dk_v, dv_v, hid_v, part_v, send_v, recv_v, dqkv_v, db_v, dp_v, dm_v, o_v, sum_v) = refs[:12]
    load_sem, store_sem, send_sem, recv_sem, open_sem, across_sem = refs[12:]
    rows, width = x_v.shape
    half = q_v.shape[1]
    wide = dp_v.shape[1]
    tile_rows = rows // TILES
    own_rows, past_rows = pl.ds(rows, rows), pl.ds(0, rows)
    scale = HEAD_DIM**-0.5

    loads = Loads(load_sem)
    opening = Opening(passing, 1, g_first, g_other, earlier, g_v, load_sem.at[BACKWARD_LOADS], open_sem)
    opening.start()
    loads.start("proj", w_proj, wp_v)
    loads.start("slope", slope, sl_v)
    loads.start("fc", w_fc, wf_v)
    loads.start("scaled2", scaled2, s2_v)
    loads.start("inverse2", inverse2, i2_v)
    loads.start("out", w_out, wo_v)
    loads.start("q", query, q_v)
    loads.start("k", keys, k_v.at[own_rows])
    loads.start("v", values, v_v.at[own_rows])
    if mode is not False:
        loads.start("k_past", k_past, k_v.at[past_rows])
        loads.start("v_past", v_past, v_v.at[past_rows])
    loads.start("mixed", mixed, m_v)
    loads.start("lse", lse, lse_v)
    if mode is not True:
        loads.start("pend_k", pend_k, dk_v.at[own_rows])
        loads.start("pend_v", pend_v, dv_v.at[own_rows])
    loads.start("qkv", w_qkv, wq_v)
    loads.start("x", x_used, x_v)
    greet_step(1, passing)
    opening.send()
    exchange = Exchange(send_v, recv_v, send_sem, recv_sem)
    across = Across(1, o_v, passed, across_sem)
    stores = []

    def store(buffer, dest):
        copy = pltpu.make_async_copy(buffer, dest, store_sem.at[len(stores)])
        copy.start()
        stores.append(copy)

    def vector(row, start=0, size=None):
        return params[row : row + 1, start : start + (size or width)]

    sum_v[...] = jnp.zeros_like(sum_v)

    def tally(row, piece, start=0):
        place = (slice(row, row + 1), slice(start, start + piece.shape[1]))
        sum_v[place] += jnp.sum(piece, axis=0, keepdims=True)

    loads.wait("proj", "slope", "fc")
    chunk = width // 2
    for tile in range(TILES):
        span = pl.ds(tile * tile_rows, tile_rows)
        opening.take(tile)
        grad = g_v[span, :]
        for part in range(wide // chunk):
            columns = pl.ds(part * chunk, chunk)
            d_act = cols_product(grad, wp_v[columns, :])
            piece = (d_act * sl_v[span, columns].astype(F32)).astype(BF)
            dp_v[span, columns] = piece
            tally(7 + part * chunk // width, piece.astype(F32), part * chunk % width)
        partial = cols_product(dp_v[span, :], wf_v[...])
        part_v[tile] = partial
        exchange.give(tile, partial)
        tally(5, grad.astype(F32))
    store(g_v, g_used)
    store(dp_v, d_pre)
    loads.wait("scaled2", "inverse2", "out")
    for tile in range(TILES):
        span = pl.ds(tile * tile_rows, tile_rows)
        d_normed = part_v[tile] + exchange.take(tile)
        scaled = s2_v[span, :].astype(F32)
        tally(3, d_normed * scaled)
        tally(4, d_normed)
        d_hidden = g_v[span, :].astype(F32) + norm_backward(
            d_normed, scaled, i2_v[span, 0:1], vector(3)
        )
        hid_v[span, :] = d_hidden
        branch = d_hidden.astype(BF)
        db_v[span, :] = branch
        tally(2, branch.astype(F32))
        dm_v[span, :] = cols_product(branch, wo_v[...]).astype(BF)
    store(db_v, d_branch)
    loads.wait("q", "k", "v", "mixed", "lse")
    if mode is not False:
        loads.wait("k_past", "v_past")
    if mode is not True:
        loads.wait("pend_k", "pend_v")

    def attention(past):
        first_key = 0 if past else rows
        if past:
            dk_v[...] = jnp.zeros_like(dk_v)
            dv_v[...] = jnp.zeros_like(dv_v)
        for tile in range(TILES):
            span = pl.ds(tile * tile_rows, tile_rows)
            length = (rows if past else 0) + (tile + 1) * tile_rows
            reach = pl.ds(first_key, length)

            def pair(number, carry):
                lanes = pl.ds(pl.multiple_of(number * 128, 128), 128)
                key, value = k_v[reach, lanes], v_v[reach, lanes]
                grads = dm_v[span, lanes]
                products = jnp.transpose(grads.astype(F32) * m_v[span, lanes].astype(F32))
                queries, grads = head_parts(q_v[span, lanes]), head_parts(grads)
                d_query = []
                d_key = d_value = None
                for head in range(2):
                    take = slice(head * HEAD_DIM, (head + 1) * HEAD_DIM)
                    scaled_query = queries[head] * BF(scale)
                    scores = masked_scores(key, scaled_query, length)
                    weights = jnp.exp(scores - lse_v[number, pl.ds(head, 1), span])
                    d_probs = cols_product(value, grads[head])
                    delta = jnp.sum(products[take], axis=0, keepdims=True)
                    d_scores = (weights * (d_probs - delta)).astype(BF)
                    one = jnp.dot(weights.astype(BF), grads[head], preferred_element_type=F32)
                    two = jnp.dot(d_scores, scaled_query, preferred_element_type=F32)
                    d_value = one if head == 0 else d_value + one
                    d_key = two if head == 0 else d_key + two
                    d_query.append(rows_product(key, d_scores)[take])
                dk_v[reach, lanes] += d_key
                dv_v[reach, lanes] += d_value
                d_query = jnp.transpose(jnp.concatenate(d_query, axis=0) * scale)
                dqkv_v[span, lanes] = d_query.astype(BF)
                return carry

            lax.fori_loop(0, half // 128, pair, 0, unroll=mode is not None)

    by_past(mode, attention)
    if mode is not False:
        store(dk_v.at[past_rows], next_k)
        store(dv_v.at[past_rows], next_v)
    loads.wait("qkv", "x")
    for tile in range(TILES):
        span = pl.ds(tile * tile_rows, tile_rows)
        later = pl.ds(rows + tile * tile_rows, tile_rows)
        dqkv_v[span, half : 2 * half] = dk_v[later, :].astype(BF)
        dqkv_v[span, 2 * half :] = dv_v[later, :].astype(BF)
        piece = dqkv_v[span, :]
        partial = cols_product(piece, wq_v[...])
        part_v[TILES + tile] = partial
        exchange.give(TILES + tile, partial)
        tally(6, piece[:, :half].astype(F32))
        tally(6, piece[:, 2 * half :].astype(F32), half)
    store(dqkv_v, d_qkv)
    for tile in range(TILES):
        span = pl.ds(tile * tile_rows, tile_rows)
        scaled, inverse = norm_parts(x_v[span, :].astype(F32))
        d_normed = part_v[TILES + tile] + exchange.take(TILES + tile)
        tally(0, d_normed * scaled)
        tally(1, d_normed)
        d_inputs = hid_v[span, :] + norm_backward(d_normed, scaled, inverse, vector(0))
        o_v[span, :] = d_inputs.astype(BF)
        if passing:
            across.send(tile)
    store(o_v, out)
    store(sum_v, sums)
    for copy in stores:
        copy.wait()
    exchange.finish(2 * TILES)
    opening.finish()
    if passing:
        for tile in range(TILES):
            across.receive(tile)
        across.finish()


def backward_step(mode, passing, grads, inputs, params, weights, kept, pending):
    rows, width = inputs.shape
    half = width // 2
    wide = weights[2].shape[1]
    pairs = half // 128
    tile_rows = rows // TILES
    spot = pl.BlockSpec(memory_space=pl.ANY)
    low = lambda columns: ((rows, columns), BF)
    outs = [
        low(width),
        low(3 * half),
        low(width),
        low(wide),
        low(width),
        ((rows, half), F32),
        ((rows, half), F32),
        ((16, width), F32),
        low(width),
    ]
    scratch = [
        low(width),
        low(width),
        *((item.shape, BF) for item in weights),
        low(half),
        ((2 * rows, half), BF),
        ((2 * rows, half), BF),
        low(half),
        ((pairs, 8, rows), F32),
        low(width),
        ((rows, 128), F32),
        low(wide),
        ((2 * rows, half), F32),
        ((2 * rows, half), F32),
        ((rows, width), F32),
        ((2 * TILES, tile_rows, width), F32),
        ((2 * TILES, tile_rows, width), BF),
        ((2 * TILES, tile_rows, width), BF),
        low(3 * half),
        low(width),
        low(wide),
        low(half),
        low(width),
        ((16, width), F32),
    ]
    number = {True: 6, None: 7, False: 8}[mode]
    return pl.pallas_call(
        functools.partial(backward_kernel, mode, passing),
        out_shape=[jax.ShapeDtypeStruct(*item) for item in outs],
        in_specs=[spot] * 4 + [pl.BlockSpec(memory_space=pltpu.VMEM)] + [spot] * 16,
        out_specs=[spot] * len(outs),
        scratch_shapes=[pltpu.VMEM(*item) for item in scratch]
        + step_sems(BACKWARD_LOADS + 1, len(outs)),
        compiler_params=pltpu.CompilerParams(
            collective_id=number, has_side_effects=True, vmem_limit_bytes=VMEM_LIMIT
        ),
        name="backward_step",
    )(*grads, inputs, params, *weights, *kept, *pending)


def shards(
    tokens,
    cotangent,
    attn_gain,
    attn_shift,
    qkv_weight,
    query_bias,
    value_bias,
    out_weight,
    out_bias,
    mlp_gain,
    mlp_shift,
    fc_weight,
    fc_bias,
    proj_weight,
    proj_bias,
):
    size = lax.axis_size("replica")
    micro = tokens.shape[1]
    assert micro == 2
    *outer, params, w_qkv, w_fc, w_out, w_proj = fetch_inputs(
        tokens[0],
        cotangent[0],
        qkv_weight[0],
        fc_weight[0],
        out_weight[0],
        proj_weight[0],
        (
            attn_gain,
            attn_shift,
            out_bias,
            mlp_gain,
            mlp_shift,
            proj_bias,
            query_bias,
            value_bias,
            fc_bias,
        ),
    )
    weights = (w_qkv, w_out, w_fc, w_proj)

    received, kept_list, outputs, past, got = [], [], [], (w_out, w_out), outer[0]
    for step in range(micro + 1):
        output = outputs[-1] if outputs else outer[0]
        used, normed1, *state, normed2, slope, act, output, got = forward_step(
            (False, None, True)[step],
            step == 1,
            (outer[min(step, micro - 1)], got, output),
            params,
            weights,
            past,
        )
        query, keys, values, mixed, lse, scaled2, inverse2 = state
        outputs.append(output)
        received.append(used)
        kept = (query, keys, values, *past, mixed, lse, scaled2, inverse2, slope)
        kept_list.append((kept, normed1, normed2, act))
        past = (keys, values)

    pending = (params, params)
    grad_received, terms_list, results, tallies, got = [], [], [], [], outer[1]
    for step in range(micro + 1):
        last = micro - step
        kept, normed1, normed2, act = kept_list[last]
        result = results[-1] if results else outer[1]
        grad, d_qkv, d_branch, d_pre, result, *pending, vector, got = backward_step(
            (True, None, False)[step],
            step == 1,
            (got, outer[max(micro - 1 - step, 0)], result),
            received[last],
            params,
            weights,
            kept,
            pending,
        )
        results.append(result)
        grad_received.append(grad)
        tallies.append(vector)
        terms_list.append((normed1, d_qkv, kept[5], d_branch, normed2, d_pre, act, grad))
    def factor(number):
        return tuple(terms_list[step][number] for step in (2, 1, 0))

    factors = [(factor(i), factor(i + 1)) for i in (0, 4, 2, 6)]
    reduced = ring_scatter(factors, tallies, size)
    reduced, packed = reduced[:4], reduced[4]
    near = []
    for i in range(micro):
        near += [outputs[i], outputs[i + 1], received[i + 1]]
        near += [results[micro - i], results[micro - 1 - i], grad_received[micro - i]]
    *gathered, activations, input_grads = ring_gather(reduced, (3, 1), near, size)
    finished = finish(gathered, packed, (activations, input_grads))
    qkv_grad, fc_grad, out_grad, proj_grad = (item[None] for item in finished[:4])
    vectors = finished[4:13]
    activations, input_grads = finished[13:]
    return (
        activations[None, None],
        input_grads[None, None],
        vectors[0],
        vectors[1],
        qkv_grad,
        vectors[6],
        vectors[7],
        out_grad,
        vectors[2],
        vectors[3],
        vectors[4],
        fc_grad,
        vectors[8],
        proj_grad,
        vectors[5],
    )


def solution(mesh):
    block = P("replica", None, "shard", None)
    layers = P("section", "replica", None, "shard", None)
    vector = P("section", "shard")
    matrix = P("section", "shard", None)
    kinds = (
        vector,
        vector,
        matrix,
        vector,
        vector,
        matrix,
        vector,
        vector,
        vector,
        matrix,
        vector,
        matrix,
        vector,
    )
    return jax.shard_map(
        shards,
        mesh=mesh,
        in_specs=(block, block) + kinds,
        out_specs=(layers, layers) + kinds,
        check_vma=False,
    )
```

```python
import functools

import jax
import jax.numpy as jnp
from jax import lax
from jax.experimental import pallas as pl
from jax.experimental.pallas import tpu as pltpu
from jax.sharding import PartitionSpec as P

HEAD_DIM = 64
EPSILON = 1e-05
GELU_SCALE = 0.7978845608028654
GELU_CUBIC = 0.044715
ROWS_CONTRACT = (((0,), (0,)), ((), ()))
COLS_CONTRACT = (((1,), (1,)), ((), ()))
BF = jnp.bfloat16
F32 = jnp.float32
MESH = pl.DeviceIdType.MESH
QTILE = 256
VMEM_LIMIT = 56 * 1024 * 1024


def rows_product(left, right):
    return lax.dot_general(left, right, ROWS_CONTRACT, preferred_element_type=F32)


def cols_product(left, right):
    return lax.dot_general(left, right, COLS_CONTRACT, preferred_element_type=F32)


def norm_parts(inputs):
    mean = jnp.mean(inputs, axis=-1, keepdims=True)
    centered = inputs - mean
    inverse = lax.rsqrt(jnp.mean(centered * centered, axis=-1, keepdims=True) + EPSILON)
    return centered * inverse, inverse


def norm_backward(d_normed, scaled, inverse, gain):
    d_scaled = d_normed * gain
    return inverse * (
        d_scaled
        - jnp.mean(d_scaled, axis=-1, keepdims=True)
        - scaled * jnp.mean(d_scaled * scaled, axis=-1, keepdims=True)
    )


def gelu_pair(pre):
    tangent = jnp.tanh(GELU_SCALE * (pre + GELU_CUBIC * pre * pre * pre))
    value = 0.5 * pre * (1.0 + tangent)
    slope = 0.5 * (1.0 + tangent) + 0.5 * pre * (1.0 - tangent * tangent) * GELU_SCALE * (
        1.0 + 3.0 * GELU_CUBIC * pre * pre
    )
    return value, slope


def head_parts(pair):
    low = lax.broadcasted_iota(jnp.int32, pair.shape, 1) < HEAD_DIM
    zero = jnp.zeros_like(pair)
    return jnp.where(low, pair, zero), jnp.where(low, zero, pair)


def masked_scores(keys, query, length):
    scores = cols_product(keys, query)
    tail = scores[length - QTILE :]
    key_pos = lax.broadcasted_iota(jnp.int32, tail.shape, 0)
    query_pos = lax.broadcasted_iota(jnp.int32, tail.shape, 1)
    tail = jnp.where(key_pos <= query_pos, tail, -1e30)
    if length == QTILE:
        return tail
    return jnp.concatenate([scores[: length - QTILE], tail], axis=0)


def ring_place(size):
    index = lax.axis_index("replica")
    odd = index % 2
    half = index // 2
    place = (1 - odd) * half + odd * (size - 1 - half)

    def device(spot):
        upper = spot // (size // 2)
        return (1 - upper) * (2 * spot) + upper * (2 * (size - 1 - spot) + 1)

    return place, device((place + 1) % size), device((place + size - 1) % size)


def neighbours():
    core, layer = lax.axis_index("section"), lax.axis_index("shard")
    sibling = {"section": 1 - core}
    across = {"shard": 1 - layer}
    diagonal = {"section": 1 - core, "shard": 1 - layer}
    return core, layer, sibling, across, diagonal


def greet(devices):
    barrier = pltpu.get_barrier_semaphore()
    for device in devices:
        pl.semaphore_signal(barrier, inc=1, device_id=device, device_id_type=MESH)
    pl.semaphore_wait(barrier, len(devices))


def scatter_kernel(size, count, *refs):
    sources, refs = refs[: 6 * count], refs[6 * count :]
    tallies, refs = refs[:3], refs[3:]
    out, refs = refs[:count], refs[count:]
    packed, refs = refs[0], refs[1:]
    held, refs = refs[: 2 * count], refs[2 * count :]
    own, refs = refs[:count], refs[count:]
    landed, refs = refs[:count], refs[count:]
    load_sem, send_sem, recv_sem, small_send, small_recv, swap_sem, total, small, small_out = refs
    place, following, previous = ring_place(size)
    targets = ({"replica": following}, {"replica": previous})
    core, layer, _, _, diagonal = neighbours()

    def load(number, which):
        rows = held[number].shape[0] // 2
        source = sources[3 * number + which]
        part = pl.ds(0 if which == 1 else rows, rows)
        return pltpu.make_async_copy(
            source, held[number].at[part], load_sem.at[number, 0 if which == 1 else 1]
        )

    for number in range(2 * count):
        load(number, 1).start()

        @pl.when(layer == 0)
        def _(number=number):
            load(number, 0).start()

        @pl.when(layer != 0)
        def _(number=number):
            load(number, 2).start()

    greet(targets + (diagonal,))

    def send(way, item, source, slot):
        return pltpu.make_async_remote_copy(
            src_ref=source,
            dst_ref=landed[item].at[way, slot],
            send_sem=send_sem.at[way, item, slot],
            recv_sem=recv_sem.at[way, item, slot],
            device_id=targets[way],
            device_id_type=MESH,
        )

    def send_small(chunk, slot):
        return pltpu.make_async_remote_copy(
            src_ref=small_out.at[chunk],
            dst_ref=small_out.at[chunk],
            send_sem=small_send.at[slot],
            recv_sem=small_recv.at[slot],
            device_id=targets[0],
            device_id_type=MESH,
        )

    def chunk_of(way, slot):
        if way == 0:
            return (place + 2 * size - 2 - slot) % size
        return (place + 2 + slot) % size

    first = ((place + size - 1) % size, (place + 1) % size)
    group = size // 2

    def product(item, way, part):
        deep = own[item].shape[2]
        columns = pl.multiple_of((way * size + part * group) * deep, 128)
        left = held[2 * item][:, pl.ds(columns, group * deep)]
        result = rows_product(left, held[2 * item + 1][...])
        for index in range(group):
            own[item][way, part * group + index] = result[index * deep : (index + 1) * deep].astype(BF)

    half = small.shape[1]

    @pl.when(layer == 0)
    def _():
        total[...] = tallies[1][...] + tallies[2][...]

    @pl.when(layer != 0)
    def _():
        total[...] = tallies[0][...] + tallies[1][...]

    small[...] = jnp.zeros_like(small)
    small[0:6, :] = total[0:6, pl.ds(pl.multiple_of(core * half, half), half)]
    for row in range(3):
        for side in range(2):
            line = 6 + 2 * row + side
            small[line : line + 1, :] = total[6 + row : 7 + row, side * half : (side + 1) * half]

    def swap():
        return pltpu.make_async_remote_copy(
            src_ref=small,
            dst_ref=small_out.at[place],
            send_sem=swap_sem.at[0],
            recv_sem=swap_sem.at[1],
            device_id=diagonal,
            device_id_type=MESH,
        )

    @pl.when(core == layer)
    def _():
        small_out[place] = small[...]

    @pl.when(core != layer)
    def _():
        swap().start()

    for item in range(count):
        for number in (2 * item, 2 * item + 1):
            load(number, 1).wait()
            load(number, 0).wait()
        for way in range(2):
            product(item, way, first[way] // group)
            send(way, item, own[item].at[way, first[way]], 0).start()

    @pl.when(core != layer)
    def _():
        swap().wait()

    send_small(place, 0).start()
    for item in range(count):
        for way in range(2):
            product(item, way, 1 - first[way] // group)

    def step(slot, carry):
        for item in range(count):
            for way in range(2):
                here = landed[item].at[way, slot]
                send(way, item, here, slot).wait_recv()
                here[...] += own[item][way, chunk_of(way, slot)]
                send(way, item, here, slot + 1).start()
        chunk = (place + size - 1 - slot) % size
        send_small(chunk, slot).wait_recv()
        send_small(chunk, slot + 1).start()
        return carry

    lax.fori_loop(0, size - 2, step, 0)
    last = size - 2
    for item in range(count):
        for way in range(2):
            here = landed[item].at[way, last]
            send(way, item, here, last).wait_recv()
            out[item][way] = here[...] + own[item][way, place]
    send_small((place + 1) % size, last).wait_recv()
    gathered = small_out[0]
    for index in range(1, size):
        gathered = gathered + small_out[index]
    packed[...] = gathered

    def finish(slot, carry):
        for item in range(count):
            for way in range(2):
                send(way, item, landed[item].at[way, slot], slot).wait_send()
        send_small(place, slot).wait_send()
        return carry

    lax.fori_loop(0, size - 1, finish, 0)


def ring_scatter(factors, tallies, size):
    count = len(factors)
    flat = [item for pair in factors for item in pair]
    half = tallies[0].shape[1] // 2
    shapes = [(2 * item[0].shape[0], item[0].shape[1]) for item in flat]
    chunks = [
        (shapes[2 * i][1] // (2 * size), shapes[2 * i + 1][1]) for i in range(count)
    ]
    whole = pl.BlockSpec(memory_space=pltpu.VMEM)
    spot = pl.BlockSpec(memory_space=pl.ANY)
    return pl.pallas_call(
        functools.partial(scatter_kernel, size, count),
        out_shape=[jax.ShapeDtypeStruct((2,) + chunk, BF) for chunk in chunks]
        + [jax.ShapeDtypeStruct((16, half), F32)],
        in_specs=[spot] * (6 * count) + [whole] * 3,
        out_specs=[whole] * (count + 1),
        scratch_shapes=[pltpu.VMEM(shape, BF) for shape in shapes]
        + [pltpu.VMEM((2, size) + chunk, BF) for chunk in chunks]
        + [pltpu.VMEM((2, size - 1) + chunk, BF) for chunk in chunks]
        + [pltpu.SemaphoreType.DMA((2 * count, 2))]
        + [pltpu.SemaphoreType.DMA((2, count, size - 1))] * 2
        + [pltpu.SemaphoreType.DMA((size - 1,))] * 2
        + [pltpu.SemaphoreType.DMA((2,))]
        + [
            pltpu.VMEM((16, 2 * half), F32),
            pltpu.VMEM((16, half), F32),
            pltpu.VMEM((size, 16, half), F32),
        ],
        compiler_params=pltpu.CompilerParams(
            collective_id=0, has_side_effects=True, vmem_limit_bytes=VMEM_LIMIT
        ),
        name="ring_scatter",
    )(*[block for item in flat for block in item], *tallies)


def gather_kernel(size, groups, *refs):
    count = 4
    own, refs = refs[:count], refs[count:]
    near, refs = refs[:12], refs[12:]
    out, refs = refs[:count], refs[count:]
    placed, refs = refs[:2], refs[2:]
    swap_send, swap_recv, send_sem, recv_sem, place_send, place_recv, load_sem, bounce = refs
    place, following, previous = ring_place(size)
    targets = ({"replica": following}, {"replica": previous})
    core, layer, sibling, across, diagonal = neighbours()
    same = core == layer
    greet(targets + (sibling, across, diagonal))

    def parts(item, source_half, sender):
        if item < len(groups):
            width = own[item].shape[2] // groups[item]
            for group in range(groups[item]):
                start = pl.multiple_of((2 * group + sender) * width, width)
                yield (
                    own[item].at[source_half, :, pl.ds(group * width, width)],
                    out[item].at[place, :, pl.ds(start, width)],
                )
        else:
            for half in range(2):
                yield own[item].at[half], out[item].at[half, place]

    def copies(item, source_half, lane, kind, device=None):
        for number, (source, target) in enumerate(parts(item, source_half, core)):
            send, recv = swap_send.at[item, lane, number], swap_recv.at[item, kind, number]
            if device is None:
                yield pltpu.make_async_copy(source, target, recv)
            else:
                yield pltpu.make_async_remote_copy(
                    src_ref=source,
                    dst_ref=target,
                    send_sem=send,
                    recv_sem=recv,
                    device_id=device,
                    device_id_type=MESH,
                )

    @pl.when(same)
    def _():
        for item in range(count):
            for copy in copies(item, layer, 0, 0):
                copy.start()
            if item < len(groups):
                for copy in copies(item, 1 - layer, 0, 2, across):
                    copy.start()

    @pl.when(core != layer)
    def _():
        for item in range(count):
            for copy in copies(item, 1 - layer, 0, 3, diagonal):
                copy.start()
            if item < len(groups):
                for copy in copies(item, layer, 1, 1, sibling):
                    copy.start()

    part = placed[0].shape[1]

    def near_rows(number, block, shard):
        return near[6 * block + number].at[pl.ds(shard * part, part)]

    def place_remote(kind, block):
        number, shard = ((1, 0), (3, 1))[kind]
        return pltpu.make_async_remote_copy(
            src_ref=near_rows(number, block, shard),
            dst_ref=placed[kind].at[block],
            send_sem=place_send.at[block],
            recv_sem=place_recv.at[block],
            device_id=across,
            device_id_type=MESH,
        )

    def place_load(number, block, shard):
        lane = 2 * (number // 3) + block
        return pltpu.make_async_copy(near_rows(number, block, shard), bounce.at[lane], load_sem.at[lane])

    def place_store(number, block):
        kind = number // 3
        lane = 2 * kind + block
        return pltpu.make_async_copy(bounce.at[lane], placed[kind].at[block], load_sem.at[lane])

    local = {(0, 0): (0, 3), (0, 1): (2,), (1, 0): (5,), (1, 1): (1, 4)}

    def on_device(action):
        for (at_core, at_layer), numbers in local.items():

            @pl.when((core == at_core) & (layer == at_layer))
            def _(numbers=numbers, at_layer=at_layer):
                for number in numbers:
                    for block in range(2):
                        action(number, block, at_layer)

    @pl.when(same & (layer == 1))
    def _():
        for block in range(2):
            place_remote(0, block).start()

    @pl.when(same & (layer == 0))
    def _():
        for block in range(2):
            place_remote(1, block).start()

    on_device(lambda number, block, shard: place_load(number, block, shard).start())

    def send(way, item, chunk, slot):
        if item < len(groups):
            deep = out[item].shape[1] // 2
            here = out[item].at[chunk, pl.ds(way * deep, deep)]
        else:
            here = out[item].at[way, chunk]
        return pltpu.make_async_remote_copy(
            src_ref=here,
            dst_ref=here,
            send_sem=send_sem.at[way, item, slot],
            recv_sem=recv_sem.at[way, item, slot],
            device_id=targets[way],
            device_id_type=MESH,
        )

    def chunk_of(way, slot):
        if way == 0:
            return (place + size - 1 - slot) % size
        return (place + 1 + slot) % size

    for item in range(count):

        @pl.when(same)
        def _(item=item):
            for copy in copies(item, layer, 0, 0):
                copy.wait()
            if item < len(groups):
                for copy in copies(item, layer, 1, 1, sibling):
                    copy.wait_recv()

        @pl.when(core != layer)
        def _(item=item):
            for copy in copies(item, layer, 0, 3, diagonal):
                copy.wait_recv()
            if item < len(groups):
                for copy in copies(item, layer, 0, 2, across):
                    copy.wait_recv()

        for way in range(2):
            send(way, item, place, 0).start()

    def step(slot, carry):
        for item in range(count):
            for way in range(2):
                chunk = chunk_of(way, slot)
                send(way, item, chunk, slot).wait_recv()
                send(way, item, chunk, slot + 1).start()
        return carry

    def moved(number, block, shard):
        place_load(number, block, shard).wait()
        place_store(number, block).start()

    on_device(moved)
    lax.fori_loop(0, size - 2, step, 0)
    last = size - 2
    for item in range(count):
        for way in range(2):
            send(way, item, chunk_of(way, last), last).wait_recv()
    on_device(lambda number, block, shard: place_store(number, block).wait())

    @pl.when(same)
    def _():
        for block in range(2):
            place_remote(0, block).wait_send()

    @pl.when((core != layer) & (layer == 0))
    def _():
        for block in range(2):
            place_remote(0, block).wait_recv()

    @pl.when((core != layer) & (layer == 1))
    def _():
        for block in range(2):
            place_remote(1, block).wait_recv()

    @pl.when(same)
    def _():
        for item in range(len(groups)):
            for copy in copies(item, 1 - layer, 0, 2, across):
                copy.wait_send()

    @pl.when(core != layer)
    def _():
        for item in range(count):
            for copy in copies(item, 1 - layer, 0, 3, diagonal):
                copy.wait_send()
            if item < len(groups):
                for copy in copies(item, layer, 1, 1, sibling):
                    copy.wait_send()

    def finish(slot, carry):
        for item in range(count):
            for way in range(2):
                send(way, item, place, slot).wait_send()
        return carry

    lax.fori_loop(0, size - 1, finish, 0)


def ring_gather(pieces, groups, near, size):
    spot = pl.BlockSpec(memory_space=pl.ANY)
    shapes = [(size, item.shape[1], 2 * item.shape[2]) for item in pieces[: len(groups)]]
    shapes += [(2, size) + item.shape[1:] for item in pieces[len(groups) :]]
    count = len(pieces)
    rows = (near[0].shape[0] // 2, near[0].shape[1])
    whole = pl.BlockSpec(memory_space=pltpu.VMEM)
    return pl.pallas_call(
        functools.partial(gather_kernel, size, groups),
        out_shape=[jax.ShapeDtypeStruct(shape, BF) for shape in shapes]
        + [jax.ShapeDtypeStruct((2,) + rows, BF)] * 2,
        in_specs=[whole] * count + [spot] * 12,
        out_specs=[spot] * (count + 2),
        scratch_shapes=[
            pltpu.SemaphoreType.DMA((count, 2, 3)),
            pltpu.SemaphoreType.DMA((count, 4, 3)),
        ]
        + [pltpu.SemaphoreType.DMA((2, count, size - 1))] * 2
        + [pltpu.SemaphoreType.DMA((2,))] * 2
        + [pltpu.SemaphoreType.DMA((4,)), pltpu.VMEM((4,) + rows, BF)],
        compiler_params=pltpu.CompilerParams(
            collective_id=1, has_side_effects=True, vmem_limit_bytes=VMEM_LIMIT
        ),
        name="ring_gather",
    )(*pieces, *near)


def finish_kernel(*refs):
    gathered, packed, placed = refs[:4], refs[4], refs[5:7]
    wide, vectors, moved = refs[7:11], refs[11:20], refs[20:22]
    low, high, bounce = refs[22:26], refs[26:30], refs[30]
    fetch_sem, store_sem, load_sem = refs[31:]

    def fetch(item, chunk):
        return pltpu.make_async_copy(
            gathered[item].at[chunk], low[item].at[chunk], fetch_sem.at[item, chunk]
        )

    def store(item, chunk):
        deep = low[item].shape[1]
        place = pl.ds(pl.multiple_of(chunk * deep, deep), deep)
        return pltpu.make_async_copy(
            high[item].at[chunk], wide[item].at[place], store_sem.at[item, chunk]
        )

    def every(action):
        for item in range(4):

            def step(chunk, carry, item=item):
                action(item, chunk)
                return carry

            lax.fori_loop(0, low[item].shape[0], step, 0)

    def widen(item, chunk):
        fetch(item, chunk).wait()
        high[item][chunk] = low[item][chunk].astype(F32)
        store(item, chunk).start()

    every(lambda item, chunk: fetch(item, chunk).start())
    loads = [pltpu.make_async_copy(placed[i], bounce.at[i], load_sem.at[i]) for i in range(2)]
    for copy in loads:
        copy.start()
    half = packed.shape[1]
    for number in range(9):
        for index in range(vectors[number].shape[1] // half):
            row = number + index
            vectors[number][:, index * half : (index + 1) * half] = packed[row : row + 1, :]
    every(widen)
    stores = []
    for i in range(2):
        loads[i].wait()
        copy = pltpu.make_async_copy(bounce.at[i], moved[i], load_sem.at[i])
        copy.start()
        stores.append(copy)
    every(lambda item, chunk: store(item, chunk).wait())
    for copy in stores:
        copy.wait()


def finish(gathered, packed, placed):
    spot = pl.BlockSpec(memory_space=pl.ANY)
    whole = pl.BlockSpec(memory_space=pltpu.VMEM)
    gathered = [item.reshape((-1,) + item.shape[-2:]) for item in gathered]
    half = packed.shape[1]
    most = max(item.shape[0] for item in gathered)
    return pl.pallas_call(
        finish_kernel,
        out_shape=[
            jax.ShapeDtypeStruct((item.shape[0] * item.shape[1], item.shape[2]), F32)
            for item in gathered
        ]
        + [jax.ShapeDtypeStruct((1, half), F32)] * 8
        + [jax.ShapeDtypeStruct((1, 4 * half), F32)]
        + [jax.ShapeDtypeStruct(item.shape, BF) for item in placed],
        in_specs=[spot] * 4 + [whole] + [spot] * 2,
        out_specs=[spot] * 4 + [whole] * 9 + [spot] * 2,
        scratch_shapes=[pltpu.VMEM(item.shape, BF) for item in gathered]
        + [pltpu.VMEM(item.shape, F32) for item in gathered]
        + [
            pltpu.VMEM((2,) + placed[0].shape, BF),
            pltpu.SemaphoreType.DMA((4, most)),
            pltpu.SemaphoreType.DMA((4, most)),
            pltpu.SemaphoreType.DMA((2,)),
        ],
        compiler_params=pltpu.CompilerParams(vmem_limit_bytes=VMEM_LIMIT),
        name="finish",
    )(*gathered, packed, *placed)


def fetch_kernel(*refs):
    tokens, cotangent, qkv, fc, out, proj = refs[:6]
    vectors, refs = refs[6:15], refs[15:]
    *outer, params, w_qkv, w_fc, w_out, w_proj = refs[:7]
    send_sem, recv_sem, extra_send, extra_recv, local_sem, vector_sem = refs[7:13]
    raw, small, small_out = refs[13:22], refs[22], refs[23]
    buffers = refs[24:]
    core, layer, sibling, across, diagonal = neighbours()
    index = lax.axis_index("replica")
    quarter = index % 4
    low, high = index % 2, (index // 2) % 2
    beside = {"replica": index + 1 - 2 * low}
    above = {"replica": index + 2 - 4 * high}
    beside_quarter = quarter + 1 - 2 * low
    above_quarter = quarter + 2 - 4 * high
    same = core == layer
    far_quarter = 3 - quarter
    for number in range(9):
        pltpu.make_async_copy(vectors[number], raw[number], vector_sem.at[number]).start()
    greet((sibling, across, diagonal, beside, above))

    depth = qkv.shape[0]
    span = qkv.shape[1] // 6
    wide = fc.shape[1] // 2
    turn = proj.shape[0] // 2
    cols = [
        (qkv, w_qkv, lambda s, g=g: pl.multiple_of((2 * g + s) * span, span), g * span, span)
        for g in range(3)
    ]
    cols.append((fc, w_fc, lambda s: pl.multiple_of(s * wide, wide), 0, wide))
    rows = [(out, w_out, 0, out.shape[0]), (proj, w_proj, 0, turn), (proj, w_proj, turn, turn)]
    order = [0, 1, 2, 4, 3, 5, 6]

    def rows_of(item):
        return depth if item < 4 else rows[item - 4][3]

    def target(item, base, which, part=None):
        deep = rows_of(item) // 4
        start = base + which * deep
        if part is not None:
            deep = deep // 2
            start = start + part * deep
        place = pl.ds(pl.multiple_of(start, deep), deep)
        if item < 4:
            return cols[item][1].at[place, pl.ds(cols[item][3], cols[item][4])]
        return rows[item - 4][1].at[place]

    def base_of(item, shard):
        return shard * depth if item < 4 else rows[item - 4][2]

    def remote(stage, item, source, dest, device, lane=0):
        return pltpu.make_async_remote_copy(
            src_ref=source,
            dst_ref=dest,
            send_sem=send_sem.at[stage + lane, item],
            recv_sem=recv_sem.at[stage, item],
            device_id=device,
            device_id_type=MESH,
        )

    def cross(item, receiver):
        deep = rows_of(item) // 4
        place = pl.multiple_of(base_of(item, 0) + quarter * deep, deep)
        dest = target(item, base_of(item, layer), quarter)
        if item < 4:
            columns = cols[item][2](receiver)
            source = cols[item][0].at[pl.ds(place, deep), pl.ds(columns, cols[item][4])]
        else:
            source = rows[item - 4][0].at[pl.ds(place, deep)]
        return source, dest

    def cross_same(item):
        return remote(0, item, *cross(item, core), across, 5)

    def cross_swap(item):
        return remote(0, item, *cross(item, 1 - core), diagonal)

    def pass_on(stage, item, which, device, part=None):
        here = target(item, base_of(item, 1 - layer), which, part)
        return remote(stage, item, here, here, device)

    def to_sibling(item):
        columns = cols[item][2](1 - core)
        source = cols[item][0].at[:, pl.ds(columns, cols[item][4])]
        start = pl.multiple_of(layer * depth, depth)
        dest = cols[item][1].at[pl.ds(start, depth), pl.ds(cols[item][3], cols[item][4])]
        return remote(6, item, source, dest, sibling)

    def through(source, dest, number):
        return (
            lambda: pltpu.make_async_copy(source, buffers[number], local_sem.at[number]),
            lambda: pltpu.make_async_copy(buffers[number], dest, local_sem.at[number]),
        )

    def keep_local(item):
        if item < 4:
            columns = cols[item][2](core)
            source = cols[item][0].at[:, pl.ds(columns, cols[item][4])]
            start = pl.multiple_of(layer * depth, depth)
            dest = cols[item][1].at[pl.ds(start, depth), pl.ds(cols[item][3], cols[item][4])]
        else:
            source, dest, start, deep = rows[item - 4]
            source, dest = source.at[pl.ds(start, deep)], dest.at[pl.ds(start, deep)]
        return through(source, dest, item)

    part = tokens.shape[1]
    half = part // 2

    def outer_rows(shard, which):
        return pl.ds(pl.multiple_of(shard * part + which * half, half), half)

    def outer_cross(block):
        place = pl.ds(pl.multiple_of(core * half, half), half)

        def copy(source):
            return pltpu.make_async_remote_copy(
                src_ref=source.at[block, place],
                dst_ref=outer[block].at[outer_rows(layer, core)],
                send_sem=extra_send.at[block],
                recv_sem=extra_recv.at[block],
                device_id=across,
                device_id_type=MESH,
            )

        return copy

    def outer_pass(block):
        here = outer[block].at[outer_rows(1 - layer, core)]
        return pltpu.make_async_remote_copy(
            src_ref=here,
            dst_ref=here,
            send_sem=extra_send.at[2 + block],
            recv_sem=extra_recv.at[2 + block],
            device_id=sibling,
            device_id_type=MESH,
        )

    def outer_local(source, block):
        place = pl.ds(pl.multiple_of(layer * part, part), part)
        return through(source.at[block], outer[block].at[place], 7 + block)

    def small_swap():
        return pltpu.make_async_remote_copy(
            src_ref=small,
            dst_ref=small_out.at[1 - core],
            send_sem=extra_send.at[4],
            recv_sem=extra_recv.at[4],
            device_id=diagonal,
            device_id_type=MESH,
        )

    def small_pass():
        return pltpu.make_async_remote_copy(
            src_ref=small_out.at[core],
            dst_ref=small_out.at[core],
            send_sem=extra_send.at[5],
            recv_sem=extra_recv.at[5],
            device_id=sibling,
            device_id_type=MESH,
        )

    def start_outer(block):
        @pl.when(layer == 0)
        def _():
            outer_cross(block)(cotangent).start()

        @pl.when(layer == 1)
        def _():
            outer_cross(block)(tokens).start()

    def crossings(item):
        if item < 4:
            cross_same(item).start()
        cross_swap(item).start()

    start_outer(0)

    @pl.when(core != layer)
    def _():
        crossings(order[0])
        crossings(order[1])
        crossings(order[2])

    @pl.when(layer == 0)
    def _():
        for block in range(2):
            outer_local(tokens, block)[0]().start()

    @pl.when(layer == 1)
    def _():
        for block in range(2):
            outer_local(cotangent, block)[0]().start()

    @pl.when(same)
    def _():
        for item in range(4):
            to_sibling(item).start()

    span_small = small.shape[1]
    for number in range(9):
        pltpu.make_async_copy(vectors[number], raw[number], vector_sem.at[number]).wait()
        values = raw[number][...].astype(F32)
        for index in range(values.shape[1] // span_small):
            row = number + index
            small[row : row + 1, :] = values[:, index * span_small : (index + 1) * span_small]

    @pl.when(same)
    def _():
        small_out[core] = small[...]

    @pl.when(core != layer)
    def _():
        small_swap().start()
        small_swap().wait_recv()

    small_pass().start()
    for block in range(2):
        load, store = outer_local(tokens, block)
        load().wait()
        store().start()

    @pl.when(same)
    def _():
        for item in range(7):
            keep_local(item)[0]().start()

    def relay(sequence, ahead):
        def onward(item):
            pass_on(1, item, beside_quarter, beside).wait_recv()
            pass_on(4, item, beside_quarter, above, 0).start()
            pass_on(2, item, above_quarter, above).wait_recv()
            pass_on(3, item, above_quarter, beside, 1).start()

        for number, item in enumerate(sequence):
            pass_on(0, item, quarter, beside).wait_recv()
            if ahead and number + 3 < len(sequence):
                crossings(sequence[number + 3])
            pass_on(1, item, quarter, beside).start()
            pass_on(2, item, quarter, above).start()
            if number >= 1:
                onward(sequence[number - 1])
            if number == 0:
                outer_cross(0)(tokens).wait_recv()
                outer_pass(0).start()
            if number == len(sequence) - 2:
                start_outer(1)
        onward(sequence[-1])
        for item in sequence:
            pass_on(3, item, far_quarter, beside, 1).wait_recv()
            pass_on(4, item, far_quarter, above, 0).wait_recv()
            for stage in (1, 2):
                pass_on(stage, item, quarter, beside).wait_send()
            for stage, which in ((3, 1), (4, 0)):
                pass_on(stage, item, quarter, beside, which).wait_send()

    @pl.when(same)
    def _():
        for item in range(7):
            load, store = keep_local(item)
            load().wait()
            store().start()
        relay([0, 1, 2, 3], False)
        for item in range(4):
            to_sibling(item).wait_send()
        for item in range(7):
            keep_local(item)[1]().wait()

    @pl.when(core != layer)
    def _():
        relay(order, True)
        for item in range(4):
            to_sibling(item).wait_recv()
            cross_same(item).wait_send()
        for item in range(7):
            cross_swap(item).wait_send()
        small_swap().wait_send()

    outer_cross(1)(tokens).wait_recv()
    outer_pass(1).start()
    for block in range(2):
        outer_local(tokens, block)[1]().wait()
    small_pass().wait()
    params[...] = jnp.zeros_like(params)
    for side in range(2):
        lanes = slice(side * span_small, (side + 1) * span_small)
        params[0:6, lanes] = small_out[side, 0:6]
        for row in range(3):
            line = 6 + 2 * row + side
            params[6 + row : 7 + row, lanes] = small_out[core, line : line + 1]
    for block in range(2):
        outer_cross(block)(tokens).wait_send()
        outer_pass(block).wait()


def fetch_inputs(tokens, cotangent, qkv, fc, out, proj, vectors):
    spot = pl.BlockSpec(memory_space=pl.ANY)
    _, part, width = tokens.shape
    shapes = [
        (2 * part, width),
        (2 * part, width),
        (2 * qkv.shape[0], qkv.shape[1] // 2),
        (2 * fc.shape[0], fc.shape[1] // 2),
        out.shape,
        proj.shape,
    ]
    return pl.pallas_call(
        fetch_kernel,
        out_shape=[jax.ShapeDtypeStruct(shape, BF) for shape in shapes[:2]]
        + [jax.ShapeDtypeStruct((16, width), F32)]
        + [jax.ShapeDtypeStruct(shape, BF) for shape in shapes[2:]],
        in_specs=[spot] * 15,
        out_specs=[spot] * 2 + [pl.BlockSpec(memory_space=pltpu.VMEM)] + [spot] * 4,
        scratch_shapes=[
            pltpu.SemaphoreType.DMA((7, 7)),
            pltpu.SemaphoreType.DMA((7, 7)),
            pltpu.SemaphoreType.DMA((6,)),
            pltpu.SemaphoreType.DMA((6,)),
            pltpu.SemaphoreType.DMA((9,)),
            pltpu.SemaphoreType.DMA((9,)),
        ]
        + [pltpu.VMEM(item.shape, BF) for item in vectors]
        + [pltpu.VMEM((16, width // 2), F32), pltpu.VMEM((2, 16, width // 2), F32)]
        + [pltpu.VMEM((qkv.shape[0], qkv.shape[1] // 6), BF)] * 3
        + [
            pltpu.VMEM((fc.shape[0], fc.shape[1] // 2), BF),
            pltpu.VMEM(out.shape, BF),
            pltpu.VMEM((proj.shape[0] // 2, width), BF),
            pltpu.VMEM((proj.shape[0] // 2, width), BF),
            pltpu.VMEM(tokens.shape[1:], BF),
            pltpu.VMEM(tokens.shape[1:], BF),
        ],
        compiler_params=pltpu.CompilerParams(
            collective_id=2, has_side_effects=True, vmem_limit_bytes=VMEM_LIMIT
        ),
        name="fetch_inputs",
    )(tokens, cotangent, qkv, fc, out, proj, *vectors)


TILES = 2


class Loads:
    def __init__(self, sem):
        self.sem, self.count, self.made = sem, 0, {}

    def start(self, name, source, buffer):
        copy = pltpu.make_async_copy(source, buffer, self.sem.at[self.count])
        self.count += 1
        copy.start()
        self.made[name] = copy

    def wait(self, *names):
        for name in names:
            self.made.pop(name).wait()


def greet_step(sender):
    core, layer, sibling, across, _ = neighbours()
    barrier = pltpu.get_barrier_semaphore()
    pl.semaphore_signal(barrier, inc=1, device_id=sibling, device_id_type=MESH)

    @pl.when(layer != sender)
    def _():
        pl.semaphore_signal(barrier, inc=1, device_id=across, device_id_type=MESH)
        pl.semaphore_wait(barrier, 1)

    @pl.when(layer == sender)
    def _():
        pl.semaphore_wait(barrier, 2)


class Exchange:
    def __init__(self, send_buf, recv_buf, send_sem, recv_sem):
        self.refs = (send_buf, recv_buf, send_sem, recv_sem)

    def copy(self, slot):
        send_buf, recv_buf, send_sem, recv_sem = self.refs
        return pltpu.make_async_remote_copy(
            src_ref=send_buf.at[slot],
            dst_ref=recv_buf.at[slot],
            send_sem=send_sem.at[slot],
            recv_sem=recv_sem.at[slot],
            device_id={"section": 1 - lax.axis_index("section")},
            device_id_type=MESH,
        )

    def give(self, slot, partial):
        self.refs[0][slot] = partial.astype(BF)
        self.copy(slot).start()

    def take(self, slot):
        self.copy(slot).wait_recv()
        return self.refs[1][slot].astype(F32)

    def finish(self, count):
        for slot in range(count):
            self.copy(slot).wait_send()


class Across:
    def __init__(self, sender, source, dest, sems):
        self.sender, self.source, self.dest, self.sems = sender, source, dest, sems
        self.core, self.layer, self.sibling, self.across, _ = neighbours()

    def copy(self, tile, stage):
        rows = self.dest.shape[0] // (2 * TILES)
        place = pl.ds(pl.multiple_of((2 * tile + self.core) * rows, rows), rows)
        source = self.source if stage == 0 else self.dest
        return pltpu.make_async_remote_copy(
            src_ref=source.at[place],
            dst_ref=self.dest.at[place],
            send_sem=self.sems.at[stage, tile],
            recv_sem=self.sems.at[2 + stage, tile],
            device_id=self.across if stage == 0 else self.sibling,
            device_id_type=MESH,
        )

    def send(self, tile):
        @pl.when(self.layer == self.sender)
        def _():
            self.copy(tile, 0).start()

    def receive(self, tile):
        @pl.when(self.layer != self.sender)
        def _():
            self.copy(tile, 0).wait_recv()
            self.copy(tile, 1).start()

    def complete(self, tile):
        @pl.when(self.layer != self.sender)
        def _():
            self.copy(tile, 1).wait_recv()

    def finish(self, tile):
        @pl.when(self.layer == self.sender)
        def _():
            self.copy(tile, 0).wait_send()

        @pl.when(self.layer != self.sender)
        def _():
            self.copy(tile, 1).wait_send()


class Opening:
    def __init__(self, starting, sender, late, refs, earlier, buffer, load_sems, sems):
        self.starting, self.sender, self.late, self.refs = starting, sender, late, refs
        self.buffer, self.load_sems, self.layer = buffer, load_sems, lax.axis_index("shard")
        self.across = Across(sender, earlier, buffer, sems)

    def load(self, ref, tile):
        rows = self.buffer.shape[0] // TILES
        place = pl.ds(tile * rows, rows)
        return pltpu.make_async_copy(ref.at[place], self.buffer.at[place], self.load_sems[tile])

    def start(self):
        for layer, ref in enumerate(self.refs):

            @pl.when(self.layer == layer)
            def _(ref=ref, layer=layer):
                for tile in range(TILES):
                    if not (self.starting and layer != self.sender and tile == self.late):
                        self.load(ref, tile).start()

    def send(self):
        if self.starting:
            self.across.send(self.late)

    def take(self, tile):
        if self.starting and tile == self.late:

            @pl.when(self.layer == self.sender)
            def _():
                self.load(self.refs[0], tile).wait()

            self.across.receive(tile)
            self.across.complete(tile)
        else:
            self.load(self.refs[0], tile).wait()

    def finish(self):
        if self.starting:
            self.across.finish(self.late)


def by_past(mode, body):
    if mode is not None:
        body(mode)
        return
    layer = lax.axis_index("shard")

    @pl.when(layer == 0)
    def _():
        body(True)

    @pl.when(layer != 0)
    def _():
        body(False)


FORWARD_LOADS = 7


def forward_kernel(mode, starting, ending, *refs):
    x_first, x_other, earlier, params, w_qkv, w_out, w_fc, w_proj, k_past, v_past = refs[:10]
    refs = refs[10:]
    (x_used, normed1, query, keys, values, mixed, lse, scaled2, inverse2, normed2, slope, act, out, passed) = refs[:14]
    refs = refs[14:]
    (x_v, wq_v, wo_v, wf_v, wp_v, k_v, v_v, hid_v, part_v, send_v, recv_v) = refs[:11]
    refs = refs[11:]
    (n1_v, q_v, m_v, lse_v, s2_v, i2_v, n2_v, sl_v, a_v, o_v) = refs[:10]
    load_sem, store_sem, send_sem, recv_sem, open_sem, across_sem = refs[10:]
    rows, width = x_v.shape
    half = q_v.shape[1]
    tile_rows = rows // TILES
    wide = a_v.shape[1]

    loads = Loads(load_sem)
    opening_sems = [load_sem.at[FORWARD_LOADS + tile] for tile in range(TILES)]
    opening = Opening(starting, 0, 1, (x_first, x_other), earlier, x_v, opening_sems, open_sem)
    opening.start()
    loads.start("qkv", w_qkv, wq_v)
    if mode is not False:
        loads.start("k", k_past, k_v.at[pl.ds(0, rows)])
        loads.start("v", v_past, v_v.at[pl.ds(0, rows)])
    loads.start("out", w_out, wo_v)
    loads.start("fc", w_fc, wf_v)
    loads.start("proj", w_proj, wp_v)
    greet_step(0)
    opening.send()
    exchange = Exchange(send_v, recv_v, send_sem, recv_sem)
    across = Across(0, o_v, passed, across_sem)
    stores = []

    def store(buffer, dest):
        copy = pltpu.make_async_copy(buffer, dest, store_sem.at[len(stores)])
        copy.start()
        stores.append(copy)

    def store_rows(tile, *pairs):
        place = pl.ds(tile * tile_rows, tile_rows)
        for buffer, dest in pairs:
            store(buffer.at[place], dest.at[place])

    def vector(row, start=0, size=None):
        return params[row : row + 1, start : start + (size or width)]

    def project(tile):
        span = pl.ds(tile * tile_rows, tile_rows)
        later = pl.ds(rows + tile * tile_rows, tile_rows)
        opening.take(tile)
        scaled, _ = norm_parts(x_v[span, :].astype(F32))
        normed = (scaled * vector(0) + vector(1)).astype(BF)
        n1_v[span, :] = normed
        if tile == 0:
            loads.wait("qkv")
        piece = jnp.dot(normed, wq_v[:, :half], preferred_element_type=F32)
        q_v[span, :] = (piece + vector(6, 0, half)).astype(BF)
        piece = jnp.dot(normed, wq_v[:, half : 2 * half], preferred_element_type=F32)
        k_v[later, :] = piece.astype(BF)
        piece = jnp.dot(normed, wq_v[:, 2 * half :], preferred_element_type=F32)
        v_v[later, :] = (piece + vector(6, half, half)).astype(BF)
        store_rows(tile, (x_v, x_used), (n1_v, normed1), (q_v, query))

    def attend(tile):
        span = pl.ds(tile * tile_rows, tile_rows)

        def attention(past):
            length = (rows if past else 0) + (tile + 1) * tile_rows
            reach = pl.ds(0 if past else rows, length)

            def pair(number, carry):
                lanes = pl.ds(pl.multiple_of(number * 128, 128), 128)
                key, value = k_v[reach, lanes], v_v[reach, lanes]
                pieces = []
                for head, part in enumerate(head_parts(q_v[span, lanes])):
                    scores = masked_scores(key, part * BF(HEAD_DIM**-0.5), length)
                    top = jnp.max(scores, axis=0, keepdims=True)
                    probs = jnp.exp(scores - top)
                    total = jnp.sum(probs, axis=0, keepdims=True)
                    lse_v[number, pl.ds(head, 1), span] = top + jnp.log(total)
                    piece = rows_product(value, probs.astype(BF))
                    piece = piece[head * HEAD_DIM : (head + 1) * HEAD_DIM]
                    pieces.append(piece * (1.0 / total))
                m_v[span, lanes] = jnp.transpose(jnp.concatenate(pieces, axis=0)).astype(BF)
                return carry

            lax.fori_loop(0, half // 128, pair, 0, unroll=mode is not None)

        by_past(mode, attention)
        partial = jnp.dot(m_v[span, :], wo_v[...], preferred_element_type=F32)
        part_v[tile] = partial
        exchange.give(tile, partial)

    def expand(tile):
        span = pl.ds(tile * tile_rows, tile_rows)
        hidden = x_v[span, :].astype(F32) + (part_v[tile] + exchange.take(tile)) + vector(2)
        hid_v[span, :] = hidden
        scaled, inverse = norm_parts(hidden)
        s2_v[span, :] = scaled.astype(BF)
        i2_v[span, :] = jnp.broadcast_to(inverse, (tile_rows, 128))
        normed = (scaled * vector(3) + vector(4)).astype(BF)
        n2_v[span, :] = normed
        store_rows(tile, (s2_v, scaled2), (i2_v, inverse2), (n2_v, normed2))
        chunk = width // 2
        for part in range(wide // chunk):
            columns = pl.ds(part * chunk, chunk)
            pre = jnp.dot(normed, wf_v[:, columns], preferred_element_type=F32)
            bias = vector(7 + part * chunk // width, part * chunk % width, chunk)
            activated, inclined = gelu_pair(pre + bias)
            a_v[span, columns] = activated.astype(BF)
            sl_v[span, columns] = inclined.astype(BF)
        store_rows(tile, (sl_v, slope), (a_v, act))
        partial = jnp.dot(a_v[span, :], wp_v[...], preferred_element_type=F32)
        part_v[TILES + tile] = partial
        exchange.give(TILES + tile, partial)

    def conclude(tile):
        span = pl.ds(tile * tile_rows, tile_rows)
        total = part_v[TILES + tile] + exchange.take(TILES + tile)
        o_v[span, :] = (hid_v[span, :] + total + vector(5)).astype(BF)
        store_rows(tile, (o_v, out))

    own_rows = pl.ds(rows, rows)
    project(0)
    if mode is not False:
        loads.wait("k", "v")
    loads.wait("out")
    attend(0)
    project(1)
    store(k_v.at[own_rows], keys)
    store(v_v.at[own_rows], values)
    loads.wait("fc", "proj")
    if ending:
        expand(0)
    attend(1)
    store(m_v, mixed)
    store(lse_v, lse)
    if ending:
        conclude(0)
        across.send(0)
        expand(1)
        across.receive(0)
    else:
        expand(0)
        expand(1)
        conclude(0)
    conclude(1)
    for copy in stores:
        copy.wait()
    exchange.finish(2 * TILES)
    opening.finish()
    if ending:
        across.complete(0)
        across.finish(0)


def step_sems(loads, stores):
    return [
        pltpu.SemaphoreType.DMA((loads,)),
        pltpu.SemaphoreType.DMA((stores,)),
        pltpu.SemaphoreType.DMA((2 * TILES,)),
        pltpu.SemaphoreType.DMA((2 * TILES,)),
        pltpu.SemaphoreType.DMA((4, TILES)),
        pltpu.SemaphoreType.DMA((4, TILES)),
    ]


def forward_step(mode, starting, ending, inputs, params, weights, past):
    rows, width = inputs[0].shape
    half = width // 2
    wide = weights[2].shape[1]
    pairs = half // 128
    tile_rows = rows // TILES
    spot = pl.BlockSpec(memory_space=pl.ANY)
    low = lambda columns: ((rows, columns), BF)
    outs = [
        low(width),
        low(width),
        low(half),
        low(half),
        low(half),
        low(half),
        ((pairs, 8, rows), F32),
        low(width),
        ((rows, 128), F32),
        low(width),
        low(wide),
        low(wide),
        low(width),
        low(width),
    ]
    scratch = [
        low(width),
        *((item.shape, BF) for item in weights),
        ((2 * rows, half), BF),
        ((2 * rows, half), BF),
        ((rows, width), F32),
        ((2 * TILES, tile_rows, width), F32),
        ((2 * TILES, tile_rows, width), BF),
        ((2 * TILES, tile_rows, width), BF),
        low(width),
        low(half),
        low(half),
        ((pairs, 8, rows), F32),
        low(width),
        ((rows, 128), F32),
        low(width),
        low(wide),
        low(wide),
        low(width),
    ]
    number = {False: 3, None: 4, True: 5}[mode]
    return pl.pallas_call(
        functools.partial(forward_kernel, mode, starting, ending),
        out_shape=[jax.ShapeDtypeStruct(*item) for item in outs],
        in_specs=[spot] * 3 + [pl.BlockSpec(memory_space=pltpu.VMEM)] + [spot] * 6,
        out_specs=[spot] * len(outs),
        scratch_shapes=[pltpu.VMEM(*item) for item in scratch]
        + step_sems(FORWARD_LOADS + TILES, 2 * len(outs)),
        compiler_params=pltpu.CompilerParams(
            collective_id=number, has_side_effects=True, vmem_limit_bytes=VMEM_LIMIT
        ),
        name="forward_step",
    )(*inputs, params, *weights, *past)


BACKWARD_LOADS = 17


def backward_kernel(mode, starting, ending, *refs):
    (g_first, g_other, earlier, x_used, params, w_qkv, w_out, w_fc, w_proj) = refs[:9]
    (query, keys, values, k_past, v_past, mixed, lse, scaled2, inverse2, slope, pend_k, pend_v) = refs[9:21]
    refs = refs[21:]
    (g_used, d_qkv, d_branch, d_pre, out, next_k, next_v, sums, passed) = refs[:9]
    refs = refs[9:]
    (g_v, x_v, wq_v, wo_v, wf_v, wp_v, q_v, k_v, v_v, m_v, lse_v, s2_v, i2_v, sl_v) = refs[:14]
    refs = refs[14:]
    (dk_v, dv_v, hid_v, part_v, send_v, recv_v, dqkv_v, db_v, dp_v, dm_v, o_v, sum_v) = refs[:12]
    load_sem, store_sem, send_sem, recv_sem, open_sem, across_sem = refs[12:]
    rows, width = x_v.shape
    half = q_v.shape[1]
    wide = dp_v.shape[1]
    tile_rows = rows // TILES
    own_rows, past_rows = pl.ds(rows, rows), pl.ds(0, rows)
    scale = HEAD_DIM**-0.5

    loads = Loads(load_sem)
    opening_sems = [load_sem.at[BACKWARD_LOADS + tile] for tile in range(TILES)]
    opening = Opening(starting, 1, 0, (g_first, g_other), earlier, g_v, opening_sems, open_sem)
    opening.start()
    loads.start("proj", w_proj, wp_v)
    loads.start("slope", slope, sl_v)
    loads.start("fc", w_fc, wf_v)
    loads.start("scaled2", scaled2, s2_v)
    loads.start("inverse2", inverse2, i2_v)
    loads.start("out", w_out, wo_v)
    loads.start("q", query, q_v)
    loads.start("k", keys, k_v.at[own_rows])
    loads.start("v", values, v_v.at[own_rows])
    if mode is not False:
        loads.start("k_past", k_past, k_v.at[past_rows])
        loads.start("v_past", v_past, v_v.at[past_rows])
    loads.start("mixed", mixed, m_v)
    loads.start("lse", lse, lse_v)
    if mode is not True:
        loads.start("pend_k", pend_k, dk_v.at[own_rows])
        loads.start("pend_v", pend_v, dv_v.at[own_rows])
    loads.start("qkv", w_qkv, wq_v)
    loads.start("x", x_used, x_v)
    greet_step(1)
    opening.send()
    exchange = Exchange(send_v, recv_v, send_sem, recv_sem)
    across = Across(1, o_v, passed, across_sem)
    stores = []

    def store(buffer, dest):
        copy = pltpu.make_async_copy(buffer, dest, store_sem.at[len(stores)])
        copy.start()
        stores.append(copy)

    def store_rows(tile, *pairs):
        place = pl.ds(tile * tile_rows, tile_rows)
        for buffer, dest in pairs:
            store(buffer.at[place], dest.at[place])

    def vector(row, start=0, size=None):
        return params[row : row + 1, start : start + (size or width)]

    sum_v[...] = jnp.zeros_like(sum_v)

    def tally(row, piece, start=0):
        place = (slice(row, row + 1), slice(start, start + piece.shape[1]))
        sum_v[place] += jnp.sum(piece, axis=0, keepdims=True)

    def contract(tile):
        span = pl.ds(tile * tile_rows, tile_rows)
        opening.take(tile)
        grad = g_v[span, :]
        chunk = width // 2
        for part in range(wide // chunk):
            columns = pl.ds(part * chunk, chunk)
            d_act = cols_product(grad, wp_v[columns, :])
            piece = (d_act * sl_v[span, columns].astype(F32)).astype(BF)
            dp_v[span, columns] = piece
            tally(7 + part * chunk // width, piece.astype(F32), part * chunk % width)
        partial = cols_product(dp_v[span, :], wf_v[...])
        part_v[tile] = partial
        exchange.give(tile, partial)
        tally(5, grad.astype(F32))
        store_rows(tile, (g_v, g_used), (dp_v, d_pre))

    def branch(tile):
        span = pl.ds(tile * tile_rows, tile_rows)
        d_normed = part_v[tile] + exchange.take(tile)
        scaled = s2_v[span, :].astype(F32)
        tally(3, d_normed * scaled)
        tally(4, d_normed)
        d_hidden = g_v[span, :].astype(F32) + norm_backward(
            d_normed, scaled, i2_v[span, 0:1], vector(3)
        )
        hid_v[span, :] = d_hidden
        low = d_hidden.astype(BF)
        db_v[span, :] = low
        tally(2, low.astype(F32))
        dm_v[span, :] = cols_product(low, wo_v[...]).astype(BF)
        store_rows(tile, (db_v, d_branch))

    def attend(tile):
        span = pl.ds(tile * tile_rows, tile_rows)

        def attention(past):
            if past and tile == TILES - 1:
                dk_v[...] = jnp.zeros_like(dk_v)
                dv_v[...] = jnp.zeros_like(dv_v)
            length = (rows if past else 0) + (tile + 1) * tile_rows
            reach = pl.ds(0 if past else rows, length)

            def pair(number, carry):
                lanes = pl.ds(pl.multiple_of(number * 128, 128), 128)
                key, value = k_v[reach, lanes], v_v[reach, lanes]
                grads = dm_v[span, lanes]
                products = jnp.transpose(grads.astype(F32) * m_v[span, lanes].astype(F32))
                queries, grads = head_parts(q_v[span, lanes]), head_parts(grads)
                d_query = []
                d_key = d_value = None
                for head in range(2):
                    take = slice(head * HEAD_DIM, (head + 1) * HEAD_DIM)
                    scaled_query = queries[head] * BF(scale)
                    scores = masked_scores(key, scaled_query, length)
                    weights = jnp.exp(scores - lse_v[number, pl.ds(head, 1), span])
                    d_probs = cols_product(value, grads[head])
                    delta = jnp.sum(products[take], axis=0, keepdims=True)
                    d_scores = (weights * (d_probs - delta)).astype(BF)
                    one = jnp.dot(weights.astype(BF), grads[head], preferred_element_type=F32)
                    two = jnp.dot(d_scores, scaled_query, preferred_element_type=F32)
                    d_value = one if head == 0 else d_value + one
                    d_key = two if head == 0 else d_key + two
                    d_query.append(rows_product(key, d_scores)[take])
                dk_v[reach, lanes] += d_key
                dv_v[reach, lanes] += d_value
                d_query = jnp.transpose(jnp.concatenate(d_query, axis=0) * scale)
                dqkv_v[span, lanes] = d_query.astype(BF)
                return carry

            lax.fori_loop(0, half // 128, pair, 0, unroll=mode is not None)

        by_past(mode, attention)

    def project(tile):
        span = pl.ds(tile * tile_rows, tile_rows)
        later = pl.ds(rows + tile * tile_rows, tile_rows)
        dqkv_v[span, half : 2 * half] = dk_v[later, :].astype(BF)
        dqkv_v[span, 2 * half :] = dv_v[later, :].astype(BF)
        piece = dqkv_v[span, :]
        partial = cols_product(piece, wq_v[...])
        part_v[TILES + tile] = partial
        exchange.give(TILES + tile, partial)
        tally(6, piece[:, :half].astype(F32))
        tally(6, piece[:, 2 * half :].astype(F32), half)
        store_rows(tile, (dqkv_v, d_qkv))

    def conclude(tile):
        span = pl.ds(tile * tile_rows, tile_rows)
        scaled, inverse = norm_parts(x_v[span, :].astype(F32))
        d_normed = part_v[TILES + tile] + exchange.take(TILES + tile)
        tally(0, d_normed * scaled)
        tally(1, d_normed)
        d_inputs = hid_v[span, :] + norm_backward(d_normed, scaled, inverse, vector(0))
        o_v[span, :] = d_inputs.astype(BF)
        store_rows(tile, (o_v, out))

    loads.wait("proj", "slope", "fc")
    contract(1)
    if not starting:
        contract(0)
    loads.wait("scaled2", "inverse2", "out")
    branch(1)
    loads.wait("q", "k", "v", "mixed", "lse")
    if mode is not False:
        loads.wait("k_past", "v_past")
    if mode is not True:
        loads.wait("pend_k", "pend_v")
    attend(1)
    loads.wait("qkv", "x")
    if starting and not ending:
        contract(0)
    project(1)
    if starting and ending:
        contract(0)
    else:
        branch(0)
    if ending:
        conclude(1)
        across.send(1)
    if starting and ending:
        branch(0)
    attend(0)
    if mode is not False:
        store(dk_v.at[past_rows], next_k)
        store(dv_v.at[past_rows], next_v)
    project(0)
    if ending:
        across.receive(1)
    else:
        conclude(1)
    conclude(0)
    store(sum_v, sums)
    for copy in stores:
        copy.wait()
    exchange.finish(2 * TILES)
    opening.finish()
    if ending:
        across.complete(1)
        across.finish(1)


def backward_step(mode, starting, ending, grads, inputs, params, weights, kept, pending):
    rows, width = inputs.shape
    half = width // 2
    wide = weights[2].shape[1]
    pairs = half // 128
    tile_rows = rows // TILES
    spot = pl.BlockSpec(memory_space=pl.ANY)
    low = lambda columns: ((rows, columns), BF)
    outs = [
        low(width),
        low(3 * half),
        low(width),
        low(wide),
        low(width),
        ((rows, half), F32),
        ((rows, half), F32),
        ((16, width), F32),
        low(width),
    ]
    scratch = [
        low(width),
        low(width),
        *((item.shape, BF) for item in weights),
        low(half),
        ((2 * rows, half), BF),
        ((2 * rows, half), BF),
        low(half),
        ((pairs, 8, rows), F32),
        low(width),
        ((rows, 128), F32),
        low(wide),
        ((2 * rows, half), F32),
        ((2 * rows, half), F32),
        ((rows, width), F32),
        ((2 * TILES, tile_rows, width), F32),
        ((2 * TILES, tile_rows, width), BF),
        ((2 * TILES, tile_rows, width), BF),
        low(3 * half),
        low(width),
        low(wide),
        low(half),
        low(width),
        ((16, width), F32),
    ]
    number = {True: 6, None: 7, False: 8}[mode]
    return pl.pallas_call(
        functools.partial(backward_kernel, mode, starting, ending),
        out_shape=[jax.ShapeDtypeStruct(*item) for item in outs],
        in_specs=[spot] * 4 + [pl.BlockSpec(memory_space=pltpu.VMEM)] + [spot] * 16,
        out_specs=[spot] * len(outs),
        scratch_shapes=[pltpu.VMEM(*item) for item in scratch]
        + step_sems(BACKWARD_LOADS + TILES, 2 * len(outs)),
        compiler_params=pltpu.CompilerParams(
            collective_id=number, has_side_effects=True, vmem_limit_bytes=VMEM_LIMIT
        ),
        name="backward_step",
    )(*grads, inputs, params, *weights, *kept, *pending)


def shards(
    tokens,
    cotangent,
    attn_gain,
    attn_shift,
    qkv_weight,
    query_bias,
    value_bias,
    out_weight,
    out_bias,
    mlp_gain,
    mlp_shift,
    fc_weight,
    fc_bias,
    proj_weight,
    proj_bias,
):
    size = lax.axis_size("replica")
    micro = tokens.shape[1]
    assert micro == 2
    *outer, params, w_qkv, w_fc, w_out, w_proj = fetch_inputs(
        tokens[0],
        cotangent[0],
        qkv_weight[0],
        fc_weight[0],
        out_weight[0],
        proj_weight[0],
        (
            attn_gain,
            attn_shift,
            out_bias,
            mlp_gain,
            mlp_shift,
            proj_bias,
            query_bias,
            value_bias,
            fc_bias,
        ),
    )
    weights = (w_qkv, w_out, w_fc, w_proj)

    received, kept_list, outputs, past, got = [], [], [], (w_out, w_out), outer[0]
    for step in range(micro + 1):
        output = outputs[-1] if outputs else outer[0]
        used, normed1, *state, normed2, slope, act, output, got = forward_step(
            (False, None, True)[step],
            step > 0,
            step < micro,
            (outer[min(step, micro - 1)], got, output),
            params,
            weights,
            past,
        )
        query, keys, values, mixed, lse, scaled2, inverse2 = state
        outputs.append(output)
        received.append(used)
        kept = (query, keys, values, *past, mixed, lse, scaled2, inverse2, slope)
        kept_list.append((kept, normed1, normed2, act))
        past = (keys, values)

    pending = (params, params)
    grad_received, terms_list, results, tallies, got = [], [], [], [], outer[1]
    for step in range(micro + 1):
        last = micro - step
        kept, normed1, normed2, act = kept_list[last]
        result = results[-1] if results else outer[1]
        grad, d_qkv, d_branch, d_pre, result, *pending, vector, got = backward_step(
            (True, None, False)[step],
            step > 0,
            step < micro,
            (got, outer[max(micro - 1 - step, 0)], result),
            received[last],
            params,
            weights,
            kept,
            pending,
        )
        results.append(result)
        grad_received.append(grad)
        tallies.append(vector)
        terms_list.append((normed1, d_qkv, kept[5], d_branch, normed2, d_pre, act, grad))
    def factor(number):
        return tuple(terms_list[step][number] for step in (2, 1, 0))

    factors = [(factor(i), factor(i + 1)) for i in (0, 4, 2, 6)]
    reduced = ring_scatter(factors, tallies, size)
    reduced, packed = reduced[:4], reduced[4]
    near = []
    for i in range(micro):
        near += [outputs[i], outputs[i + 1], received[i + 1]]
        near += [results[micro - i], results[micro - 1 - i], grad_received[micro - i]]
    *gathered, activations, input_grads = ring_gather(reduced, (3, 1), near, size)
    finished = finish(gathered, packed, (activations, input_grads))
    qkv_grad, fc_grad, out_grad, proj_grad = (item[None] for item in finished[:4])
    vectors = finished[4:13]
    activations, input_grads = finished[13:]
    return (
        activations[None, None],
        input_grads[None, None],
        vectors[0],
        vectors[1],
        qkv_grad,
        vectors[6],
        vectors[7],
        out_grad,
        vectors[2],
        vectors[3],
        vectors[4],
        fc_grad,
        vectors[8],
        proj_grad,
        vectors[5],
    )


def solution(mesh):
    block = P("replica", None, "shard", None)
    layers = P("section", "replica", None, "shard", None)
    vector = P("section", "shard")
    matrix = P("section", "shard", None)
    kinds = (
        vector,
        vector,
        matrix,
        vector,
        vector,
        matrix,
        vector,
        vector,
        vector,
        matrix,
        vector,
        matrix,
        vector,
    )
    return jax.shard_map(
        shards,
        mesh=mesh,
        in_specs=(block, block) + kinds,
        out_specs=(layers, layers) + kinds,
        check_vma=False,
    )
```

```python
import functools

import jax
import jax.numpy as jnp
from jax import lax
from jax.experimental import pallas as pl
from jax.experimental.pallas import tpu as pltpu
from jax.sharding import PartitionSpec as P

HEAD_DIM = 64
EPSILON = 1e-05
GELU_SCALE = 0.7978845608028654
GELU_CUBIC = 0.044715
ROWS_CONTRACT = (((0,), (0,)), ((), ()))
COLS_CONTRACT = (((1,), (1,)), ((), ()))
BF = jnp.bfloat16
F32 = jnp.float32
MESH = pl.DeviceIdType.MESH
QTILE = 256
VMEM_LIMIT = 56 * 1024 * 1024


def rows_product(left, right):
    return lax.dot_general(left, right, ROWS_CONTRACT, preferred_element_type=F32)


def cols_product(left, right):
    return lax.dot_general(left, right, COLS_CONTRACT, preferred_element_type=F32)


def norm_parts(inputs):
    mean = jnp.mean(inputs, axis=-1, keepdims=True)
    centered = inputs - mean
    inverse = lax.rsqrt(jnp.mean(centered * centered, axis=-1, keepdims=True) + EPSILON)
    return centered * inverse, inverse


def norm_backward(d_normed, scaled, inverse, gain):
    d_scaled = d_normed * gain
    return inverse * (
        d_scaled
        - jnp.mean(d_scaled, axis=-1, keepdims=True)
        - scaled * jnp.mean(d_scaled * scaled, axis=-1, keepdims=True)
    )


def gelu_pair(pre):
    tangent = jnp.tanh(GELU_SCALE * (pre + GELU_CUBIC * pre * pre * pre))
    value = 0.5 * pre * (1.0 + tangent)
    slope = 0.5 * (1.0 + tangent) + 0.5 * pre * (1.0 - tangent * tangent) * GELU_SCALE * (
        1.0 + 3.0 * GELU_CUBIC * pre * pre
    )
    return value, slope


def head_parts(pair):
    low = lax.broadcasted_iota(jnp.int32, pair.shape, 1) < HEAD_DIM
    zero = jnp.zeros_like(pair)
    return jnp.where(low, pair, zero), jnp.where(low, zero, pair)


def masked_scores(keys, query, length):
    scores = cols_product(keys, query)
    tail = scores[length - QTILE :]
    key_pos = lax.broadcasted_iota(jnp.int32, tail.shape, 0)
    query_pos = lax.broadcasted_iota(jnp.int32, tail.shape, 1)
    tail = jnp.where(key_pos <= query_pos, tail, -1e30)
    if length == QTILE:
        return tail
    return jnp.concatenate([scores[: length - QTILE], tail], axis=0)


def ring_place(size):
    index = lax.axis_index("replica")
    odd = index % 2
    half = index // 2
    place = (1 - odd) * half + odd * (size - 1 - half)

    def device(spot):
        upper = spot // (size // 2)
        return (1 - upper) * (2 * spot) + upper * (2 * (size - 1 - spot) + 1)

    return place, device((place + 1) % size), device((place + size - 1) % size)


def neighbours():
    core, layer = lax.axis_index("section"), lax.axis_index("shard")
    sibling = {"section": 1 - core}
    across = {"shard": 1 - layer}
    diagonal = {"section": 1 - core, "shard": 1 - layer}
    return core, layer, sibling, across, diagonal


def greet(devices):
    barrier = pltpu.get_barrier_semaphore()
    for device in devices:
        pl.semaphore_signal(barrier, inc=1, device_id=device, device_id_type=MESH)
    pl.semaphore_wait(barrier, len(devices))


def scatter_kernel(size, count, *refs):
    sources, refs = refs[: 6 * count], refs[6 * count :]
    tallies, refs = refs[:3], refs[3:]
    out, refs = refs[:count], refs[count:]
    packed, refs = refs[0], refs[1:]
    held, refs = refs[: 2 * count], refs[2 * count :]
    own, refs = refs[:count], refs[count:]
    landed, refs = refs[:count], refs[count:]
    load_sem, send_sem, recv_sem, small_send, small_recv, swap_sem, total, small, small_out = refs
    place, following, previous = ring_place(size)
    targets = ({"replica": following}, {"replica": previous})
    core, layer, _, _, diagonal = neighbours()

    def load(number, which):
        rows = held[number].shape[0] // 2
        source = sources[3 * number + which]
        part = pl.ds(0 if which == 1 else rows, rows)
        return pltpu.make_async_copy(
            source, held[number].at[part], load_sem.at[number, 0 if which == 1 else 1]
        )

    def load_item(item):
        for number in (2 * item, 2 * item + 1):
            load(number, 1).start()

            @pl.when(layer == 0)
            def _(number=number):
                load(number, 0).start()

            @pl.when(layer != 0)
            def _(number=number):
                load(number, 2).start()

    load_item(0)
    greet(targets + (diagonal,))

    def send(way, item, source, slot):
        return pltpu.make_async_remote_copy(
            src_ref=source,
            dst_ref=landed[item].at[way, slot],
            send_sem=send_sem.at[way, item, slot],
            recv_sem=recv_sem.at[way, item, slot],
            device_id=targets[way],
            device_id_type=MESH,
        )

    def send_small(chunk, slot):
        return pltpu.make_async_remote_copy(
            src_ref=small_out.at[chunk],
            dst_ref=small_out.at[chunk],
            send_sem=small_send.at[slot],
            recv_sem=small_recv.at[slot],
            device_id=targets[0],
            device_id_type=MESH,
        )

    def chunk_of(way, slot):
        if way == 0:
            return (place + 2 * size - 2 - slot) % size
        return (place + 2 + slot) % size

    first = ((place + size - 1) % size, (place + 1) % size)
    group = size // 2

    def product(item, way, part):
        deep = own[item].shape[2]
        columns = pl.multiple_of((way * size + part * group) * deep, 128)
        left = held[2 * item][:, pl.ds(columns, group * deep)]
        result = rows_product(left, held[2 * item + 1][...])
        for index in range(group):
            own[item][way, part * group + index] = result[index * deep : (index + 1) * deep].astype(BF)

    half = small.shape[1]

    @pl.when(layer == 0)
    def _():
        total[...] = tallies[1][...] + tallies[2][...]

    @pl.when(layer != 0)
    def _():
        total[...] = tallies[0][...] + tallies[1][...]

    small[...] = jnp.zeros_like(small)
    small[0:6, :] = total[0:6, pl.ds(pl.multiple_of(core * half, half), half)]
    for row in range(3):
        for side in range(2):
            line = 6 + 2 * row + side
            small[line : line + 1, :] = total[6 + row : 7 + row, side * half : (side + 1) * half]

    def swap():
        return pltpu.make_async_remote_copy(
            src_ref=small,
            dst_ref=small_out.at[place],
            send_sem=swap_sem.at[0],
            recv_sem=swap_sem.at[1],
            device_id=diagonal,
            device_id_type=MESH,
        )

    @pl.when(core == layer)
    def _():
        small_out[place] = small[...]

    @pl.when(core != layer)
    def _():
        swap().start()

    for item in range(count):
        for number in (2 * item, 2 * item + 1):
            load(number, 1).wait()
            load(number, 0).wait()
        if item + 1 < count:
            load_item(item + 1)
        for way in range(2):
            product(item, way, first[way] // group)
            send(way, item, own[item].at[way, first[way]], 0).start()

    @pl.when(core != layer)
    def _():
        swap().wait()

    send_small(place, 0).start()

    def relay(item, way, slot):
        here = landed[item].at[way, slot]
        send(way, item, here, slot).wait_recv()
        here[...] += own[item][way, chunk_of(way, slot)]
        send(way, item, here, slot + 1).start()

    def relay_small(slot):
        chunk = (place + size - 1 - slot) % size
        send_small(chunk, slot).wait_recv()
        send_small(chunk, slot + 1).start()

    for item in range(count):
        for way in range(2):
            product(item, way, 1 - first[way] // group)
            relay(item, way, 0)
    relay_small(0)

    def step(slot, carry):
        for item in range(count):
            for way in range(2):
                relay(item, way, slot)
        relay_small(slot)
        return carry

    lax.fori_loop(1, size - 2, step, 0)
    last = size - 2
    for item in range(count):
        for way in range(2):
            here = landed[item].at[way, last]
            send(way, item, here, last).wait_recv()
            out[item][way] = here[...] + own[item][way, place]
    send_small((place + 1) % size, last).wait_recv()
    gathered = small_out[0]
    for index in range(1, size):
        gathered = gathered + small_out[index]
    packed[...] = gathered

    def finish(slot, carry):
        for item in range(count):
            for way in range(2):
                send(way, item, landed[item].at[way, slot], slot).wait_send()
        send_small(place, slot).wait_send()
        return carry

    lax.fori_loop(0, size - 1, finish, 0)


def ring_scatter(factors, tallies, size):
    count = len(factors)
    flat = [item for pair in factors for item in pair]
    half = tallies[0].shape[1] // 2
    shapes = [(2 * item[0].shape[0], item[0].shape[1]) for item in flat]
    chunks = [
        (shapes[2 * i][1] // (2 * size), shapes[2 * i + 1][1]) for i in range(count)
    ]
    whole = pl.BlockSpec(memory_space=pltpu.VMEM)
    spot = pl.BlockSpec(memory_space=pl.ANY)
    return pl.pallas_call(
        functools.partial(scatter_kernel, size, count),
        out_shape=[jax.ShapeDtypeStruct((2,) + chunk, BF) for chunk in chunks]
        + [jax.ShapeDtypeStruct((16, half), F32)],
        in_specs=[spot] * (6 * count) + [whole] * 3,
        out_specs=[whole] * (count + 1),
        scratch_shapes=[pltpu.VMEM(shape, BF) for shape in shapes]
        + [pltpu.VMEM((2, size) + chunk, BF) for chunk in chunks]
        + [pltpu.VMEM((2, size - 1) + chunk, BF) for chunk in chunks]
        + [pltpu.SemaphoreType.DMA((2 * count, 2))]
        + [pltpu.SemaphoreType.DMA((2, count, size - 1))] * 2
        + [pltpu.SemaphoreType.DMA((size - 1,))] * 2
        + [pltpu.SemaphoreType.DMA((2,))]
        + [
            pltpu.VMEM((16, 2 * half), F32),
            pltpu.VMEM((16, half), F32),
            pltpu.VMEM((size, 16, half), F32),
        ],
        compiler_params=pltpu.CompilerParams(
            collective_id=0, has_side_effects=True, vmem_limit_bytes=VMEM_LIMIT
        ),
        name="ring_scatter",
    )(*[block for item in flat for block in item], *tallies)


def gather_kernel(size, groups, *refs):
    count = 4
    own, refs = refs[:count], refs[count:]
    near, refs = refs[:12], refs[12:]
    out, refs = refs[:count], refs[count:]
    placed, refs = refs[:2], refs[2:]
    swap_send, swap_recv, send_sem, recv_sem, place_send, place_recv, load_sem, bounce = refs
    place, following, previous = ring_place(size)
    targets = ({"replica": following}, {"replica": previous})
    core, layer, sibling, across, diagonal = neighbours()
    same = core == layer
    greet(targets + (sibling, across, diagonal))

    def parts(item, source_half, sender):
        if item < len(groups):
            width = own[item].shape[2] // groups[item]
            for group in range(groups[item]):
                start = pl.multiple_of((2 * group + sender) * width, width)
                yield (
                    own[item].at[source_half, :, pl.ds(group * width, width)],
                    out[item].at[place, :, pl.ds(start, width)],
                )
        else:
            for half in range(2):
                yield own[item].at[half], out[item].at[half, place]

    def copies(item, source_half, lane, kind, device=None):
        for number, (source, target) in enumerate(parts(item, source_half, core)):
            send, recv = swap_send.at[item, lane, number], swap_recv.at[item, kind, number]
            if device is None:
                yield pltpu.make_async_copy(source, target, recv)
            else:
                yield pltpu.make_async_remote_copy(
                    src_ref=source,
                    dst_ref=target,
                    send_sem=send,
                    recv_sem=recv,
                    device_id=device,
                    device_id_type=MESH,
                )

    @pl.when(same)
    def _():
        for item in range(count):
            for copy in copies(item, layer, 0, 0):
                copy.start()
            if item < len(groups):
                for copy in copies(item, 1 - layer, 0, 2, across):
                    copy.start()

    @pl.when(core != layer)
    def _():
        for item in range(count):
            for copy in copies(item, 1 - layer, 0, 3, diagonal):
                copy.start()
            if item < len(groups):
                for copy in copies(item, layer, 1, 1, sibling):
                    copy.start()

    part = placed[0].shape[1]

    def near_rows(number, block, shard):
        return near[6 * block + number].at[pl.ds(shard * part, part)]

    def place_remote(kind, block):
        number, shard = ((1, 0), (3, 1))[kind]
        return pltpu.make_async_remote_copy(
            src_ref=near_rows(number, block, shard),
            dst_ref=placed[kind].at[block],
            send_sem=place_send.at[block],
            recv_sem=place_recv.at[block],
            device_id=across,
            device_id_type=MESH,
        )

    def place_load(number, block, shard):
        lane = 2 * (number // 3) + block
        return pltpu.make_async_copy(near_rows(number, block, shard), bounce.at[lane], load_sem.at[lane])

    def place_store(number, block):
        kind = number // 3
        lane = 2 * kind + block
        return pltpu.make_async_copy(bounce.at[lane], placed[kind].at[block], load_sem.at[lane])

    local = {(0, 0): (0, 3), (0, 1): (2,), (1, 0): (5,), (1, 1): (1, 4)}

    def on_device(action):
        for (at_core, at_layer), numbers in local.items():

            @pl.when((core == at_core) & (layer == at_layer))
            def _(numbers=numbers, at_layer=at_layer):
                for number in numbers:
                    for block in range(2):
                        action(number, block, at_layer)

    @pl.when(same & (layer == 1))
    def _():
        for block in range(2):
            place_remote(0, block).start()

    @pl.when(same & (layer == 0))
    def _():
        for block in range(2):
            place_remote(1, block).start()

    on_device(lambda number, block, shard: place_load(number, block, shard).start())

    def send(way, item, chunk, slot):
        if item < len(groups):
            deep = out[item].shape[1] // 2
            here = out[item].at[chunk, pl.ds(way * deep, deep)]
        else:
            here = out[item].at[way, chunk]
        return pltpu.make_async_remote_copy(
            src_ref=here,
            dst_ref=here,
            send_sem=send_sem.at[way, item, slot],
            recv_sem=recv_sem.at[way, item, slot],
            device_id=targets[way],
            device_id_type=MESH,
        )

    def chunk_of(way, slot):
        if way == 0:
            return (place + size - 1 - slot) % size
        return (place + 1 + slot) % size

    for item in range(count):

        @pl.when(same)
        def _(item=item):
            for copy in copies(item, layer, 0, 0):
                copy.wait()
            if item < len(groups):
                for copy in copies(item, layer, 1, 1, sibling):
                    copy.wait_recv()

        @pl.when(core != layer)
        def _(item=item):
            for copy in copies(item, layer, 0, 3, diagonal):
                copy.wait_recv()
            if item < len(groups):
                for copy in copies(item, layer, 0, 2, across):
                    copy.wait_recv()

        for way in range(2):
            send(way, item, place, 0).start()

    def step(slot, carry):
        for item in range(count):
            for way in range(2):
                chunk = chunk_of(way, slot)
                send(way, item, chunk, slot).wait_recv()
                send(way, item, chunk, slot + 1).start()
        return carry

    def moved(number, block, shard):
        place_load(number, block, shard).wait()
        place_store(number, block).start()

    on_device(moved)
    lax.fori_loop(0, size - 2, step, 0)
    last = size - 2
    for item in range(count):
        for way in range(2):
            send(way, item, chunk_of(way, last), last).wait_recv()
    on_device(lambda number, block, shard: place_store(number, block).wait())

    @pl.when(same)
    def _():
        for block in range(2):
            place_remote(0, block).wait_send()

    @pl.when((core != layer) & (layer == 0))
    def _():
        for block in range(2):
            place_remote(0, block).wait_recv()

    @pl.when((core != layer) & (layer == 1))
    def _():
        for block in range(2):
            place_remote(1, block).wait_recv()

    @pl.when(same)
    def _():
        for item in range(len(groups)):
            for copy in copies(item, 1 - layer, 0, 2, across):
                copy.wait_send()

    @pl.when(core != layer)
    def _():
        for item in range(count):
            for copy in copies(item, 1 - layer, 0, 3, diagonal):
                copy.wait_send()
            if item < len(groups):
                for copy in copies(item, layer, 1, 1, sibling):
                    copy.wait_send()

    def finish(slot, carry):
        for item in range(count):
            for way in range(2):
                send(way, item, place, slot).wait_send()
        return carry

    lax.fori_loop(0, size - 1, finish, 0)


def ring_gather(pieces, groups, near, size):
    spot = pl.BlockSpec(memory_space=pl.ANY)
    shapes = [(size, item.shape[1], 2 * item.shape[2]) for item in pieces[: len(groups)]]
    shapes += [(2, size) + item.shape[1:] for item in pieces[len(groups) :]]
    count = len(pieces)
    rows = (near[0].shape[0] // 2, near[0].shape[1])
    whole = pl.BlockSpec(memory_space=pltpu.VMEM)
    return pl.pallas_call(
        functools.partial(gather_kernel, size, groups),
        out_shape=[jax.ShapeDtypeStruct(shape, BF) for shape in shapes]
        + [jax.ShapeDtypeStruct((2,) + rows, BF)] * 2,
        in_specs=[whole] * count + [spot] * 12,
        out_specs=[spot] * (count + 2),
        scratch_shapes=[
            pltpu.SemaphoreType.DMA((count, 2, 3)),
            pltpu.SemaphoreType.DMA((count, 4, 3)),
        ]
        + [pltpu.SemaphoreType.DMA((2, count, size - 1))] * 2
        + [pltpu.SemaphoreType.DMA((2,))] * 2
        + [pltpu.SemaphoreType.DMA((4,)), pltpu.VMEM((4,) + rows, BF)],
        compiler_params=pltpu.CompilerParams(
            collective_id=1, has_side_effects=True, vmem_limit_bytes=VMEM_LIMIT
        ),
        name="ring_gather",
    )(*pieces, *near)


def finish_kernel(*refs):
    packed, placed, vectors, moved = refs[0], refs[1:3], refs[3:12], refs[12:14]
    bounce, load_sem = refs[14:]
    loads = [pltpu.make_async_copy(placed[i], bounce.at[i], load_sem.at[i]) for i in range(2)]
    for copy in loads:
        copy.start()
    half = packed.shape[1]
    for number in range(9):
        for index in range(vectors[number].shape[1] // half):
            row = number + index
            vectors[number][:, index * half : (index + 1) * half] = packed[row : row + 1, :]
    stores = []
    for i in range(2):
        loads[i].wait()
        copy = pltpu.make_async_copy(bounce.at[i], moved[i], load_sem.at[i])
        copy.start()
        stores.append(copy)
    for copy in stores:
        copy.wait()


def finish(packed, placed):
    spot = pl.BlockSpec(memory_space=pl.ANY)
    whole = pl.BlockSpec(memory_space=pltpu.VMEM)
    half = packed.shape[1]
    return pl.pallas_call(
        finish_kernel,
        out_shape=[jax.ShapeDtypeStruct((1, half), F32)] * 8
        + [jax.ShapeDtypeStruct((1, 4 * half), F32)]
        + [jax.ShapeDtypeStruct(item.shape, BF) for item in placed],
        in_specs=[whole] + [spot] * 2,
        out_specs=[whole] * 9 + [spot] * 2,
        scratch_shapes=[
            pltpu.VMEM((2,) + placed[0].shape, BF),
            pltpu.SemaphoreType.DMA((2,)),
        ],
        name="finish",
    )(packed, *placed)


def fetch_kernel(*refs):
    tokens, cotangent, qkv, fc, out, proj = refs[:6]
    vectors, refs = refs[6:15], refs[15:]
    *outer, params, w_qkv, w_fc, w_out, w_proj = refs[:7]
    send_sem, recv_sem, extra_send, extra_recv, local_sem, vector_sem = refs[7:13]
    raw, small, small_out = refs[13:22], refs[22], refs[23]
    buffers = refs[24:]
    core, layer, sibling, across, diagonal = neighbours()
    index = lax.axis_index("replica")
    quarter = index % 4
    low, high = index % 2, (index // 2) % 2
    beside = {"replica": index + 1 - 2 * low}
    above = {"replica": index + 2 - 4 * high}
    beside_quarter = quarter + 1 - 2 * low
    above_quarter = quarter + 2 - 4 * high
    same = core == layer
    far_quarter = 3 - quarter
    for number in range(9):
        pltpu.make_async_copy(vectors[number], raw[number], vector_sem.at[number]).start()
    greet((sibling, across, diagonal, beside, above))

    depth = qkv.shape[0]
    span = qkv.shape[1] // 6
    wide = fc.shape[1] // 2
    strip, turn = wide // 2, proj.shape[0] // 4
    cols = [
        (qkv, w_qkv, lambda s, g=g: pl.multiple_of((2 * g + s) * span, span), g * span, span)
        for g in range(3)
    ]
    cols += [
        (fc, w_fc, lambda s, g=g: pl.multiple_of(s * wide + g * strip, strip), g * strip, strip)
        for g in range(2)
    ]
    rows = [(out, w_out, 0, out.shape[0])]
    rows += [(proj, w_proj, g * turn, turn) for g in range(4)]
    narrow, total = len(cols), len(cols) + len(rows)
    order = [0, 1, 2, 5, 3, 4, 6, 7, 8, 9]

    def rows_of(item):
        return depth if item < narrow else rows[item - narrow][3]

    def target(item, base, which, part=None):
        deep = rows_of(item) // 4
        start = base + which * deep
        if part is not None:
            deep = deep // 2
            start = start + part * deep
        place = pl.ds(pl.multiple_of(start, deep), deep)
        if item < narrow:
            return cols[item][1].at[place, pl.ds(cols[item][3], cols[item][4])]
        return rows[item - narrow][1].at[place]

    def base_of(item, shard):
        return shard * depth if item < narrow else rows[item - narrow][2]

    def remote(stage, item, source, dest, device, lane=0):
        return pltpu.make_async_remote_copy(
            src_ref=source,
            dst_ref=dest,
            send_sem=send_sem.at[stage + lane, item],
            recv_sem=recv_sem.at[stage, item],
            device_id=device,
            device_id_type=MESH,
        )

    def cross(item, receiver):
        deep = rows_of(item) // 4
        place = pl.multiple_of(base_of(item, 0) + quarter * deep, deep)
        dest = target(item, base_of(item, layer), quarter)
        if item < narrow:
            columns = cols[item][2](receiver)
            source = cols[item][0].at[pl.ds(place, deep), pl.ds(columns, cols[item][4])]
        else:
            source = rows[item - narrow][0].at[pl.ds(place, deep)]
        return source, dest

    def cross_same(item):
        return remote(0, item, *cross(item, core), across, 5)

    def cross_swap(item):
        return remote(0, item, *cross(item, 1 - core), diagonal)

    def pass_on(stage, item, which, device, part=None):
        here = target(item, base_of(item, 1 - layer), which, part)
        return remote(stage, item, here, here, device)

    def to_sibling(item):
        columns = cols[item][2](1 - core)
        source = cols[item][0].at[:, pl.ds(columns, cols[item][4])]
        start = pl.multiple_of(layer * depth, depth)
        dest = cols[item][1].at[pl.ds(start, depth), pl.ds(cols[item][3], cols[item][4])]
        return remote(6, item, source, dest, sibling)

    def through(source, dest, number):
        return (
            lambda: pltpu.make_async_copy(source, buffers[number], local_sem.at[number]),
            lambda: pltpu.make_async_copy(buffers[number], dest, local_sem.at[number]),
        )

    def keep_local(item):
        if item < narrow:
            columns = cols[item][2](core)
            source = cols[item][0].at[:, pl.ds(columns, cols[item][4])]
            start = pl.multiple_of(layer * depth, depth)
            dest = cols[item][1].at[pl.ds(start, depth), pl.ds(cols[item][3], cols[item][4])]
        else:
            source, dest, start, deep = rows[item - narrow]
            source, dest = source.at[pl.ds(start, deep)], dest.at[pl.ds(start, deep)]
        return through(source, dest, item)

    part = tokens.shape[1]
    half = part // 2

    def outer_rows(shard, which):
        return pl.ds(pl.multiple_of(shard * part + which * half, half), half)

    def outer_cross(block):
        place = pl.ds(pl.multiple_of(core * half, half), half)

        def copy(source):
            return pltpu.make_async_remote_copy(
                src_ref=source.at[block, place],
                dst_ref=outer[block].at[outer_rows(layer, core)],
                send_sem=extra_send.at[block],
                recv_sem=extra_recv.at[block],
                device_id=across,
                device_id_type=MESH,
            )

        return copy

    def outer_pass(block):
        here = outer[block].at[outer_rows(1 - layer, core)]
        return pltpu.make_async_remote_copy(
            src_ref=here,
            dst_ref=here,
            send_sem=extra_send.at[2 + block],
            recv_sem=extra_recv.at[2 + block],
            device_id=sibling,
            device_id_type=MESH,
        )

    def outer_local(source, block):
        place = pl.ds(pl.multiple_of(layer * part, part), part)
        return through(source.at[block], outer[block].at[place], total + block)

    def small_swap():
        return pltpu.make_async_remote_copy(
            src_ref=small,
            dst_ref=small_out.at[1 - core],
            send_sem=extra_send.at[4],
            recv_sem=extra_recv.at[4],
            device_id=diagonal,
            device_id_type=MESH,
        )

    def small_pass():
        return pltpu.make_async_remote_copy(
            src_ref=small_out.at[core],
            dst_ref=small_out.at[core],
            send_sem=extra_send.at[5],
            recv_sem=extra_recv.at[5],
            device_id=sibling,
            device_id_type=MESH,
        )

    def start_outer(block):
        @pl.when(layer == 0)
        def _():
            outer_cross(block)(cotangent).start()

        @pl.when(layer == 1)
        def _():
            outer_cross(block)(tokens).start()

    def crossings(item):
        if item < narrow:
            cross_same(item).start()
        cross_swap(item).start()

    start_outer(0)

    @pl.when(core != layer)
    def _():
        crossings(order[0])
        crossings(order[1])
        crossings(order[2])

    @pl.when(layer == 0)
    def _():
        for block in range(2):
            outer_local(tokens, block)[0]().start()

    @pl.when(layer == 1)
    def _():
        for block in range(2):
            outer_local(cotangent, block)[0]().start()

    @pl.when(same)
    def _():
        for item in range(narrow):
            to_sibling(item).start()

    span_small = small.shape[1]
    for number in range(9):
        pltpu.make_async_copy(vectors[number], raw[number], vector_sem.at[number]).wait()
        values = raw[number][...].astype(F32)
        for index in range(values.shape[1] // span_small):
            row = number + index
            small[row : row + 1, :] = values[:, index * span_small : (index + 1) * span_small]

    @pl.when(same)
    def _():
        small_out[core] = small[...]

    @pl.when(core != layer)
    def _():
        small_swap().start()
        small_swap().wait_recv()

    small_pass().start()
    for block in range(2):
        load, store = outer_local(tokens, block)
        load().wait()
        store().start()

    @pl.when(same)
    def _():
        for item in range(total):
            keep_local(item)[0]().start()

    def relay(sequence, ahead):
        def onward(item):
            pass_on(1, item, beside_quarter, beside).wait_recv()
            pass_on(4, item, beside_quarter, above, 0).start()
            pass_on(2, item, above_quarter, above).wait_recv()
            pass_on(3, item, above_quarter, beside, 1).start()

        for number, item in enumerate(sequence):
            pass_on(0, item, quarter, beside).wait_recv()
            if ahead and number + 3 < len(sequence):
                crossings(sequence[number + 3])
            pass_on(1, item, quarter, beside).start()
            pass_on(2, item, quarter, above).start()
            if number >= 1:
                onward(sequence[number - 1])
            if number == 0:
                outer_cross(0)(tokens).wait_recv()
                outer_pass(0).start()
            if number == len(sequence) - 2:
                start_outer(1)
        onward(sequence[-1])
        for item in sequence:
            pass_on(3, item, far_quarter, beside, 1).wait_recv()
            pass_on(4, item, far_quarter, above, 0).wait_recv()
            for stage in (1, 2):
                pass_on(stage, item, quarter, beside).wait_send()
            for stage, which in ((3, 1), (4, 0)):
                pass_on(stage, item, quarter, beside, which).wait_send()

    @pl.when(same)
    def _():
        for item in range(total):
            load, store = keep_local(item)
            load().wait()
            store().start()
        relay(list(range(narrow)), False)
        for item in range(narrow):
            to_sibling(item).wait_send()
        for item in range(total):
            keep_local(item)[1]().wait()

    @pl.when(core != layer)
    def _():
        relay(order, True)
        for item in range(narrow):
            to_sibling(item).wait_recv()
            cross_same(item).wait_send()
        for item in range(total):
            cross_swap(item).wait_send()
        small_swap().wait_send()

    outer_cross(1)(tokens).wait_recv()
    outer_pass(1).start()
    for block in range(2):
        outer_local(tokens, block)[1]().wait()
    small_pass().wait()
    params[...] = jnp.zeros_like(params)
    for side in range(2):
        lanes = slice(side * span_small, (side + 1) * span_small)
        params[0:6, lanes] = small_out[side, 0:6]
        for row in range(3):
            line = 6 + 2 * row + side
            params[6 + row : 7 + row, lanes] = small_out[core, line : line + 1]
    for block in range(2):
        outer_cross(block)(tokens).wait_send()
        outer_pass(block).wait()


def fetch_inputs(tokens, cotangent, qkv, fc, out, proj, vectors):
    spot = pl.BlockSpec(memory_space=pl.ANY)
    _, part, width = tokens.shape
    shapes = [
        (2 * part, width),
        (2 * part, width),
        (2 * qkv.shape[0], qkv.shape[1] // 2),
        (2 * fc.shape[0], fc.shape[1] // 2),
        out.shape,
        proj.shape,
    ]
    return pl.pallas_call(
        fetch_kernel,
        out_shape=[jax.ShapeDtypeStruct(shape, BF) for shape in shapes[:2]]
        + [jax.ShapeDtypeStruct((16, width), F32)]
        + [jax.ShapeDtypeStruct(shape, BF) for shape in shapes[2:]],
        in_specs=[spot] * 15,
        out_specs=[spot] * 2 + [pl.BlockSpec(memory_space=pltpu.VMEM)] + [spot] * 4,
        scratch_shapes=[
            pltpu.SemaphoreType.DMA((7, 10)),
            pltpu.SemaphoreType.DMA((7, 10)),
            pltpu.SemaphoreType.DMA((6,)),
            pltpu.SemaphoreType.DMA((6,)),
            pltpu.SemaphoreType.DMA((12,)),
            pltpu.SemaphoreType.DMA((9,)),
        ]
        + [pltpu.VMEM(item.shape, BF) for item in vectors]
        + [pltpu.VMEM((16, width // 2), F32), pltpu.VMEM((2, 16, width // 2), F32)]
        + [pltpu.VMEM((qkv.shape[0], qkv.shape[1] // 6), BF)] * 3
        + [pltpu.VMEM((fc.shape[0], fc.shape[1] // 4), BF)] * 2
        + [pltpu.VMEM(out.shape, BF)]
        + [pltpu.VMEM((proj.shape[0] // 4, width), BF)] * 4
        + [
            pltpu.VMEM(tokens.shape[1:], BF),
            pltpu.VMEM(tokens.shape[1:], BF),
        ],
        compiler_params=pltpu.CompilerParams(
            collective_id=2, has_side_effects=True, vmem_limit_bytes=VMEM_LIMIT
        ),
        name="fetch_inputs",
    )(tokens, cotangent, qkv, fc, out, proj, *vectors)


TILES = 2


class Loads:
    def __init__(self, sem):
        self.sem, self.count, self.made = sem, 0, {}

    def start(self, name, source, buffer):
        copy = pltpu.make_async_copy(source, buffer, self.sem.at[self.count])
        self.count += 1
        copy.start()
        self.made[name] = copy

    def wait(self, *names):
        for name in names:
            self.made.pop(name).wait()


def greet_step(sender):
    core, layer, sibling, across, _ = neighbours()
    barrier = pltpu.get_barrier_semaphore()
    pl.semaphore_signal(barrier, inc=1, device_id=sibling, device_id_type=MESH)

    @pl.when(layer != sender)
    def _():
        pl.semaphore_signal(barrier, inc=1, device_id=across, device_id_type=MESH)
        pl.semaphore_wait(barrier, 1)

    @pl.when(layer == sender)
    def _():
        pl.semaphore_wait(barrier, 2)


class Exchange:
    def __init__(self, send_buf, recv_buf, send_sem, recv_sem):
        self.refs = (send_buf, recv_buf, send_sem, recv_sem)

    def copy(self, slot):
        send_buf, recv_buf, send_sem, recv_sem = self.refs
        return pltpu.make_async_remote_copy(
            src_ref=send_buf.at[slot],
            dst_ref=recv_buf.at[slot],
            send_sem=send_sem.at[slot],
            recv_sem=recv_sem.at[slot],
            device_id={"section": 1 - lax.axis_index("section")},
            device_id_type=MESH,
        )

    def give(self, slot, partial):
        self.refs[0][slot] = partial.astype(BF)
        self.copy(slot).start()

    def take(self, slot):
        self.copy(slot).wait_recv()
        return self.refs[1][slot].astype(F32)

    def finish(self, count):
        for slot in range(count):
            self.copy(slot).wait_send()


class Across:
    def __init__(self, sender, source, dest, sems):
        self.sender, self.source, self.dest, self.sems = sender, source, dest, sems
        self.core, self.layer, self.sibling, self.across, _ = neighbours()

    def copy(self, tile, stage):
        rows = self.dest.shape[0] // (2 * TILES)
        place = pl.ds(pl.multiple_of((2 * tile + self.core) * rows, rows), rows)
        source = self.source if stage == 0 else self.dest
        return pltpu.make_async_remote_copy(
            src_ref=source.at[place],
            dst_ref=self.dest.at[place],
            send_sem=self.sems.at[stage, tile],
            recv_sem=self.sems.at[2 + stage, tile],
            device_id=self.across if stage == 0 else self.sibling,
            device_id_type=MESH,
        )

    def send(self, tile):
        @pl.when(self.layer == self.sender)
        def _():
            self.copy(tile, 0).start()

    def receive(self, tile):
        @pl.when(self.layer != self.sender)
        def _():
            self.copy(tile, 0).wait_recv()
            self.copy(tile, 1).start()

    def complete(self, tile):
        @pl.when(self.layer != self.sender)
        def _():
            self.copy(tile, 1).wait_recv()

    def finish(self, tile):
        @pl.when(self.layer == self.sender)
        def _():
            self.copy(tile, 0).wait_send()

        @pl.when(self.layer != self.sender)
        def _():
            self.copy(tile, 1).wait_send()


class Opening:
    def __init__(self, starting, sender, late, refs, earlier, buffer, load_sems, sems):
        self.starting, self.sender, self.late, self.refs = starting, sender, late, refs
        self.buffer, self.load_sems, self.layer = buffer, load_sems, lax.axis_index("shard")
        self.across = Across(sender, earlier, buffer, sems)

    def load(self, ref, tile):
        rows = self.buffer.shape[0] // TILES
        place = pl.ds(tile * rows, rows)
        return pltpu.make_async_copy(ref.at[place], self.buffer.at[place], self.load_sems[tile])

    def start(self):
        for layer, ref in enumerate(self.refs):

            @pl.when(self.layer == layer)
            def _(ref=ref, layer=layer):
                for tile in range(TILES):
                    if not (self.starting and layer != self.sender and tile == self.late):
                        self.load(ref, tile).start()

    def send(self):
        if self.starting:
            self.across.send(self.late)

    def take(self, tile):
        if self.starting and tile == self.late:

            @pl.when(self.layer == self.sender)
            def _():
                self.load(self.refs[0], tile).wait()

            self.across.receive(tile)
            self.across.complete(tile)
        else:
            self.load(self.refs[0], tile).wait()

    def finish(self):
        if self.starting:
            self.across.finish(self.late)


def by_past(mode, body):
    if mode is not None:
        body(mode)
        return
    layer = lax.axis_index("shard")

    @pl.when(layer == 0)
    def _():
        body(True)

    @pl.when(layer != 0)
    def _():
        body(False)


FORWARD_LOADS = 7


def forward_kernel(mode, starting, ending, *refs):
    x_first, x_other, earlier, params, w_qkv, w_out, w_fc, w_proj, k_past, v_past = refs[:10]
    refs = refs[10:]
    (x_used, normed1, query, keys, values, mixed, lse, scaled2, inverse2, normed2, slope, act, out, passed) = refs[:14]
    refs = refs[14:]
    (x_v, wq_v, wo_v, wf_v, wp_v, k_v, v_v, hid_v, part_v, send_v, recv_v) = refs[:11]
    refs = refs[11:]
    (n1_v, q_v, m_v, lse_v, s2_v, i2_v, n2_v, sl_v, a_v, o_v) = refs[:10]
    load_sem, store_sem, send_sem, recv_sem, open_sem, across_sem = refs[10:]
    rows, width = x_v.shape
    half = q_v.shape[1]
    tile_rows = rows // TILES
    wide = a_v.shape[1]

    loads = Loads(load_sem)
    opening_sems = [load_sem.at[FORWARD_LOADS + tile] for tile in range(TILES)]
    opening = Opening(starting, 0, 1, (x_first, x_other), earlier, x_v, opening_sems, open_sem)
    opening.start()
    loads.start("qkv", w_qkv, wq_v)
    if mode is not False:
        loads.start("k", k_past, k_v.at[pl.ds(0, rows)])
        loads.start("v", v_past, v_v.at[pl.ds(0, rows)])
    loads.start("out", w_out, wo_v)
    loads.start("fc", w_fc, wf_v)
    loads.start("proj", w_proj, wp_v)
    greet_step(0)
    opening.send()
    exchange = Exchange(send_v, recv_v, send_sem, recv_sem)
    across = Across(0, o_v, passed, across_sem)
    stores = []

    def store(buffer, dest):
        copy = pltpu.make_async_copy(buffer, dest, store_sem.at[len(stores)])
        copy.start()
        stores.append(copy)

    def store_rows(tile, *pairs):
        place = pl.ds(tile * tile_rows, tile_rows)
        for buffer, dest in pairs:
            store(buffer.at[place], dest.at[place])

    def vector(row, start=0, size=None):
        return params[row : row + 1, start : start + (size or width)]

    def project(tile):
        span = pl.ds(tile * tile_rows, tile_rows)
        later = pl.ds(rows + tile * tile_rows, tile_rows)
        opening.take(tile)
        scaled, _ = norm_parts(x_v[span, :].astype(F32))
        normed = (scaled * vector(0) + vector(1)).astype(BF)
        n1_v[span, :] = normed
        if tile == 0:
            loads.wait("qkv")
        piece = jnp.dot(normed, wq_v[:, :half], preferred_element_type=F32)
        q_v[span, :] = (piece + vector(6, 0, half)).astype(BF)
        piece = jnp.dot(normed, wq_v[:, half : 2 * half], preferred_element_type=F32)
        k_v[later, :] = piece.astype(BF)
        piece = jnp.dot(normed, wq_v[:, 2 * half :], preferred_element_type=F32)
        v_v[later, :] = (piece + vector(6, half, half)).astype(BF)
        store_rows(tile, (x_v, x_used), (n1_v, normed1), (q_v, query))

    def attend(tile):
        span = pl.ds(tile * tile_rows, tile_rows)

        def attention(past):
            length = (rows if past else 0) + (tile + 1) * tile_rows
            reach = pl.ds(0 if past else rows, length)

            def pair(number, carry):
                lanes = pl.ds(pl.multiple_of(number * 128, 128), 128)
                key, value = k_v[reach, lanes], v_v[reach, lanes]
                pieces = []
                for head, part in enumerate(head_parts(q_v[span, lanes])):
                    scores = masked_scores(key, part * BF(HEAD_DIM**-0.5), length)
                    top = jnp.max(scores, axis=0, keepdims=True)
                    probs = jnp.exp(scores - top)
                    total = jnp.sum(probs, axis=0, keepdims=True)
                    lse_v[number, pl.ds(head, 1), span] = top + jnp.log(total)
                    piece = rows_product(value, probs.astype(BF))
                    piece = piece[head * HEAD_DIM : (head + 1) * HEAD_DIM]
                    pieces.append(piece * (1.0 / total))
                m_v[span, lanes] = jnp.transpose(jnp.concatenate(pieces, axis=0)).astype(BF)
                return carry

            lax.fori_loop(0, half // 128, pair, 0, unroll=mode is not None)

        by_past(mode, attention)
        partial = jnp.dot(m_v[span, :], wo_v[...], preferred_element_type=F32)
        part_v[tile] = partial
        exchange.give(tile, partial)

    def expand(tile):
        span = pl.ds(tile * tile_rows, tile_rows)
        hidden = x_v[span, :].astype(F32) + (part_v[tile] + exchange.take(tile)) + vector(2)
        hid_v[span, :] = hidden
        scaled, inverse = norm_parts(hidden)
        s2_v[span, :] = scaled.astype(BF)
        i2_v[span, :] = jnp.broadcast_to(inverse, (tile_rows, 128))
        normed = (scaled * vector(3) + vector(4)).astype(BF)
        n2_v[span, :] = normed
        store_rows(tile, (s2_v, scaled2), (i2_v, inverse2), (n2_v, normed2))
        chunk = width // 2
        for part in range(wide // chunk):
            columns = pl.ds(part * chunk, chunk)
            pre = jnp.dot(normed, wf_v[:, columns], preferred_element_type=F32)
            bias = vector(7 + part * chunk // width, part * chunk % width, chunk)
            activated, inclined = gelu_pair(pre + bias)
            a_v[span, columns] = activated.astype(BF)
            sl_v[span, columns] = inclined.astype(BF)
        store_rows(tile, (sl_v, slope), (a_v, act))
        partial = jnp.dot(a_v[span, :], wp_v[...], preferred_element_type=F32)
        part_v[TILES + tile] = partial
        exchange.give(TILES + tile, partial)

    def conclude(tile):
        span = pl.ds(tile * tile_rows, tile_rows)
        total = part_v[TILES + tile] + exchange.take(TILES + tile)
        o_v[span, :] = (hid_v[span, :] + total + vector(5)).astype(BF)
        store_rows(tile, (o_v, out))

    own_rows = pl.ds(rows, rows)
    project(0)
    if mode is not False:
        loads.wait("k", "v")
    loads.wait("out")
    attend(0)
    project(1)
    store(k_v.at[own_rows], keys)
    store(v_v.at[own_rows], values)
    loads.wait("fc", "proj")
    if ending:
        expand(0)
    attend(1)
    store(m_v, mixed)
    store(lse_v, lse)
    if ending:
        conclude(0)
        across.send(0)
        expand(1)
        across.receive(0)
    else:
        expand(0)
        expand(1)
        conclude(0)
    conclude(1)
    for copy in stores:
        copy.wait()
    exchange.finish(2 * TILES)
    opening.finish()
    if ending:
        across.complete(0)
        across.finish(0)


def step_sems(loads, stores):
    return [
        pltpu.SemaphoreType.DMA((loads,)),
        pltpu.SemaphoreType.DMA((stores,)),
        pltpu.SemaphoreType.DMA((2 * TILES,)),
        pltpu.SemaphoreType.DMA((2 * TILES,)),
        pltpu.SemaphoreType.DMA((4, TILES)),
        pltpu.SemaphoreType.DMA((4, TILES)),
    ]


def forward_step(mode, starting, ending, inputs, params, weights, past):
    rows, width = inputs[0].shape
    half = width // 2
    wide = weights[2].shape[1]
    pairs = half // 128
    tile_rows = rows // TILES
    spot = pl.BlockSpec(memory_space=pl.ANY)
    low = lambda columns: ((rows, columns), BF)
    outs = [
        low(width),
        low(width),
        low(half),
        low(half),
        low(half),
        low(half),
        ((pairs, 8, rows), F32),
        low(width),
        ((rows, 128), F32),
        low(width),
        low(wide),
        low(wide),
        low(width),
        low(width),
    ]
    scratch = [
        low(width),
        *((item.shape, BF) for item in weights),
        ((2 * rows, half), BF),
        ((2 * rows, half), BF),
        ((rows, width), F32),
        ((2 * TILES, tile_rows, width), F32),
        ((2 * TILES, tile_rows, width), BF),
        ((2 * TILES, tile_rows, width), BF),
        low(width),
        low(half),
        low(half),
        ((pairs, 8, rows), F32),
        low(width),
        ((rows, 128), F32),
        low(width),
        low(wide),
        low(wide),
        low(width),
    ]
    number = {False: 3, None: 4, True: 5}[mode]
    return pl.pallas_call(
        functools.partial(forward_kernel, mode, starting, ending),
        out_shape=[jax.ShapeDtypeStruct(*item) for item in outs],
        in_specs=[spot] * 3 + [pl.BlockSpec(memory_space=pltpu.VMEM)] + [spot] * 6,
        out_specs=[spot] * len(outs),
        scratch_shapes=[pltpu.VMEM(*item) for item in scratch]
        + step_sems(FORWARD_LOADS + TILES, 2 * len(outs)),
        compiler_params=pltpu.CompilerParams(
            collective_id=number, has_side_effects=True, vmem_limit_bytes=VMEM_LIMIT
        ),
        name="forward_step",
    )(*inputs, params, *weights, *past)


BACKWARD_LOADS = 17


def backward_kernel(mode, starting, ending, *refs):
    (g_first, g_other, earlier, x_used, params, w_qkv, w_out, w_fc, w_proj) = refs[:9]
    (query, keys, values, k_past, v_past, mixed, lse, scaled2, inverse2, slope, pend_k, pend_v) = refs[9:21]
    refs = refs[21:]
    (g_used, d_qkv, d_branch, d_pre, out, next_k, next_v, sums, passed) = refs[:9]
    refs = refs[9:]
    (g_v, x_v, wq_v, wo_v, wf_v, wp_v, q_v, k_v, v_v, m_v, lse_v, s2_v, i2_v, sl_v) = refs[:14]
    refs = refs[14:]
    (dk_v, dv_v, hid_v, part_v, send_v, recv_v, dqkv_v, db_v, dp_v, dm_v, o_v, sum_v) = refs[:12]
    load_sem, store_sem, send_sem, recv_sem, open_sem, across_sem = refs[12:]
    rows, width = x_v.shape
    half = q_v.shape[1]
    wide = dp_v.shape[1]
    tile_rows = rows // TILES
    own_rows, past_rows = pl.ds(rows, rows), pl.ds(0, rows)
    scale = HEAD_DIM**-0.5

    loads = Loads(load_sem)
    opening_sems = [load_sem.at[BACKWARD_LOADS + tile] for tile in range(TILES)]
    opening = Opening(starting, 1, 0, (g_first, g_other), earlier, g_v, opening_sems, open_sem)
    opening.start()
    loads.start("proj", w_proj, wp_v)
    loads.start("slope", slope, sl_v)
    loads.start("fc", w_fc, wf_v)
    loads.start("scaled2", scaled2, s2_v)
    loads.start("inverse2", inverse2, i2_v)
    loads.start("out", w_out, wo_v)
    loads.start("q", query, q_v)
    loads.start("k", keys, k_v.at[own_rows])
    loads.start("v", values, v_v.at[own_rows])
    if mode is not False:
        loads.start("k_past", k_past, k_v.at[past_rows])
        loads.start("v_past", v_past, v_v.at[past_rows])
    loads.start("mixed", mixed, m_v)
    loads.start("lse", lse, lse_v)
    if mode is not True:
        loads.start("pend_k", pend_k, dk_v.at[own_rows])
        loads.start("pend_v", pend_v, dv_v.at[own_rows])
    loads.start("qkv", w_qkv, wq_v)
    loads.start("x", x_used, x_v)
    greet_step(1)
    opening.send()
    exchange = Exchange(send_v, recv_v, send_sem, recv_sem)
    across = Across(1, o_v, passed, across_sem)
    stores = []

    def store(buffer, dest):
        copy = pltpu.make_async_copy(buffer, dest, store_sem.at[len(stores)])
        copy.start()
        stores.append(copy)

    def store_rows(tile, *pairs):
        place = pl.ds(tile * tile_rows, tile_rows)
        for buffer, dest in pairs:
            store(buffer.at[place], dest.at[place])

    def vector(row, start=0, size=None):
        return params[row : row + 1, start : start + (size or width)]

    sum_v[...] = jnp.zeros_like(sum_v)

    def tally(row, piece, start=0):
        place = (slice(row, row + 1), slice(start, start + piece.shape[1]))
        sum_v[place] += jnp.sum(piece, axis=0, keepdims=True)

    def contract(tile):
        span = pl.ds(tile * tile_rows, tile_rows)
        opening.take(tile)
        grad = g_v[span, :]
        chunk = width // 2
        for part in range(wide // chunk):
            columns = pl.ds(part * chunk, chunk)
            d_act = cols_product(grad, wp_v[columns, :])
            piece = (d_act * sl_v[span, columns].astype(F32)).astype(BF)
            dp_v[span, columns] = piece
            tally(7 + part * chunk // width, piece.astype(F32), part * chunk % width)
        partial = cols_product(dp_v[span, :], wf_v[...])
        part_v[tile] = partial
        exchange.give(tile, partial)
        tally(5, grad.astype(F32))
        store_rows(tile, (g_v, g_used), (dp_v, d_pre))

    def branch(tile):
        span = pl.ds(tile * tile_rows, tile_rows)
        d_normed = part_v[tile] + exchange.take(tile)
        scaled = s2_v[span, :].astype(F32)
        tally(3, d_normed * scaled)
        tally(4, d_normed)
        d_hidden = g_v[span, :].astype(F32) + norm_backward(
            d_normed, scaled, i2_v[span, 0:1], vector(3)
        )
        hid_v[span, :] = d_hidden
        low = d_hidden.astype(BF)
        db_v[span, :] = low
        tally(2, low.astype(F32))
        dm_v[span, :] = cols_product(low, wo_v[...]).astype(BF)
        store_rows(tile, (db_v, d_branch))

    def attend(tile):
        span = pl.ds(tile * tile_rows, tile_rows)

        def attention(past):
            if past and tile == TILES - 1:
                dk_v[...] = jnp.zeros_like(dk_v)
                dv_v[...] = jnp.zeros_like(dv_v)
            length = (rows if past else 0) + (tile + 1) * tile_rows
            reach = pl.ds(0 if past else rows, length)

            def pair(number, carry):
                lanes = pl.ds(pl.multiple_of(number * 128, 128), 128)
                key, value = k_v[reach, lanes], v_v[reach, lanes]
                grads = dm_v[span, lanes]
                products = jnp.transpose(grads.astype(F32) * m_v[span, lanes].astype(F32))
                queries, grads = head_parts(q_v[span, lanes]), head_parts(grads)
                d_query = []
                d_key = d_value = None
                for head in range(2):
                    take = slice(head * HEAD_DIM, (head + 1) * HEAD_DIM)
                    scaled_query = queries[head] * BF(scale)
                    scores = masked_scores(key, scaled_query, length)
                    weights = jnp.exp(scores - lse_v[number, pl.ds(head, 1), span])
                    d_probs = cols_product(value, grads[head])
                    delta = jnp.sum(products[take], axis=0, keepdims=True)
                    d_scores = (weights * (d_probs - delta)).astype(BF)
                    one = jnp.dot(weights.astype(BF), grads[head], preferred_element_type=F32)
                    two = jnp.dot(d_scores, scaled_query, preferred_element_type=F32)
                    d_value = one if head == 0 else d_value + one
                    d_key = two if head == 0 else d_key + two
                    d_query.append(rows_product(key, d_scores)[take])
                dk_v[reach, lanes] += d_key
                dv_v[reach, lanes] += d_value
                d_query = jnp.transpose(jnp.concatenate(d_query, axis=0) * scale)
                dqkv_v[span, lanes] = d_query.astype(BF)
                return carry

            lax.fori_loop(0, half // 128, pair, 0, unroll=mode is not None)

        by_past(mode, attention)

    def project(tile):
        span = pl.ds(tile * tile_rows, tile_rows)
        later = pl.ds(rows + tile * tile_rows, tile_rows)
        dqkv_v[span, half : 2 * half] = dk_v[later, :].astype(BF)
        dqkv_v[span, 2 * half :] = dv_v[later, :].astype(BF)
        piece = dqkv_v[span, :]
        partial = cols_product(piece, wq_v[...])
        part_v[TILES + tile] = partial
        exchange.give(TILES + tile, partial)
        tally(6, piece[:, :half].astype(F32))
        tally(6, piece[:, 2 * half :].astype(F32), half)
        store_rows(tile, (dqkv_v, d_qkv))

    def conclude(tile):
        span = pl.ds(tile * tile_rows, tile_rows)
        scaled, inverse = norm_parts(x_v[span, :].astype(F32))
        d_normed = part_v[TILES + tile] + exchange.take(TILES + tile)
        tally(0, d_normed * scaled)
        tally(1, d_normed)
        d_inputs = hid_v[span, :] + norm_backward(d_normed, scaled, inverse, vector(0))
        o_v[span, :] = d_inputs.astype(BF)
        store_rows(tile, (o_v, out))

    loads.wait("proj", "slope", "fc")
    contract(1)
    if not starting:
        contract(0)
    loads.wait("scaled2", "inverse2", "out")
    branch(1)
    loads.wait("q", "k", "v", "mixed", "lse")
    if mode is not False:
        loads.wait("k_past", "v_past")
    if mode is not True:
        loads.wait("pend_k", "pend_v")
    attend(1)
    loads.wait("qkv", "x")
    if starting and not ending:
        contract(0)
    project(1)
    if starting and ending:
        contract(0)
    else:
        branch(0)
    if ending:
        conclude(1)
        across.send(1)
    if starting and ending:
        branch(0)
    attend(0)
    if mode is not False:
        store(dk_v.at[past_rows], next_k)
        store(dv_v.at[past_rows], next_v)
    project(0)
    if ending:
        across.receive(1)
    else:
        conclude(1)
    conclude(0)
    store(sum_v, sums)
    for copy in stores:
        copy.wait()
    exchange.finish(2 * TILES)
    opening.finish()
    if ending:
        across.complete(1)
        across.finish(1)


def backward_step(mode, starting, ending, grads, inputs, params, weights, kept, pending):
    rows, width = inputs.shape
    half = width // 2
    wide = weights[2].shape[1]
    pairs = half // 128
    tile_rows = rows // TILES
    spot = pl.BlockSpec(memory_space=pl.ANY)
    low = lambda columns: ((rows, columns), BF)
    outs = [
        low(width),
        low(3 * half),
        low(width),
        low(wide),
        low(width),
        ((rows, half), F32),
        ((rows, half), F32),
        ((16, width), F32),
        low(width),
    ]
    scratch = [
        low(width),
        low(width),
        *((item.shape, BF) for item in weights),
        low(half),
        ((2 * rows, half), BF),
        ((2 * rows, half), BF),
        low(half),
        ((pairs, 8, rows), F32),
        low(width),
        ((rows, 128), F32),
        low(wide),
        ((2 * rows, half), F32),
        ((2 * rows, half), F32),
        ((rows, width), F32),
        ((2 * TILES, tile_rows, width), F32),
        ((2 * TILES, tile_rows, width), BF),
        ((2 * TILES, tile_rows, width), BF),
        low(3 * half),
        low(width),
        low(wide),
        low(half),
        low(width),
        ((16, width), F32),
    ]
    number = {True: 6, None: 7, False: 8}[mode]
    return pl.pallas_call(
        functools.partial(backward_kernel, mode, starting, ending),
        out_shape=[jax.ShapeDtypeStruct(*item) for item in outs],
        in_specs=[spot] * 4 + [pl.BlockSpec(memory_space=pltpu.VMEM)] + [spot] * 16,
        out_specs=[spot] * len(outs),
        scratch_shapes=[pltpu.VMEM(*item) for item in scratch]
        + step_sems(BACKWARD_LOADS + TILES, 2 * len(outs)),
        compiler_params=pltpu.CompilerParams(
            collective_id=number, has_side_effects=True, vmem_limit_bytes=VMEM_LIMIT
        ),
        name="backward_step",
    )(*grads, inputs, params, *weights, *kept, *pending)


def shards(
    tokens,
    cotangent,
    attn_gain,
    attn_shift,
    qkv_weight,
    query_bias,
    value_bias,
    out_weight,
    out_bias,
    mlp_gain,
    mlp_shift,
    fc_weight,
    fc_bias,
    proj_weight,
    proj_bias,
):
    size = lax.axis_size("replica")
    micro = tokens.shape[1]
    assert micro == 2
    *outer, params, w_qkv, w_fc, w_out, w_proj = fetch_inputs(
        tokens[0],
        cotangent[0],
        qkv_weight[0],
        fc_weight[0],
        out_weight[0],
        proj_weight[0],
        (
            attn_gain,
            attn_shift,
            out_bias,
            mlp_gain,
            mlp_shift,
            proj_bias,
            query_bias,
            value_bias,
            fc_bias,
        ),
    )
    weights = (w_qkv, w_out, w_fc, w_proj)

    received, kept_list, outputs, past, got = [], [], [], (w_out, w_out), outer[0]
    for step in range(micro + 1):
        output = outputs[-1] if outputs else outer[0]
        used, normed1, *state, normed2, slope, act, output, got = forward_step(
            (False, None, True)[step],
            step > 0,
            step < micro,
            (outer[min(step, micro - 1)], got, output),
            params,
            weights,
            past,
        )
        query, keys, values, mixed, lse, scaled2, inverse2 = state
        outputs.append(output)
        received.append(used)
        kept = (query, keys, values, *past, mixed, lse, scaled2, inverse2, slope)
        kept_list.append((kept, normed1, normed2, act))
        past = (keys, values)

    pending = (params, params)
    grad_received, terms_list, results, tallies, got = [], [], [], [], outer[1]
    for step in range(micro + 1):
        last = micro - step
        kept, normed1, normed2, act = kept_list[last]
        result = results[-1] if results else outer[1]
        grad, d_qkv, d_branch, d_pre, result, *pending, vector, got = backward_step(
            (True, None, False)[step],
            step > 0,
            step < micro,
            (got, outer[max(micro - 1 - step, 0)], result),
            received[last],
            params,
            weights,
            kept,
            pending,
        )
        results.append(result)
        grad_received.append(grad)
        tallies.append(vector)
        terms_list.append((normed1, d_qkv, kept[5], d_branch, normed2, d_pre, act, grad))
    def factor(number):
        return tuple(terms_list[step][number] for step in (2, 1, 0))

    factors = [(factor(i), factor(i + 1)) for i in (0, 4, 2, 6)]
    reduced = ring_scatter(factors, tallies, size)
    reduced, packed = reduced[:4], reduced[4]
    near = []
    for i in range(micro):
        near += [outputs[i], outputs[i + 1], received[i + 1]]
        near += [results[micro - i], results[micro - 1 - i], grad_received[micro - i]]
    *gathered, activations, input_grads = ring_gather(reduced, (3, 1), near, size)
    *vectors, activations, input_grads = finish(packed, (activations, input_grads))
    qkv_grad, fc_grad, out_grad, proj_grad = (
        item.reshape(1, -1, item.shape[-1]).astype(F32) for item in gathered
    )
    return (
        activations[None, None],
        input_grads[None, None],
        vectors[0],
        vectors[1],
        qkv_grad,
        vectors[6],
        vectors[7],
        out_grad,
        vectors[2],
        vectors[3],
        vectors[4],
        fc_grad,
        vectors[8],
        proj_grad,
        vectors[5],
    )


def solution(mesh):
    block = P("replica", None, "shard", None)
    layers = P("section", "replica", None, "shard", None)
    vector = P("section", "shard")
    matrix = P("section", "shard", None)
    kinds = (
        vector,
        vector,
        matrix,
        vector,
        vector,
        matrix,
        vector,
        vector,
        vector,
        matrix,
        vector,
        matrix,
        vector,
    )
    return jax.shard_map(
        shards,
        mesh=mesh,
        in_specs=(block, block) + kinds,
        out_specs=(layers, layers) + kinds,
        check_vma=False,
    )
```
